32 devices in a mesh: fsdp: 4 (over y, core), ctx: 8 (over z, x).
Axes of the slice: x: 2, y: 2, z: 4, core: 2. Of those that a mesh axis runs over, the one named last changes fastest.
Arguments:
- inputs: bfloat16 [4, 4096, 1536], P('fsdp', 'ctx'), may hold values from -8 to 8
- segment_ids: int32 [4, 4096], P('fsdp', 'ctx'), may hold values from 0 to 3, never falling along the last dimension, each value on 1 to 2048 neighbouring positions
- out_grad: bfloat16 [4, 4096, 1536], P('fsdp', 'ctx'), may hold values from -6 to 6
- in_matrix: bfloat16 [1536, 6448], P('fsdp'), may hold values from -0.15625 to 0.15625
- out_matrix: bfloat16 [3072, 1536], P('fsdp'), may hold values from -0.109375 to 0.109375
- conv_taps: bfloat16 [3328, 4], P('fsdp'), may hold values from -3 to 3
- conv_bias: bfloat16 [3328], P('fsdp'), may hold values from -2.5 to 2.5
- dt_bias: bfloat16 [48], P('fsdp'), may hold values from -6 to -2
- decay_log: bfloat16 [48], P('fsdp'), may hold values from -7 to 2.5
- skip_scale: bfloat16 [48], P('fsdp'), may hold values from 0.5 to 2
- mixer_gain: bfloat16 [3072], P('fsdp'), may hold values from 0.5 to 1.5
- input_gain: bfloat16 [1536], P('fsdp'), may hold values from 0.5 to 1.5
Outputs:
- block_out: bfloat16 [4, 4096, 1536], P('fsdp', 'ctx')
- input_grad: bfloat16 [4, 4096, 1536], P('fsdp', 'ctx')
- in_matrix_grad: float32 [1536, 6448], P('fsdp')
- out_matrix_grad: float32 [3072, 1536], P('fsdp')
- conv_taps_grad: float32 [3328, 4], P('fsdp')
- conv_bias_grad: float32 [3328], P('fsdp')
- dt_bias_grad: float32 [48], P('fsdp')
- decay_log_grad: float32 [48], P('fsdp')
- skip_scale_grad: float32 [48], P('fsdp')
- mixer_gain_grad: float32 [3072], P('fsdp')
- input_gain_grad: float32 [1536], P('fsdp')
- rms_stats: float32 [2], replicated
The draws below stay inside these ranges and needn't reach their ends.
Inputs may be any that keep to these rules, and one draw needn't show every extreme that they name: `segment_ids`: along each sequence the numbers never fall; a run of equal numbers is one document; every number of 0 to 3 is used, and the longest document has exactly 2048 tokens.
All inputs are finite; a program needn't handle non-finite values.
Results may differ from the reference program's by a relative error of at most 0.015.
Values may be sent and summed in bfloat16 or wider, within the bound.
A program may use at most 320 MiB of HBM per device.

```python
import math
import jax
import jax.numpy as jnp
import numpy as np
from jax import lax

D = 1536
HEADS = 48
HDIM = 64
STATE = 128
CONV = 4
GROUP = 256
INNER = 3072
XBC = 3328
PROJ = 6448
SEQS = 4
LEN = 4096
DOCS = 4
LONGEST = 2048


def draw_inputs(key, part):
    position = jnp.arange(LEN, dtype=jnp.float32) / LEN
    base_draw = jnp.clip(jax.random.normal(key, (SEQS, LEN, D), jnp.float32), -4.0, 4.0)
    row_scale = 0.6 * 3.0 ** position
    return (base_draw * row_scale[None, :, None]).astype(jnp.bfloat16)


def steps_of(stream_key, dims, split, smallest, top_value):
    def one(dim, blocks):
        steps = jax.random.uniform(jax.random.fold_in(jax.random.fold_in(stream_key, 6), dim), (blocks,), jnp.float32, smallest / len(split), top_value / len(split))
        return jnp.repeat(jnp.exp(steps), dims[dim] // blocks).reshape((-1,) + (1,) * (len(dims) - dim - 1))

    loudness = one(*split[0])
    for cut in split[1:]:
        loudness = loudness * one(*cut)
    return loudness


def length_profile(amount, total, bound, skew):
    loads = [(1 << 20) // math.isqrt(rank ** skew) + 1 for rank in range(2, amount + 1)]
    spare, holding = total - bound - (amount - 1), [1] * (amount - 1)
    while spare > 0:
        free = [i for i in range(amount - 1) if holding[i] < bound]
        pool, remaining = sum([loads[i] for i in free]), spare
        for i in free:
            more = min(bound - holding[i], max(1, remaining * loads[i] // pool), spare)
            holding[i] = holding[i] + more
            spare = spare - more
    return np.array([bound] + holding)


def ragged_sizes(own_key, number_of, total, most, lean):
    if number_of == 2:
        one = jax.random.randint(own_key, (), max(1, total - most), min(most, total - 1) + 1)
        return jnp.stack([one, total - one])
    lengths = jnp.asarray(length_profile(number_of, total, most, lean), jnp.int32)
    couples = (number_of - 1) // 2
    source_of, sink = lengths[1:1 + 2 * couples:2], lengths[2:2 + 2 * couples:2]
    slack = jnp.minimum(source_of - 1, most - sink)
    passed = jax.random.randint(jax.random.fold_in(own_key, 1), (couples,), 0, 1 << 20) % (slack + 1)
    lengths = lengths.at[1:1 + 2 * couples:2].set(source_of - passed).at[2:2 + 2 * couples:2].set(sink + passed)
    return lengths[jax.random.permutation(jax.random.fold_in(own_key, 2), number_of)]


def gaussian(rng, dims, width, reach, split=(), held_as=jnp.bfloat16):
    result = jax.random.normal(rng, dims, jnp.float32) * width
    if len(split) > 0:
        result = steps_of(rng, dims, split, -0.22, 0.18) * result
    return jnp.clip(result, min=-reach, max=reach).astype(held_as)


def setup_inputs(seed: int = 0) -> dict:
    arg_keys = jax.random.split(jax.random.key(seed), 13)
    inputs = draw_inputs(jax.random.fold_in(arg_keys[12], 71), 0)
    segment_ids = jax.vmap(lambda own: jnp.searchsorted(jnp.cumsum(ragged_sizes(own, DOCS, LEN, LONGEST, 2)), jnp.arange(LEN), side="right"))(jax.random.split(arg_keys[1], SEQS)).reshape((SEQS, LEN)).astype(jnp.int32)
    out_grad = gaussian(arg_keys[2], (SEQS, LEN, D), 1.0, 6.0, ((0, 4), (1, 8)))
    in_matrix = gaussian(arg_keys[3], (D, PROJ), D ** -0.5, 0.15625, ((0, 4),))
    out_matrix = gaussian(arg_keys[4], (INNER, D), INNER ** -0.5, 0.109375, ((0, 4),))
    conv_taps = gaussian(arg_keys[5], (XBC, CONV), CONV ** -0.5, 3.0, ((0, 4),))
    conv_bias = gaussian(arg_keys[6], (XBC,), 0.3, 2.5, ((0, 4),))
    dt_bias = jnp.clip(-6.0 + 4.0 * jax.random.uniform(arg_keys[7], (HEADS,), jnp.float32) ** steps_of(arg_keys[7], (HEADS,), ((0, 4),), -0.2, 0.2), -6.0, -2.0).astype(jnp.bfloat16)
    decay_log = jnp.clip(-7.0 + 9.5 * jax.random.uniform(arg_keys[8], (HEADS,), jnp.float32) ** steps_of(arg_keys[8], (HEADS,), ((0, 4),), -0.2, 0.2), -7.0, 2.5).astype(jnp.bfloat16)
    skip_scale = jnp.clip(0.5 + 1.5 * jax.random.uniform(arg_keys[9], (HEADS,), jnp.float32) ** steps_of(arg_keys[9], (HEADS,), ((0, 4),), -0.2, 0.2), 0.5, 2.0).astype(jnp.bfloat16)
    mixer_gain = jnp.clip(1.0 + 0.1 * jax.random.normal(arg_keys[10], (INNER,), jnp.float32), 0.5, 1.5).astype(jnp.bfloat16)
    input_gain = jnp.clip(1.0 + 0.1 * jax.random.normal(arg_keys[11], (D,), jnp.float32), 0.5, 1.5).astype(jnp.bfloat16)
    return dict(inputs=inputs, segment_ids=segment_ids, out_grad=out_grad, in_matrix=in_matrix, out_matrix=out_matrix, conv_taps=conv_taps, conv_bias=conv_bias, dt_bias=dt_bias, decay_log=decay_log, skip_scale=skip_scale, mixer_gain=mixer_gain, input_gain=input_gain)


epsilon = 1e-05
precise = lax.Precision.HIGHEST

@jax.custom_vjp
def low(v):
    return lax.optimization_barrier(v.astype(jnp.bfloat16)).astype(jnp.float32)

@jax.custom_vjp
def low_back(v):
    return v

def low_keep(v):
    return (low(v), None)

def low_pass(kept, grad):
    return (grad,)

def back_keep(v):
    return (v, None)

def back_low(kept, grad):
    return (low(grad),)
low.defvjp(low_keep, low_pass)
low_back.defvjp(back_keep, back_low)

def block_step(carry_pair, sliced):
    carried, seg_before, offset = carry_pair
    xblock, bblock, cblock, dblock, lblock, sblock = sliced
    block_len = sblock.shape[0]
    running = jnp.cumsum(lblock, axis=0)
    rowpos = lax.broadcasted_iota(jnp.int32, (block_len, block_len), 0)
    colpos = lax.broadcasted_iota(jnp.int32, (block_len, block_len), 1)
    allowed = (sblock[:, None] == sblock[None, :]) & (colpos <= rowpos)
    log_gap = running.T[:, :, None] - running.T[:, None, :]
    decays = jnp.exp(jnp.where(allowed[None], log_gap, -1e+30))
    scores = jnp.dot(cblock, bblock.T, precision=precise)
    mixing = decays * scores[None] * dblock.T[:, None, :]
    y_diag = jnp.einsum('hts,shp->thp', mixing, xblock, precision=precise)
    carry_in = (sblock == seg_before).astype(jnp.float32)
    y_off = (jnp.exp(running) * carry_in[:, None])[:, :, None] * jnp.einsum('tn,hpn->thp', cblock, carried, precision=precise)
    final_log = running[block_len - 1]
    tail_weight = jnp.exp(final_log[None, :] - running) * (sblock == sblock[block_len - 1]).astype(jnp.float32)[:, None] * dblock
    retain = jnp.exp(final_log) * (sblock[block_len - 1] == seg_before).astype(jnp.float32)
    carried = retain[:, None, None] * carried + jnp.einsum('sh,shp,sn->hpn', tail_weight, xblock, bblock, precision=precise)
    return ((carried, sblock[block_len - 1], offset + final_log), (y_diag + y_off, running + offset[None, :]))

def scan_ssd(values, b_rows, c_rows, dt_rows, log_decay, seg_ids, seg_start):
    length = seg_ids.shape[0]
    blocks = length // GROUP
    sliced = (values.reshape(blocks, GROUP, HEADS, HDIM), b_rows.reshape(blocks, GROUP, STATE), c_rows.reshape(blocks, GROUP, STATE), dt_rows.reshape(blocks, GROUP, HEADS), log_decay.reshape(blocks, GROUP, HEADS), seg_ids.reshape(blocks, GROUP))
    initial = (jnp.zeros((HEADS, HDIM, STATE), jnp.float32), seg_start, jnp.zeros((HEADS,), jnp.float32))
    finish, (outputs, running) = lax.scan(jax.checkpoint(block_step), initial, sliced)
    return (outputs.reshape(length, HEADS, HDIM), running.reshape(length, HEADS), finish[0])

def mixer_front(ext_rows, dt_raw, conv_taps, conv_bias, dt_bias, decay_log, seg_ext, seg_ids, seg_start):
    length = seg_ids.shape[0]
    summed = jnp.broadcast_to(conv_bias, (length, conv_bias.shape[0]))
    for tap_index in range(CONV):
        same_doc = (seg_ext[tap_index:tap_index + length] == seg_ids).astype(jnp.float32)
        summed = summed + conv_taps[:, tap_index] * ext_rows[tap_index:tap_index + length] * same_doc[:, None]
    active = jax.nn.silu(summed)
    values = active[:, :INNER].reshape(length, HEADS, HDIM)
    b_rows = active[:, INNER:INNER + STATE]
    c_rows = active[:, INNER + STATE:]
    dt_rows = jax.nn.softplus(dt_raw + dt_bias)
    log_decay = -dt_rows * jnp.exp(decay_log)
    y_local, running, carried = scan_ssd(values, b_rows, c_rows, dt_rows, log_decay, seg_ids, seg_start)
    retain = jnp.exp(running[length - 1]) * (seg_ids[length - 1] == seg_start).astype(jnp.float32)
    return (values, c_rows, running, y_local, carried, retain)

def mixer_tail(values, c_rows, running, y_local, carried_in, gate_part, skip_scale, mixer_gain, carry_flag):
    length = gate_part.shape[0]
    incoming = jnp.einsum('tn,hpn->thp', c_rows, carried_in, precision=precise)
    weights = jnp.exp(running) * carry_flag[:, None]
    mixed_ssd = y_local + weights[:, :, None] * incoming + skip_scale[None, :, None] * values
    gated = mixed_ssd.reshape(length, INNER) * jax.nn.silu(gate_part)
    return gated * lax.rsqrt(lax.optimization_barrier(jnp.mean(gated * gated, axis=-1, keepdims=True)) + epsilon) * mixer_gain

def block_forward(units, weights, seg_ids):
    in_matrix, out_matrix, conv_taps, conv_bias, dt_bias, decay_log, skip_scale, mixer_gain, input_gain = weights
    length = units.shape[0]
    inv_rms = lax.rsqrt(lax.optimization_barrier(jnp.mean(units * units, axis=-1, keepdims=True)) + epsilon)
    normed = low(units * inv_rms * input_gain)
    projected = low_back(low(jnp.dot(normed, in_matrix, precision=precise)))
    gate_part = projected[:, :INNER]
    conv_input = projected[:, INNER:INNER + XBC]
    dt_raw = projected[:, INNER + XBC:]
    ext_rows = jnp.concatenate([jnp.zeros((CONV - 1, XBC), jnp.float32), conv_input], axis=0)
    seg_ext = jnp.concatenate([jnp.full((CONV - 1,), -1, jnp.int32), seg_ids], axis=0)
    seg_start = jnp.array(-1, jnp.int32)
    values, c_rows, running, y_local, carried, retain = mixer_front(ext_rows, dt_raw, conv_taps, conv_bias, dt_bias, decay_log, seg_ext, seg_ids, seg_start)
    zero_state = jnp.zeros((HEADS, HDIM, STATE), jnp.float32)
    no_flag = jnp.zeros((length,), jnp.float32)
    mixer_out = low(mixer_tail(values, c_rows, running, y_local, zero_state, gate_part, skip_scale, mixer_gain, no_flag))
    mixed = jnp.dot(mixer_out, out_matrix, precision=precise)
    return (units + mixed, mixed)

def reference(inputs, segment_ids, out_grad, in_matrix, out_matrix, conv_taps, conv_bias, dt_bias, decay_log, skip_scale, mixer_gain, input_gain):
    weights = tuple((tensor.astype(jnp.float32) for tensor in (in_matrix, out_matrix, conv_taps, conv_bias, dt_bias, decay_log, skip_scale, mixer_gain, input_gain)))
    zero_grads = jax.tree.map(jnp.zeros_like, weights)

    def one_sequence(running_sum, sliced):
        grad_sum, square_sums = running_sum
        rows_in, seg_ids, cot_rows = sliced
        units = rows_in.astype(jnp.float32)
        summed_out, back_fn, mixed = jax.vjp(lambda first_arg, second: block_forward(first_arg, second, seg_ids), units, weights, has_aux=True)
        d_units, d_weights = back_fn(cot_rows.astype(jnp.float32))
        grad_sum = jax.tree.map(jnp.add, grad_sum, d_weights)
        square_sums = square_sums + jnp.stack([jnp.sum(summed_out * summed_out), jnp.sum(mixed * mixed)])
        return ((grad_sum, square_sums), (summed_out.astype(jnp.bfloat16), d_units.astype(jnp.bfloat16)))
    (grad_sum, square_sums), (block_out, input_grad) = lax.scan(one_sequence, (zero_grads, jnp.zeros((2,), jnp.float32)), (inputs, segment_ids, out_grad))
    entries = SEQS * LEN * D
    rms_stats = jnp.sqrt(square_sums / entries)
    return (block_out, input_grad, grad_sum[0], grad_sum[1], grad_sum[2], grad_sum[3], grad_sum[4], grad_sum[5], grad_sum[6], grad_sum[7], grad_sum[8], rms_stats)
```

```python
import functools

import jax
import jax.numpy as jnp
from jax import lax
from jax.experimental import pallas as pl
from jax.experimental.pallas import tpu as pltpu
from jax.sharding import PartitionSpec as P

D = 1536
HEADS = 48
HDIM = 64
STATE = 128
CONV = 4
INNER = 3072
XBC = 3328
PROJ = 6448

BLK = 256
GROUP = BLK // HDIM
STEPS = INNER // BLK
Q = 128
PAD = 8

epsilon = 1e-05
F32, BF16 = jnp.float32, jnp.bfloat16
HIGHEST = lax.Precision.HIGHEST
VMEM_LIMIT = 60 * 1024 * 1024


def dot(a, b):
    return jnp.dot(a, b, preferred_element_type=F32)


def dot_nt(a, b):
    return lax.dot_general(a, b, (((1,), (1,)), ((), ())), preferred_element_type=F32)


def iota(shape, dim):
    return lax.broadcasted_iota(jnp.int32, shape, dim)


def sigmoid(v):
    return 1.0 / (1.0 + jnp.exp(-v))


def in_two(a):
    high = a.astype(BF16)
    return high, (a - high.astype(F32)).astype(BF16)


def chosen(step):
    columns = step * GROUP + lax.shift_right_logical(iota((128, BLK), 1), 6)
    return (iota((128, BLK), 0) == columns).astype(BF16)


def chosen_back(step):
    heads = step * GROUP + lax.shift_right_logical(iota((BLK, 128), 0), 6)
    return (iota((BLK, 128), 1) == heads).astype(BF16)


def widen(per_head, select):
    high, low = in_two(per_head)
    return dot(high, select) + dot(low, select)


def halves(pair):
    first = iota(pair.shape, 1) < HDIM
    zero = jnp.zeros_like(pair)
    return jnp.concatenate([jnp.where(first, pair, zero), jnp.where(first, zero, pair)], axis=0)


def both(mask):
    return jnp.concatenate([mask, mask], axis=1)


def conv_rows(ext_ref, seg_ref, taps_ref, start, rows):
    own = seg_ref[start + PAD : start + PAD + rows, :]
    total = taps_ref[4:5, :] + taps_ref[3:4, :] * ext_ref[start + PAD : start + PAD + rows, :]
    for back in range(1, CONV):
        at = start + PAD - back
        same = both(seg_ref[at : at + rows, :] == own)
        total = total + jnp.where(
            same, taps_ref[3 - back : 4 - back, :] * ext_ref[at : at + rows, :], 0.0
        )
    return total


def chunk_flags(seg_ref, k):
    own = seg_ref[PAD + k * Q : PAD + (k + 1) * Q, :]
    before = seg_ref[PAD + k * Q - 1 : PAD + k * Q, :]
    last = seg_ref[PAD + (k + 1) * Q - 1 : PAD + (k + 1) * Q, :]
    return (own == before).astype(F32), (own == last).astype(F32)


def masked_scores(seg_ref, row_ref, b_rows, c_rows, k):
    own = seg_ref[PAD + k * Q : PAD + (k + 1) * Q, :]
    row = row_ref[0:1, k * Q : (k + 1) * Q]
    keep = (own == row) & (iota((Q, Q), 1) <= iota((Q, Q), 0))
    return jnp.where(keep, dot_nt(c_rows, b_rows), 0.0)


def front_kernel(
    x_ref, bc_ref, dtraw_ref, halo_ref, halo_bc_ref, taps_ref, taps_bc_ref, heads_ref, seg_ref, row_ref,
    xs_ref, y_ref, state_ref, b_ref, c_ref, dt_ref, run_ref, in_ref, keep_ref,
    ext, scores, run_t, b_t, enter, leave,
):
    step = pl.program_id(0)
    length = x_ref.shape[0]
    chunks = length // Q

    @pl.when(step == 0)
    def _():
        ext[0:PAD, :] = halo_bc_ref[...]
        ext[PAD:, :] = bc_ref[...].astype(F32)
        lane = iota((Q, 128), 1)
        lower = (iota((Q, Q), 1) <= iota((Q, Q), 0)).astype(F32)
        offset = jnp.zeros((1, 128), F32)
        for k in range(chunks):
            rows = slice(k * Q, (k + 1) * Q)
            total = conv_rows(ext, seg_ref, taps_bc_ref, k * Q, Q)
            active = total * sigmoid(total)
            b_rows, c_rows = active[:, :STATE], active[:, STATE:].astype(BF16)
            b_t[:, rows] = b_rows.T.astype(BF16)
            b_rows = b_rows.astype(BF16)
            b_ref[rows, :] = b_rows
            c_ref[rows, :] = c_rows
            scores[rows, :] = masked_scores(seg_ref, row_ref, b_rows, c_rows, k)
            raw = jnp.where(lane < HEADS, dtraw_ref[rows, :128].astype(F32), 0.0) + heads_ref[0:1, :]
            dt = jnp.maximum(raw, 0.0) + jnp.log1p(jnp.exp(-jnp.abs(raw)))
            log_decay = -dt * jnp.exp(heads_ref[1:2, :])
            running = jnp.dot(lower, log_decay, precision=HIGHEST, preferred_element_type=F32)
            dt_ref[rows, :] = dt
            run_ref[rows, :] = running
            run_t[k] = running.T
            carry, tail = chunk_flags(seg_ref, k)
            enter[rows, :] = jnp.exp(running) * carry
            leave[rows, :] = jnp.exp(running[Q - 1 : Q, :] - running) * tail
            same = (seg_ref[PAD + k * Q : PAD + (k + 1) * Q, :] == seg_ref[PAD - 1 : PAD, :]).astype(F32)
            whole = jnp.exp(running + offset) * same
            in_ref[rows, :] = whole
            offset = offset + running[Q - 1 : Q, :]
        keep_ref[...] = jnp.broadcast_to(whole[Q - 1 : Q, :], (8, 128))

    ext[0:PAD, :] = halo_ref[...]
    ext[PAD:, :] = x_ref[...].astype(F32)
    select = chosen(step)
    state = jnp.zeros((STATE, BLK), F32)
    for k in range(chunks):
        rows = slice(k * Q, (k + 1) * Q)
        total = conv_rows(ext, seg_ref, taps_ref, k * Q, Q)
        values = total * sigmoid(total)
        xs_ref[rows, :] = values.astype(BF16)
        scaled = (values * widen(dt_ref[rows, :], select)).astype(BF16)
        entering = widen(enter[rows, :], select)
        running = pltpu.roll(run_ref[rows, :], lax.rem(128 - step * GROUP, 128), 1)
        parts = []
        for pair in range(2):
            mixing = []
            for one in range(2):
                head = 2 * pair + one
                gap = running[:, head : head + 1] - run_t[k, pl.ds(step * GROUP + head, 1), :]
                mixing.append((jnp.exp(jnp.minimum(gap, 0.0)) * scores[rows, :]).astype(BF16))
            parts.append(
                dot(jnp.concatenate(mixing, axis=1), halves(scaled[:, pair * 128 : (pair + 1) * 128]))
            )
        inside = jnp.concatenate(parts, axis=1)
        y_ref[rows, :] = (inside + entering * dot(c_ref[rows, :], state.astype(BF16))).astype(BF16)
        weighted = (scaled.astype(F32) * widen(leave[rows, :], select)).astype(BF16)
        state = entering[Q - 1 : Q, :] * state + dot(b_t[:, rows], weighted)
    state_ref[...] = state.astype(BF16)


def front(projected, halo, taps, heads, seg_lanes, seg_row):
    length = projected.shape[0]
    whole = lambda *shape: pl.BlockSpec(shape, lambda j: (0,) * len(shape))
    columns = lambda rows, at: pl.BlockSpec((rows, BLK), at)
    return pl.pallas_call(
        front_kernel,
        grid=(STEPS,),
        in_specs=[
            columns(length, lambda j: (0, STEPS + j)),
            columns(length, lambda j: (0, 2 * STEPS)),
            columns(length, lambda j: (0, 2 * STEPS + 1)),
            columns(PAD, lambda j: (0, j)),
            columns(PAD, lambda j: (0, STEPS)),
            columns(8, lambda j: (0, j)),
            columns(8, lambda j: (0, STEPS)),
            whole(8, 128),
            whole(length + 2 * PAD, 128),
            whole(8, length),
        ],
        out_specs=[
            columns(length, lambda j: (0, j)),
            columns(length, lambda j: (0, j)),
            columns(STATE, lambda j: (0, j)),
            whole(length, 128),
            whole(length, 128),
            whole(length, 128),
            whole(length, 128),
            whole(length, 128),
            whole(8, 128),
        ],
        out_shape=[
            jax.ShapeDtypeStruct((length, INNER), BF16),
            jax.ShapeDtypeStruct((length, INNER), BF16),
            jax.ShapeDtypeStruct((STATE, INNER), BF16),
            jax.ShapeDtypeStruct((length, 128), BF16),
            jax.ShapeDtypeStruct((length, 128), BF16),
            jax.ShapeDtypeStruct((length, 128), F32),
            jax.ShapeDtypeStruct((length, 128), F32),
            jax.ShapeDtypeStruct((length, 128), F32),
            jax.ShapeDtypeStruct((8, 128), F32),
        ],
        scratch_shapes=[
            pltpu.VMEM((length + PAD, BLK), F32),
            pltpu.VMEM((length, Q), F32),
            pltpu.VMEM((length // Q, 128, Q), F32),
            pltpu.VMEM((128, length), BF16),
            pltpu.VMEM((length, 128), F32),
            pltpu.VMEM((length, 128), F32),
        ],
        compiler_params=pltpu.CompilerParams(vmem_limit_bytes=VMEM_LIMIT),
        cost_estimate=pl.CostEstimate(
            flops=6 * 10**9, bytes_accessed=16 * 10**6, transcendentals=10**7
        ),
        name="front",
    )(projected, projected, projected, halo, halo, taps, taps, heads, seg_lanes, seg_row)


def weights_of_parts(kept_ref, place, before):
    count = kept_ref.shape[0]
    result = [None] * count
    run = jnp.ones((1, 128), F32)
    for part in range(count - 1, -1, -1) if before else range(count):
        inside = (part < place) if before else (part > place)
        result[part] = jnp.where(inside, run, 0.0)
        run = run * jnp.where(inside, kept_ref[part, 0:1, :], 1.0)
    return result


def joined_states(states_ref, kept_ref, place, select, before):
    weights = weights_of_parts(kept_ref, place, before)
    count = len(weights)
    stacked = jnp.concatenate(weights + [jnp.zeros((-count % 8, 128), F32)] * (count % 8 > 0), axis=0)
    wide = widen(stacked, select)
    total = jnp.zeros((STATE, BLK), F32)
    for part in range(count):
        total = total + wide[part : part + 1, :] * states_ref[part].astype(F32)
    return total


def tail_kernel(
    place_ref, y_ref, xs_ref, gate_ref, states_ref, kept_ref, out_ref, c_ref, in_ref, heads_ref, gain_ref, g_ref, units_ref,
    mixer_ref, dproj_ref, dy_ref, sin_ref, dsin_ref, sums_ref, block_ref, stats_ref,
    full, dmix, squares, products, mixed, c_t,
):
    step = pl.program_id(0)
    length = y_ref.shape[0]
    group = lax.rem(step, STEPS)
    select = chosen(group)
    half = length // 2

    @pl.when(step == 0)
    def _():
        squares[...] = jnp.zeros_like(squares)
        products[...] = jnp.zeros_like(products)
        for k in range(length // Q):
            rows = slice(k * Q, (k + 1) * Q)
            c_t[:, rows] = c_ref[rows, :].astype(F32).T.astype(BF16)

    @pl.when(step < STEPS)
    def _():
        incoming = joined_states(states_ref, kept_ref, place_ref[0], select, True).astype(BF16)
        sin_ref[...] = incoming
        skip = widen(heads_ref[...], select)[2:3, :]
        for k in range(2):
            rows = slice(k * half, (k + 1) * half)
            y = y_ref[rows, :].astype(F32)
            y = y + widen(in_ref[rows, :], select) * dot(c_ref[rows, :], incoming)
            y = y + skip * xs_ref[rows, :].astype(F32)
            full[step, rows, :] = y
            gate = gate_ref[rows, :].astype(F32)
            gated = y * gate * sigmoid(gate)
            d_mixer = dot_nt(g_ref[rows, :], out_ref[...])
            dmix[step, rows, :] = d_mixer
            square = gated * gated
            product = gated * d_mixer * gain_ref[0:1, :]
            squares[rows, :] += square[:, :128] + square[:, 128:]
            products[rows, :] += product[:, :128] + product[:, 128:]

    @pl.when(step == STEPS)
    def _():
        norm = lax.rsqrt(jnp.sum(squares[...], axis=1, keepdims=True) * (1.0 / INNER) + epsilon)
        mean = norm * jnp.sum(products[...], axis=1, keepdims=True) * (1.0 / INNER)
        squares[...] = jnp.broadcast_to(norm, squares.shape)
        products[...] = jnp.broadcast_to(mean, products.shape)

    @pl.when(step >= STEPS)
    def _():
        gain = gain_ref[0:1, :]
        d_gain = jnp.zeros((1, BLK), F32)
        d_skip = jnp.zeros((1, BLK), F32)
        d_state = jnp.zeros((STATE, BLK), F32)
        for k in range(2):
            rows = slice(k * half, (k + 1) * half)
            norm, mean = both(squares[rows, :]), both(products[rows, :])
            y = full[group, rows, :]
            d_mixer = dmix[group, rows, :]
            gate = gate_ref[rows, :].astype(F32)
            sig = sigmoid(gate)
            silu = gate * sig
            unit = y * silu * norm
            low = (unit * gain).astype(BF16)
            mixer_ref[rows, :] = low
            part = dot(low, out_ref[...])

            @pl.when(step == STEPS)
            def _():
                mixed[rows, :] = part

            @pl.when(step > STEPS)
            def _():
                mixed[rows, :] += part

            d_gain = d_gain + jnp.sum(d_mixer * unit, axis=0, keepdims=True)
            d_gated = norm * (d_mixer * gain - unit * mean)
            dproj_ref[rows, :] = (d_gated * y * (sig * (1.0 + gate * (1.0 - sig)))).astype(BF16)
            dy = (d_gated * silu).astype(BF16)
            dy_ref[rows, :] = dy
            dy = dy.astype(F32)
            d_skip = d_skip + jnp.sum(dy * xs_ref[rows, :].astype(F32), axis=0, keepdims=True)
            d_state = d_state + dot(c_t[:, rows], (dy * widen(in_ref[rows, :], select)).astype(BF16))
        dsin_ref[...] = d_state.astype(BF16)
        sums_ref[...] = jnp.concatenate([d_gain, d_skip, jnp.zeros((6, BLK), F32)], axis=0)

    @pl.when(step == 2 * STEPS - 1)
    def _():
        total = units_ref[...].astype(F32) + mixed[...]
        block_ref[...] = total.astype(BF16)
        first = jnp.sum(total * total, axis=0, keepdims=True)
        second = jnp.sum(mixed[...] * mixed[...], axis=0, keepdims=True)
        stats_ref[...] = jnp.concatenate([first, second, jnp.zeros((6, D), F32)], axis=0)


def tail(place, y, xs, projected, states, kept, out_whole, c_rows, entering, heads, gain, cot, units):
    length = y.shape[0]
    count = states.shape[0]
    early = lambda rows: pl.BlockSpec((rows, BLK), lambda i: (0, jnp.minimum(i, STEPS - 1)))
    late = lambda rows: pl.BlockSpec((rows, BLK), lambda i: (0, jnp.maximum(i - STEPS, 0)))
    each = lambda rows: pl.BlockSpec((rows, BLK), lambda i: (0, lax.rem(i, STEPS)))
    whole = lambda *shape: pl.BlockSpec(shape, lambda i: (0,) * len(shape))
    return pl.pallas_call(
        tail_kernel,
        grid=(2 * STEPS,),
        in_specs=[
            pl.BlockSpec(memory_space=pltpu.SMEM),
            early(length),
            each(length),
            each(length),
            pl.BlockSpec((count, STATE, BLK), lambda i: (0, 0, jnp.minimum(i, STEPS - 1))),
            whole(count, 8, 128),
            pl.BlockSpec((BLK, D), lambda i: (lax.rem(i, STEPS), 0)),
            whole(length, 128),
            whole(length, 128),
            whole(8, 128),
            each(8),
            whole(length, D),
            whole(length, D),
        ],
        out_specs=[
            late(length),
            late(length),
            late(length),
            early(STATE),
            late(STATE),
            late(8),
            whole(length, D),
            whole(8, D),
        ],
        out_shape=[
            jax.ShapeDtypeStruct((length, INNER), BF16),
            jax.ShapeDtypeStruct((length, PROJ), BF16),
            jax.ShapeDtypeStruct((length, INNER), BF16),
            jax.ShapeDtypeStruct((STATE, INNER), BF16),
            jax.ShapeDtypeStruct((STATE, INNER), BF16),
            jax.ShapeDtypeStruct((8, INNER), F32),
            jax.ShapeDtypeStruct((length, D), BF16),
            jax.ShapeDtypeStruct((8, D), F32),
        ],
        scratch_shapes=[
            pltpu.VMEM((STEPS, length, BLK), F32),
            pltpu.VMEM((STEPS, length, BLK), F32),
            pltpu.VMEM((length, 128), F32),
            pltpu.VMEM((length, 128), F32),
            pltpu.VMEM((length, D), F32),
            pltpu.VMEM((128, length), BF16),
        ],
        compiler_params=pltpu.CompilerParams(vmem_limit_bytes=VMEM_LIMIT),
        cost_estimate=pl.CostEstimate(
            flops=12 * 10**9, bytes_accessed=50 * 10**6, transcendentals=4 * 10**6
        ),
        name="tail",
    )(place, y, xs, projected, states, kept, out_whole, c_rows, entering, heads, gain, cot, units)


def back_kernel(
    place_ref, x_ref, dtraw_ref, halo_ref, taps_ref, heads_ref, seg_ref, row_ref, b_ref, c_ref, dt_ref, run_ref,
    dy_ref, sin_ref, dstates_ref, kept_ref, given_ref,
    dproj_ref, dhalo_ref, dtaps_ref, dheads_ref,
    ext, pre, dact, dbuf, scores, dscores, run_t, b_t, c_t, enter, leave, d_b, d_c, suffix, prefix, d_dt, fixed, states,
):
    step = pl.program_id(0)
    length = x_ref.shape[0]
    chunks = length // Q

    @pl.when(step == 0)
    def _():
        for k in range(chunks):
            rows = slice(k * Q, (k + 1) * Q)
            b_rows, c_rows = b_ref[rows, :], c_ref[rows, :]
            b_t[:, rows] = b_rows.astype(F32).T.astype(BF16)
            c_t[:, rows] = c_rows.astype(F32).T.astype(BF16)
            scores[rows, :] = masked_scores(seg_ref, row_ref, b_rows, c_rows, k)
            running = run_ref[rows, :]
            run_t[k] = running.T
            carry, tail = chunk_flags(seg_ref, k)
            enter[rows, :] = jnp.exp(running) * carry
            leave[rows, :] = jnp.exp(running[Q - 1 : Q, :] - running) * tail
        for each in (dscores, d_b, d_c, suffix, prefix, d_dt, fixed):
            each[...] = jnp.zeros_like(each)
        dbuf[0:PAD, :] = jnp.zeros((PAD, BLK), F32)
        dbuf[PAD + length :, :] = jnp.zeros((PAD, BLK), F32)

    @pl.when(step <= STEPS)
    def _():
        ext[0:PAD, :] = halo_ref[...]
        ext[PAD:, :] = x_ref[...].astype(F32)
        for k in range(chunks):
            pre[k * Q : (k + 1) * Q, :] = conv_rows(ext, seg_ref, taps_ref, k * Q, Q)

    @pl.when(step < STEPS)
    def _():
        select = chosen(step)
        gather = chosen_back(step)
        skip = widen(heads_ref[...], select)[2:3, :]
        state = sin_ref[...].astype(F32)
        for k in range(chunks):
            rows = slice(k * Q, (k + 1) * Q)
            states[k] = state
            if k + 1 < chunks:
                total = pre[rows, :]
                scaled = total * sigmoid(total) * widen(dt_ref[rows, :], select)
                weighted = (scaled.astype(BF16).astype(F32) * widen(leave[rows, :], select)).astype(BF16)
                last = widen(enter[rows.stop - 8 : rows.stop, :], select)[7:8, :]
                state = last * state + dot(b_t[:, rows], weighted)
        d_state = joined_states(dstates_ref, kept_ref, place_ref[0], select, False)
        for k in range(chunks - 1, -1, -1):
            rows = slice(k * Q, (k + 1) * Q)
            total = pre[rows, :]
            values = total * sigmoid(total)
            step_size = widen(dt_ref[rows, :], select)
            entering = widen(enter[rows, :], select)
            leaving = widen(leave[rows, :], select)
            scaled = (values * step_size).astype(BF16)
            scaled_wide = scaled.astype(F32)
            dy = dy_ref[rows, :]
            dy_wide = dy.astype(F32)
            before = states[k]
            before_low = before.astype(BF16)
            d_low = d_state.astype(BF16)
            running = pltpu.roll(run_ref[rows, :], lax.rem(128 - step * GROUP, 128), 1)
            insides, backs = [], []
            d_score = dscores[rows, :]
            for pair in range(2):
                lanes = slice(pair * 128, (pair + 1) * 128)
                mixing, turned, decays = [], [], []
                for one in range(2):
                    head = 2 * pair + one
                    gap = running[:, head : head + 1] - run_t[k, pl.ds(step * GROUP + head, 1), :]
                    decay = jnp.exp(jnp.minimum(gap, 0.0))
                    mixed = decay * scores[rows, :]
                    decays.append(decay)
                    mixing.append(mixed.astype(BF16))
                    turned.append(mixed.T.astype(BF16))
                spread = halves(scaled[:, lanes])
                insides.append(dot(jnp.concatenate(mixing, axis=1), spread))
                backs.append(dot(jnp.concatenate(turned, axis=1), halves(dy[:, lanes])))
                products = dot_nt(dy[:, lanes], spread)
                d_score = d_score + decays[0] * products[:, :Q] + decays[1] * products[:, Q:]
            dscores[rows, :] = d_score
            inside = jnp.concatenate(insides, axis=1) + entering * dot(c_ref[rows, :], before_low)
            back_inside = jnp.concatenate(backs, axis=1)
            back_state = leaving * dot(b_ref[rows, :], d_low)
            high, low = in_two(dy_wide * inside - scaled_wide * back_inside)
            suffix[rows, :] += dot(high, gather) + dot(low, gather)
            prefix[rows, :] += dot((scaled_wide * back_state).astype(BF16), gather)
            back = back_inside + back_state
            d_dt[rows, :] += dot((values * back).astype(BF16), gather)
            entered = (dy_wide * entering).astype(BF16)
            d_c[rows, :] += dot_nt(entered, before_low)
            d_b[rows, :] += dot_nt((scaled_wide * leaving).astype(BF16), d_low)
            kept = entering[Q - 1 : Q, :]
            through = jnp.sum(before * d_state, axis=0, keepdims=True) * kept
            high, low = in_two(jnp.broadcast_to(through, (8, BLK)))
            fixed[k * 8 : (k + 1) * 8, :] += dot(high, gather) + dot(low, gather)
            d_state = kept * d_state + dot(c_t[:, rows], entered)
            dact[rows, :] = back * step_size + skip * dy_wide

    @pl.when(step == STEPS)
    def _():
        for k in range(chunks):
            rows = slice(k * Q, (k + 1) * Q)
            own = seg_ref[PAD + k * Q : PAD + (k + 1) * Q, :]
            keep = (own == row_ref[0:1, rows]) & (iota((Q, Q), 1) <= iota((Q, Q), 0))
            d_score = jnp.where(keep, dscores[rows, :], 0.0)
            dact[rows, STATE:] = d_c[rows, :] + dot(d_score.astype(BF16), b_ref[rows, :])
            dact[rows, :STATE] = d_b[rows, :] + dot(d_score.T.astype(BF16), c_ref[rows, :])

    @pl.when(step <= STEPS)
    def _():
        sums = [jnp.zeros((1, BLK), F32) for _ in range(CONV + 1)]
        for k in range(chunks):
            rows = slice(k * Q, (k + 1) * Q)
            total = pre[rows, :]
            sig = sigmoid(total)
            d_conv = dact[rows, :] * (sig * (1.0 + total * (1.0 - sig)))
            dbuf[PAD + k * Q : PAD + (k + 1) * Q, :] = d_conv
            sums[4] = sums[4] + jnp.sum(d_conv, axis=0, keepdims=True)
            own = seg_ref[PAD + k * Q : PAD + (k + 1) * Q, :]
            for shift in range(CONV):
                at = PAD + k * Q - shift
                term = d_conv * ext[at : at + Q, :]
                if shift:
                    term = jnp.where(both(seg_ref[at : at + Q, :] == own), term, 0.0)
                sums[3 - shift] = sums[3 - shift] + jnp.sum(term, axis=0, keepdims=True)
        dtaps_ref[...] = jnp.concatenate(sums + [jnp.zeros((3, BLK), F32)], axis=0)

        def returned(at, rows):
            own = seg_ref[at : at + rows, :]
            result = taps_ref[3:4, :] * dbuf[at : at + rows, :]
            for shift in range(1, CONV):
                same = both(seg_ref[at + shift : at + shift + rows, :] == own)
                result = result + jnp.where(
                    same, taps_ref[3 - shift : 4 - shift, :] * dbuf[at + shift : at + shift + rows, :], 0.0
                )
            return result

        dhalo_ref[...] = returned(0, PAD)
        for k in range(chunks):
            dproj_ref[k * Q : (k + 1) * Q, :] = returned(PAD + k * Q, Q).astype(BF16)

    @pl.when(step == STEPS + 1)
    def _():
        lower = (iota((Q, Q), 1) < iota((Q, Q), 0)).astype(F32)
        upper = (iota((Q, Q), 1) >= iota((Q, Q), 0)).astype(F32)
        lane = iota((Q, 128), 1)
        rate = jnp.exp(heads_ref[1:2, :])
        bias_sum = jnp.zeros((1, 128), F32)
        decay_sum = jnp.zeros((1, 128), F32)
        for k in range(chunks):
            rows = slice(k * Q, (k + 1) * Q)
            d_log = jnp.dot(upper, suffix[rows, :], precision=HIGHEST, preferred_element_type=F32)
            d_log = d_log + jnp.dot(lower, prefix[rows, :], precision=HIGHEST, preferred_element_type=F32)
            d_log = d_log + fixed[k * 8 : k * 8 + 1, :]
            raw = jnp.where(lane < HEADS, dtraw_ref[rows, :128].astype(F32), 0.0) + heads_ref[0:1, :]
            d_raw = jnp.where(lane < HEADS, (d_dt[rows, :] - rate * d_log) * sigmoid(raw), 0.0)
            bias_sum = bias_sum + jnp.sum(d_raw, axis=0, keepdims=True)
            decay_sum = decay_sum - jnp.sum(d_log * dt_ref[rows, :] * rate, axis=0, keepdims=True)
            dproj_ref[rows, :] = jnp.concatenate([d_raw, jnp.zeros_like(d_raw)], axis=1).astype(BF16)
        dheads_ref[...] = jnp.concatenate([bias_sum, decay_sum, jnp.zeros((6, 128), F32)], axis=0)


def back(place, projected, halo, taps, heads, seg_lanes, seg_row, b_rows, c_rows, dt, running, dy, incoming, dstates, kept, given):
    length = projected.shape[0]
    count = dstates.shape[0]
    whole = lambda *shape: pl.BlockSpec(shape, lambda j: (0,) * len(shape))
    upto = lambda last, first=0: lambda j: (0, first + jnp.minimum(j, last))
    return pl.pallas_call(
        back_kernel,
        grid=(STEPS + 2,),
        in_specs=[
            pl.BlockSpec(memory_space=pltpu.SMEM),
            pl.BlockSpec((length, BLK), upto(STEPS, STEPS)),
            pl.BlockSpec((length, BLK), lambda j: (0, 2 * STEPS + 1)),
            pl.BlockSpec((PAD, BLK), upto(STEPS)),
            pl.BlockSpec((8, BLK), upto(STEPS)),
            whole(8, 128),
            whole(length + 2 * PAD, 128),
            whole(8, length),
            whole(length, 128),
            whole(length, 128),
            whole(length, 128),
            whole(length, 128),
            pl.BlockSpec((length, BLK), upto(STEPS - 1)),
            pl.BlockSpec((STATE, BLK), upto(STEPS - 1)),
            pl.BlockSpec((count, STATE, BLK), lambda j: (0, 0, jnp.minimum(j, STEPS - 1))),
            whole(count, 8, 128),
            pl.BlockSpec(memory_space=pl.ANY),
        ],
        out_specs=[
            pl.BlockSpec((length, BLK), lambda j: (0, STEPS + j)),
            pl.BlockSpec((PAD, BLK), upto(STEPS)),
            pl.BlockSpec((8, BLK), upto(STEPS)),
            whole(8, 128),
        ],
        out_shape=[
            jax.ShapeDtypeStruct((length, PROJ), BF16),
            jax.ShapeDtypeStruct((PAD, XBC), F32),
            jax.ShapeDtypeStruct((8, XBC), F32),
            jax.ShapeDtypeStruct((8, 128), F32),
        ],
        scratch_shapes=[
            pltpu.VMEM((length + PAD, BLK), F32),
            pltpu.VMEM((length, BLK), F32),
            pltpu.VMEM((length, BLK), F32),
            pltpu.VMEM((length + 2 * PAD, BLK), F32),
            pltpu.VMEM((length, Q), F32),
            pltpu.VMEM((length, Q), F32),
            pltpu.VMEM((length // Q, 128, Q), F32),
            pltpu.VMEM((128, length), BF16),
            pltpu.VMEM((128, length), BF16),
            pltpu.VMEM((length, 128), F32),
            pltpu.VMEM((length, 128), F32),
            pltpu.VMEM((length, 128), F32),
            pltpu.VMEM((length, 128), F32),
            pltpu.VMEM((length, 128), F32),
            pltpu.VMEM((length, 128), F32),
            pltpu.VMEM((length, 128), F32),
            pltpu.VMEM((8 * (length // Q), 128), F32),
            pltpu.VMEM((length // Q, STATE, BLK), F32),
        ],
        input_output_aliases={16: 0},
        compiler_params=pltpu.CompilerParams(vmem_limit_bytes=VMEM_LIMIT),
        cost_estimate=pl.CostEstimate(
            flops=12 * 10**9, bytes_accessed=30 * 10**6, transcendentals=2 * 10**7
        ),
        name="back",
    )(
        place, projected, projected, halo, taps, heads, seg_lanes, seg_row, b_rows, c_rows, dt, running, dy, incoming, dstates, kept, given
    )


def passed_along(block, axis, distance):
    devices = range(lax.axis_size(axis))
    route = [(i - distance, i) for i in devices if i - distance in devices]
    return lax.ppermute(block, axis, route)


def pack_small(conv_taps, conv_bias, dt_bias, decay_log, skip_scale, mixer_gain, input_gain):
    width = conv_bias.shape[0]

    def line(*parts):
        flat = jnp.concatenate(parts)
        return jnp.pad(flat, (0, width - flat.shape[0]))[None]

    return jnp.concatenate(
        [
            conv_taps.T,
            conv_bias[None],
            line(mixer_gain),
            line(input_gain),
            line(dt_bias, decay_log, skip_scale),
        ],
        axis=0,
    )


def unpack_small(whole):
    shards, _, width = whole.shape
    joined = jnp.swapaxes(whole, 0, 1)
    taps = jnp.pad(joined[:5].reshape(5, shards * width).astype(F32), ((0, 3), (0, 0)))
    gain = joined[5, :, : INNER // shards].reshape(1, INNER).astype(F32)
    input_gain = joined[6, :, : D // shards].reshape(1, D).astype(F32)
    own = HEADS // shards
    heads = joined[7, :, : 3 * own].reshape(shards, 3, own).swapaxes(0, 1).reshape(3, HEADS)
    heads = jnp.pad(heads.astype(F32), ((0, 5), (0, 128 - HEADS)))
    return taps, jnp.pad(gain, ((0, 7), (0, 0))), input_gain, heads


def on_device(
    inputs,
    segment_ids,
    out_grad,
    in_matrix,
    out_matrix,
    conv_taps,
    conv_bias,
    dt_bias,
    decay_log,
    skip_scale,
    mixer_gain,
    input_gain,
):
    shards, parts = lax.axis_size("fsdp"), lax.axis_size("ctx")
    place = jnp.reshape(lax.axis_index("ctx"), (1,)).astype(jnp.int32)
    units_low, cot = inputs[0], out_grad[0]
    units = units_low.astype(F32)
    seg_ids = segment_ids[0]
    length = units.shape[0]
    small = lax.all_gather(
        pack_small(conv_taps, conv_bias, dt_bias, decay_log, skip_scale, mixer_gain, input_gain), "fsdp"
    )
    w_whole = lax.all_gather(in_matrix, "fsdp", axis=0, tiled=True)
    out_whole = lax.all_gather(out_matrix, "fsdp", axis=0, tiled=True)
    taps, gain, g_float, heads = unpack_small(small)
    rim_seg = passed_along(seg_ids[length - CONV + 1 :], "ctx", 1)
    seg_ext = jnp.concatenate(
        [
            jnp.full((PAD - CONV + 1,), -1, jnp.int32),
            rim_seg,
            seg_ids,
            jnp.full((PAD,), -2, jnp.int32),
        ]
    )
    seg_lanes = jnp.broadcast_to(seg_ext[:, None], (length + 2 * PAD, 128))
    seg_row = jnp.broadcast_to(seg_ids[None], (8, length))

    inv_rms = lax.rsqrt(jnp.mean(units * units, axis=-1, keepdims=True) + epsilon)
    base_rows = units * inv_rms
    part_rows = (base_rows * g_float).astype(BF16)
    projected = dot(part_rows, w_whole).astype(BF16)
    rim_rows = passed_along(projected[length - CONV + 1 :, INNER : INNER + XBC], "ctx", 1)
    halo = jnp.pad(rim_rows, ((PAD - CONV + 1, 0), (0, 0))).astype(F32)

    xs, y_local, state, b_rows, c_rows, dt, running, entering, keep = front(
        projected, halo, taps, heads, seg_lanes, seg_row
    )
    kept = lax.all_gather(keep, "ctx")
    states = lax.all_gather(state, "ctx")
    mixer_low, dproj, dy, incoming, d_incoming, column_sums, block_out, stats = tail(
        place, y_local, xs, projected, states, kept, out_whole, c_rows, entering, heads, gain, cot, units_low
    )
    dstates = lax.all_gather(d_incoming, "ctx")
    d_out_matrix = lax.dot_general(mixer_low, cot, (((0,), (0,)), ((), ())), preferred_element_type=F32)
    dproj, d_halo, d_taps, d_heads = back(
        place, projected, halo, taps, heads, seg_lanes, seg_row, b_rows, c_rows, dt, running, dy, incoming, dstates, kept, dproj
    )
    returned = passed_along(d_halo.astype(BF16), "ctx", -1)
    last = lax.slice(dproj, (length - PAD, INNER), (length, INNER + XBC))
    last = (last.astype(F32) + returned.astype(F32)).astype(BF16)
    dproj = lax.dynamic_update_slice(dproj, last, (length - PAD, INNER))

    d_in_matrix = lax.dot_general(part_rows, dproj, (((0,), (0,)), ((), ())), preferred_element_type=F32)
    d_normed = dot_nt(dproj, w_whole)
    d_input_gain = jnp.sum(d_normed * base_rows, axis=0)
    d_base = d_normed * g_float
    d_units = inv_rms * (d_base - base_rows * jnp.mean(d_base * base_rows, axis=-1, keepdims=True))
    input_grad = (cot.astype(F32) + d_units).astype(BF16)

    def scattered(grad):
        return lax.psum_scatter(grad.astype(BF16), "fsdp", scatter_dimension=0, tiled=True)

    d_in = lax.psum(scattered(d_in_matrix), "ctx").astype(F32)
    d_out = lax.psum(scattered(d_out_matrix), "ctx").astype(F32)
    row = jnp.concatenate(
        [
            d_taps[:5].reshape(-1),
            column_sums[0],
            d_input_gain,
            d_heads[0, :HEADS],
            d_heads[1, :HEADS],
            jnp.sum(column_sums[1].reshape(HEADS, HDIM), axis=1),
            jnp.sum(stats[:2], axis=1),
        ]
    )
    row = jnp.pad(row, (0, -row.shape[0] % 1024)).reshape(-1, 128)
    row = lax.psum(row, ("fsdp", "ctx")).reshape(-1)
    me = lax.axis_index("fsdp")

    def own(flat):
        size = flat.shape[-1] // shards
        return lax.dynamic_slice_in_dim(flat, me * size, size, flat.ndim - 1)

    at = 5 * XBC
    taps_sum = row[:at].reshape(5, XBC)
    gain_sum = row[at : at + INNER]
    input_gain_sum = row[at + INNER : at + INNER + D]
    at = at + INNER + D
    head_sums = row[at : at + 3 * HEADS].reshape(3, HEADS)
    stat_sums = row[at + 3 * HEADS : at + 3 * HEADS + 2]
    rms_stats = jnp.sqrt(stat_sums / (length * shards * parts * D))
    return (
        block_out[None],
        input_grad[None],
        d_in,
        d_out,
        own(taps_sum[:4]).T,
        own(taps_sum[4]),
        own(head_sums[0]),
        own(head_sums[1]),
        own(head_sums[2]),
        own(gain_sum),
        own(input_gain_sum),
        rms_stats,
    )


def solution(mesh):
    return jax.shard_map(
        on_device,
        mesh=mesh,
        in_specs=(
            P("fsdp", "ctx", None),
            P("fsdp", "ctx"),
            P("fsdp", "ctx", None),
            P("fsdp", None),
            P("fsdp", None),
            P("fsdp", None),
            P("fsdp"),
            P("fsdp"),
            P("fsdp"),
            P("fsdp"),
            P("fsdp"),
            P("fsdp"),
        ),
        out_specs=(
            P("fsdp", "ctx", None),
            P("fsdp", "ctx", None),
            P("fsdp", None),
            P("fsdp", None),
            P("fsdp", None),
            P("fsdp"),
            P("fsdp"),
            P("fsdp"),
            P("fsdp"),
            P("fsdp"),
            P("fsdp"),
            P(),
        ),
        check_vma=False,
    )
```

```python
import functools

import jax
import jax.numpy as jnp
from jax import lax
from jax.experimental import pallas as pl
from jax.experimental.pallas import tpu as pltpu
from jax.sharding import PartitionSpec as P

D = 1536
HEADS = 48
HDIM = 64
STATE = 128
CONV = 4
INNER = 3072
XBC = 3328
PROJ = 6448

BLK = 256
GROUP = BLK // HDIM
STEPS = INNER // BLK
Q = 128
PAD = 8

epsilon = 1e-05
F32, BF16 = jnp.float32, jnp.bfloat16
HIGHEST = lax.Precision.HIGHEST
VMEM_LIMIT = 60 * 1024 * 1024


def dot(a, b):
    return jnp.dot(a, b, preferred_element_type=F32)


def dot_nt(a, b):
    return lax.dot_general(a, b, (((1,), (1,)), ((), ())), preferred_element_type=F32)


def iota(shape, dim):
    return lax.broadcasted_iota(jnp.int32, shape, dim)


def sigmoid(v):
    return 1.0 / (1.0 + jnp.exp(-v))


def in_two(a):
    high = a.astype(BF16)
    return high, (a - high.astype(F32)).astype(BF16)


def chosen(step):
    columns = step * GROUP + lax.shift_right_logical(iota((128, BLK), 1), 6)
    return (iota((128, BLK), 0) == columns).astype(BF16)


def chosen_back(step):
    heads = step * GROUP + lax.shift_right_logical(iota((BLK, 128), 0), 6)
    return (iota((BLK, 128), 1) == heads).astype(BF16)


def widen(per_head, select):
    high, low = in_two(per_head)
    return dot(high, select) + dot(low, select)


def halves(pair):
    first = iota(pair.shape, 1) < HDIM
    zero = jnp.zeros_like(pair)
    return jnp.concatenate([jnp.where(first, pair, zero), jnp.where(first, zero, pair)], axis=0)


def both(mask):
    return jnp.concatenate([mask, mask], axis=1)


def conv_rows(ext_ref, seg_ref, taps_ref, start, rows):
    own = seg_ref[start + PAD : start + PAD + rows, :]
    total = taps_ref[4:5, :] + taps_ref[3:4, :] * ext_ref[start + PAD : start + PAD + rows, :]
    for back in range(1, CONV):
        at = start + PAD - back
        same = both(seg_ref[at : at + rows, :] == own)
        total = total + jnp.where(
            same, taps_ref[3 - back : 4 - back, :] * ext_ref[at : at + rows, :], 0.0
        )
    return total


def chunk_flags(seg_ref, k):
    own = seg_ref[PAD + k * Q : PAD + (k + 1) * Q, :]
    before = seg_ref[PAD + k * Q - 1 : PAD + k * Q, :]
    last = seg_ref[PAD + (k + 1) * Q - 1 : PAD + (k + 1) * Q, :]
    return (own == before).astype(F32), (own == last).astype(F32)


def masked_scores(seg_ref, row_ref, b_rows, c_rows, k):
    own = seg_ref[PAD + k * Q : PAD + (k + 1) * Q, :]
    row = row_ref[0:1, k * Q : (k + 1) * Q]
    keep = (own == row) & (iota((Q, Q), 1) <= iota((Q, Q), 0))
    return jnp.where(keep, dot_nt(c_rows, b_rows), 0.0)


def front_kernel(
    x_ref, bc_ref, dtraw_ref, halo_ref, halo_bc_ref, taps_ref, taps_bc_ref, heads_ref, seg_ref, row_ref,
    xs_ref, y_ref, state_ref, b_ref, c_ref, dt_ref, run_ref, in_ref, keep_ref,
    ext, scores, run_t, b_t, enter, leave,
):
    step = pl.program_id(0)
    length = x_ref.shape[0]
    chunks = length // Q

    @pl.when(step == 0)
    def _():
        ext[0:PAD, :] = halo_bc_ref[...]
        ext[PAD:, :] = bc_ref[...].astype(F32)
        lane = iota((Q, 128), 1)
        lower = (iota((Q, Q), 1) <= iota((Q, Q), 0)).astype(F32)
        offset = jnp.zeros((1, 128), F32)
        for k in range(chunks):
            rows = slice(k * Q, (k + 1) * Q)
            total = conv_rows(ext, seg_ref, taps_bc_ref, k * Q, Q)
            active = total * sigmoid(total)
            b_rows, c_rows = active[:, :STATE], active[:, STATE:].astype(BF16)
            b_t[:, rows] = b_rows.T.astype(BF16)
            b_rows = b_rows.astype(BF16)
            b_ref[rows, :] = b_rows
            c_ref[rows, :] = c_rows
            scores[rows, :] = masked_scores(seg_ref, row_ref, b_rows, c_rows, k)
            raw = jnp.where(lane < HEADS, dtraw_ref[rows, :128].astype(F32), 0.0) + heads_ref[0:1, :]
            dt = jnp.maximum(raw, 0.0) + jnp.log1p(jnp.exp(-jnp.abs(raw)))
            log_decay = -dt * jnp.exp(heads_ref[1:2, :])
            running = jnp.dot(lower, log_decay, precision=HIGHEST, preferred_element_type=F32)
            dt_ref[rows, :] = dt
            run_ref[rows, :] = running
            run_t[k] = running.T
            carry, tail = chunk_flags(seg_ref, k)
            enter[rows, :] = jnp.exp(running) * carry
            leave[rows, :] = jnp.exp(running[Q - 1 : Q, :] - running) * tail
            same = (seg_ref[PAD + k * Q : PAD + (k + 1) * Q, :] == seg_ref[PAD - 1 : PAD, :]).astype(F32)
            whole = jnp.exp(running + offset) * same
            in_ref[rows, :] = whole
            offset = offset + running[Q - 1 : Q, :]
        keep_ref[...] = jnp.broadcast_to(whole[Q - 1 : Q, :], (8, 128))

    ext[0:PAD, :] = halo_ref[...]
    ext[PAD:, :] = x_ref[...].astype(F32)
    select = chosen(step)
    state = jnp.zeros((STATE, BLK), F32)
    for k in range(chunks):
        rows = slice(k * Q, (k + 1) * Q)
        total = conv_rows(ext, seg_ref, taps_ref, k * Q, Q)
        values = total * sigmoid(total)
        xs_ref[rows, :] = values.astype(BF16)
        scaled = (values * widen(dt_ref[rows, :], select)).astype(BF16)
        entering = widen(enter[rows, :], select)
        running = pltpu.roll(run_ref[rows, :], lax.rem(128 - step * GROUP, 128), 1)
        parts = []
        for pair in range(2):
            mixing = []
            for one in range(2):
                head = 2 * pair + one
                gap = running[:, head : head + 1] - run_t[k, pl.ds(step * GROUP + head, 1), :]
                mixing.append((jnp.exp(jnp.minimum(gap, 0.0)) * scores[rows, :]).astype(BF16))
            parts.append(
                dot(jnp.concatenate(mixing, axis=1), halves(scaled[:, pair * 128 : (pair + 1) * 128]))
            )
        inside = jnp.concatenate(parts, axis=1)
        y_ref[rows, :] = (inside + entering * dot(c_ref[rows, :], state.astype(BF16))).astype(BF16)
        weighted = (scaled.astype(F32) * widen(leave[rows, :], select)).astype(BF16)
        state = entering[Q - 1 : Q, :] * state + dot(b_t[:, rows], weighted)
    state_ref[...] = state.astype(BF16)


def front(projected, halo, taps, heads, seg_lanes, seg_row):
    length = projected.shape[0]
    whole = lambda *shape: pl.BlockSpec(shape, lambda j: (0,) * len(shape))
    columns = lambda rows, at: pl.BlockSpec((rows, BLK), at)
    return pl.pallas_call(
        front_kernel,
        grid=(STEPS,),
        in_specs=[
            columns(length, lambda j: (0, STEPS + j)),
            columns(length, lambda j: (0, 2 * STEPS)),
            columns(length, lambda j: (0, 2 * STEPS + 1)),
            columns(PAD, lambda j: (0, j)),
            columns(PAD, lambda j: (0, STEPS)),
            columns(8, lambda j: (0, j)),
            columns(8, lambda j: (0, STEPS)),
            whole(8, 128),
            whole(length + 2 * PAD, 128),
            whole(8, length),
        ],
        out_specs=[
            columns(length, lambda j: (0, j)),
            columns(length, lambda j: (0, j)),
            columns(STATE, lambda j: (0, j)),
            whole(length, 128),
            whole(length, 128),
            whole(length, 128),
            whole(length, 128),
            whole(length, 128),
            whole(8, 128),
        ],
        out_shape=[
            jax.ShapeDtypeStruct((length, INNER), BF16),
            jax.ShapeDtypeStruct((length, INNER), BF16),
            jax.ShapeDtypeStruct((STATE, INNER), BF16),
            jax.ShapeDtypeStruct((length, 128), BF16),
            jax.ShapeDtypeStruct((length, 128), BF16),
            jax.ShapeDtypeStruct((length, 128), F32),
            jax.ShapeDtypeStruct((length, 128), F32),
            jax.ShapeDtypeStruct((length, 128), F32),
            jax.ShapeDtypeStruct((8, 128), F32),
        ],
        scratch_shapes=[
            pltpu.VMEM((length + PAD, BLK), F32),
            pltpu.VMEM((length, Q), F32),
            pltpu.VMEM((length // Q, 128, Q), F32),
            pltpu.VMEM((128, length), BF16),
            pltpu.VMEM((length, 128), F32),
            pltpu.VMEM((length, 128), F32),
        ],
        compiler_params=pltpu.CompilerParams(vmem_limit_bytes=VMEM_LIMIT),
        cost_estimate=pl.CostEstimate(
            flops=6 * 10**9, bytes_accessed=16 * 10**6, transcendentals=10**7
        ),
        name="front",
    )(projected, projected, projected, halo, halo, taps, taps, heads, seg_lanes, seg_row)


def weights_of_parts(kept_ref, place, before):
    count = kept_ref.shape[0]
    result = [None] * count
    run = jnp.ones((1, 128), F32)
    for part in range(count - 1, -1, -1) if before else range(count):
        inside = (part < place) if before else (part > place)
        result[part] = jnp.where(inside, run, 0.0)
        run = run * jnp.where(inside, kept_ref[part, 0:1, :], 1.0)
    return result


def joined_states(states_ref, kept_ref, place, select, before):
    weights = weights_of_parts(kept_ref, place, before)
    count = len(weights)
    stacked = jnp.concatenate(weights + [jnp.zeros((-count % 8, 128), F32)] * (count % 8 > 0), axis=0)
    wide = widen(stacked, select)
    total = jnp.zeros((STATE, BLK), F32)
    for part in range(count):
        total = total + wide[part : part + 1, :] * states_ref[part].astype(F32)
    return total


def tail_kernel(
    place_ref, y_ref, xs_ref, gate_ref, states_ref, kept_ref, out_ref, c_ref, in_ref, heads_ref, gain_ref, g_ref, units_ref,
    mixer_ref, dproj_ref, dy_ref, sin_ref, dsin_ref, sums_ref, block_ref, stats_ref,
    full, dmix, squares, products, mixed, c_t,
):
    step = pl.program_id(0)
    length = y_ref.shape[0]
    group = lax.rem(step, STEPS)
    select = chosen(group)
    half = length // 2

    @pl.when(step == 0)
    def _():
        squares[...] = jnp.zeros_like(squares)
        products[...] = jnp.zeros_like(products)
        for k in range(length // Q):
            rows = slice(k * Q, (k + 1) * Q)
            c_t[:, rows] = c_ref[rows, :].astype(F32).T.astype(BF16)

    @pl.when(step < STEPS)
    def _():
        incoming = joined_states(states_ref, kept_ref, place_ref[0], select, True).astype(BF16)
        sin_ref[...] = incoming
        skip = widen(heads_ref[...], select)[2:3, :]
        for k in range(2):
            rows = slice(k * half, (k + 1) * half)
            y = y_ref[rows, :].astype(F32)
            y = y + widen(in_ref[rows, :], select) * dot(c_ref[rows, :], incoming)
            y = y + skip * xs_ref[rows, :].astype(F32)
            full[step, rows, :] = y
            gate = gate_ref[rows, :].astype(F32)
            gated = y * gate * sigmoid(gate)
            d_mixer = dot_nt(g_ref[rows, :], out_ref[...])
            dmix[step, rows, :] = d_mixer
            square = gated * gated
            product = gated * d_mixer * gain_ref[0:1, :]
            squares[rows, :] += square[:, :128] + square[:, 128:]
            products[rows, :] += product[:, :128] + product[:, 128:]

    @pl.when(step == STEPS)
    def _():
        norm = lax.rsqrt(jnp.sum(squares[...], axis=1, keepdims=True) * (1.0 / INNER) + epsilon)
        mean = norm * jnp.sum(products[...], axis=1, keepdims=True) * (1.0 / INNER)
        squares[...] = jnp.broadcast_to(norm, squares.shape)
        products[...] = jnp.broadcast_to(mean, products.shape)

    @pl.when(step >= STEPS)
    def _():
        gain = gain_ref[0:1, :]
        d_gain = jnp.zeros((1, BLK), F32)
        d_skip = jnp.zeros((1, BLK), F32)
        d_state = jnp.zeros((STATE, BLK), F32)
        for k in range(2):
            rows = slice(k * half, (k + 1) * half)
            norm, mean = both(squares[rows, :]), both(products[rows, :])
            y = full[group, rows, :]
            d_mixer = dmix[group, rows, :]
            gate = gate_ref[rows, :].astype(F32)
            sig = sigmoid(gate)
            silu = gate * sig
            unit = y * silu * norm
            low = (unit * gain).astype(BF16)
            mixer_ref[:, rows] = (unit * gain).T.astype(BF16)
            part = dot(low, out_ref[...])

            @pl.when(step == STEPS)
            def _():
                mixed[rows, :] = part

            @pl.when(step > STEPS)
            def _():
                mixed[rows, :] += part

            d_gain = d_gain + jnp.sum(d_mixer * unit, axis=0, keepdims=True)
            d_gated = norm * (d_mixer * gain - unit * mean)
            dproj_ref[rows, :] = (d_gated * y * (sig * (1.0 + gate * (1.0 - sig)))).astype(BF16)
            dy = (d_gated * silu).astype(BF16)
            dy_ref[rows, :] = dy
            dy = dy.astype(F32)
            d_skip = d_skip + jnp.sum(dy * xs_ref[rows, :].astype(F32), axis=0, keepdims=True)
            d_state = d_state + dot(c_t[:, rows], (dy * widen(in_ref[rows, :], select)).astype(BF16))
        dsin_ref[...] = d_state.astype(BF16)
        sums_ref[...] = jnp.concatenate([d_gain, d_skip, jnp.zeros((6, BLK), F32)], axis=0)

    @pl.when(step == 2 * STEPS - 1)
    def _():
        total = units_ref[...].astype(F32) + mixed[...]
        block_ref[...] = total.astype(BF16)
        first = jnp.sum(total * total, axis=0, keepdims=True)
        second = jnp.sum(mixed[...] * mixed[...], axis=0, keepdims=True)
        stats_ref[...] = jnp.concatenate([first, second, jnp.zeros((6, D), F32)], axis=0)


def tail(place, y, xs, projected, states, kept, out_whole, c_rows, entering, heads, gain, cot, units):
    length = y.shape[0]
    count = states.shape[0]
    early = lambda rows: pl.BlockSpec((rows, BLK), lambda i: (0, jnp.minimum(i, STEPS - 1)))
    late = lambda rows: pl.BlockSpec((rows, BLK), lambda i: (0, jnp.maximum(i - STEPS, 0)))
    each = lambda rows: pl.BlockSpec((rows, BLK), lambda i: (0, lax.rem(i, STEPS)))
    whole = lambda *shape: pl.BlockSpec(shape, lambda i: (0,) * len(shape))
    return pl.pallas_call(
        tail_kernel,
        grid=(2 * STEPS,),
        in_specs=[
            pl.BlockSpec(memory_space=pltpu.SMEM),
            early(length),
            each(length),
            each(length),
            pl.BlockSpec((count, STATE, BLK), lambda i: (0, 0, jnp.minimum(i, STEPS - 1))),
            whole(count, 8, 128),
            pl.BlockSpec((BLK, D), lambda i: (lax.rem(i, STEPS), 0)),
            whole(length, 128),
            whole(length, 128),
            whole(8, 128),
            each(8),
            whole(length, D),
            whole(length, D),
        ],
        out_specs=[
            pl.BlockSpec((BLK, length), lambda i: (jnp.maximum(i - STEPS, 0), 0)),
            late(length),
            late(length),
            early(STATE),
            late(STATE),
            late(8),
            whole(length, D),
            whole(8, D),
        ],
        out_shape=[
            jax.ShapeDtypeStruct((INNER, length), BF16),
            jax.ShapeDtypeStruct((length, PROJ), BF16),
            jax.ShapeDtypeStruct((length, INNER), BF16),
            jax.ShapeDtypeStruct((STATE, INNER), BF16),
            jax.ShapeDtypeStruct((STATE, INNER), BF16),
            jax.ShapeDtypeStruct((8, INNER), F32),
            jax.ShapeDtypeStruct((length, D), BF16),
            jax.ShapeDtypeStruct((8, D), F32),
        ],
        scratch_shapes=[
            pltpu.VMEM((STEPS, length, BLK), F32),
            pltpu.VMEM((STEPS, length, BLK), F32),
            pltpu.VMEM((length, 128), F32),
            pltpu.VMEM((length, 128), F32),
            pltpu.VMEM((length, D), F32),
            pltpu.VMEM((128, length), BF16),
        ],
        compiler_params=pltpu.CompilerParams(vmem_limit_bytes=VMEM_LIMIT),
        cost_estimate=pl.CostEstimate(
            flops=12 * 10**9, bytes_accessed=50 * 10**6, transcendentals=4 * 10**6
        ),
        name="tail",
    )(place, y, xs, projected, states, kept, out_whole, c_rows, entering, heads, gain, cot, units)


def back_kernel(
    place_ref, x_ref, dtraw_ref, halo_ref, taps_ref, heads_ref, seg_ref, row_ref, b_ref, c_ref, dt_ref, run_ref,
    dy_ref, sin_ref, dstates_ref, kept_ref, given_ref,
    dproj_ref, dhalo_ref, dtaps_ref, dheads_ref,
    ext, pre, dact, dbuf, scores, dscores, run_t, b_t, c_t, enter, leave, d_b, d_c, suffix, prefix, d_dt, fixed, states,
):
    step = pl.program_id(0)
    length = x_ref.shape[0]
    chunks = length // Q

    @pl.when(step == 0)
    def _():
        for k in range(chunks):
            rows = slice(k * Q, (k + 1) * Q)
            b_rows, c_rows = b_ref[rows, :], c_ref[rows, :]
            b_t[:, rows] = b_rows.astype(F32).T.astype(BF16)
            c_t[:, rows] = c_rows.astype(F32).T.astype(BF16)
            scores[rows, :] = masked_scores(seg_ref, row_ref, b_rows, c_rows, k)
            running = run_ref[rows, :]
            run_t[k] = running.T
            carry, tail = chunk_flags(seg_ref, k)
            enter[rows, :] = jnp.exp(running) * carry
            leave[rows, :] = jnp.exp(running[Q - 1 : Q, :] - running) * tail
        for each in (dscores, d_b, d_c, suffix, prefix, d_dt, fixed):
            each[...] = jnp.zeros_like(each)
        dbuf[0:PAD, :] = jnp.zeros((PAD, BLK), F32)
        dbuf[PAD + length :, :] = jnp.zeros((PAD, BLK), F32)

    @pl.when(step <= STEPS)
    def _():
        ext[0:PAD, :] = halo_ref[...]
        ext[PAD:, :] = x_ref[...].astype(F32)
        for k in range(chunks):
            pre[k * Q : (k + 1) * Q, :] = conv_rows(ext, seg_ref, taps_ref, k * Q, Q)

    @pl.when(step < STEPS)
    def _():
        select = chosen(step)
        gather = chosen_back(step)
        skip = widen(heads_ref[...], select)[2:3, :]
        state = sin_ref[...].astype(F32)
        for k in range(chunks):
            rows = slice(k * Q, (k + 1) * Q)
            states[k] = state
            if k + 1 < chunks:
                total = pre[rows, :]
                scaled = total * sigmoid(total) * widen(dt_ref[rows, :], select)
                weighted = (scaled.astype(BF16).astype(F32) * widen(leave[rows, :], select)).astype(BF16)
                last = widen(enter[rows.stop - 8 : rows.stop, :], select)[7:8, :]
                state = last * state + dot(b_t[:, rows], weighted)
        d_state = joined_states(dstates_ref, kept_ref, place_ref[0], select, False)
        for k in range(chunks - 1, -1, -1):
            rows = slice(k * Q, (k + 1) * Q)
            total = pre[rows, :]
            values = total * sigmoid(total)
            step_size = widen(dt_ref[rows, :], select)
            entering = widen(enter[rows, :], select)
            leaving = widen(leave[rows, :], select)
            scaled = (values * step_size).astype(BF16)
            scaled_wide = scaled.astype(F32)
            dy = dy_ref[rows, :]
            dy_wide = dy.astype(F32)
            before = states[k]
            before_low = before.astype(BF16)
            d_low = d_state.astype(BF16)
            running = pltpu.roll(run_ref[rows, :], lax.rem(128 - step * GROUP, 128), 1)
            insides, backs = [], []
            d_score = dscores[rows, :]
            for pair in range(2):
                lanes = slice(pair * 128, (pair + 1) * 128)
                mixing, turned, decays = [], [], []
                for one in range(2):
                    head = 2 * pair + one
                    gap = running[:, head : head + 1] - run_t[k, pl.ds(step * GROUP + head, 1), :]
                    decay = jnp.exp(jnp.minimum(gap, 0.0))
                    mixed = decay * scores[rows, :]
                    decays.append(decay)
                    mixing.append(mixed.astype(BF16))
                    turned.append(mixed.T.astype(BF16))
                spread = halves(scaled[:, lanes])
                insides.append(dot(jnp.concatenate(mixing, axis=1), spread))
                backs.append(dot(jnp.concatenate(turned, axis=1), halves(dy[:, lanes])))
                products = dot_nt(dy[:, lanes], spread)
                d_score = d_score + decays[0] * products[:, :Q] + decays[1] * products[:, Q:]
            dscores[rows, :] = d_score
            inside = jnp.concatenate(insides, axis=1) + entering * dot(c_ref[rows, :], before_low)
            back_inside = jnp.concatenate(backs, axis=1)
            back_state = leaving * dot(b_ref[rows, :], d_low)
            high, low = in_two(dy_wide * inside - scaled_wide * back_inside)
            suffix[rows, :] += dot(high, gather) + dot(low, gather)
            prefix[rows, :] += dot((scaled_wide * back_state).astype(BF16), gather)
            back = back_inside + back_state
            d_dt[rows, :] += dot((values * back).astype(BF16), gather)
            entered = (dy_wide * entering).astype(BF16)
            d_c[rows, :] += dot_nt(entered, before_low)
            d_b[rows, :] += dot_nt((scaled_wide * leaving).astype(BF16), d_low)
            kept = entering[Q - 1 : Q, :]
            through = jnp.sum(before * d_state, axis=0, keepdims=True) * kept
            high, low = in_two(jnp.broadcast_to(through, (8, BLK)))
            fixed[k * 8 : (k + 1) * 8, :] += dot(high, gather) + dot(low, gather)
            d_state = kept * d_state + dot(c_t[:, rows], entered)
            dact[rows, :] = back * step_size + skip * dy_wide

    @pl.when(step == STEPS)
    def _():
        for k in range(chunks):
            rows = slice(k * Q, (k + 1) * Q)
            own = seg_ref[PAD + k * Q : PAD + (k + 1) * Q, :]
            keep = (own == row_ref[0:1, rows]) & (iota((Q, Q), 1) <= iota((Q, Q), 0))
            d_score = jnp.where(keep, dscores[rows, :], 0.0)
            dact[rows, STATE:] = d_c[rows, :] + dot(d_score.astype(BF16), b_ref[rows, :])
            dact[rows, :STATE] = d_b[rows, :] + dot(d_score.T.astype(BF16), c_ref[rows, :])

    @pl.when(step <= STEPS)
    def _():
        sums = [jnp.zeros((1, BLK), F32) for _ in range(CONV + 1)]
        for k in range(chunks):
            rows = slice(k * Q, (k + 1) * Q)
            total = pre[rows, :]
            sig = sigmoid(total)
            d_conv = dact[rows, :] * (sig * (1.0 + total * (1.0 - sig)))
            dbuf[PAD + k * Q : PAD + (k + 1) * Q, :] = d_conv
            sums[4] = sums[4] + jnp.sum(d_conv, axis=0, keepdims=True)
            own = seg_ref[PAD + k * Q : PAD + (k + 1) * Q, :]
            for shift in range(CONV):
                at = PAD + k * Q - shift
                term = d_conv * ext[at : at + Q, :]
                if shift:
                    term = jnp.where(both(seg_ref[at : at + Q, :] == own), term, 0.0)
                sums[3 - shift] = sums[3 - shift] + jnp.sum(term, axis=0, keepdims=True)
        dtaps_ref[...] = jnp.concatenate(sums + [jnp.zeros((3, BLK), F32)], axis=0)

        def returned(at, rows):
            own = seg_ref[at : at + rows, :]
            result = taps_ref[3:4, :] * dbuf[at : at + rows, :]
            for shift in range(1, CONV):
                same = both(seg_ref[at + shift : at + shift + rows, :] == own)
                result = result + jnp.where(
                    same, taps_ref[3 - shift : 4 - shift, :] * dbuf[at + shift : at + shift + rows, :], 0.0
                )
            return result

        dhalo_ref[...] = returned(0, PAD)
        for k in range(chunks):
            dproj_ref[k * Q : (k + 1) * Q, :] = returned(PAD + k * Q, Q).astype(BF16)

    @pl.when(step == STEPS + 1)
    def _():
        lower = (iota((Q, Q), 1) < iota((Q, Q), 0)).astype(F32)
        upper = (iota((Q, Q), 1) >= iota((Q, Q), 0)).astype(F32)
        lane = iota((Q, 128), 1)
        rate = jnp.exp(heads_ref[1:2, :])
        bias_sum = jnp.zeros((1, 128), F32)
        decay_sum = jnp.zeros((1, 128), F32)
        for k in range(chunks):
            rows = slice(k * Q, (k + 1) * Q)
            d_log = jnp.dot(upper, suffix[rows, :], precision=HIGHEST, preferred_element_type=F32)
            d_log = d_log + jnp.dot(lower, prefix[rows, :], precision=HIGHEST, preferred_element_type=F32)
            d_log = d_log + fixed[k * 8 : k * 8 + 1, :]
            raw = jnp.where(lane < HEADS, dtraw_ref[rows, :128].astype(F32), 0.0) + heads_ref[0:1, :]
            d_raw = jnp.where(lane < HEADS, (d_dt[rows, :] - rate * d_log) * sigmoid(raw), 0.0)
            bias_sum = bias_sum + jnp.sum(d_raw, axis=0, keepdims=True)
            decay_sum = decay_sum - jnp.sum(d_log * dt_ref[rows, :] * rate, axis=0, keepdims=True)
            dproj_ref[rows, :] = jnp.concatenate([d_raw, jnp.zeros_like(d_raw)], axis=1).astype(BF16)
        dheads_ref[...] = jnp.concatenate([bias_sum, decay_sum, jnp.zeros((6, 128), F32)], axis=0)


def back(place, projected, halo, taps, heads, seg_lanes, seg_row, b_rows, c_rows, dt, running, dy, incoming, dstates, kept, given):
    length = projected.shape[0]
    count = dstates.shape[0]
    whole = lambda *shape: pl.BlockSpec(shape, lambda j: (0,) * len(shape))
    upto = lambda last, first=0: lambda j: (0, first + jnp.minimum(j, last))
    return pl.pallas_call(
        back_kernel,
        grid=(STEPS + 2,),
        in_specs=[
            pl.BlockSpec(memory_space=pltpu.SMEM),
            pl.BlockSpec((length, BLK), upto(STEPS, STEPS)),
            pl.BlockSpec((length, BLK), lambda j: (0, 2 * STEPS + 1)),
            pl.BlockSpec((PAD, BLK), upto(STEPS)),
            pl.BlockSpec((8, BLK), upto(STEPS)),
            whole(8, 128),
            whole(length + 2 * PAD, 128),
            whole(8, length),
            whole(length, 128),
            whole(length, 128),
            whole(length, 128),
            whole(length, 128),
            pl.BlockSpec((length, BLK), upto(STEPS - 1)),
            pl.BlockSpec((STATE, BLK), upto(STEPS - 1)),
            pl.BlockSpec((count, STATE, BLK), lambda j: (0, 0, jnp.minimum(j, STEPS - 1))),
            whole(count, 8, 128),
            pl.BlockSpec(memory_space=pl.ANY),
        ],
        out_specs=[
            pl.BlockSpec((length, BLK), lambda j: (0, STEPS + j)),
            pl.BlockSpec((PAD, BLK), upto(STEPS)),
            pl.BlockSpec((8, BLK), upto(STEPS)),
            whole(8, 128),
        ],
        out_shape=[
            jax.ShapeDtypeStruct((length, PROJ), BF16),
            jax.ShapeDtypeStruct((PAD, XBC), F32),
            jax.ShapeDtypeStruct((8, XBC), F32),
            jax.ShapeDtypeStruct((8, 128), F32),
        ],
        scratch_shapes=[
            pltpu.VMEM((length + PAD, BLK), F32),
            pltpu.VMEM((length, BLK), F32),
            pltpu.VMEM((length, BLK), F32),
            pltpu.VMEM((length + 2 * PAD, BLK), F32),
            pltpu.VMEM((length, Q), F32),
            pltpu.VMEM((length, Q), F32),
            pltpu.VMEM((length // Q, 128, Q), F32),
            pltpu.VMEM((128, length), BF16),
            pltpu.VMEM((128, length), BF16),
            pltpu.VMEM((length, 128), F32),
            pltpu.VMEM((length, 128), F32),
            pltpu.VMEM((length, 128), F32),
            pltpu.VMEM((length, 128), F32),
            pltpu.VMEM((length, 128), F32),
            pltpu.VMEM((length, 128), F32),
            pltpu.VMEM((length, 128), F32),
            pltpu.VMEM((8 * (length // Q), 128), F32),
            pltpu.VMEM((length // Q, STATE, BLK), F32),
        ],
        input_output_aliases={16: 0},
        compiler_params=pltpu.CompilerParams(vmem_limit_bytes=VMEM_LIMIT),
        cost_estimate=pl.CostEstimate(
            flops=12 * 10**9, bytes_accessed=30 * 10**6, transcendentals=2 * 10**7
        ),
        name="back",
    )(
        place, projected, projected, halo, taps, heads, seg_lanes, seg_row, b_rows, c_rows, dt, running, dy, incoming, dstates, kept, given
    )


WIDE = 512
OUT_CHUNKS = 2 * D // WIDE
IN_CHUNKS = -(-PROJ // WIDE)
CHUNKS = OUT_CHUNKS + IN_CHUNKS
LAGS = 8
SHARD = D // 4
PIECE = SHARD // 8
SMALL_ROWS = 168


def flipped(index, bit):
    return index + bit - 2 * bit * lax.rem(index // bit, 2)


def reduce_kernel(
    lhs_in, lhs_out, rhs_in, rhs_out, small_ref,
    din_ref, dout_ref, total_ref,
    own, core_send, core_recv, y_recv, x_recv, z_recv, w_recv, final, small_send, small_recv,
    send_sems, recv_sems, small_send_sems, small_recv_sems,
):
    step = pl.program_id(0)
    shard, part = lax.axis_index("fsdp"), lax.axis_index("ctx")
    core, y = lax.rem(shard, 2), shard // 2
    x, z = lax.rem(part, 2), part // 2
    near, far = lax.rem(z, 2), z // 2
    peers = (
        {"fsdp": flipped(shard, 1)},
        {"fsdp": flipped(shard, 2)},
        {"ctx": flipped(part, 1)},
        {"ctx": flipped(part, 2)},
        {"ctx": flipped(part, 4)},
    )

    def sent(stage, k, source, target, peer):
        return pltpu.make_async_remote_copy(
            src_ref=source,
            dst_ref=target,
            send_sem=send_sems.at[stage, k],
            recv_sem=recv_sems.at[stage, k],
            device_id=peers[peer],
            device_id_type=pl.DeviceIdType.MESH,
        )

    copies = (
        lambda k: sent(0, k, core_send.at[lax.rem(k, 2)], core_recv.at[k], 0),
        lambda k: sent(1, k, core_recv.at[k, 1 - y], y_recv.at[k], 1),
        lambda k: sent(2, k, y_recv.at[k, 1 - x], x_recv.at[k], 2),
        lambda k: sent(3, k, x_recv.at[k, 1 - near], z_recv.at[k], 3),
        lambda k: sent(4, k, z_recv.at[k, 1 - far], w_recv.at[k], 4),
        lambda k: sent(5, k, final.at[k, x, near, far], final.at[k, x, near, far], 4),
        lambda k: sent(6, k, final.at[k, x, near], final.at[k, x, near], 3),
        lambda k: sent(7, k, final.at[k, x], final.at[k, x], 2),
    )
    arrivals = copies[:5] + (
        lambda k: sent(5, k, final.at[k, x, near, 1 - far], final.at[k, x, near, 1 - far], 4),
        lambda k: sent(6, k, final.at[k, x, 1 - near], final.at[k, x, 1 - near], 3),
        lambda k: sent(7, k, final.at[k, 1 - x], final.at[k, 1 - x], 2),
    )

    def small_copy(stage):
        return pltpu.make_async_remote_copy(
            src_ref=small_send.at[stage],
            dst_ref=small_recv.at[stage],
            send_sem=small_send_sems.at[stage],
            recv_sem=small_recv_sems.at[stage],
            device_id=peers[stage],
            device_id_type=pl.DeviceIdType.MESH,
        )

    @pl.when(step == 0)
    def _():
        barrier = pltpu.get_barrier_semaphore()
        for peer in peers:
            pl.semaphore_signal(barrier, inc=1, device_id=peer, device_id_type=pl.DeviceIdType.MESH)
        pl.semaphore_wait(barrier, len(peers))
        small_send[0] = small_ref[...]
        small_copy(0).start()

    for stage in range(5):

        @pl.when(step == stage + 1)
        def _():
            small_copy(stage).wait()
            total = small_send[stage] + small_recv[stage]
            if stage < 4:
                small_send[stage + 1] = total
                small_copy(stage + 1).start()
            else:
                total_ref[...] = total

    def partial(lhs_of, rhs):
        for row in range(2):
            value = dot(lhs_of(2 * row + 1 - core), rhs).astype(BF16)
            core_send[lax.rem(step, 2), row] = value.reshape(2, 2, 2, PIECE, WIDE)
        copies[0](step).start()
        for row in range(2):
            own[row] = dot(lhs_of(2 * row + core), rhs).reshape(2, 2, 2, PIECE, WIDE)

    @pl.when(step < OUT_CHUNKS)
    def _():
        partial(lambda s: lhs_out[s, step // (D // WIDE)], rhs_out[...])

    @pl.when((step >= OUT_CHUNKS) & (step < CHUNKS))
    def _():
        rhs = rhs_in[...]
        columns = iota(rhs.shape, 1) + (step - OUT_CHUNKS) * WIDE
        partial(lambda s: lhs_in[s], jnp.where(columns < PROJ, rhs, jnp.zeros_like(rhs)))

    @pl.when(step < CHUNKS)
    def _():
        arrivals[0](step).wait_recv()
        for row in (1 - y, y):
            core_recv[step, row] = (own[row] + core_recv[step, row].astype(F32)).astype(BF16)
        copies[1](step).start()

    def stage(lag):
        def decorate(body):
            k = step - lag

            @pl.when((k >= 0) & (k < CHUNKS))
            def _():
                body(k)

        return decorate

    def summed(a, b):
        return (a.astype(F32) + b.astype(F32)).astype(BF16)

    @stage(1)
    def _(k):
        arrivals[1](k).wait_recv()
        kept = core_recv.at[k, y]
        y_recv[k] = summed(y_recv[k], kept[...])
        copies[2](k).start()
        copies[0](k).wait_send()

    @stage(2)
    def _(k):
        arrivals[2](k).wait_recv()
        x_recv[k] = summed(x_recv[k], y_recv[k, x])
        copies[3](k).start()

    @stage(3)
    def _(k):
        arrivals[3](k).wait_recv()
        z_recv[k] = summed(z_recv[k], x_recv[k, near])
        copies[4](k).start()

    @stage(4)
    def _(k):
        arrivals[4](k).wait_recv()
        final[k, x, near, far] = summed(w_recv[k], z_recv[k, far])
        copies[5](k).start()

    @stage(5)
    def _(k):
        arrivals[5](k).wait_recv()
        copies[6](k).start()

    @stage(6)
    def _(k):
        arrivals[6](k).wait_recv()
        copies[7](k).start()

    @stage(7)
    def _(k):
        arrivals[7](k).wait_recv()
        for one in range(1, 8):
            copies[one](k).wait_send()
        whole = final[k].reshape(SHARD, WIDE).astype(F32)

        @pl.when(k < OUT_CHUNKS)
        def _():
            dout_ref[...] = whole

        @pl.when(k >= OUT_CHUNKS)
        def _():
            din_ref[...] = whole


def reduce(part_t, mixer_t, dproj, cot, small):
    length = cot.shape[0]
    per_half = D // WIDE
    whole = lambda *shape: pl.BlockSpec(shape, lambda t: (0,) * len(shape))

    def out_block(t):
        k = jnp.clip(t - LAGS + 1, 0, OUT_CHUNKS - 1)
        return (k // per_half, lax.rem(k, per_half))

    slots = lambda *shape: pltpu.VMEM((CHUNKS, *shape, PIECE, WIDE), BF16)
    return pl.pallas_call(
        reduce_kernel,
        grid=(CHUNKS + LAGS - 1,),
        in_specs=[
            whole(4, SHARD, length),
            whole(4, 2, SHARD, length),
            pl.BlockSpec((length, WIDE), lambda t: (0, jnp.clip(t - OUT_CHUNKS, 0, IN_CHUNKS - 1))),
            pl.BlockSpec((length, WIDE), lambda t: (0, lax.rem(jnp.minimum(t, OUT_CHUNKS - 1), per_half))),
            whole(SMALL_ROWS, 128),
        ],
        out_specs=[
            pl.BlockSpec((SHARD, WIDE), lambda t: (0, jnp.clip(t - LAGS + 1 - OUT_CHUNKS, 0, IN_CHUNKS - 1))),
            pl.BlockSpec((SHARD, WIDE), out_block),
            whole(SMALL_ROWS, 128),
        ],
        out_shape=[
            jax.ShapeDtypeStruct((SHARD, PROJ), F32),
            jax.ShapeDtypeStruct((2 * SHARD, D), F32),
            jax.ShapeDtypeStruct((SMALL_ROWS, 128), F32),
        ],
        scratch_shapes=[
            pltpu.VMEM((2, 2, 2, 2, PIECE, WIDE), F32),
            pltpu.VMEM((2, 2, 2, 2, 2, PIECE, WIDE), BF16),
            slots(2, 2, 2, 2),
            slots(2, 2, 2),
            slots(2, 2),
            slots(2),
            slots(),
            slots(2, 2, 2),
            pltpu.VMEM((5, SMALL_ROWS, 128), F32),
            pltpu.VMEM((5, SMALL_ROWS, 128), F32),
            pltpu.SemaphoreType.DMA((8, CHUNKS)),
            pltpu.SemaphoreType.DMA((8, CHUNKS)),
            pltpu.SemaphoreType.DMA((5,)),
            pltpu.SemaphoreType.DMA((5,)),
        ],
        compiler_params=pltpu.CompilerParams(
            vmem_limit_bytes=VMEM_LIMIT, collective_id=0, has_side_effects=True
        ),
        name="reduce",
    )(part_t, mixer_t, dproj, cot, small)


def passed_along(block, axis, distance):
    devices = range(lax.axis_size(axis))
    route = [(i - distance, i) for i in devices if i - distance in devices]
    return lax.ppermute(block, axis, route)


def pack_small(conv_taps, conv_bias, dt_bias, decay_log, skip_scale, mixer_gain, input_gain):
    width = conv_bias.shape[0]

    def line(*parts):
        flat = jnp.concatenate(parts)
        return jnp.pad(flat, (0, width - flat.shape[0]))[None]

    return jnp.concatenate(
        [
            conv_taps.T,
            conv_bias[None],
            line(mixer_gain),
            line(input_gain),
            line(dt_bias, decay_log, skip_scale),
        ],
        axis=0,
    )


def unpack_small(whole):
    shards, _, width = whole.shape
    joined = jnp.swapaxes(whole, 0, 1)
    taps = jnp.pad(joined[:5].reshape(5, shards * width).astype(F32), ((0, 3), (0, 0)))
    gain = joined[5, :, : INNER // shards].reshape(1, INNER).astype(F32)
    input_gain = joined[6, :, : D // shards].reshape(1, D).astype(F32)
    own = HEADS // shards
    heads = joined[7, :, : 3 * own].reshape(shards, 3, own).swapaxes(0, 1).reshape(3, HEADS)
    heads = jnp.pad(heads.astype(F32), ((0, 5), (0, 128 - HEADS)))
    return taps, jnp.pad(gain, ((0, 7), (0, 0))), input_gain, heads


def on_device(
    inputs,
    segment_ids,
    out_grad,
    in_matrix,
    out_matrix,
    conv_taps,
    conv_bias,
    dt_bias,
    decay_log,
    skip_scale,
    mixer_gain,
    input_gain,
):
    shards, parts = lax.axis_size("fsdp"), lax.axis_size("ctx")
    place = jnp.reshape(lax.axis_index("ctx"), (1,)).astype(jnp.int32)
    units_low, cot = inputs[0], out_grad[0]
    units = units_low.astype(F32)
    seg_ids = segment_ids[0]
    length = units.shape[0]
    small = lax.all_gather(
        pack_small(conv_taps, conv_bias, dt_bias, decay_log, skip_scale, mixer_gain, input_gain), "fsdp"
    )
    w_whole = lax.all_gather(in_matrix, "fsdp", axis=0, tiled=True)
    out_whole = lax.all_gather(out_matrix, "fsdp", axis=0, tiled=True)
    taps, gain, g_float, heads = unpack_small(small)
    rim_seg = passed_along(seg_ids[length - CONV + 1 :], "ctx", 1)
    seg_ext = jnp.concatenate(
        [
            jnp.full((PAD - CONV + 1,), -1, jnp.int32),
            rim_seg,
            seg_ids,
            jnp.full((PAD,), -2, jnp.int32),
        ]
    )
    seg_lanes = jnp.broadcast_to(seg_ext[:, None], (length + 2 * PAD, 128))
    seg_row = jnp.broadcast_to(seg_ids[None], (8, length))

    inv_rms = lax.rsqrt(jnp.mean(units * units, axis=-1, keepdims=True) + epsilon)
    base_rows = units * inv_rms
    part_rows = (base_rows * g_float).astype(BF16)
    projected = dot(part_rows, w_whole).astype(BF16)
    rim_rows = passed_along(projected[length - CONV + 1 :, INNER : INNER + XBC], "ctx", 1)
    halo = jnp.pad(rim_rows, ((PAD - CONV + 1, 0), (0, 0))).astype(F32)

    xs, y_local, state, b_rows, c_rows, dt, running, entering, keep = front(
        projected, halo, taps, heads, seg_lanes, seg_row
    )
    kept = lax.all_gather(keep, "ctx")
    states = lax.all_gather(state, "ctx")
    mixer_t, dproj, dy, incoming, d_incoming, column_sums, block_out, stats = tail(
        place, y_local, xs, projected, states, kept, out_whole, c_rows, entering, heads, gain, cot, units_low
    )
    dstates = lax.all_gather(d_incoming, "ctx")
    dproj, d_halo, d_taps, d_heads = back(
        place, projected, halo, taps, heads, seg_lanes, seg_row, b_rows, c_rows, dt, running, dy, incoming, dstates, kept, dproj
    )
    returned = passed_along(d_halo.astype(BF16), "ctx", -1)
    last = lax.slice(dproj, (length - PAD, INNER), (length, INNER + XBC))
    last = (last.astype(F32) + returned.astype(F32)).astype(BF16)
    dproj = lax.dynamic_update_slice(dproj, last, (length - PAD, INNER))

    d_normed = dot_nt(dproj, w_whole)
    d_input_gain = jnp.sum(d_normed * base_rows, axis=0)
    d_base = d_normed * g_float
    d_units = inv_rms * (d_base - base_rows * jnp.mean(d_base * base_rows, axis=-1, keepdims=True))
    input_grad = (cot.astype(F32) + d_units).astype(BF16)

    row = jnp.concatenate(
        [
            d_taps[:5].reshape(-1),
            column_sums[0],
            d_input_gain,
            d_heads[0, :HEADS],
            d_heads[1, :HEADS],
            jnp.sum(column_sums[1].reshape(HEADS, HDIM), axis=1),
            jnp.sum(stats[:2], axis=1),
        ]
    )
    row = jnp.pad(row, (0, SMALL_ROWS * 128 - row.shape[0])).reshape(SMALL_ROWS, 128)
    if (shards, parts) == (4, 8):
        d_in, d_out, row = reduce(
            part_rows.T.reshape(4, SHARD, length), mixer_t.reshape(4, 2, SHARD, length), dproj, cot, row
        )
    else:
        d_in = jnp.dot(part_rows.T, dproj, preferred_element_type=F32)
        d_out = jnp.dot(mixer_t, cot, preferred_element_type=F32)

        def scattered(grad):
            return lax.psum_scatter(grad.astype(BF16), "fsdp", scatter_dimension=0, tiled=True)

        d_in = lax.psum(scattered(d_in), "ctx").astype(F32)
        d_out = lax.psum(scattered(d_out), "ctx").astype(F32)
        row = lax.psum(row, ("fsdp", "ctx"))
    row = row.reshape(-1)
    me = lax.axis_index("fsdp")

    def own(flat):
        size = flat.shape[-1] // shards
        return lax.dynamic_slice_in_dim(flat, me * size, size, flat.ndim - 1)

    at = 5 * XBC
    taps_sum = row[:at].reshape(5, XBC)
    gain_sum = row[at : at + INNER]
    input_gain_sum = row[at + INNER : at + INNER + D]
    at = at + INNER + D
    head_sums = row[at : at + 3 * HEADS].reshape(3, HEADS)
    stat_sums = row[at + 3 * HEADS : at + 3 * HEADS + 2]
    rms_stats = jnp.sqrt(stat_sums / (length * shards * parts * D))
    return (
        block_out[None],
        input_grad[None],
        d_in,
        d_out,
        own(taps_sum[:4]).T,
        own(taps_sum[4]),
        own(head_sums[0]),
        own(head_sums[1]),
        own(head_sums[2]),
        own(gain_sum),
        own(input_gain_sum),
        rms_stats,
    )


def solution(mesh):
    return jax.shard_map(
        on_device,
        mesh=mesh,
        in_specs=(
            P("fsdp", "ctx", None),
            P("fsdp", "ctx"),
            P("fsdp", "ctx", None),
            P("fsdp", None),
            P("fsdp", None),
            P("fsdp", None),
            P("fsdp"),
            P("fsdp"),
            P("fsdp"),
            P("fsdp"),
            P("fsdp"),
            P("fsdp"),
        ),
        out_specs=(
            P("fsdp", "ctx", None),
            P("fsdp", "ctx", None),
            P("fsdp", None),
            P("fsdp", None),
            P("fsdp", None),
            P("fsdp"),
            P("fsdp"),
            P("fsdp"),
            P("fsdp"),
            P("fsdp"),
            P("fsdp"),
            P(),
        ),
        check_vma=False,
    )
```

```python
import functools

import jax
import jax.numpy as jnp
from jax import lax
from jax.experimental import pallas as pl
from jax.experimental.pallas import tpu as pltpu
from jax.sharding import PartitionSpec as P

D = 1536
HEADS = 48
HDIM = 64
STATE = 128
CONV = 4
INNER = 3072
XBC = 3328
PROJ = 6448

BLK = 256
GROUP = BLK // HDIM
STEPS = INNER // BLK
Q = 128
PAD = 8

epsilon = 1e-05
F32, BF16 = jnp.float32, jnp.bfloat16
HIGHEST = lax.Precision.HIGHEST
VMEM_LIMIT = 60 * 1024 * 1024


def communicating(number, exchanging):
    if not exchanging:
        return pltpu.CompilerParams(vmem_limit_bytes=VMEM_LIMIT)
    return pltpu.CompilerParams(
        vmem_limit_bytes=VMEM_LIMIT, collective_id=number, has_side_effects=True
    )


def dot(a, b):
    return jnp.dot(a, b, preferred_element_type=F32)


def dot_nt(a, b):
    return lax.dot_general(a, b, (((1,), (1,)), ((), ())), preferred_element_type=F32)


def iota(shape, dim):
    return lax.broadcasted_iota(jnp.int32, shape, dim)


def sigmoid(v):
    return 1.0 / (1.0 + jnp.exp(-v))


def in_two(a):
    high = a.astype(BF16)
    return high, (a - high.astype(F32)).astype(BF16)


def chosen(step):
    columns = step * GROUP + lax.shift_right_logical(iota((128, BLK), 1), 6)
    return (iota((128, BLK), 0) == columns).astype(BF16)


def chosen_back(step):
    heads = step * GROUP + lax.shift_right_logical(iota((BLK, 128), 0), 6)
    return (iota((BLK, 128), 1) == heads).astype(BF16)


def widen(per_head, select):
    high, low = in_two(per_head)
    return dot(high, select) + dot(low, select)


def halves(pair):
    first = iota(pair.shape, 1) < HDIM
    zero = jnp.zeros_like(pair)
    return jnp.concatenate([jnp.where(first, pair, zero), jnp.where(first, zero, pair)], axis=0)


def both(mask):
    return jnp.concatenate([mask, mask], axis=1)


def conv_rows(ext_ref, seg_ref, taps_ref, start, rows):
    own = seg_ref[start + PAD : start + PAD + rows, :]
    total = taps_ref[4:5, :] + taps_ref[3:4, :] * ext_ref[start + PAD : start + PAD + rows, :]
    for back in range(1, CONV):
        at = start + PAD - back
        same = both(seg_ref[at : at + rows, :] == own)
        total = total + jnp.where(
            same, taps_ref[3 - back : 4 - back, :] * ext_ref[at : at + rows, :], 0.0
        )
    return total


def chunk_flags(seg_ref, k):
    own = seg_ref[PAD + k * Q : PAD + (k + 1) * Q, :]
    before = seg_ref[PAD + k * Q - 1 : PAD + k * Q, :]
    last = seg_ref[PAD + (k + 1) * Q - 1 : PAD + (k + 1) * Q, :]
    return (own == before).astype(F32), (own == last).astype(F32)


def masked_scores(seg_ref, row_ref, b_rows, c_rows, k):
    own = seg_ref[PAD + k * Q : PAD + (k + 1) * Q, :]
    row = row_ref[0:1, k * Q : (k + 1) * Q]
    keep = (own == row) & (iota((Q, Q), 1) <= iota((Q, Q), 0))
    return jnp.where(keep, dot_nt(c_rows, b_rows), 0.0)


PARTS = 8
SLAB = STATE // PARTS
JOIN, DONE = 2, 4


class Exchange:
    def __init__(self, held, gathered, joined, incoming, sems):
        self.held, self.gathered, self.joined, self.incoming, self.sems = held, gathered, joined, incoming, sems
        self.me = lax.axis_index("ctx")

    def others(self):
        return [lax.rem(self.me + hop, PARTS) for hop in range(1, PARTS)]

    def greet(self):
        barrier = pltpu.get_barrier_semaphore()
        for other in self.others():
            pl.semaphore_signal(
                barrier, inc=1, device_id={"ctx": other}, device_id_type=pl.DeviceIdType.MESH
            )
        pl.semaphore_wait(barrier, PARTS - 1)

    def copy(self, source, target, kind, group, other):
        return pltpu.make_async_remote_copy(
            src_ref=source,
            dst_ref=target,
            send_sem=self.sems.at[2 * kind, group],
            recv_sem=self.sems.at[2 * kind + 1, group],
            device_id={"ctx": other},
            device_id_type=pl.DeviceIdType.MESH,
        )

    def all_of(self, kind, group):
        source, target = ((self.held, self.gathered), (self.joined, self.incoming))[kind]
        some = pl.ds(0, PARTS - 1)
        return self.copy(source.at[group, some], target.at[group, some], kind, group, self.others()[0])

    def spread(self, group, state):
        self.held[group] = state.astype(BF16).reshape(PARTS, SLAB, BLK)
        self.gathered[group, self.me] = self.held[group, self.me]
        for other in self.others():
            self.copy(self.held.at[group, other], self.gathered.at[group, self.me], 0, group, other).start()

    def join(self, group, kept, forward):
        self.all_of(0, group).wait_recv()
        total = jnp.zeros((SLAB, BLK), F32)
        for part in range(PARTS) if forward else range(PARTS - 1, -1, -1):
            self.joined[group, part] = total.astype(BF16)
            total = kept[part : part + 1, :] * total + self.gathered[group, part].astype(F32)
        self.incoming[group, self.me] = self.joined[group, self.me]
        for other in self.others():
            self.copy(self.joined.at[group, other], self.incoming.at[group, self.me], 1, group, other).start()

    def finish(self, group):
        self.all_of(1, group).wait_recv()
        self.all_of(0, group).wait_send()
        self.all_of(1, group).wait_send()
        return self.incoming[group].reshape(STATE, BLK)


def exchange_scratch():
    return [pltpu.VMEM((STEPS, PARTS, SLAB, BLK), BF16) for _ in range(4)] + [pltpu.SemaphoreType.DMA((4, STEPS))]


def first_rows(kept_ref):
    return jnp.concatenate([kept_ref[part, 0:1, :] for part in range(PARTS)], axis=0)


def joined_plainly(states, kept, place, forward):
    factors = jnp.repeat(kept[:, 0, :HEADS], HDIM, axis=1)[:, None, :]
    total = jnp.zeros(states.shape[1:], F32)
    result = total
    count = states.shape[0]
    for part in range(count) if forward else range(count - 1, -1, -1):
        result = jnp.where(place == part, total, result)
        total = factors[part] * total + states[part].astype(F32)
    return result.astype(BF16)


def front_kernel(
    x_ref, bc_ref, dtraw_ref, halo_ref, halo_bc_ref, taps_ref, taps_bc_ref, heads_ref, seg_ref, row_ref,
    xs_ref, y_ref, state_ref, b_ref, c_ref, dt_ref, run_ref, in_ref, keep_ref,
    ext, scores, run_t, b_t, enter, leave, *parts,
):
    step = pl.program_id(0)
    length = x_ref.shape[0]
    chunks = length // Q
    if parts:
        exchange = Exchange(*parts[:5])
        own_keep, keeps, keep_sends, keep_arrivals = parts[5:]

        def keep_copy(hop):
            return pltpu.make_async_remote_copy(
                src_ref=own_keep,
                dst_ref=keeps.at[exchange.me],
                send_sem=keep_sends.at[hop],
                recv_sem=keep_arrivals.at[hop],
                device_id={"ctx": lax.rem(exchange.me + hop + 1, PARTS)},
                device_id_type=pl.DeviceIdType.MESH,
            )

    @pl.when(step == 0)
    def _():
        ext[0:PAD, :] = halo_bc_ref[...]
        ext[PAD:, :] = bc_ref[...].astype(F32)
        lane = iota((Q, 128), 1)
        lower = (iota((Q, Q), 1) <= iota((Q, Q), 0)).astype(F32)
        offset = jnp.zeros((1, 128), F32)
        for k in range(chunks):
            rows = slice(k * Q, (k + 1) * Q)
            total = conv_rows(ext, seg_ref, taps_bc_ref, k * Q, Q)
            active = total * sigmoid(total)
            b_rows, c_rows = active[:, :STATE], active[:, STATE:].astype(BF16)
            b_t[:, rows] = b_rows.T.astype(BF16)
            b_rows = b_rows.astype(BF16)
            b_ref[rows, :] = b_rows
            c_ref[rows, :] = c_rows
            scores[rows, :] = masked_scores(seg_ref, row_ref, b_rows, c_rows, k)
            raw = jnp.where(lane < HEADS, dtraw_ref[rows, :128].astype(F32), 0.0) + heads_ref[0:1, :]
            dt = jnp.maximum(raw, 0.0) + jnp.log1p(jnp.exp(-jnp.abs(raw)))
            log_decay = -dt * jnp.exp(heads_ref[1:2, :])
            running = jnp.dot(lower, log_decay, precision=HIGHEST, preferred_element_type=F32)
            dt_ref[rows, :] = dt
            run_ref[rows, :] = running
            run_t[k] = running.T
            carry, tail = chunk_flags(seg_ref, k)
            enter[rows, :] = jnp.exp(running) * carry
            leave[rows, :] = jnp.exp(running[Q - 1 : Q, :] - running) * tail
            same = (seg_ref[PAD + k * Q : PAD + (k + 1) * Q, :] == seg_ref[PAD - 1 : PAD, :]).astype(F32)
            whole = jnp.exp(running + offset) * same
            in_ref[rows, :] = whole
            offset = offset + running[Q - 1 : Q, :]
        keep = jnp.broadcast_to(whole[Q - 1 : Q, :], (8, 128))
        if parts:
            own_keep[...] = keep
            keeps[exchange.me] = keep
            exchange.greet()
            for hop in range(PARTS - 1):
                keep_copy(hop).start()
        else:
            keep_ref[0] = keep

    @pl.when(step < STEPS)
    def _():
        state = local_scan(
            step, x_ref, halo_ref, taps_ref, seg_ref, xs_ref, y_ref, c_ref, dt_ref, run_ref,
            ext, scores, run_t, b_t, enter, leave,
        )
        if parts:
            exchange.spread(step, state)
        else:
            state_ref[...] = state.astype(BF16)

    if parts:

        @pl.when(step == JOIN)
        def _():
            for hop in range(PARTS - 1):
                keep_copy(hop).wait()
            keep_ref[...] = keeps[...]

        @pl.when((step >= JOIN) & (step < STEPS + JOIN))
        def _():
            group = step - JOIN
            exchange.join(group, widen(first_rows(keeps), chosen(group)), True)

        @pl.when(step >= DONE)
        def _():
            state_ref[...] = exchange.finish(step - DONE)


def local_scan(
    step, x_ref, halo_ref, taps_ref, seg_ref, xs_ref, y_ref, c_ref, dt_ref, run_ref,
    ext, scores, run_t, b_t, enter, leave,
):
    chunks = x_ref.shape[0] // Q
    ext[0:PAD, :] = halo_ref[...]
    ext[PAD:, :] = x_ref[...].astype(F32)
    select = chosen(step)
    state = jnp.zeros((STATE, BLK), F32)
    for k in range(chunks):
        rows = slice(k * Q, (k + 1) * Q)
        total = conv_rows(ext, seg_ref, taps_ref, k * Q, Q)
        values = total * sigmoid(total)
        xs_ref[rows, :] = values.astype(BF16)
        scaled = (values * widen(dt_ref[rows, :], select)).astype(BF16)
        entering = widen(enter[rows, :], select)
        running = pltpu.roll(run_ref[rows, :], lax.rem(128 - step * GROUP, 128), 1)
        parts = []
        for pair in range(2):
            mixing = []
            for one in range(2):
                head = 2 * pair + one
                gap = running[:, head : head + 1] - run_t[k, pl.ds(step * GROUP + head, 1), :]
                mixing.append((jnp.exp(jnp.minimum(gap, 0.0)) * scores[rows, :]).astype(BF16))
            parts.append(
                dot(jnp.concatenate(mixing, axis=1), halves(scaled[:, pair * 128 : (pair + 1) * 128]))
            )
        inside = jnp.concatenate(parts, axis=1)
        y_ref[rows, :] = (inside + entering * dot(c_ref[rows, :], state.astype(BF16))).astype(BF16)
        weighted = (scaled.astype(F32) * widen(leave[rows, :], select)).astype(BF16)
        state = entering[Q - 1 : Q, :] * state + dot(b_t[:, rows], weighted)
    return state


def front(projected, halo, taps, heads, seg_lanes, seg_row, exchanging):
    length = projected.shape[0]
    last = STEPS - 1
    keeps = PARTS if exchanging else 1
    whole = lambda *shape: pl.BlockSpec(shape, lambda j: (0,) * len(shape))
    columns = lambda rows, at: pl.BlockSpec((rows, BLK), at)
    return pl.pallas_call(
        front_kernel,
        grid=(STEPS + DONE * exchanging,),
        in_specs=[
            columns(length, lambda j: (0, STEPS + jnp.minimum(j, last))),
            columns(length, lambda j: (0, 2 * STEPS)),
            columns(length, lambda j: (0, 2 * STEPS + 1)),
            columns(PAD, lambda j: (0, jnp.minimum(j, last))),
            columns(PAD, lambda j: (0, STEPS)),
            columns(8, lambda j: (0, jnp.minimum(j, last))),
            columns(8, lambda j: (0, STEPS)),
            whole(8, 128),
            whole(length + 2 * PAD, 128),
            whole(8, length),
        ],
        out_specs=[
            columns(length, lambda j: (0, jnp.minimum(j, last))),
            columns(length, lambda j: (0, jnp.minimum(j, last))),
            columns(STATE, lambda j: (0, jnp.maximum(j - DONE * exchanging, 0))),
            whole(length, 128),
            whole(length, 128),
            whole(length, 128),
            whole(length, 128),
            whole(length, 128),
            whole(keeps, 8, 128),
        ],
        out_shape=[
            jax.ShapeDtypeStruct((length, INNER), BF16),
            jax.ShapeDtypeStruct((length, INNER), BF16),
            jax.ShapeDtypeStruct((STATE, INNER), BF16),
            jax.ShapeDtypeStruct((length, 128), BF16),
            jax.ShapeDtypeStruct((length, 128), BF16),
            jax.ShapeDtypeStruct((length, 128), F32),
            jax.ShapeDtypeStruct((length, 128), F32),
            jax.ShapeDtypeStruct((length, 128), F32),
            jax.ShapeDtypeStruct((keeps, 8, 128), F32),
        ],
        scratch_shapes=[
            pltpu.VMEM((length + PAD, BLK), F32),
            pltpu.VMEM((length, Q), F32),
            pltpu.VMEM((length // Q, 128, Q), F32),
            pltpu.VMEM((128, length), BF16),
            pltpu.VMEM((length, 128), F32),
            pltpu.VMEM((length, 128), F32),
        ]
        + (
            exchange_scratch()
            + [
                pltpu.VMEM((8, 128), F32),
                pltpu.VMEM((PARTS, 8, 128), F32),
                pltpu.SemaphoreType.DMA((PARTS - 1,)),
                pltpu.SemaphoreType.DMA((PARTS - 1,)),
            ]
        )
        * exchanging,
        compiler_params=communicating(1, exchanging),
        cost_estimate=pl.CostEstimate(
            flops=6 * 10**9, bytes_accessed=16 * 10**6, transcendentals=10**7
        ),
        name="front",
    )(projected, projected, projected, halo, halo, taps, taps, heads, seg_lanes, seg_row)


def tail_kernel(
    y_ref, xs_ref, gate_ref, incoming_ref, kept_ref, out_ref, c_ref, in_ref, heads_ref, gain_ref, g_ref, units_ref,
    mixer_ref, dproj_ref, dy_ref, dsin_ref, sums_ref, block_ref, stats_ref,
    full, dmix, squares, products, mixed, c_t, *parts,
):
    step = pl.program_id(0)
    length = y_ref.shape[0]
    group = jnp.where(step < STEPS, step, jnp.minimum(step - STEPS, STEPS - 1))
    select = chosen(group)
    half = length // 2
    if parts:
        exchange = Exchange(*parts)

        @pl.when(step == 0)
        def _():
            exchange.greet()

    @pl.when(step == 0)
    def _():
        squares[...] = jnp.zeros_like(squares)
        products[...] = jnp.zeros_like(products)
        for k in range(length // Q):
            rows = slice(k * Q, (k + 1) * Q)
            c_t[:, rows] = c_ref[rows, :].astype(F32).T.astype(BF16)

    @pl.when(step < STEPS)
    def _():
        incoming = incoming_ref[...]
        skip = widen(heads_ref[...], select)[2:3, :]
        for k in range(2):
            rows = slice(k * half, (k + 1) * half)
            y = y_ref[rows, :].astype(F32)
            y = y + widen(in_ref[rows, :], select) * dot(c_ref[rows, :], incoming)
            y = y + skip * xs_ref[rows, :].astype(F32)
            full[step, rows, :] = y
            gate = gate_ref[rows, :].astype(F32)
            gated = y * gate * sigmoid(gate)
            d_mixer = dot_nt(g_ref[rows, :], out_ref[...])
            dmix[step, rows, :] = d_mixer
            square = gated * gated
            product = gated * d_mixer * gain_ref[0:1, :]
            squares[rows, :] += square[:, :128] + square[:, 128:]
            products[rows, :] += product[:, :128] + product[:, 128:]

    @pl.when(step == STEPS)
    def _():
        norm = lax.rsqrt(jnp.sum(squares[...], axis=1, keepdims=True) * (1.0 / INNER) + epsilon)
        mean = norm * jnp.sum(products[...], axis=1, keepdims=True) * (1.0 / INNER)
        squares[...] = jnp.broadcast_to(norm, squares.shape)
        products[...] = jnp.broadcast_to(mean, products.shape)

    @pl.when((step >= STEPS) & (step < 2 * STEPS))
    def _():
        gain = gain_ref[0:1, :]
        d_gain = jnp.zeros((1, BLK), F32)
        d_skip = jnp.zeros((1, BLK), F32)
        d_state = jnp.zeros((STATE, BLK), F32)
        for k in range(2):
            rows = slice(k * half, (k + 1) * half)
            norm, mean = both(squares[rows, :]), both(products[rows, :])
            y = full[group, rows, :]
            d_mixer = dmix[group, rows, :]
            gate = gate_ref[rows, :].astype(F32)
            sig = sigmoid(gate)
            silu = gate * sig
            unit = y * silu * norm
            low = (unit * gain).astype(BF16)
            mixer_ref[:, rows] = (unit * gain).T.astype(BF16)
            part = dot(low, out_ref[...])

            @pl.when(step == STEPS)
            def _():
                mixed[rows, :] = part

            @pl.when(step > STEPS)
            def _():
                mixed[rows, :] += part

            d_gain = d_gain + jnp.sum(d_mixer * unit, axis=0, keepdims=True)
            d_gated = norm * (d_mixer * gain - unit * mean)
            dproj_ref[rows, :] = (d_gated * y * (sig * (1.0 + gate * (1.0 - sig)))).astype(BF16)
            dy = (d_gated * silu).astype(BF16)
            dy_ref[rows, :] = dy
            dy = dy.astype(F32)
            d_skip = d_skip + jnp.sum(dy * xs_ref[rows, :].astype(F32), axis=0, keepdims=True)
            d_state = d_state + dot(c_t[:, rows], (dy * widen(in_ref[rows, :], select)).astype(BF16))
        if parts:
            exchange.spread(group, d_state)
        else:
            dsin_ref[...] = d_state.astype(BF16)
        sums_ref[...] = jnp.concatenate([d_gain, d_skip, jnp.zeros((6, BLK), F32)], axis=0)

    @pl.when(step == 2 * STEPS - 1)
    def _():
        total = units_ref[...].astype(F32) + mixed[...]
        block_ref[...] = total.astype(BF16)
        first = jnp.sum(total * total, axis=0, keepdims=True)
        second = jnp.sum(mixed[...] * mixed[...], axis=0, keepdims=True)
        stats_ref[...] = jnp.concatenate([first, second, jnp.zeros((6, D), F32)], axis=0)

    if parts:
        at = step - STEPS

        @pl.when((at >= JOIN) & (at < STEPS + JOIN))
        def _():
            done = at - JOIN
            exchange.join(done, widen(first_rows(kept_ref), chosen(done)), False)

        @pl.when(at >= DONE)
        def _():
            dsin_ref[...] = exchange.finish(at - DONE)


def tail(y, xs, projected, incoming, kept, out_whole, c_rows, entering, heads, gain, cot, units, exchanging):
    length = y.shape[0]
    group = lambda i: jnp.where(i < STEPS, i, jnp.minimum(i - STEPS, STEPS - 1))
    second = lambda i: jnp.clip(i - STEPS, 0, STEPS - 1)
    early = lambda rows: pl.BlockSpec((rows, BLK), lambda i: (0, jnp.minimum(i, STEPS - 1)))
    late = lambda rows: pl.BlockSpec((rows, BLK), lambda i: (0, second(i)))
    each = lambda rows: pl.BlockSpec((rows, BLK), lambda i: (0, group(i)))
    whole = lambda *shape: pl.BlockSpec(shape, lambda i: (0,) * len(shape))
    return pl.pallas_call(
        tail_kernel,
        grid=(2 * STEPS + DONE * exchanging,),
        in_specs=[
            early(length),
            each(length),
            each(length),
            early(STATE),
            whole(*kept.shape),
            pl.BlockSpec((BLK, D), lambda i: (group(i), 0)),
            whole(length, 128),
            whole(length, 128),
            whole(8, 128),
            each(8),
            whole(length, D),
            whole(length, D),
        ],
        out_specs=[
            pl.BlockSpec((BLK, length), lambda i: (second(i), 0)),
            late(length),
            late(length),
            pl.BlockSpec((STATE, BLK), lambda i: (0, second(i - DONE * exchanging))),
            late(8),
            whole(length, D),
            whole(8, D),
        ],
        out_shape=[
            jax.ShapeDtypeStruct((INNER, length), BF16),
            jax.ShapeDtypeStruct((length, PROJ), BF16),
            jax.ShapeDtypeStruct((length, INNER), BF16),
            jax.ShapeDtypeStruct((STATE, INNER), BF16),
            jax.ShapeDtypeStruct((8, INNER), F32),
            jax.ShapeDtypeStruct((length, D), BF16),
            jax.ShapeDtypeStruct((8, D), F32),
        ],
        scratch_shapes=[
            pltpu.VMEM((STEPS, length, BLK), F32),
            pltpu.VMEM((STEPS, length, BLK), F32),
            pltpu.VMEM((length, 128), F32),
            pltpu.VMEM((length, 128), F32),
            pltpu.VMEM((length, D), F32),
            pltpu.VMEM((128, length), BF16),
        ]
        + exchange_scratch() * exchanging,
        compiler_params=communicating(2, exchanging),
        cost_estimate=pl.CostEstimate(
            flops=12 * 10**9, bytes_accessed=50 * 10**6, transcendentals=4 * 10**6
        ),
        name="tail",
    )(y, xs, projected, incoming, kept, out_whole, c_rows, entering, heads, gain, cot, units)


def back_kernel(
    x_ref, dtraw_ref, halo_ref, taps_ref, heads_ref, seg_ref, row_ref, b_ref, c_ref, dt_ref, run_ref,
    dy_ref, sin_ref, dout_ref, given_ref,
    dproj_ref, dhalo_ref, dtaps_ref, dheads_ref,
    ext, pre, dact, dbuf, scores, dscores, run_t, b_t, c_t, enter, leave, d_b, d_c, suffix, prefix, d_dt, fixed, states,
):
    step = pl.program_id(0)
    length = x_ref.shape[0]
    chunks = length // Q

    @pl.when(step == 0)
    def _():
        for k in range(chunks):
            rows = slice(k * Q, (k + 1) * Q)
            b_rows, c_rows = b_ref[rows, :], c_ref[rows, :]
            b_t[:, rows] = b_rows.astype(F32).T.astype(BF16)
            c_t[:, rows] = c_rows.astype(F32).T.astype(BF16)
            scores[rows, :] = masked_scores(seg_ref, row_ref, b_rows, c_rows, k)
            running = run_ref[rows, :]
            run_t[k] = running.T
            carry, tail = chunk_flags(seg_ref, k)
            enter[rows, :] = jnp.exp(running) * carry
            leave[rows, :] = jnp.exp(running[Q - 1 : Q, :] - running) * tail
        for each in (dscores, d_b, d_c, suffix, prefix, d_dt, fixed):
            each[...] = jnp.zeros_like(each)
        dbuf[0:PAD, :] = jnp.zeros((PAD, BLK), F32)
        dbuf[PAD + length :, :] = jnp.zeros((PAD, BLK), F32)

    @pl.when(step <= STEPS)
    def _():
        ext[0:PAD, :] = halo_ref[...]
        ext[PAD:, :] = x_ref[...].astype(F32)
        for k in range(chunks):
            pre[k * Q : (k + 1) * Q, :] = conv_rows(ext, seg_ref, taps_ref, k * Q, Q)

    @pl.when(step < STEPS)
    def _():
        select = chosen(step)
        gather = chosen_back(step)
        skip = widen(heads_ref[...], select)[2:3, :]
        state = sin_ref[...].astype(F32)
        for k in range(chunks):
            rows = slice(k * Q, (k + 1) * Q)
            states[k] = state
            if k + 1 < chunks:
                total = pre[rows, :]
                scaled = total * sigmoid(total) * widen(dt_ref[rows, :], select)
                weighted = (scaled.astype(BF16).astype(F32) * widen(leave[rows, :], select)).astype(BF16)
                last = widen(enter[rows.stop - 8 : rows.stop, :], select)[7:8, :]
                state = last * state + dot(b_t[:, rows], weighted)
        d_state = dout_ref[...].astype(F32)
        for k in range(chunks - 1, -1, -1):
            rows = slice(k * Q, (k + 1) * Q)
            total = pre[rows, :]
            values = total * sigmoid(total)
            step_size = widen(dt_ref[rows, :], select)
            entering = widen(enter[rows, :], select)
            leaving = widen(leave[rows, :], select)
            scaled = (values * step_size).astype(BF16)
            scaled_wide = scaled.astype(F32)
            dy = dy_ref[rows, :]
            dy_wide = dy.astype(F32)
            before = states[k]
            before_low = before.astype(BF16)
            d_low = d_state.astype(BF16)
            running = pltpu.roll(run_ref[rows, :], lax.rem(128 - step * GROUP, 128), 1)
            insides, backs = [], []
            d_score = dscores[rows, :]
            for pair in range(2):
                lanes = slice(pair * 128, (pair + 1) * 128)
                mixing, turned, decays = [], [], []
                for one in range(2):
                    head = 2 * pair + one
                    gap = running[:, head : head + 1] - run_t[k, pl.ds(step * GROUP + head, 1), :]
                    decay = jnp.exp(jnp.minimum(gap, 0.0))
                    mixed = decay * scores[rows, :]
                    decays.append(decay)
                    mixing.append(mixed.astype(BF16))
                    turned.append(mixed.T.astype(BF16))
                spread = halves(scaled[:, lanes])
                insides.append(dot(jnp.concatenate(mixing, axis=1), spread))
                backs.append(dot(jnp.concatenate(turned, axis=1), halves(dy[:, lanes])))
                products = dot_nt(dy[:, lanes], spread)
                d_score = d_score + decays[0] * products[:, :Q] + decays[1] * products[:, Q:]
            dscores[rows, :] = d_score
            inside = jnp.concatenate(insides, axis=1) + entering * dot(c_ref[rows, :], before_low)
            back_inside = jnp.concatenate(backs, axis=1)
            back_state = leaving * dot(b_ref[rows, :], d_low)
            high, low = in_two(dy_wide * inside - scaled_wide * back_inside)
            suffix[rows, :] += dot(high, gather) + dot(low, gather)
            prefix[rows, :] += dot((scaled_wide * back_state).astype(BF16), gather)
            back = back_inside + back_state
            d_dt[rows, :] += dot((values * back).astype(BF16), gather)
            entered = (dy_wide * entering).astype(BF16)
            d_c[rows, :] += dot_nt(entered, before_low)
            d_b[rows, :] += dot_nt((scaled_wide * leaving).astype(BF16), d_low)
            kept = entering[Q - 1 : Q, :]
            through = jnp.sum(before * d_state, axis=0, keepdims=True) * kept
            high, low = in_two(jnp.broadcast_to(through, (8, BLK)))
            fixed[k * 8 : (k + 1) * 8, :] += dot(high, gather) + dot(low, gather)
            d_state = kept * d_state + dot(c_t[:, rows], entered)
            dact[rows, :] = back * step_size + skip * dy_wide

    @pl.when(step == STEPS)
    def _():
        for k in range(chunks):
            rows = slice(k * Q, (k + 1) * Q)
            own = seg_ref[PAD + k * Q : PAD + (k + 1) * Q, :]
            keep = (own == row_ref[0:1, rows]) & (iota((Q, Q), 1) <= iota((Q, Q), 0))
            d_score = jnp.where(keep, dscores[rows, :], 0.0)
            dact[rows, STATE:] = d_c[rows, :] + dot(d_score.astype(BF16), b_ref[rows, :])
            dact[rows, :STATE] = d_b[rows, :] + dot(d_score.T.astype(BF16), c_ref[rows, :])

    @pl.when(step <= STEPS)
    def _():
        sums = [jnp.zeros((1, BLK), F32) for _ in range(CONV + 1)]
        for k in range(chunks):
            rows = slice(k * Q, (k + 1) * Q)
            total = pre[rows, :]
            sig = sigmoid(total)
            d_conv = dact[rows, :] * (sig * (1.0 + total * (1.0 - sig)))
            dbuf[PAD + k * Q : PAD + (k + 1) * Q, :] = d_conv
            sums[4] = sums[4] + jnp.sum(d_conv, axis=0, keepdims=True)
            own = seg_ref[PAD + k * Q : PAD + (k + 1) * Q, :]
            for shift in range(CONV):
                at = PAD + k * Q - shift
                term = d_conv * ext[at : at + Q, :]
                if shift:
                    term = jnp.where(both(seg_ref[at : at + Q, :] == own), term, 0.0)
                sums[3 - shift] = sums[3 - shift] + jnp.sum(term, axis=0, keepdims=True)
        dtaps_ref[...] = jnp.concatenate(sums + [jnp.zeros((3, BLK), F32)], axis=0)

        def returned(at, rows):
            own = seg_ref[at : at + rows, :]
            result = taps_ref[3:4, :] * dbuf[at : at + rows, :]
            for shift in range(1, CONV):
                same = both(seg_ref[at + shift : at + shift + rows, :] == own)
                result = result + jnp.where(
                    same, taps_ref[3 - shift : 4 - shift, :] * dbuf[at + shift : at + shift + rows, :], 0.0
                )
            return result

        dhalo_ref[...] = returned(0, PAD)
        for k in range(chunks):
            dproj_ref[k * Q : (k + 1) * Q, :] = returned(PAD + k * Q, Q).astype(BF16)

    @pl.when(step == STEPS + 1)
    def _():
        lower = (iota((Q, Q), 1) < iota((Q, Q), 0)).astype(F32)
        upper = (iota((Q, Q), 1) >= iota((Q, Q), 0)).astype(F32)
        lane = iota((Q, 128), 1)
        rate = jnp.exp(heads_ref[1:2, :])
        bias_sum = jnp.zeros((1, 128), F32)
        decay_sum = jnp.zeros((1, 128), F32)
        for k in range(chunks):
            rows = slice(k * Q, (k + 1) * Q)
            d_log = jnp.dot(upper, suffix[rows, :], precision=HIGHEST, preferred_element_type=F32)
            d_log = d_log + jnp.dot(lower, prefix[rows, :], precision=HIGHEST, preferred_element_type=F32)
            d_log = d_log + fixed[k * 8 : k * 8 + 1, :]
            raw = jnp.where(lane < HEADS, dtraw_ref[rows, :128].astype(F32), 0.0) + heads_ref[0:1, :]
            d_raw = jnp.where(lane < HEADS, (d_dt[rows, :] - rate * d_log) * sigmoid(raw), 0.0)
            bias_sum = bias_sum + jnp.sum(d_raw, axis=0, keepdims=True)
            decay_sum = decay_sum - jnp.sum(d_log * dt_ref[rows, :] * rate, axis=0, keepdims=True)
            dproj_ref[rows, :] = jnp.concatenate([d_raw, jnp.zeros_like(d_raw)], axis=1).astype(BF16)
        dheads_ref[...] = jnp.concatenate([bias_sum, decay_sum, jnp.zeros((6, 128), F32)], axis=0)


def back(projected, halo, taps, heads, seg_lanes, seg_row, b_rows, c_rows, dt, running, dy, incoming, outgoing, given):
    length = projected.shape[0]
    whole = lambda *shape: pl.BlockSpec(shape, lambda j: (0,) * len(shape))
    upto = lambda last, first=0: lambda j: (0, first + jnp.minimum(j, last))
    return pl.pallas_call(
        back_kernel,
        grid=(STEPS + 2,),
        in_specs=[
            pl.BlockSpec((length, BLK), upto(STEPS, STEPS)),
            pl.BlockSpec((length, BLK), lambda j: (0, 2 * STEPS + 1)),
            pl.BlockSpec((PAD, BLK), upto(STEPS)),
            pl.BlockSpec((8, BLK), upto(STEPS)),
            whole(8, 128),
            whole(length + 2 * PAD, 128),
            whole(8, length),
            whole(length, 128),
            whole(length, 128),
            whole(length, 128),
            whole(length, 128),
            pl.BlockSpec((length, BLK), upto(STEPS - 1)),
            pl.BlockSpec((STATE, BLK), upto(STEPS - 1)),
            pl.BlockSpec((STATE, BLK), upto(STEPS - 1)),
            pl.BlockSpec(memory_space=pl.ANY),
        ],
        out_specs=[
            pl.BlockSpec((length, BLK), lambda j: (0, STEPS + j)),
            pl.BlockSpec((PAD, BLK), upto(STEPS)),
            pl.BlockSpec((8, BLK), upto(STEPS)),
            whole(8, 128),
        ],
        out_shape=[
            jax.ShapeDtypeStruct((length, PROJ), BF16),
            jax.ShapeDtypeStruct((PAD, XBC), F32),
            jax.ShapeDtypeStruct((8, XBC), F32),
            jax.ShapeDtypeStruct((8, 128), F32),
        ],
        scratch_shapes=[
            pltpu.VMEM((length + PAD, BLK), F32),
            pltpu.VMEM((length, BLK), F32),
            pltpu.VMEM((length, BLK), F32),
            pltpu.VMEM((length + 2 * PAD, BLK), F32),
            pltpu.VMEM((length, Q), F32),
            pltpu.VMEM((length, Q), F32),
            pltpu.VMEM((length // Q, 128, Q), F32),
            pltpu.VMEM((128, length), BF16),
            pltpu.VMEM((128, length), BF16),
            pltpu.VMEM((length, 128), F32),
            pltpu.VMEM((length, 128), F32),
            pltpu.VMEM((length, 128), F32),
            pltpu.VMEM((length, 128), F32),
            pltpu.VMEM((length, 128), F32),
            pltpu.VMEM((length, 128), F32),
            pltpu.VMEM((length, 128), F32),
            pltpu.VMEM((8 * (length // Q), 128), F32),
            pltpu.VMEM((length // Q, STATE, BLK), F32),
        ],
        input_output_aliases={14: 0},
        compiler_params=pltpu.CompilerParams(vmem_limit_bytes=VMEM_LIMIT),
        cost_estimate=pl.CostEstimate(
            flops=12 * 10**9, bytes_accessed=30 * 10**6, transcendentals=2 * 10**7
        ),
        name="back",
    )(
        projected, projected, halo, taps, heads, seg_lanes, seg_row, b_rows, c_rows, dt, running, dy, incoming, outgoing, given
    )


WIDE = 512
OUT_CHUNKS = 2 * D // WIDE
IN_CHUNKS = -(-PROJ // WIDE)
CHUNKS = OUT_CHUNKS + IN_CHUNKS
LAGS = 8
SHARD = D // 4
PIECE = SHARD // 8
SMALL_ROWS = 168


def flipped(index, bit):
    return index + bit - 2 * bit * lax.rem(index // bit, 2)


def reduce_kernel(
    lhs_in, lhs_out, rhs_in, rhs_out, small_ref,
    din_ref, dout_ref, total_ref,
    own, core_send, core_recv, y_recv, x_recv, z_recv, w_recv, final, small_send, small_recv,
    send_sems, recv_sems, small_send_sems, small_recv_sems,
):
    step = pl.program_id(0)
    shard, part = lax.axis_index("fsdp"), lax.axis_index("ctx")
    core, y = lax.rem(shard, 2), shard // 2
    x, z = lax.rem(part, 2), part // 2
    near, far = lax.rem(z, 2), z // 2
    peers = (
        {"fsdp": flipped(shard, 1)},
        {"fsdp": flipped(shard, 2)},
        {"ctx": flipped(part, 1)},
        {"ctx": flipped(part, 2)},
        {"ctx": flipped(part, 4)},
    )

    def sent(stage, k, source, target, peer):
        return pltpu.make_async_remote_copy(
            src_ref=source,
            dst_ref=target,
            send_sem=send_sems.at[stage, k],
            recv_sem=recv_sems.at[stage, k],
            device_id=peers[peer],
            device_id_type=pl.DeviceIdType.MESH,
        )

    copies = (
        lambda k: sent(0, k, core_send.at[lax.rem(k, 2)], core_recv.at[k], 0),
        lambda k: sent(1, k, core_recv.at[k, 1 - y], y_recv.at[k], 1),
        lambda k: sent(2, k, y_recv.at[k, 1 - x], x_recv.at[k], 2),
        lambda k: sent(3, k, x_recv.at[k, 1 - near], z_recv.at[k], 3),
        lambda k: sent(4, k, z_recv.at[k, 1 - far], w_recv.at[k], 4),
        lambda k: sent(5, k, final.at[k, x, near, far], final.at[k, x, near, far], 4),
        lambda k: sent(6, k, final.at[k, x, near], final.at[k, x, near], 3),
        lambda k: sent(7, k, final.at[k, x], final.at[k, x], 2),
    )
    arrivals = copies[:5] + (
        lambda k: sent(5, k, final.at[k, x, near, 1 - far], final.at[k, x, near, 1 - far], 4),
        lambda k: sent(6, k, final.at[k, x, 1 - near], final.at[k, x, 1 - near], 3),
        lambda k: sent(7, k, final.at[k, 1 - x], final.at[k, 1 - x], 2),
    )

    def small_copy(stage):
        return pltpu.make_async_remote_copy(
            src_ref=small_send.at[stage],
            dst_ref=small_recv.at[stage],
            send_sem=small_send_sems.at[stage],
            recv_sem=small_recv_sems.at[stage],
            device_id=peers[stage],
            device_id_type=pl.DeviceIdType.MESH,
        )

    @pl.when(step == 0)
    def _():
        barrier = pltpu.get_barrier_semaphore()
        for peer in peers:
            pl.semaphore_signal(barrier, inc=1, device_id=peer, device_id_type=pl.DeviceIdType.MESH)
        pl.semaphore_wait(barrier, len(peers))
        small_send[0] = small_ref[...]
        small_copy(0).start()

    for stage in range(5):

        @pl.when(step == stage + 1)
        def _():
            small_copy(stage).wait()
            total = small_send[stage] + small_recv[stage]
            if stage < 4:
                small_send[stage + 1] = total
                small_copy(stage + 1).start()
            else:
                total_ref[...] = total

    def partial(lhs_of, rhs):
        for row in range(2):
            value = dot(lhs_of(2 * row + 1 - core), rhs).astype(BF16)
            core_send[lax.rem(step, 2), row] = value.reshape(2, 2, 2, PIECE, WIDE)
        copies[0](step).start()
        for row in range(2):
            own[row] = dot(lhs_of(2 * row + core), rhs).reshape(2, 2, 2, PIECE, WIDE)

    @pl.when(step < OUT_CHUNKS)
    def _():
        partial(lambda s: lhs_out[s, step // (D // WIDE)], rhs_out[...])

    @pl.when((step >= OUT_CHUNKS) & (step < CHUNKS))
    def _():
        rhs = rhs_in[...]
        columns = iota(rhs.shape, 1) + (step - OUT_CHUNKS) * WIDE
        partial(lambda s: lhs_in[s], jnp.where(columns < PROJ, rhs, jnp.zeros_like(rhs)))

    @pl.when(step < CHUNKS)
    def _():
        arrivals[0](step).wait_recv()
        for row in (1 - y, y):
            core_recv[step, row] = (own[row] + core_recv[step, row].astype(F32)).astype(BF16)
        copies[1](step).start()

    def stage(lag):
        def decorate(body):
            k = step - lag

            @pl.when((k >= 0) & (k < CHUNKS))
            def _():
                body(k)

        return decorate

    def summed(a, b):
        return (a.astype(F32) + b.astype(F32)).astype(BF16)

    @stage(1)
    def _(k):
        arrivals[1](k).wait_recv()
        kept = core_recv.at[k, y]
        y_recv[k] = summed(y_recv[k], kept[...])
        copies[2](k).start()
        copies[0](k).wait_send()

    @stage(2)
    def _(k):
        arrivals[2](k).wait_recv()
        x_recv[k] = summed(x_recv[k], y_recv[k, x])
        copies[3](k).start()

    @stage(3)
    def _(k):
        arrivals[3](k).wait_recv()
        z_recv[k] = summed(z_recv[k], x_recv[k, near])
        copies[4](k).start()

    @stage(4)
    def _(k):
        arrivals[4](k).wait_recv()
        final[k, x, near, far] = summed(w_recv[k], z_recv[k, far])
        copies[5](k).start()

    @stage(5)
    def _(k):
        arrivals[5](k).wait_recv()
        copies[6](k).start()

    @stage(6)
    def _(k):
        arrivals[6](k).wait_recv()
        copies[7](k).start()

    @stage(7)
    def _(k):
        arrivals[7](k).wait_recv()
        for one in range(1, 8):
            copies[one](k).wait_send()
        whole = final[k].reshape(SHARD, WIDE).astype(F32)

        @pl.when(k < OUT_CHUNKS)
        def _():
            dout_ref[...] = whole

        @pl.when(k >= OUT_CHUNKS)
        def _():
            din_ref[...] = whole


def reduce(part_t, mixer_t, dproj, cot, small):
    length = cot.shape[0]
    per_half = D // WIDE
    whole = lambda *shape: pl.BlockSpec(shape, lambda t: (0,) * len(shape))

    def out_block(t):
        k = jnp.clip(t - LAGS + 1, 0, OUT_CHUNKS - 1)
        return (k // per_half, lax.rem(k, per_half))

    slots = lambda *shape: pltpu.VMEM((CHUNKS, *shape, PIECE, WIDE), BF16)
    return pl.pallas_call(
        reduce_kernel,
        grid=(CHUNKS + LAGS - 1,),
        in_specs=[
            whole(4, SHARD, length),
            whole(4, 2, SHARD, length),
            pl.BlockSpec((length, WIDE), lambda t: (0, jnp.clip(t - OUT_CHUNKS, 0, IN_CHUNKS - 1))),
            pl.BlockSpec((length, WIDE), lambda t: (0, lax.rem(jnp.minimum(t, OUT_CHUNKS - 1), per_half))),
            whole(SMALL_ROWS, 128),
        ],
        out_specs=[
            pl.BlockSpec((SHARD, WIDE), lambda t: (0, jnp.clip(t - LAGS + 1 - OUT_CHUNKS, 0, IN_CHUNKS - 1))),
            pl.BlockSpec((SHARD, WIDE), out_block),
            whole(SMALL_ROWS, 128),
        ],
        out_shape=[
            jax.ShapeDtypeStruct((SHARD, PROJ), F32),
            jax.ShapeDtypeStruct((2 * SHARD, D), F32),
            jax.ShapeDtypeStruct((SMALL_ROWS, 128), F32),
        ],
        scratch_shapes=[
            pltpu.VMEM((2, 2, 2, 2, PIECE, WIDE), F32),
            pltpu.VMEM((2, 2, 2, 2, 2, PIECE, WIDE), BF16),
            slots(2, 2, 2, 2),
            slots(2, 2, 2),
            slots(2, 2),
            slots(2),
            slots(),
            slots(2, 2, 2),
            pltpu.VMEM((5, SMALL_ROWS, 128), F32),
            pltpu.VMEM((5, SMALL_ROWS, 128), F32),
            pltpu.SemaphoreType.DMA((8, CHUNKS)),
            pltpu.SemaphoreType.DMA((8, CHUNKS)),
            pltpu.SemaphoreType.DMA((5,)),
            pltpu.SemaphoreType.DMA((5,)),
        ],
        compiler_params=pltpu.CompilerParams(
            vmem_limit_bytes=VMEM_LIMIT, collective_id=0, has_side_effects=True
        ),
        name="reduce",
    )(part_t, mixer_t, dproj, cot, small)


def passed_along(block, axis, distance):
    devices = range(lax.axis_size(axis))
    route = [(i - distance, i) for i in devices if i - distance in devices]
    return lax.ppermute(block, axis, route)


def pack_small(conv_taps, conv_bias, dt_bias, decay_log, skip_scale, mixer_gain, input_gain):
    width = conv_bias.shape[0]

    def line(*parts):
        flat = jnp.concatenate(parts)
        return jnp.pad(flat, (0, width - flat.shape[0]))[None]

    return jnp.concatenate(
        [
            conv_taps.T,
            conv_bias[None],
            line(mixer_gain),
            line(input_gain),
            line(dt_bias, decay_log, skip_scale),
        ],
        axis=0,
    )


def unpack_small(whole):
    shards, _, width = whole.shape
    joined = jnp.swapaxes(whole, 0, 1)
    taps = jnp.pad(joined[:5].reshape(5, shards * width).astype(F32), ((0, 3), (0, 0)))
    gain = joined[5, :, : INNER // shards].reshape(1, INNER).astype(F32)
    input_gain = joined[6, :, : D // shards].reshape(1, D).astype(F32)
    own = HEADS // shards
    heads = joined[7, :, : 3 * own].reshape(shards, 3, own).swapaxes(0, 1).reshape(3, HEADS)
    heads = jnp.pad(heads.astype(F32), ((0, 5), (0, 128 - HEADS)))
    return taps, jnp.pad(gain, ((0, 7), (0, 0))), input_gain, heads


def on_device(
    inputs,
    segment_ids,
    out_grad,
    in_matrix,
    out_matrix,
    conv_taps,
    conv_bias,
    dt_bias,
    decay_log,
    skip_scale,
    mixer_gain,
    input_gain,
):
    shards, parts = lax.axis_size("fsdp"), lax.axis_size("ctx")
    place = lax.axis_index("ctx")
    units_low, cot = inputs[0], out_grad[0]
    units = units_low.astype(F32)
    seg_ids = segment_ids[0]
    length = units.shape[0]
    small = lax.all_gather(
        pack_small(conv_taps, conv_bias, dt_bias, decay_log, skip_scale, mixer_gain, input_gain), "fsdp"
    )
    w_whole = lax.all_gather(in_matrix, "fsdp", axis=0, tiled=True)
    out_whole = lax.all_gather(out_matrix, "fsdp", axis=0, tiled=True)
    taps, gain, g_float, heads = unpack_small(small)
    rim_seg = passed_along(seg_ids[length - CONV + 1 :], "ctx", 1)
    seg_ext = jnp.concatenate(
        [
            jnp.full((PAD - CONV + 1,), -1, jnp.int32),
            rim_seg,
            seg_ids,
            jnp.full((PAD,), -2, jnp.int32),
        ]
    )
    seg_lanes = jnp.broadcast_to(seg_ext[:, None], (length + 2 * PAD, 128))
    seg_row = jnp.broadcast_to(seg_ids[None], (8, length))

    inv_rms = lax.rsqrt(jnp.mean(units * units, axis=-1, keepdims=True) + epsilon)
    base_rows = units * inv_rms
    part_rows = (base_rows * g_float).astype(BF16)
    projected = dot(part_rows, w_whole).astype(BF16)
    rim_rows = passed_along(projected[length - CONV + 1 :, INNER : INNER + XBC], "ctx", 1)
    halo = jnp.pad(rim_rows, ((PAD - CONV + 1, 0), (0, 0))).astype(F32)

    here = (shards, parts) == (4, PARTS)
    xs, y_local, incoming, b_rows, c_rows, dt, running, entering, kept = front(
        projected, halo, taps, heads, seg_lanes, seg_row, here
    )
    if not here:
        kept = lax.all_gather(kept[0], "ctx")
        incoming = joined_plainly(lax.all_gather(incoming, "ctx"), kept, place, True)
    mixer_t, dproj, dy, outgoing, column_sums, block_out, stats = tail(
        y_local, xs, projected, incoming, kept, out_whole, c_rows, entering, heads, gain, cot, units_low, here
    )
    if not here:
        outgoing = joined_plainly(lax.all_gather(outgoing, "ctx"), kept, place, False)
    dproj, d_halo, d_taps, d_heads = back(
        projected, halo, taps, heads, seg_lanes, seg_row, b_rows, c_rows, dt, running, dy, incoming, outgoing, dproj
    )
    returned = passed_along(d_halo.astype(BF16), "ctx", -1)
    last = lax.slice(dproj, (length - PAD, INNER), (length, INNER + XBC))
    last = (last.astype(F32) + returned.astype(F32)).astype(BF16)
    dproj = lax.dynamic_update_slice(dproj, last, (length - PAD, INNER))

    d_normed = dot_nt(dproj, w_whole)
    d_input_gain = jnp.sum(d_normed * base_rows, axis=0)
    d_base = d_normed * g_float
    d_units = inv_rms * (d_base - base_rows * jnp.mean(d_base * base_rows, axis=-1, keepdims=True))
    input_grad = (cot.astype(F32) + d_units).astype(BF16)

    row = jnp.concatenate(
        [
            d_taps[:5].reshape(-1),
            column_sums[0],
            d_input_gain,
            d_heads[0, :HEADS],
            d_heads[1, :HEADS],
            jnp.sum(column_sums[1].reshape(HEADS, HDIM), axis=1),
            jnp.sum(stats[:2], axis=1),
        ]
    )
    row = jnp.pad(row, (0, SMALL_ROWS * 128 - row.shape[0])).reshape(SMALL_ROWS, 128)
    if here:
        d_in, d_out, row = reduce(
            part_rows.T.reshape(4, SHARD, length), mixer_t.reshape(4, 2, SHARD, length), dproj, cot, row
        )
    else:
        d_in = jnp.dot(part_rows.T, dproj, preferred_element_type=F32)
        d_out = jnp.dot(mixer_t, cot, preferred_element_type=F32)

        def scattered(grad):
            return lax.psum_scatter(grad.astype(BF16), "fsdp", scatter_dimension=0, tiled=True)

        d_in = lax.psum(scattered(d_in), "ctx").astype(F32)
        d_out = lax.psum(scattered(d_out), "ctx").astype(F32)
        row = lax.psum(row, ("fsdp", "ctx"))
    row = row.reshape(-1)
    me = lax.axis_index("fsdp")

    def own(flat):
        size = flat.shape[-1] // shards
        return lax.dynamic_slice_in_dim(flat, me * size, size, flat.ndim - 1)

    at = 5 * XBC
    taps_sum = row[:at].reshape(5, XBC)
    gain_sum = row[at : at + INNER]
    input_gain_sum = row[at + INNER : at + INNER + D]
    at = at + INNER + D
    head_sums = row[at : at + 3 * HEADS].reshape(3, HEADS)
    stat_sums = row[at + 3 * HEADS : at + 3 * HEADS + 2]
    rms_stats = jnp.sqrt(stat_sums / (length * shards * parts * D))
    return (
        block_out[None],
        input_grad[None],
        d_in,
        d_out,
        own(taps_sum[:4]).T,
        own(taps_sum[4]),
        own(head_sums[0]),
        own(head_sums[1]),
        own(head_sums[2]),
        own(gain_sum),
        own(input_gain_sum),
        rms_stats,
    )


def solution(mesh):
    return jax.shard_map(
        on_device,
        mesh=mesh,
        in_specs=(
            P("fsdp", "ctx", None),
            P("fsdp", "ctx"),
            P("fsdp", "ctx", None),
            P("fsdp", None),
            P("fsdp", None),
            P("fsdp", None),
            P("fsdp"),
            P("fsdp"),
            P("fsdp"),
            P("fsdp"),
            P("fsdp"),
            P("fsdp"),
        ),
        out_specs=(
            P("fsdp", "ctx", None),
            P("fsdp", "ctx", None),
            P("fsdp", None),
            P("fsdp", None),
            P("fsdp", None),
            P("fsdp"),
            P("fsdp"),
            P("fsdp"),
            P("fsdp"),
            P("fsdp"),
            P("fsdp"),
            P(),
        ),
        check_vma=False,
    )
```

```python
import functools

import jax
import jax.numpy as jnp
from jax import lax
from jax.experimental import pallas as pl
from jax.experimental.pallas import tpu as pltpu
from jax.sharding import PartitionSpec as P

D = 1536
HEADS = 48
HDIM = 64
STATE = 128
CONV = 4
INNER = 3072
XBC = 3328
PROJ = 6448
WIDTH = 6656

BLK = 256
GROUP = BLK // HDIM
STEPS = INNER // BLK
Q = 128
PAD = 8
WIDE = 512
SHARD = D // 4
PIECE = SHARD // 8
SMALL_WIDTH = 896
AHEAD = 2

epsilon = 1e-05
F32, BF16 = jnp.float32, jnp.bfloat16
HIGHEST = lax.Precision.HIGHEST
VMEM_LIMIT = 60 * 1024 * 1024


def communicating(number, exchanging):
    if not exchanging:
        return pltpu.CompilerParams(vmem_limit_bytes=VMEM_LIMIT)
    return pltpu.CompilerParams(
        vmem_limit_bytes=VMEM_LIMIT, collective_id=number, has_side_effects=True
    )


def dot(a, b):
    return jnp.dot(a, b, preferred_element_type=F32)


def dot_nt(a, b):
    return lax.dot_general(a, b, (((1,), (1,)), ((), ())), preferred_element_type=F32)


def iota(shape, dim):
    return lax.broadcasted_iota(jnp.int32, shape, dim)


def sigmoid(v):
    return 1.0 / (1.0 + jnp.exp(-v))


def in_two(a):
    high = a.astype(BF16)
    return high, (a - high.astype(F32)).astype(BF16)


def chosen(step):
    columns = step * GROUP + lax.shift_right_logical(iota((128, BLK), 1), 6)
    return (iota((128, BLK), 0) == columns).astype(BF16)


def chosen_back(step):
    heads = step * GROUP + lax.shift_right_logical(iota((BLK, 128), 0), 6)
    return (iota((BLK, 128), 1) == heads).astype(BF16)


def widen(per_head, select):
    high, low = in_two(per_head)
    return dot(high, select) + dot(low, select)


def halves(pair):
    first = iota(pair.shape, 1) < HDIM
    zero = jnp.zeros_like(pair)
    return jnp.concatenate([jnp.where(first, pair, zero), jnp.where(first, zero, pair)], axis=0)


def both(mask):
    return jnp.concatenate([mask, mask], axis=1)


def conv_rows(ext_ref, seg_ref, taps_ref, start, rows):
    own = seg_ref[start + PAD : start + PAD + rows, :]
    total = taps_ref[4:5, :] + taps_ref[3:4, :] * ext_ref[start + PAD : start + PAD + rows, :]
    for back in range(1, CONV):
        at = start + PAD - back
        same = both(seg_ref[at : at + rows, :] == own)
        total = total + jnp.where(
            same, taps_ref[3 - back : 4 - back, :] * ext_ref[at : at + rows, :], 0.0
        )
    return total


def chunk_flags(seg_ref, k):
    own = seg_ref[PAD + k * Q : PAD + (k + 1) * Q, :]
    before = seg_ref[PAD + k * Q - 1 : PAD + k * Q, :]
    last = seg_ref[PAD + (k + 1) * Q - 1 : PAD + (k + 1) * Q, :]
    return (own == before).astype(F32), (own == last).astype(F32)


def masked_scores(seg_ref, row_ref, b_rows, c_rows, k):
    own = seg_ref[PAD + k * Q : PAD + (k + 1) * Q, :]
    row = row_ref[0:1, k * Q : (k + 1) * Q]
    keep = (own == row) & (iota((Q, Q), 1) <= iota((Q, Q), 0))
    return jnp.where(keep, dot_nt(c_rows, b_rows), 0.0)


def flipped(index, bit):
    return index + bit - 2 * bit * lax.rem(index // bit, 2)


class Gather:
    def __init__(self, target, loads, sends, arrivals):
        self.target, self.loads, self.sends, self.arrivals = target, loads, sends, arrivals
        shard, part = lax.axis_index("fsdp"), lax.axis_index("ctx")
        self.own, self.other = shard, flipped(shard, 2)
        self.sibling, self.opposite = flipped(shard, 1), flipped(flipped(shard, 2), 1)
        x, near = lax.rem(part, 2), lax.rem(part // 2, 2)
        self.mine, self.over_x, self.over_z = 2 * x + near, 2 * (1 - x) + near, 2 * x + 1 - near
        self.across = 2 * (1 - x) + 1 - near
        self.peers = {
            "core": {"fsdp": flipped(shard, 1)},
            "y": {"fsdp": flipped(shard, 2)},
            "x": {"ctx": flipped(part, 1)},
            "z": {"ctx": flipped(part, 2)},
        }

    def whole(self, shard, k):
        return self.target.at[k, shard]

    def quarter(self, shard, k, which):
        rows = self.target.shape[2] // 4
        return self.target.at[k, shard, pl.ds(pl.multiple_of(which * rows, rows), rows)]

    def half(self, shard, k, which, second):
        rows = self.target.shape[2] // 8
        return self.target.at[k, shard, pl.ds(pl.multiple_of(which * 2 * rows + second * rows, rows), rows)]

    def copy(self, place, kind, k, peer):
        return pltpu.make_async_remote_copy(
            src_ref=place,
            dst_ref=place,
            send_sem=self.sends.at[kind, k],
            recv_sem=self.arrivals.at[kind, k],
            device_id=self.peers[peer],
            device_id_type=pl.DeviceIdType.MESH,
        )

    def outgoing(self, kind, k):
        own, other = self.own, self.other
        if kind == 0:
            return self.copy(self.whole(own, k), kind, k, "core")
        if kind == 1:
            return self.copy(self.quarter(own, k, self.mine), kind, k, "y")
        if kind == 2:
            return self.copy(self.quarter(other, k, self.mine), kind, k, "x")
        if kind == 3:
            return self.copy(self.quarter(other, k, self.mine), kind, k, "z")
        if kind == 4:
            return self.copy(self.half(other, k, self.over_x, 0), kind, k, "z")
        if kind == 5:
            return self.copy(self.half(other, k, self.over_z, 1), kind, k, "x")
        which = (self.mine, self.over_x, self.over_z, self.across)[kind - 6]
        return self.copy(self.quarter(other, k, which), kind, k, "core")

    def arrived(self, kind, k):
        other, opposite = self.other, self.opposite
        if kind == 0:
            place = self.whole(self.sibling, k)
        elif kind < 4:
            place = self.quarter(other, k, (self.mine, self.over_x, self.over_z)[kind - 1])
        elif kind < 6:
            place = self.half(other, k, self.across, kind - 4)
        else:
            place = self.quarter(opposite, k, (self.mine, self.over_x, self.over_z, self.across)[kind - 6])
        self.copy(place, kind, k, "core").wait_recv()

    def load(self, k, source):
        return pltpu.make_async_copy(source, self.whole(self.own, k), self.loads.at[k])

    def begin(self, k):
        self.load(k, self.whole(self.own, k)).wait()
        self.outgoing(1, k).start()
        self.outgoing(0, k).start()

    def first(self, k):
        self.arrived(1, k)
        for kind in (2, 3, 6):
            self.outgoing(kind, k).start()

    def second(self, k):
        self.arrived(2, k)
        self.outgoing(4, k).start()
        self.outgoing(7, k).start()
        self.arrived(3, k)
        self.outgoing(5, k).start()
        self.outgoing(8, k).start()

    def third(self, k):
        self.arrived(4, k)
        self.arrived(5, k)
        self.outgoing(9, k).start()

    def complete(self, k):
        for kind in (0, 6, 7, 8, 9):
            self.arrived(kind, k)

    def drain(self, k):
        for kind in range(10):
            self.outgoing(kind, k).wait_send()


def gather_sems(chunks):
    return [
        pltpu.SemaphoreType.DMA((chunks,)),
        pltpu.SemaphoreType.DMA((10, chunks)),
        pltpu.SemaphoreType.DMA((10, chunks)),
    ]


def project_kernel(
    main_ref, rest_ref, units_ref, small_ref, seg_ref,
    weight_ref, projected_ref, normed_t_ref, smalls_ref, halo_ref, seg_before_ref,
    normed, gathered, own_small, smalls, own_seg, seg_before, edges, halos,
    loads, sends, arrivals, stores, small_sends, small_arrivals, edge_sends, edge_arrivals,
):
    step = pl.program_id(0)
    chunks = WIDTH // WIDE
    length = units_ref.shape[0]
    gather = Gather(gathered, loads, sends, arrivals)
    shard, part = lax.axis_index("fsdp"), lax.axis_index("ctx")
    others = ({"fsdp": flipped(shard, 1)}, {"fsdp": flipped(shard, 2)}, {"fsdp": flipped(flipped(shard, 1), 2)})
    following, outer = lax.rem(part + 1, PARTS), lax.rem(part + PARTS - 1 + 2 * lax.rem(part, 2), PARTS)

    def remote(source, target, send, arrival, peer):
        return pltpu.make_async_remote_copy(
            src_ref=source,
            dst_ref=target,
            send_sem=send,
            recv_sem=arrival,
            device_id=peer,
            device_id_type=pl.DeviceIdType.MESH,
        )

    def small_copy(hop):
        return remote(own_small, smalls.at[shard], small_sends.at[hop], small_arrivals.at[hop], others[hop])

    def seg_copy():
        return remote(own_seg, seg_before, small_sends.at[3], small_arrivals.at[3], {"ctx": following})

    def edge_copy(k):
        return remote(edges.at[k], halos.at[k], edge_sends.at[k], edge_arrivals.at[k], {"ctx": following})

    def store(k):
        columns = pl.ds(pl.multiple_of(k * WIDE, WIDE), WIDE)
        return pltpu.make_async_copy(gathered.at[k], weight_ref.at[:, :, columns], stores.at[k])

    @pl.when(step == 0)
    def _():
        barrier = pltpu.get_barrier_semaphore()
        near = [*others, {"ctx": flipped(part, 1)}, {"ctx": flipped(part, 2)}, {"ctx": outer}]
        for peer in near:
            pl.semaphore_signal(barrier, inc=1, device_id=peer, device_id_type=pl.DeviceIdType.MESH)
        for k in range(chunks):
            gather.load(k, main_ref.at[:, k * WIDE : (k + 1) * WIDE] if k + 1 < chunks else rest_ref).start()
        own_small[...] = small_ref[...]
        own_seg[...] = seg_ref[...]
        smalls[shard] = small_ref[...]
        pl.semaphore_wait(barrier, len(near))
        for hop in range(3):
            small_copy(hop).start()
        seg_copy().start()
        for k in range(AHEAD):
            gather.begin(k)
        for hop in range(3):
            small_copy(hop).wait()
        seg_copy().wait()
        smalls_ref[...] = smalls[...]
        seg_before_ref[...] = jnp.where(part == 0, -1, seg_before[...])
        gain = jnp.concatenate([smalls[s, 6:7, :SHARD] for s in range(4)], axis=1)
        for k in range(length // Q):
            rows = slice(k * Q, (k + 1) * Q)
            units = units_ref[rows, :].astype(F32)
            norm = lax.rsqrt(jnp.sum(units * units, axis=1, keepdims=True) * (1.0 / D) + epsilon)
            value = units * norm * gain
            normed[rows, :] = value.astype(BF16)
            for s in range(4):
                normed_t_ref[s, :, rows] = value[:, s * SHARD : (s + 1) * SHARD].T.astype(BF16)

    def stage(lag):
        def decorate(body):
            k = step - lag

            @pl.when((k >= 0) & (k < chunks))
            def _():
                body(k)

        return decorate

    stage(-AHEAD)(lambda k: pl.when(k >= AHEAD)(lambda: gather.begin(k)))
    stage(0)(gather.first)
    stage(1)(gather.second)
    stage(2)(gather.third)

    @stage(3)
    def _(k):
        gather.complete(k)
        store(k).start()
        low = dot(normed[...], gathered[k].reshape(D, WIDE)).astype(BF16)
        projected_ref[...] = low
        edges[k] = low[length - 16 :, :].astype(F32)[8:, :]
        edge_copy(k).start()

    @stage(4)
    def _(k):
        edge_copy(k).wait()
        gather.drain(k)
        store(k).wait()
        halo_ref[...] = jnp.where(part == 0, 0.0, halos[k])


def project(in_matrix, units, small, seg_ids):
    length = units.shape[0]
    chunks = WIDTH // WIDE
    rest = jnp.pad(in_matrix[:, (chunks - 1) * WIDE :], ((0, 0), (0, WIDTH - PROJ)))
    whole = lambda *shape: pl.BlockSpec(shape, lambda t: (0,) * len(shape))
    column = lambda lag: lambda t: (0, jnp.clip(t - lag, 0, chunks - 1))
    anywhere = pl.BlockSpec(memory_space=pl.ANY)
    return pl.pallas_call(
        project_kernel,
        grid=(chunks + 4,),
        in_specs=[
            anywhere,
            anywhere,
            whole(length, D),
            whole(8, SMALL_WIDTH),
            whole(length // 128, 128),
        ],
        out_specs=[
            anywhere,
            pl.BlockSpec((length, WIDE), column(3)),
            whole(4, SHARD, length),
            whole(4, 8, SMALL_WIDTH),
            pl.BlockSpec((PAD, WIDE), column(4)),
            whole(length // 128, 128),
        ],
        out_shape=[
            jax.ShapeDtypeStruct((4, SHARD, WIDTH), BF16),
            jax.ShapeDtypeStruct((length, WIDTH), BF16),
            jax.ShapeDtypeStruct((4, SHARD, length), BF16),
            jax.ShapeDtypeStruct((4, 8, SMALL_WIDTH), F32),
            jax.ShapeDtypeStruct((PAD, WIDTH), F32),
            jax.ShapeDtypeStruct((length // 128, 128), jnp.int32),
        ],
        scratch_shapes=[
            pltpu.VMEM((length, D), BF16),
            pltpu.VMEM((chunks, 4, SHARD, WIDE), BF16),
            pltpu.VMEM((8, SMALL_WIDTH), F32),
            pltpu.VMEM((4, 8, SMALL_WIDTH), F32),
            pltpu.VMEM((length // 128, 128), jnp.int32),
            pltpu.VMEM((length // 128, 128), jnp.int32),
            pltpu.VMEM((chunks, PAD, WIDE), F32),
            pltpu.VMEM((chunks, PAD, WIDE), F32),
            *gather_sems(chunks),
            pltpu.SemaphoreType.DMA((chunks,)),
            pltpu.SemaphoreType.DMA((4,)),
            pltpu.SemaphoreType.DMA((4,)),
            pltpu.SemaphoreType.DMA((chunks,)),
            pltpu.SemaphoreType.DMA((chunks,)),
        ],
        compiler_params=communicating(3, True),
        name="project",
    )(in_matrix, rest, units, small, seg_ids.reshape(length // 128, 128))


PARTS = 8
SLAB = STATE // PARTS
JOIN, DONE = 2, 4


class Exchange:
    def __init__(self, held, gathered, joined, incoming, sems):
        self.held, self.gathered, self.joined, self.incoming, self.sems = held, gathered, joined, incoming, sems
        self.me = lax.axis_index("ctx")

    def others(self):
        return [lax.rem(self.me + hop, PARTS) for hop in range(1, PARTS)]

    def greet(self, *further):
        barrier = pltpu.get_barrier_semaphore()
        peers = [{"ctx": other} for other in self.others()] + list(further)
        for peer in peers:
            pl.semaphore_signal(barrier, inc=1, device_id=peer, device_id_type=pl.DeviceIdType.MESH)
        pl.semaphore_wait(barrier, len(peers))

    def copy(self, source, target, kind, group, other):
        return pltpu.make_async_remote_copy(
            src_ref=source,
            dst_ref=target,
            send_sem=self.sems.at[2 * kind, group],
            recv_sem=self.sems.at[2 * kind + 1, group],
            device_id={"ctx": other},
            device_id_type=pl.DeviceIdType.MESH,
        )

    def all_of(self, kind, group):
        source, target = ((self.held, self.gathered), (self.joined, self.incoming))[kind]
        some = pl.ds(0, PARTS - 1)
        return self.copy(source.at[group, some], target.at[group, some], kind, group, self.others()[0])

    def spread(self, group, state):
        self.held[group] = state.astype(BF16).reshape(PARTS, SLAB, BLK)
        self.gathered[group, self.me] = self.held[group, self.me]
        for other in self.others():
            self.copy(self.held.at[group, other], self.gathered.at[group, self.me], 0, group, other).start()

    def join(self, group, kept, forward):
        self.all_of(0, group).wait_recv()
        total = jnp.zeros((SLAB, BLK), F32)
        for part in range(PARTS) if forward else range(PARTS - 1, -1, -1):
            self.joined[group, part] = total.astype(BF16)
            total = kept[part : part + 1, :] * total + self.gathered[group, part].astype(F32)
        self.incoming[group, self.me] = self.joined[group, self.me]
        for other in self.others():
            self.copy(self.joined.at[group, other], self.incoming.at[group, self.me], 1, group, other).start()

    def finish(self, group):
        self.all_of(1, group).wait_recv()
        self.all_of(0, group).wait_send()
        self.all_of(1, group).wait_send()
        return self.incoming[group].reshape(STATE, BLK)


def exchange_scratch():
    return [pltpu.VMEM((STEPS, PARTS, SLAB, BLK), BF16) for _ in range(4)] + [pltpu.SemaphoreType.DMA((4, STEPS))]


def first_rows(kept_ref):
    return jnp.concatenate([kept_ref[part, 0:1, :] for part in range(PARTS)], axis=0)


def joined_plainly(states, kept, place, forward):
    factors = jnp.repeat(kept[:, 0, :HEADS], HDIM, axis=1)[:, None, :]
    total = jnp.zeros(states.shape[1:], F32)
    result = total
    count = states.shape[0]
    for part in range(count) if forward else range(count - 1, -1, -1):
        result = jnp.where(place == part, total, result)
        total = factors[part] * total + states[part].astype(F32)
    return result.astype(BF16)


def front_kernel(
    x_ref, bc_ref, dtraw_ref, halo_ref, halo_bc_ref, taps_ref, taps_bc_ref, heads_ref, seg_ref, row_ref, shard_ref,
    xs_ref, y_ref, state_ref, b_ref, c_ref, dt_ref, run_ref, in_ref, keep_ref, whole_ref,
    ext, scores, run_t, b_t, enter, leave, *parts,
):
    step = pl.program_id(0)
    length = x_ref.shape[0]
    chunks = length // Q
    if parts:
        exchange = Exchange(*parts[:5])
        own_keep, keeps, keep_sends, keep_arrivals, gathered, loads, sends, arrivals, stores = parts[5:]
        gather = Gather(gathered, loads, sends, arrivals)

        def store(k):
            columns = pl.ds(pl.multiple_of(k * WIDE, WIDE), WIDE)
            return pltpu.make_async_copy(gathered.at[k], whole_ref.at[:, :, columns], stores.at[k])


        def keep_copy(hop):
            return pltpu.make_async_remote_copy(
                src_ref=own_keep,
                dst_ref=keeps.at[exchange.me],
                send_sem=keep_sends.at[hop],
                recv_sem=keep_arrivals.at[hop],
                device_id={"ctx": lax.rem(exchange.me + hop + 1, PARTS)},
                device_id_type=pl.DeviceIdType.MESH,
            )

    @pl.when(step == 0)
    def _():
        ext[0:PAD, :] = halo_bc_ref[...]
        ext[PAD:, :] = bc_ref[...].astype(F32)
        lane = iota((Q, 128), 1)
        lower = (iota((Q, Q), 1) <= iota((Q, Q), 0)).astype(F32)
        offset = jnp.zeros((1, 128), F32)
        for k in range(chunks):
            rows = slice(k * Q, (k + 1) * Q)
            total = conv_rows(ext, seg_ref, taps_bc_ref, k * Q, Q)
            active = total * sigmoid(total)
            b_rows, c_rows = active[:, :STATE], active[:, STATE:].astype(BF16)
            b_t[:, rows] = b_rows.T.astype(BF16)
            b_rows = b_rows.astype(BF16)
            b_ref[rows, :] = b_rows
            c_ref[rows, :] = c_rows
            scores[rows, :] = masked_scores(seg_ref, row_ref, b_rows, c_rows, k)
            raw = jnp.where(lane < HEADS, dtraw_ref[rows, :128].astype(F32), 0.0) + heads_ref[0:1, :]
            dt = jnp.maximum(raw, 0.0) + jnp.log1p(jnp.exp(-jnp.abs(raw)))
            log_decay = -dt * jnp.exp(heads_ref[1:2, :])
            running = jnp.dot(lower, log_decay, precision=HIGHEST, preferred_element_type=F32)
            dt_ref[rows, :] = dt
            run_ref[rows, :] = running
            run_t[k] = running.T
            carry, tail = chunk_flags(seg_ref, k)
            enter[rows, :] = jnp.exp(running) * carry
            leave[rows, :] = jnp.exp(running[Q - 1 : Q, :] - running) * tail
            same = (seg_ref[PAD + k * Q : PAD + (k + 1) * Q, :] == seg_ref[PAD - 1 : PAD, :]).astype(F32)
            whole = jnp.exp(running + offset) * same
            in_ref[rows, :] = whole
            offset = offset + running[Q - 1 : Q, :]
        keep = jnp.broadcast_to(whole[Q - 1 : Q, :], (8, 128))
        if parts:
            own_keep[...] = keep
            keeps[exchange.me] = keep
            exchange.greet(gather.peers["core"], gather.peers["y"])
            for hop in range(PARTS - 1):
                keep_copy(hop).start()
            for k in range(D // WIDE):
                gather.load(k, shard_ref.at[:, k * WIDE : (k + 1) * WIDE]).start()
            for k in range(D // WIDE):
                gather.begin(k)
        else:
            keep_ref[0] = keep

    @pl.when(step < STEPS)
    def _():
        state = local_scan(
            step, x_ref, halo_ref, taps_ref, seg_ref, xs_ref, y_ref, c_ref, dt_ref, run_ref,
            ext, scores, run_t, b_t, enter, leave,
        )
        if parts:
            exchange.spread(step, state)
        else:
            state_ref[...] = state.astype(BF16)

    if parts:

        @pl.when(step == JOIN)
        def _():
            for hop in range(PARTS - 1):
                keep_copy(hop).wait()
            keep_ref[...] = keeps[...]

        @pl.when((step >= JOIN) & (step < STEPS + JOIN))
        def _():
            group = step - JOIN
            exchange.join(group, widen(first_rows(keeps), chosen(group)), True)

        @pl.when(step >= DONE)
        def _():
            state_ref[...] = exchange.finish(step - DONE)

        def complete(k):
            gather.complete(k)
            store(k).start()

        def drain(k):
            gather.drain(k)
            store(k).wait()

        for lag, advance in enumerate((gather.first, gather.second, gather.third, complete, drain)):
            k = step - 2 - 2 * lag

            @pl.when((k >= 0) & (k < D // WIDE))
            def _():
                advance(k)


def local_scan(
    step, x_ref, halo_ref, taps_ref, seg_ref, xs_ref, y_ref, c_ref, dt_ref, run_ref,
    ext, scores, run_t, b_t, enter, leave,
):
    chunks = x_ref.shape[0] // Q
    ext[0:PAD, :] = halo_ref[...]
    ext[PAD:, :] = x_ref[...].astype(F32)
    select = chosen(step)
    state = jnp.zeros((STATE, BLK), F32)
    for k in range(chunks):
        rows = slice(k * Q, (k + 1) * Q)
        total = conv_rows(ext, seg_ref, taps_ref, k * Q, Q)
        values = total * sigmoid(total)
        xs_ref[rows, :] = values.astype(BF16)
        scaled = (values * widen(dt_ref[rows, :], select)).astype(BF16)
        entering = widen(enter[rows, :], select)
        running = pltpu.roll(run_ref[rows, :], lax.rem(128 - step * GROUP, 128), 1)
        parts = []
        for pair in range(2):
            mixing = []
            for one in range(2):
                head = 2 * pair + one
                gap = running[:, head : head + 1] - run_t[k, pl.ds(step * GROUP + head, 1), :]
                mixing.append((jnp.exp(jnp.minimum(gap, 0.0)) * scores[rows, :]).astype(BF16))
            parts.append(
                dot(jnp.concatenate(mixing, axis=1), halves(scaled[:, pair * 128 : (pair + 1) * 128]))
            )
        inside = jnp.concatenate(parts, axis=1)
        y_ref[rows, :] = (inside + entering * dot(c_ref[rows, :], state.astype(BF16))).astype(BF16)
        weighted = (scaled.astype(F32) * widen(leave[rows, :], select)).astype(BF16)
        state = entering[Q - 1 : Q, :] * state + dot(b_t[:, rows], weighted)
    return state


def front(projected, halo, taps, heads, seg_lanes, seg_row, out_matrix, exchanging):
    length = projected.shape[0]
    last = STEPS - 1
    keeps = PARTS if exchanging else 1
    whole = lambda *shape: pl.BlockSpec(shape, lambda j: (0,) * len(shape))
    columns = lambda rows, at: pl.BlockSpec((rows, BLK), at)
    return pl.pallas_call(
        front_kernel,
        grid=(STEPS + DONE * exchanging,),
        in_specs=[
            columns(length, lambda j: (0, STEPS + jnp.minimum(j, last))),
            columns(length, lambda j: (0, 2 * STEPS)),
            columns(length, lambda j: (0, 2 * STEPS + 1)),
            columns(PAD, lambda j: (0, STEPS + jnp.minimum(j, last))),
            columns(PAD, lambda j: (0, 2 * STEPS)),
            columns(8, lambda j: (0, jnp.minimum(j, last))),
            columns(8, lambda j: (0, STEPS)),
            whole(8, 128),
            whole(length + 2 * PAD, 128),
            whole(8, length),
            pl.BlockSpec(memory_space=pl.ANY),
        ],
        out_specs=[
            columns(length, lambda j: (0, jnp.minimum(j, last))),
            columns(length, lambda j: (0, jnp.minimum(j, last))),
            columns(STATE, lambda j: (0, jnp.maximum(j - DONE * exchanging, 0))),
            whole(length, 128),
            whole(length, 128),
            whole(length, 128),
            whole(length, 128),
            whole(length, 128),
            whole(keeps, 8, 128),
            pl.BlockSpec(memory_space=pl.ANY),
        ],
        out_shape=[
            jax.ShapeDtypeStruct((length, INNER), BF16),
            jax.ShapeDtypeStruct((length, INNER), BF16),
            jax.ShapeDtypeStruct((STATE, INNER), BF16),
            jax.ShapeDtypeStruct((length, 128), BF16),
            jax.ShapeDtypeStruct((length, 128), BF16),
            jax.ShapeDtypeStruct((length, 128), F32),
            jax.ShapeDtypeStruct((length, 128), F32),
            jax.ShapeDtypeStruct((length, 128), F32),
            jax.ShapeDtypeStruct((keeps, 8, 128), F32),
            jax.ShapeDtypeStruct((4, *out_matrix.shape), BF16),
        ],
        scratch_shapes=[
            pltpu.VMEM((length + PAD, BLK), F32),
            pltpu.VMEM((length, Q), F32),
            pltpu.VMEM((length // Q, 128, Q), F32),
            pltpu.VMEM((128, length), BF16),
            pltpu.VMEM((length, 128), F32),
            pltpu.VMEM((length, 128), F32),
        ]
        + (
            exchange_scratch()
            + [
                pltpu.VMEM((8, 128), F32),
                pltpu.VMEM((PARTS, 8, 128), F32),
                pltpu.SemaphoreType.DMA((PARTS - 1,)),
                pltpu.SemaphoreType.DMA((PARTS - 1,)),
                pltpu.VMEM((D // WIDE, 4, 2 * SHARD, WIDE), BF16),
                *gather_sems(D // WIDE),
                pltpu.SemaphoreType.DMA((D // WIDE,)),
            ]
        )
        * exchanging,
        compiler_params=communicating(1, exchanging),
        cost_estimate=pl.CostEstimate(
            flops=6 * 10**9, bytes_accessed=16 * 10**6, transcendentals=10**7
        ),
        name="front",
    )(projected, projected, projected, halo, halo, taps, taps, heads, seg_lanes, seg_row, out_matrix)


def tail_kernel(
    y_ref, xs_ref, gate_ref, incoming_ref, kept_ref, out_ref, c_ref, in_ref, heads_ref, gain_ref, g_ref, units_ref,
    mixer_ref, dproj_ref, dy_ref, dsin_ref, sums_ref, block_ref, stats_ref,
    full, dmix, squares, products, mixed, c_t, *parts,
):
    step = pl.program_id(0)
    length = y_ref.shape[0]
    group = jnp.where(step < STEPS, step, jnp.minimum(step - STEPS, STEPS - 1))
    select = chosen(group)
    half = length // 2
    if parts:
        exchange = Exchange(*parts)

        @pl.when(step == 0)
        def _():
            exchange.greet()

    @pl.when(step == 0)
    def _():
        squares[...] = jnp.zeros_like(squares)
        products[...] = jnp.zeros_like(products)
        for k in range(length // Q):
            rows = slice(k * Q, (k + 1) * Q)
            c_t[:, rows] = c_ref[rows, :].astype(F32).T.astype(BF16)

    @pl.when(step < STEPS)
    def _():
        incoming = incoming_ref[...]
        skip = widen(heads_ref[...], select)[2:3, :]
        for k in range(2):
            rows = slice(k * half, (k + 1) * half)
            y = y_ref[rows, :].astype(F32)
            y = y + widen(in_ref[rows, :], select) * dot(c_ref[rows, :], incoming)
            y = y + skip * xs_ref[rows, :].astype(F32)
            full[step, rows, :] = y
            gate = gate_ref[rows, :].astype(F32)
            gated = y * gate * sigmoid(gate)
            d_mixer = dot_nt(g_ref[rows, :], out_ref[...])
            dmix[step, rows, :] = d_mixer
            square = gated * gated
            product = gated * d_mixer * gain_ref[0:1, :]
            squares[rows, :] += square[:, :128] + square[:, 128:]
            products[rows, :] += product[:, :128] + product[:, 128:]

    @pl.when(step == STEPS)
    def _():
        norm = lax.rsqrt(jnp.sum(squares[...], axis=1, keepdims=True) * (1.0 / INNER) + epsilon)
        mean = norm * jnp.sum(products[...], axis=1, keepdims=True) * (1.0 / INNER)
        squares[...] = jnp.broadcast_to(norm, squares.shape)
        products[...] = jnp.broadcast_to(mean, products.shape)

    @pl.when((step >= STEPS) & (step < 2 * STEPS))
    def _():
        gain = gain_ref[0:1, :]
        d_gain = jnp.zeros((1, BLK), F32)
        d_skip = jnp.zeros((1, BLK), F32)
        d_state = jnp.zeros((STATE, BLK), F32)
        for k in range(2):
            rows = slice(k * half, (k + 1) * half)
            norm, mean = both(squares[rows, :]), both(products[rows, :])
            y = full[group, rows, :]
            d_mixer = dmix[group, rows, :]
            gate = gate_ref[rows, :].astype(F32)
            sig = sigmoid(gate)
            silu = gate * sig
            unit = y * silu * norm
            low = (unit * gain).astype(BF16)
            mixer_ref[:, rows] = (unit * gain).T.astype(BF16)
            part = dot(low, out_ref[...])

            @pl.when(step == STEPS)
            def _():
                mixed[rows, :] = part

            @pl.when(step > STEPS)
            def _():
                mixed[rows, :] += part

            d_gain = d_gain + jnp.sum(d_mixer * unit, axis=0, keepdims=True)
            d_gated = norm * (d_mixer * gain - unit * mean)
            dproj_ref[rows, :] = (d_gated * y * (sig * (1.0 + gate * (1.0 - sig)))).astype(BF16)
            dy = (d_gated * silu).astype(BF16)
            dy_ref[rows, :] = dy
            dy = dy.astype(F32)
            d_skip = d_skip + jnp.sum(dy * xs_ref[rows, :].astype(F32), axis=0, keepdims=True)
            d_state = d_state + dot(c_t[:, rows], (dy * widen(in_ref[rows, :], select)).astype(BF16))
        if parts:
            exchange.spread(group, d_state)
        else:
            dsin_ref[...] = d_state.astype(BF16)
        sums_ref[...] = jnp.concatenate([d_gain, d_skip, jnp.zeros((6, BLK), F32)], axis=0)

    @pl.when(step == 2 * STEPS - 1)
    def _():
        total = units_ref[...].astype(F32) + mixed[...]
        block_ref[...] = total.astype(BF16)
        first = jnp.sum(total * total, axis=0, keepdims=True)
        second = jnp.sum(mixed[...] * mixed[...], axis=0, keepdims=True)
        stats_ref[...] = jnp.concatenate([first, second, jnp.zeros((6, D), F32)], axis=0)

    if parts:
        at = step - STEPS

        @pl.when((at >= JOIN) & (at < STEPS + JOIN))
        def _():
            done = at - JOIN
            exchange.join(done, widen(first_rows(kept_ref), chosen(done)), False)

        @pl.when(at >= DONE)
        def _():
            dsin_ref[...] = exchange.finish(at - DONE)


def tail(y, xs, projected, incoming, kept, out_whole, c_rows, entering, heads, gain, cot, units, exchanging):
    length = y.shape[0]
    group = lambda i: jnp.where(i < STEPS, i, jnp.minimum(i - STEPS, STEPS - 1))
    second = lambda i: jnp.clip(i - STEPS, 0, STEPS - 1)
    early = lambda rows: pl.BlockSpec((rows, BLK), lambda i: (0, jnp.minimum(i, STEPS - 1)))
    late = lambda rows: pl.BlockSpec((rows, BLK), lambda i: (0, second(i)))
    each = lambda rows: pl.BlockSpec((rows, BLK), lambda i: (0, group(i)))
    whole = lambda *shape: pl.BlockSpec(shape, lambda i: (0,) * len(shape))
    return pl.pallas_call(
        tail_kernel,
        grid=(2 * STEPS + DONE * exchanging,),
        in_specs=[
            early(length),
            each(length),
            each(length),
            early(STATE),
            whole(*kept.shape),
            pl.BlockSpec((BLK, D), lambda i: (group(i), 0)),
            whole(length, 128),
            whole(length, 128),
            whole(8, 128),
            each(8),
            whole(length, D),
            whole(length, D),
        ],
        out_specs=[
            pl.BlockSpec((BLK, length), lambda i: (second(i), 0)),
            late(length),
            late(length),
            pl.BlockSpec((STATE, BLK), lambda i: (0, second(i - DONE * exchanging))),
            late(8),
            whole(length, D),
            whole(8, D),
        ],
        out_shape=[
            jax.ShapeDtypeStruct((INNER, length), BF16),
            jax.ShapeDtypeStruct((length, WIDTH), BF16),
            jax.ShapeDtypeStruct((length, INNER), BF16),
            jax.ShapeDtypeStruct((STATE, INNER), BF16),
            jax.ShapeDtypeStruct((8, INNER), F32),
            jax.ShapeDtypeStruct((length, D), BF16),
            jax.ShapeDtypeStruct((8, D), F32),
        ],
        scratch_shapes=[
            pltpu.VMEM((STEPS, length, BLK), F32),
            pltpu.VMEM((STEPS, length, BLK), F32),
            pltpu.VMEM((length, 128), F32),
            pltpu.VMEM((length, 128), F32),
            pltpu.VMEM((length, D), F32),
            pltpu.VMEM((128, length), BF16),
        ]
        + exchange_scratch() * exchanging,
        compiler_params=communicating(2, exchanging),
        cost_estimate=pl.CostEstimate(
            flops=12 * 10**9, bytes_accessed=50 * 10**6, transcendentals=4 * 10**6
        ),
        name="tail",
    )(y, xs, projected, incoming, kept, out_whole, c_rows, entering, heads, gain, cot, units)


def back_kernel(
    x_ref, dtraw_ref, halo_ref, taps_ref, heads_ref, seg_ref, row_ref, b_ref, c_ref, dt_ref, run_ref,
    dy_ref, sin_ref, dout_ref, given_ref,
    dproj_ref, dhalo_ref, dtaps_ref, dheads_ref,
    ext, pre, dact, dbuf, scores, dscores, run_t, b_t, c_t, enter, leave, d_b, d_c, suffix, prefix, d_dt, fixed, states,
):
    step = pl.program_id(0)
    length = x_ref.shape[0]
    chunks = length // Q

    @pl.when(step == 0)
    def _():
        for k in range(chunks):
            rows = slice(k * Q, (k + 1) * Q)
            b_rows, c_rows = b_ref[rows, :], c_ref[rows, :]
            b_t[:, rows] = b_rows.astype(F32).T.astype(BF16)
            c_t[:, rows] = c_rows.astype(F32).T.astype(BF16)
            scores[rows, :] = masked_scores(seg_ref, row_ref, b_rows, c_rows, k)
            running = run_ref[rows, :]
            run_t[k] = running.T
            carry, tail = chunk_flags(seg_ref, k)
            enter[rows, :] = jnp.exp(running) * carry
            leave[rows, :] = jnp.exp(running[Q - 1 : Q, :] - running) * tail
        for each in (dscores, d_b, d_c, suffix, prefix, d_dt, fixed):
            each[...] = jnp.zeros_like(each)
        dbuf[0:PAD, :] = jnp.zeros((PAD, BLK), F32)
        dbuf[PAD + length :, :] = jnp.zeros((PAD, BLK), F32)

    @pl.when(step <= STEPS)
    def _():
        ext[0:PAD, :] = halo_ref[...]
        ext[PAD:, :] = x_ref[...].astype(F32)
        for k in range(chunks):
            pre[k * Q : (k + 1) * Q, :] = conv_rows(ext, seg_ref, taps_ref, k * Q, Q)

    @pl.when(step < STEPS)
    def _():
        select = chosen(step)
        gather = chosen_back(step)
        skip = widen(heads_ref[...], select)[2:3, :]
        state = sin_ref[...].astype(F32)
        for k in range(chunks):
            rows = slice(k * Q, (k + 1) * Q)
            states[k] = state
            if k + 1 < chunks:
                total = pre[rows, :]
                scaled = total * sigmoid(total) * widen(dt_ref[rows, :], select)
                weighted = (scaled.astype(BF16).astype(F32) * widen(leave[rows, :], select)).astype(BF16)
                last = widen(enter[rows.stop - 8 : rows.stop, :], select)[7:8, :]
                state = last * state + dot(b_t[:, rows], weighted)
        d_state = dout_ref[...].astype(F32)
        for k in range(chunks - 1, -1, -1):
            rows = slice(k * Q, (k + 1) * Q)
            total = pre[rows, :]
            values = total * sigmoid(total)
            step_size = widen(dt_ref[rows, :], select)
            entering = widen(enter[rows, :], select)
            leaving = widen(leave[rows, :], select)
            scaled = (values * step_size).astype(BF16)
            scaled_wide = scaled.astype(F32)
            dy = dy_ref[rows, :]
            dy_wide = dy.astype(F32)
            before = states[k]
            before_low = before.astype(BF16)
            d_low = d_state.astype(BF16)
            running = pltpu.roll(run_ref[rows, :], lax.rem(128 - step * GROUP, 128), 1)
            insides, backs = [], []
            d_score = dscores[rows, :]
            for pair in range(2):
                lanes = slice(pair * 128, (pair + 1) * 128)
                mixing, turned, decays = [], [], []
                for one in range(2):
                    head = 2 * pair + one
                    gap = running[:, head : head + 1] - run_t[k, pl.ds(step * GROUP + head, 1), :]
                    decay = jnp.exp(jnp.minimum(gap, 0.0))
                    mixed = decay * scores[rows, :]
                    decays.append(decay)
                    mixing.append(mixed.astype(BF16))
                    turned.append(mixed.T.astype(BF16))
                spread = halves(scaled[:, lanes])
                insides.append(dot(jnp.concatenate(mixing, axis=1), spread))
                backs.append(dot(jnp.concatenate(turned, axis=1), halves(dy[:, lanes])))
                products = dot_nt(dy[:, lanes], spread)
                d_score = d_score + decays[0] * products[:, :Q] + decays[1] * products[:, Q:]
            dscores[rows, :] = d_score
            inside = jnp.concatenate(insides, axis=1) + entering * dot(c_ref[rows, :], before_low)
            back_inside = jnp.concatenate(backs, axis=1)
            back_state = leaving * dot(b_ref[rows, :], d_low)
            high, low = in_two(dy_wide * inside - scaled_wide * back_inside)
            suffix[rows, :] += dot(high, gather) + dot(low, gather)
            prefix[rows, :] += dot((scaled_wide * back_state).astype(BF16), gather)
            back = back_inside + back_state
            d_dt[rows, :] += dot((values * back).astype(BF16), gather)
            entered = (dy_wide * entering).astype(BF16)
            d_c[rows, :] += dot_nt(entered, before_low)
            d_b[rows, :] += dot_nt((scaled_wide * leaving).astype(BF16), d_low)
            kept = entering[Q - 1 : Q, :]
            through = jnp.sum(before * d_state, axis=0, keepdims=True) * kept
            high, low = in_two(jnp.broadcast_to(through, (8, BLK)))
            fixed[k * 8 : (k + 1) * 8, :] += dot(high, gather) + dot(low, gather)
            d_state = kept * d_state + dot(c_t[:, rows], entered)
            dact[rows, :] = back * step_size + skip * dy_wide

    @pl.when(step == STEPS)
    def _():
        for k in range(chunks):
            rows = slice(k * Q, (k + 1) * Q)
            own = seg_ref[PAD + k * Q : PAD + (k + 1) * Q, :]
            keep = (own == row_ref[0:1, rows]) & (iota((Q, Q), 1) <= iota((Q, Q), 0))
            d_score = jnp.where(keep, dscores[rows, :], 0.0)
            dact[rows, STATE:] = d_c[rows, :] + dot(d_score.astype(BF16), b_ref[rows, :])
            dact[rows, :STATE] = d_b[rows, :] + dot(d_score.T.astype(BF16), c_ref[rows, :])

    @pl.when(step <= STEPS)
    def _():
        sums = [jnp.zeros((1, BLK), F32) for _ in range(CONV + 1)]
        for k in range(chunks):
            rows = slice(k * Q, (k + 1) * Q)
            total = pre[rows, :]
            sig = sigmoid(total)
            d_conv = dact[rows, :] * (sig * (1.0 + total * (1.0 - sig)))
            dbuf[PAD + k * Q : PAD + (k + 1) * Q, :] = d_conv
            sums[4] = sums[4] + jnp.sum(d_conv, axis=0, keepdims=True)
            own = seg_ref[PAD + k * Q : PAD + (k + 1) * Q, :]
            for shift in range(CONV):
                at = PAD + k * Q - shift
                term = d_conv * ext[at : at + Q, :]
                if shift:
                    term = jnp.where(both(seg_ref[at : at + Q, :] == own), term, 0.0)
                sums[3 - shift] = sums[3 - shift] + jnp.sum(term, axis=0, keepdims=True)
        dtaps_ref[...] = jnp.concatenate(sums + [jnp.zeros((3, BLK), F32)], axis=0)

        def returned(at, rows):
            own = seg_ref[at : at + rows, :]
            result = taps_ref[3:4, :] * dbuf[at : at + rows, :]
            for shift in range(1, CONV):
                same = both(seg_ref[at + shift : at + shift + rows, :] == own)
                result = result + jnp.where(
                    same, taps_ref[3 - shift : 4 - shift, :] * dbuf[at + shift : at + shift + rows, :], 0.0
                )
            return result

        dhalo_ref[...] = returned(0, PAD)
        for k in range(chunks):
            dproj_ref[k * Q : (k + 1) * Q, :] = returned(PAD + k * Q, Q).astype(BF16)

    @pl.when(step == STEPS + 1)
    def _():
        lower = (iota((Q, Q), 1) < iota((Q, Q), 0)).astype(F32)
        upper = (iota((Q, Q), 1) >= iota((Q, Q), 0)).astype(F32)
        lane = iota((Q, 128), 1)
        rate = jnp.exp(heads_ref[1:2, :])
        bias_sum = jnp.zeros((1, 128), F32)
        decay_sum = jnp.zeros((1, 128), F32)
        for k in range(chunks):
            rows = slice(k * Q, (k + 1) * Q)
            d_log = jnp.dot(upper, suffix[rows, :], precision=HIGHEST, preferred_element_type=F32)
            d_log = d_log + jnp.dot(lower, prefix[rows, :], precision=HIGHEST, preferred_element_type=F32)
            d_log = d_log + fixed[k * 8 : k * 8 + 1, :]
            raw = jnp.where(lane < HEADS, dtraw_ref[rows, :128].astype(F32), 0.0) + heads_ref[0:1, :]
            d_raw = jnp.where(lane < HEADS, (d_dt[rows, :] - rate * d_log) * sigmoid(raw), 0.0)
            bias_sum = bias_sum + jnp.sum(d_raw, axis=0, keepdims=True)
            decay_sum = decay_sum - jnp.sum(d_log * dt_ref[rows, :] * rate, axis=0, keepdims=True)
            dproj_ref[rows, :] = jnp.concatenate([d_raw, jnp.zeros_like(d_raw)], axis=1).astype(BF16)
        dheads_ref[...] = jnp.concatenate([bias_sum, decay_sum, jnp.zeros((6, 128), F32)], axis=0)


def back(projected, halo, taps, heads, seg_lanes, seg_row, b_rows, c_rows, dt, running, dy, incoming, outgoing, given):
    length = projected.shape[0]
    whole = lambda *shape: pl.BlockSpec(shape, lambda j: (0,) * len(shape))
    upto = lambda last, first=0: lambda j: (0, first + jnp.minimum(j, last))
    return pl.pallas_call(
        back_kernel,
        grid=(STEPS + 2,),
        in_specs=[
            pl.BlockSpec((length, BLK), upto(STEPS, STEPS)),
            pl.BlockSpec((length, BLK), lambda j: (0, 2 * STEPS + 1)),
            pl.BlockSpec((PAD, BLK), upto(STEPS, STEPS)),
            pl.BlockSpec((8, BLK), upto(STEPS)),
            whole(8, 128),
            whole(length + 2 * PAD, 128),
            whole(8, length),
            whole(length, 128),
            whole(length, 128),
            whole(length, 128),
            whole(length, 128),
            pl.BlockSpec((length, BLK), upto(STEPS - 1)),
            pl.BlockSpec((STATE, BLK), upto(STEPS - 1)),
            pl.BlockSpec((STATE, BLK), upto(STEPS - 1)),
            pl.BlockSpec(memory_space=pl.ANY),
        ],
        out_specs=[
            pl.BlockSpec((length, BLK), lambda j: (0, STEPS + j)),
            pl.BlockSpec((PAD, BLK), upto(STEPS)),
            pl.BlockSpec((8, BLK), upto(STEPS)),
            whole(8, 128),
        ],
        out_shape=[
            jax.ShapeDtypeStruct((length, WIDTH), BF16),
            jax.ShapeDtypeStruct((PAD, XBC), F32),
            jax.ShapeDtypeStruct((8, XBC), F32),
            jax.ShapeDtypeStruct((8, 128), F32),
        ],
        scratch_shapes=[
            pltpu.VMEM((length + PAD, BLK), F32),
            pltpu.VMEM((length, BLK), F32),
            pltpu.VMEM((length, BLK), F32),
            pltpu.VMEM((length + 2 * PAD, BLK), F32),
            pltpu.VMEM((length, Q), F32),
            pltpu.VMEM((length, Q), F32),
            pltpu.VMEM((length // Q, 128, Q), F32),
            pltpu.VMEM((128, length), BF16),
            pltpu.VMEM((128, length), BF16),
            pltpu.VMEM((length, 128), F32),
            pltpu.VMEM((length, 128), F32),
            pltpu.VMEM((length, 128), F32),
            pltpu.VMEM((length, 128), F32),
            pltpu.VMEM((length, 128), F32),
            pltpu.VMEM((length, 128), F32),
            pltpu.VMEM((length, 128), F32),
            pltpu.VMEM((8 * (length // Q), 128), F32),
            pltpu.VMEM((length // Q, STATE, BLK), F32),
        ],
        input_output_aliases={14: 0},
        compiler_params=pltpu.CompilerParams(vmem_limit_bytes=VMEM_LIMIT),
        cost_estimate=pl.CostEstimate(
            flops=12 * 10**9, bytes_accessed=30 * 10**6, transcendentals=2 * 10**7
        ),
        name="back",
    )(
        projected, projected, halo, taps, heads, seg_lanes, seg_row, b_rows, c_rows, dt, running, dy, incoming, outgoing, given
    )


OUT_CHUNKS = 2 * D // WIDE
IN_CHUNKS = WIDTH // WIDE
CHUNKS = OUT_CHUNKS + IN_CHUNKS
LAGS = 8
SMALL_ROWS = 168


def reduce_kernel(
    lhs_in, lhs_out, rhs_in, rhs_out, small_ref,
    din_ref, dout_ref, total_ref,
    own, core_send, core_recv, y_recv, x_recv, z_recv, w_recv, final, small_send, small_recv,
    send_sems, recv_sems, small_send_sems, small_recv_sems,
):
    step = pl.program_id(0)
    shard, part = lax.axis_index("fsdp"), lax.axis_index("ctx")
    core, y = lax.rem(shard, 2), shard // 2
    x, z = lax.rem(part, 2), part // 2
    near, far = lax.rem(z, 2), z // 2
    peers = (
        {"fsdp": flipped(shard, 1)},
        {"fsdp": flipped(shard, 2)},
        {"ctx": flipped(part, 1)},
        {"ctx": flipped(part, 2)},
        {"ctx": flipped(part, 4)},
    )

    def sent(stage, k, source, target, peer):
        return pltpu.make_async_remote_copy(
            src_ref=source,
            dst_ref=target,
            send_sem=send_sems.at[stage, k],
            recv_sem=recv_sems.at[stage, k],
            device_id=peers[peer],
            device_id_type=pl.DeviceIdType.MESH,
        )

    copies = (
        lambda k: sent(0, k, core_send.at[lax.rem(k, 2)], core_recv.at[k], 0),
        lambda k: sent(1, k, core_recv.at[k, 1 - y], y_recv.at[k], 1),
        lambda k: sent(2, k, y_recv.at[k, 1 - x], x_recv.at[k], 2),
        lambda k: sent(3, k, x_recv.at[k, 1 - near], z_recv.at[k], 3),
        lambda k: sent(4, k, z_recv.at[k, 1 - far], w_recv.at[k], 4),
        lambda k: sent(5, k, final.at[k, x, near, far], final.at[k, x, near, far], 4),
        lambda k: sent(6, k, final.at[k, x, near], final.at[k, x, near], 3),
        lambda k: sent(7, k, final.at[k, x], final.at[k, x], 2),
    )
    arrivals = copies[:5] + (
        lambda k: sent(5, k, final.at[k, x, near, 1 - far], final.at[k, x, near, 1 - far], 4),
        lambda k: sent(6, k, final.at[k, x, 1 - near], final.at[k, x, 1 - near], 3),
        lambda k: sent(7, k, final.at[k, 1 - x], final.at[k, 1 - x], 2),
    )

    def small_copy(stage):
        return pltpu.make_async_remote_copy(
            src_ref=small_send.at[stage],
            dst_ref=small_recv.at[stage],
            send_sem=small_send_sems.at[stage],
            recv_sem=small_recv_sems.at[stage],
            device_id=peers[stage],
            device_id_type=pl.DeviceIdType.MESH,
        )

    @pl.when(step == 0)
    def _():
        barrier = pltpu.get_barrier_semaphore()
        for peer in peers:
            pl.semaphore_signal(barrier, inc=1, device_id=peer, device_id_type=pl.DeviceIdType.MESH)
        pl.semaphore_wait(barrier, len(peers))
        small_send[0] = small_ref[...]
        small_copy(0).start()

    for stage in range(5):

        @pl.when(step == stage + 1)
        def _():
            small_copy(stage).wait()
            total = small_send[stage] + small_recv[stage]
            if stage < 4:
                small_send[stage + 1] = total
                small_copy(stage + 1).start()
            else:
                total_ref[...] = total

    def partial(lhs_of, rhs):
        for row in range(2):
            value = dot(lhs_of(2 * row + 1 - core), rhs).astype(BF16)
            core_send[lax.rem(step, 2), row] = value.reshape(2, 2, 2, PIECE, WIDE)
        copies[0](step).start()
        for row in range(2):
            own[row] = dot(lhs_of(2 * row + core), rhs).reshape(2, 2, 2, PIECE, WIDE)

    @pl.when(step < OUT_CHUNKS)
    def _():
        partial(lambda s: lhs_out[s, step // (D // WIDE)], rhs_out[...])

    @pl.when((step >= OUT_CHUNKS) & (step < CHUNKS))
    def _():
        partial(lambda s: lhs_in[s], rhs_in[...])

    @pl.when(step < CHUNKS)
    def _():
        arrivals[0](step).wait_recv()
        for row in (1 - y, y):
            core_recv[step, row] = (own[row] + core_recv[step, row].astype(F32)).astype(BF16)
        copies[1](step).start()

    def stage(lag):
        def decorate(body):
            k = step - lag

            @pl.when((k >= 0) & (k < CHUNKS))
            def _():
                body(k)

        return decorate

    def summed(a, b):
        return (a.astype(F32) + b.astype(F32)).astype(BF16)

    @stage(1)
    def _(k):
        arrivals[1](k).wait_recv()
        kept = core_recv.at[k, y]
        y_recv[k] = summed(y_recv[k], kept[...])
        copies[2](k).start()
        copies[0](k).wait_send()

    @stage(2)
    def _(k):
        arrivals[2](k).wait_recv()
        x_recv[k] = summed(x_recv[k], y_recv[k, x])
        copies[3](k).start()

    @stage(3)
    def _(k):
        arrivals[3](k).wait_recv()
        z_recv[k] = summed(z_recv[k], x_recv[k, near])
        copies[4](k).start()

    @stage(4)
    def _(k):
        arrivals[4](k).wait_recv()
        final[k, x, near, far] = summed(w_recv[k], z_recv[k, far])
        copies[5](k).start()

    @stage(5)
    def _(k):
        arrivals[5](k).wait_recv()
        copies[6](k).start()

    @stage(6)
    def _(k):
        arrivals[6](k).wait_recv()
        copies[7](k).start()

    @stage(7)
    def _(k):
        arrivals[7](k).wait_recv()
        for one in range(1, 8):
            copies[one](k).wait_send()
        whole = final[k].reshape(SHARD, WIDE)

        @pl.when(k < OUT_CHUNKS)
        def _():
            dout_ref[...] = whole

        @pl.when(k >= OUT_CHUNKS)
        def _():
            din_ref[...] = whole


def reduce(part_t, mixer_t, dproj, cot, small):
    length = cot.shape[0]
    per_half = D // WIDE
    whole = lambda *shape: pl.BlockSpec(shape, lambda t: (0,) * len(shape))

    def out_block(t):
        k = jnp.clip(t - LAGS + 1, 0, OUT_CHUNKS - 1)
        return (k // per_half, lax.rem(k, per_half))

    slots = lambda *shape: pltpu.VMEM((CHUNKS, *shape, PIECE, WIDE), BF16)
    return pl.pallas_call(
        reduce_kernel,
        grid=(CHUNKS + LAGS - 1,),
        in_specs=[
            whole(4, SHARD, length),
            whole(4, 2, SHARD, length),
            pl.BlockSpec((length, WIDE), lambda t: (0, jnp.clip(t - OUT_CHUNKS, 0, IN_CHUNKS - 1))),
            pl.BlockSpec((length, WIDE), lambda t: (0, lax.rem(jnp.minimum(t, OUT_CHUNKS - 1), per_half))),
            whole(SMALL_ROWS, 128),
        ],
        out_specs=[
            pl.BlockSpec((SHARD, WIDE), lambda t: (0, jnp.clip(t - LAGS + 1 - OUT_CHUNKS, 0, IN_CHUNKS - 1))),
            pl.BlockSpec((SHARD, WIDE), out_block),
            whole(SMALL_ROWS, 128),
        ],
        out_shape=[
            jax.ShapeDtypeStruct((SHARD, PROJ), BF16),
            jax.ShapeDtypeStruct((2 * SHARD, D), BF16),
            jax.ShapeDtypeStruct((SMALL_ROWS, 128), F32),
        ],
        scratch_shapes=[
            pltpu.VMEM((2, 2, 2, 2, PIECE, WIDE), F32),
            pltpu.VMEM((2, 2, 2, 2, 2, PIECE, WIDE), BF16),
            slots(2, 2, 2, 2),
            slots(2, 2, 2),
            slots(2, 2),
            slots(2),
            slots(),
            slots(2, 2, 2),
            pltpu.VMEM((5, SMALL_ROWS, 128), F32),
            pltpu.VMEM((5, SMALL_ROWS, 128), F32),
            pltpu.SemaphoreType.DMA((8, CHUNKS)),
            pltpu.SemaphoreType.DMA((8, CHUNKS)),
            pltpu.SemaphoreType.DMA((5,)),
            pltpu.SemaphoreType.DMA((5,)),
        ],
        compiler_params=pltpu.CompilerParams(
            vmem_limit_bytes=VMEM_LIMIT, collective_id=0, has_side_effects=True
        ),
        name="reduce",
    )(part_t, mixer_t, dproj, cot, small)


def passed_along(block, axis, distance):
    devices = range(lax.axis_size(axis))
    route = [(i - distance, i) for i in devices if i - distance in devices]
    return lax.ppermute(block, axis, route)


def pack_small(conv_taps, conv_bias, dt_bias, decay_log, skip_scale, mixer_gain, input_gain):
    width = conv_bias.shape[0]

    def line(*parts):
        flat = jnp.concatenate(parts)
        return jnp.pad(flat, (0, width - flat.shape[0]))[None]

    rows = jnp.concatenate(
        [
            conv_taps.T,
            conv_bias[None],
            line(mixer_gain),
            line(input_gain),
            line(dt_bias, decay_log, skip_scale),
        ],
        axis=0,
    )
    return jnp.pad(rows.astype(F32), ((0, 0), (0, SMALL_WIDTH - width)))


def unpack_small(whole, width):
    shards = whole.shape[0]
    joined = jnp.swapaxes(whole, 0, 1)
    taps = jnp.pad(joined[:5, :, :width].reshape(5, shards * width).astype(F32), ((0, 3), (0, 0)))
    gain = joined[5, :, : INNER // shards].reshape(1, INNER).astype(F32)
    input_gain = joined[6, :, : D // shards].reshape(1, D).astype(F32)
    own = HEADS // shards
    heads = joined[7, :, : 3 * own].reshape(shards, 3, own).swapaxes(0, 1).reshape(3, HEADS)
    heads = jnp.pad(heads.astype(F32), ((0, 5), (0, 128 - HEADS)))
    return taps, jnp.pad(gain, ((0, 7), (0, 0))), input_gain, heads


def on_device(
    inputs,
    segment_ids,
    out_grad,
    in_matrix,
    out_matrix,
    conv_taps,
    conv_bias,
    dt_bias,
    decay_log,
    skip_scale,
    mixer_gain,
    input_gain,
):
    shards, parts = lax.axis_size("fsdp"), lax.axis_size("ctx")
    place = lax.axis_index("ctx")
    units_low, cot = inputs[0], out_grad[0]
    units = units_low.astype(F32)
    seg_ids = segment_ids[0]
    length = units.shape[0]
    here = (shards, parts) == (4, PARTS)
    small = pack_small(conv_taps, conv_bias, dt_bias, decay_log, skip_scale, mixer_gain, input_gain)
    inv_rms = lax.rsqrt(jnp.mean(units * units, axis=-1, keepdims=True) + epsilon)
    base_rows = units * inv_rms
    if here:
        w_whole, projected, normed_t, smalls, halo, seg_before = project(in_matrix, units_low, small, seg_ids)
        w_whole = w_whole.reshape(D, WIDTH)
        rim_seg = seg_before.reshape(length)[length - CONV + 1 :]
        taps, gain, g_float, heads = unpack_small(smalls, conv_bias.shape[0])
    else:
        w_whole = jnp.pad(in_matrix, ((0, 0), (0, WIDTH - PROJ)))
        w_whole = lax.all_gather(w_whole, "fsdp", axis=0, tiled=True)
        rim_seg = passed_along(seg_ids[length - CONV + 1 :], "ctx", 1)
        taps, gain, g_float, heads = unpack_small(lax.all_gather(small, "fsdp"), conv_bias.shape[0])
        normed = (base_rows * g_float).astype(BF16)
        normed_t = normed.T
        projected = dot(normed, w_whole).astype(BF16)
        rim_rows = passed_along(projected[length - CONV + 1 :], "ctx", 1)
        halo = jnp.pad(rim_rows, ((PAD - CONV + 1, 0), (0, 0))).astype(F32)
    seg_ext = jnp.concatenate(
        [
            jnp.full((PAD - CONV + 1,), -1, jnp.int32),
            rim_seg,
            seg_ids,
            jnp.full((PAD,), -2, jnp.int32),
        ]
    )
    seg_lanes = jnp.broadcast_to(seg_ext[:, None], (length + 2 * PAD, 128))
    seg_row = jnp.broadcast_to(seg_ids[None], (8, length))

    xs, y_local, incoming, b_rows, c_rows, dt, running, entering, kept, out_whole = front(
        projected, halo, taps, heads, seg_lanes, seg_row, out_matrix, here
    )
    out_whole = out_whole.reshape(-1, D)
    if not here:
        out_whole = lax.all_gather(out_matrix, "fsdp", axis=0, tiled=True)
        kept = lax.all_gather(kept[0], "ctx")
        incoming = joined_plainly(lax.all_gather(incoming, "ctx"), kept, place, True)
    mixer_t, dproj, dy, outgoing, column_sums, block_out, stats = tail(
        y_local, xs, projected, incoming, kept, out_whole, c_rows, entering, heads, gain, cot, units_low, here
    )
    if not here:
        outgoing = joined_plainly(lax.all_gather(outgoing, "ctx"), kept, place, False)
    dproj, d_halo, d_taps, d_heads = back(
        projected, halo, taps, heads, seg_lanes, seg_row, b_rows, c_rows, dt, running, dy, incoming, outgoing, dproj
    )
    returned = passed_along(d_halo.astype(BF16), "ctx", -1)
    last = lax.slice(dproj, (length - PAD, INNER), (length, INNER + XBC))
    last = (last.astype(F32) + returned.astype(F32)).astype(BF16)
    dproj = lax.dynamic_update_slice(dproj, last, (length - PAD, INNER))

    d_normed = dot_nt(dproj, w_whole)
    d_input_gain = jnp.sum(d_normed * base_rows, axis=0)
    d_base = d_normed * g_float
    d_units = inv_rms * (d_base - base_rows * jnp.mean(d_base * base_rows, axis=-1, keepdims=True))
    input_grad = (cot.astype(F32) + d_units).astype(BF16)

    row = jnp.concatenate(
        [
            d_taps[:5].reshape(-1),
            column_sums[0],
            d_input_gain,
            d_heads[0, :HEADS],
            d_heads[1, :HEADS],
            jnp.sum(column_sums[1].reshape(HEADS, HDIM), axis=1),
            jnp.sum(stats[:2], axis=1),
        ]
    )
    row = jnp.pad(row, (0, SMALL_ROWS * 128 - row.shape[0])).reshape(SMALL_ROWS, 128)
    if here:
        d_in, d_out, row = reduce(normed_t, mixer_t.reshape(4, 2, SHARD, length), dproj, cot, row)
        d_in, d_out = d_in.astype(F32), d_out.astype(F32)
    else:
        d_in = jnp.dot(normed_t, dproj, preferred_element_type=F32)[:, :PROJ]
        d_out = jnp.dot(mixer_t, cot, preferred_element_type=F32)

        def scattered(grad):
            return lax.psum_scatter(grad.astype(BF16), "fsdp", scatter_dimension=0, tiled=True)

        d_in = lax.psum(scattered(d_in), "ctx").astype(F32)
        d_out = lax.psum(scattered(d_out), "ctx").astype(F32)
        row = lax.psum(row, ("fsdp", "ctx"))
    row = row.reshape(-1)
    me = lax.axis_index("fsdp")

    def own(flat):
        size = flat.shape[-1] // shards
        return lax.dynamic_slice_in_dim(flat, me * size, size, flat.ndim - 1)

    at = 5 * XBC
    taps_sum = row[:at].reshape(5, XBC)
    gain_sum = row[at : at + INNER]
    input_gain_sum = row[at + INNER : at + INNER + D]
    at = at + INNER + D
    head_sums = row[at : at + 3 * HEADS].reshape(3, HEADS)
    stat_sums = row[at + 3 * HEADS : at + 3 * HEADS + 2]
    rms_stats = jnp.sqrt(stat_sums / (length * shards * parts * D))
    return (
        block_out[None],
        input_grad[None],
        d_in,
        d_out,
        own(taps_sum[:4]).T,
        own(taps_sum[4]),
        own(head_sums[0]),
        own(head_sums[1]),
        own(head_sums[2]),
        own(gain_sum),
        own(input_gain_sum),
        rms_stats,
    )


def solution(mesh):
    return jax.shard_map(
        on_device,
        mesh=mesh,
        in_specs=(
            P("fsdp", "ctx", None),
            P("fsdp", "ctx"),
            P("fsdp", "ctx", None),
            P("fsdp", None),
            P("fsdp", None),
            P("fsdp", None),
            P("fsdp"),
            P("fsdp"),
            P("fsdp"),
            P("fsdp"),
            P("fsdp"),
            P("fsdp"),
        ),
        out_specs=(
            P("fsdp", "ctx", None),
            P("fsdp", "ctx", None),
            P("fsdp", None),
            P("fsdp", None),
            P("fsdp", None),
            P("fsdp"),
            P("fsdp"),
            P("fsdp"),
            P("fsdp"),
            P("fsdp"),
            P("fsdp"),
            P(),
        ),
        check_vma=False,
    )
```

```python
import functools

import jax
import jax.numpy as jnp
from jax import lax
from jax.experimental import pallas as pl
from jax.experimental.pallas import tpu as pltpu
from jax.sharding import PartitionSpec as P

D = 1536
HEADS = 48
HDIM = 64
STATE = 128
CONV = 4
INNER = 3072
XBC = 3328
PROJ = 6448
WIDTH = 6656

BLK = 256
GROUP = BLK // HDIM
STEPS = INNER // BLK
Q = 128
PAD = 8
WIDE = 512
SHARD = D // 4
PIECE = SHARD // 8
SMALL_WIDTH = 896
AHEAD = 2

epsilon = 1e-05
F32, BF16 = jnp.float32, jnp.bfloat16
HIGHEST = lax.Precision.HIGHEST
VMEM_LIMIT = 60 * 1024 * 1024


def communicating(number, exchanging):
    if not exchanging:
        return pltpu.CompilerParams(vmem_limit_bytes=VMEM_LIMIT)
    return pltpu.CompilerParams(
        vmem_limit_bytes=VMEM_LIMIT, collective_id=number, has_side_effects=True
    )


def dot(a, b):
    return jnp.dot(a, b, preferred_element_type=F32)


def dot_nt(a, b):
    return lax.dot_general(a, b, (((1,), (1,)), ((), ())), preferred_element_type=F32)


def iota(shape, dim):
    return lax.broadcasted_iota(jnp.int32, shape, dim)


def sigmoid(v):
    return 1.0 / (1.0 + jnp.exp(-v))


def in_two(a):
    high = a.astype(BF16)
    return high, (a - high.astype(F32)).astype(BF16)


def chosen(step):
    columns = step * GROUP + lax.shift_right_logical(iota((128, BLK), 1), 6)
    return (iota((128, BLK), 0) == columns).astype(BF16)


def chosen_back(step):
    heads = step * GROUP + lax.shift_right_logical(iota((BLK, 128), 0), 6)
    return (iota((BLK, 128), 1) == heads).astype(BF16)


def widen(per_head, select):
    high, low = in_two(per_head)
    return dot(high, select) + dot(low, select)


def halves(pair):
    first = iota(pair.shape, 1) < HDIM
    zero = jnp.zeros_like(pair)
    return jnp.concatenate([jnp.where(first, pair, zero), jnp.where(first, zero, pair)], axis=0)


def both(mask):
    return jnp.concatenate([mask, mask], axis=1)


def conv_rows(ext_ref, seg_ref, taps_ref, start, rows):
    own = seg_ref[start + PAD : start + PAD + rows, :]
    total = taps_ref[4:5, :] + taps_ref[3:4, :] * ext_ref[start + PAD : start + PAD + rows, :]
    for back in range(1, CONV):
        at = start + PAD - back
        same = both(seg_ref[at : at + rows, :] == own)
        total = total + jnp.where(
            same, taps_ref[3 - back : 4 - back, :] * ext_ref[at : at + rows, :], 0.0
        )
    return total


def chunk_flags(seg_ref, k):
    own = seg_ref[PAD + k * Q : PAD + (k + 1) * Q, :]
    before = seg_ref[PAD + k * Q - 1 : PAD + k * Q, :]
    last = seg_ref[PAD + (k + 1) * Q - 1 : PAD + (k + 1) * Q, :]
    return (own == before).astype(F32), (own == last).astype(F32)


def masked_scores(seg_ref, row_ref, b_rows, c_rows, k):
    own = seg_ref[PAD + k * Q : PAD + (k + 1) * Q, :]
    row = row_ref[0:1, k * Q : (k + 1) * Q]
    keep = (own == row) & (iota((Q, Q), 1) <= iota((Q, Q), 0))
    return jnp.where(keep, dot_nt(c_rows, b_rows), 0.0)


def flipped(index, bit):
    return index + bit - 2 * bit * lax.rem(index // bit, 2)


class Gather:
    def __init__(self, locate, rows, loads, sends, arrivals):
        self.locate, self.rows = locate, rows
        self.loads, self.sends, self.arrivals = loads, sends, arrivals
        shard, part = lax.axis_index("fsdp"), lax.axis_index("ctx")
        self.own, self.other = shard, flipped(shard, 2)
        self.sibling, self.opposite = flipped(shard, 1), flipped(flipped(shard, 2), 1)
        x, near = lax.rem(part, 2), lax.rem(part // 2, 2)
        self.mine, self.over_x, self.over_z = 2 * x + near, 2 * (1 - x) + near, 2 * x + 1 - near
        self.across = 2 * (1 - x) + 1 - near
        self.peers = {
            "core": {"fsdp": flipped(shard, 1)},
            "y": {"fsdp": flipped(shard, 2)},
            "x": {"ctx": flipped(part, 1)},
            "z": {"ctx": flipped(part, 2)},
        }

    def whole(self, shard, k):
        return self.locate(k, shard, 0, self.rows)

    def quarter(self, shard, k, which):
        return self.locate(k, shard, which * (self.rows // 4), self.rows // 4)

    def half(self, shard, k, which, second):
        return self.locate(k, shard, (2 * which + second) * (self.rows // 8), self.rows // 8)

    def copy(self, place, kind, k, peer):
        return pltpu.make_async_remote_copy(
            src_ref=place,
            dst_ref=place,
            send_sem=self.sends.at[kind, k],
            recv_sem=self.arrivals.at[kind, k],
            device_id=self.peers[peer],
            device_id_type=pl.DeviceIdType.MESH,
        )

    def outgoing(self, kind, k):
        own, other = self.own, self.other
        if kind == 0:
            return self.copy(self.whole(own, k), kind, k, "core")
        if kind == 1:
            return self.copy(self.quarter(own, k, self.mine), kind, k, "y")
        if kind == 2:
            return self.copy(self.quarter(other, k, self.mine), kind, k, "x")
        if kind == 3:
            return self.copy(self.quarter(other, k, self.mine), kind, k, "z")
        if kind == 4:
            return self.copy(self.half(other, k, self.over_x, 0), kind, k, "z")
        if kind == 5:
            return self.copy(self.half(other, k, self.over_z, 1), kind, k, "x")
        which = (self.mine, self.over_x, self.over_z, self.across)[kind - 6]
        return self.copy(self.quarter(other, k, which), kind, k, "core")

    def arrived(self, kind, k):
        other, opposite = self.other, self.opposite
        if kind == 0:
            place = self.whole(self.sibling, k)
        elif kind < 4:
            place = self.quarter(other, k, (self.mine, self.over_x, self.over_z)[kind - 1])
        elif kind < 6:
            place = self.half(other, k, self.across, kind - 4)
        else:
            place = self.quarter(opposite, k, (self.mine, self.over_x, self.over_z, self.across)[kind - 6])
        self.copy(place, kind, k, "core").wait_recv()

    def load(self, k, source):
        return pltpu.make_async_copy(source, self.whole(self.own, k), self.loads.at[k])

    def begin(self, k):
        self.load(k, self.whole(self.own, k)).wait()
        self.outgoing(1, k).start()
        self.outgoing(0, k).start()

    def first(self, k):
        self.arrived(1, k)
        for kind in (2, 3, 6):
            self.outgoing(kind, k).start()

    def second(self, k):
        self.arrived(2, k)
        self.outgoing(4, k).start()
        self.outgoing(7, k).start()
        self.arrived(3, k)
        self.outgoing(5, k).start()
        self.outgoing(8, k).start()

    def third(self, k):
        self.arrived(4, k)
        self.arrived(5, k)
        self.outgoing(9, k).start()

    def complete(self, k):
        for kind in (0, 6, 7, 8, 9):
            self.arrived(kind, k)

    def drain(self, k):
        for kind in range(10):
            self.outgoing(kind, k).wait_send()


def gather_sems(chunks):
    return [
        pltpu.SemaphoreType.DMA((chunks,)),
        pltpu.SemaphoreType.DMA((10, chunks)),
        pltpu.SemaphoreType.DMA((10, chunks)),
    ]


def project_kernel(
    main_ref, rest_ref, units_ref, small_ref, seg_ref,
    weight_ref, projected_ref, normed_t_ref, smalls_ref, halo_ref, seg_before_ref,
    normed, gathered, own_small, smalls, own_seg, seg_before, edges, halos,
    loads, sends, arrivals, stores, small_sends, small_arrivals, edge_sends, edge_arrivals,
):
    step = pl.program_id(0)
    chunks = WIDTH // WIDE
    length = units_ref.shape[0]

    def locate(k, s, start, size):
        rows, columns = pl.multiple_of(start, size), pl.multiple_of(s * SHARD, SHARD)
        return gathered.at[k, pl.ds(rows, size), pl.ds(columns, SHARD)]

    gather = Gather(locate, WIDE, loads, sends, arrivals)
    shard, part = lax.axis_index("fsdp"), lax.axis_index("ctx")
    others = ({"fsdp": flipped(shard, 1)}, {"fsdp": flipped(shard, 2)}, {"fsdp": flipped(flipped(shard, 1), 2)})
    following, outer = lax.rem(part + 1, PARTS), lax.rem(part + PARTS - 1 + 2 * lax.rem(part, 2), PARTS)

    def remote(source, target, send, arrival, peer):
        return pltpu.make_async_remote_copy(
            src_ref=source,
            dst_ref=target,
            send_sem=send,
            recv_sem=arrival,
            device_id=peer,
            device_id_type=pl.DeviceIdType.MESH,
        )

    def small_copy(hop):
        return remote(own_small, smalls.at[shard], small_sends.at[hop], small_arrivals.at[hop], others[hop])

    def seg_copy():
        return remote(own_seg, seg_before, small_sends.at[3], small_arrivals.at[3], {"ctx": following})

    def edge_copy(k):
        return remote(edges.at[k], halos.at[k], edge_sends.at[k], edge_arrivals.at[k], {"ctx": following})

    def store(k):
        rows = pl.ds(pl.multiple_of(k * WIDE, WIDE), WIDE)
        return pltpu.make_async_copy(gathered.at[k], weight_ref.at[rows], stores.at[k])

    @pl.when(step == 0)
    def _():
        barrier = pltpu.get_barrier_semaphore()
        near = [*others, {"ctx": flipped(part, 1)}, {"ctx": flipped(part, 2)}, {"ctx": outer}]
        for peer in near:
            pl.semaphore_signal(barrier, inc=1, device_id=peer, device_id_type=pl.DeviceIdType.MESH)
        for k in range(chunks):
            gather.load(k, main_ref.at[k * WIDE : (k + 1) * WIDE, :] if k + 1 < chunks else rest_ref).start()
        own_small[...] = small_ref[...]
        own_seg[...] = seg_ref[...]
        smalls[shard] = small_ref[...]
        pl.semaphore_wait(barrier, len(near))
        for hop in range(3):
            small_copy(hop).start()
        seg_copy().start()
        for k in range(AHEAD):
            gather.begin(k)
        for hop in range(3):
            small_copy(hop).wait()
        seg_copy().wait()
        smalls_ref[...] = smalls[...]
        seg_before_ref[...] = jnp.where(part == 0, -1, seg_before[...])
        gain = jnp.concatenate([smalls[s, 6:7, :SHARD] for s in range(4)], axis=1)
        for k in range(length // Q):
            rows = slice(k * Q, (k + 1) * Q)
            units = units_ref[rows, :].astype(F32)
            norm = lax.rsqrt(jnp.sum(units * units, axis=1, keepdims=True) * (1.0 / D) + epsilon)
            value = units * norm * gain
            normed[rows, :] = value.astype(BF16)
            for s in range(4):
                normed_t_ref[s, :, rows] = value[:, s * SHARD : (s + 1) * SHARD].T.astype(BF16)

    def stage(lag):
        def decorate(body):
            k = step - lag

            @pl.when((k >= 0) & (k < chunks))
            def _():
                body(k)

        return decorate

    stage(-AHEAD)(lambda k: pl.when(k >= AHEAD)(lambda: gather.begin(k)))
    stage(0)(gather.first)
    stage(1)(gather.second)
    stage(2)(gather.third)

    @stage(3)
    def _(k):
        gather.complete(k)
        store(k).start()
        low = dot_nt(normed[...], gathered[k]).astype(BF16)
        projected_ref[...] = low
        edges[k] = low[length - 16 :, :].astype(F32)[8:, :]
        edge_copy(k).start()

    @stage(4)
    def _(k):
        edge_copy(k).wait()
        gather.drain(k)
        store(k).wait()
        halo_ref[...] = jnp.where(part == 0, 0.0, halos[k])


def project(in_matrix, units, small, seg_ids):
    length = units.shape[0]
    chunks = WIDTH // WIDE
    turned = in_matrix.T
    rest = jnp.pad(turned[(chunks - 1) * WIDE :], ((0, WIDTH - PROJ), (0, 0)))
    whole = lambda *shape: pl.BlockSpec(shape, lambda t: (0,) * len(shape))
    column = lambda lag: lambda t: (0, jnp.clip(t - lag, 0, chunks - 1))
    anywhere = pl.BlockSpec(memory_space=pl.ANY)
    return pl.pallas_call(
        project_kernel,
        grid=(chunks + 4,),
        in_specs=[
            anywhere,
            anywhere,
            whole(length, D),
            whole(8, SMALL_WIDTH),
            whole(length // 128, 128),
        ],
        out_specs=[
            anywhere,
            pl.BlockSpec((length, WIDE), column(3)),
            whole(4, SHARD, length),
            whole(4, 8, SMALL_WIDTH),
            pl.BlockSpec((PAD, WIDE), column(4)),
            whole(length // 128, 128),
        ],
        out_shape=[
            jax.ShapeDtypeStruct((WIDTH, D), BF16),
            jax.ShapeDtypeStruct((length, WIDTH), BF16),
            jax.ShapeDtypeStruct((4, SHARD, length), BF16),
            jax.ShapeDtypeStruct((4, 8, SMALL_WIDTH), F32),
            jax.ShapeDtypeStruct((PAD, WIDTH), F32),
            jax.ShapeDtypeStruct((length // 128, 128), jnp.int32),
        ],
        scratch_shapes=[
            pltpu.VMEM((length, D), BF16),
            pltpu.VMEM((chunks, WIDE, D), BF16),
            pltpu.VMEM((8, SMALL_WIDTH), F32),
            pltpu.VMEM((4, 8, SMALL_WIDTH), F32),
            pltpu.VMEM((length // 128, 128), jnp.int32),
            pltpu.VMEM((length // 128, 128), jnp.int32),
            pltpu.VMEM((chunks, PAD, WIDE), F32),
            pltpu.VMEM((chunks, PAD, WIDE), F32),
            *gather_sems(chunks),
            pltpu.SemaphoreType.DMA((chunks,)),
            pltpu.SemaphoreType.DMA((4,)),
            pltpu.SemaphoreType.DMA((4,)),
            pltpu.SemaphoreType.DMA((chunks,)),
            pltpu.SemaphoreType.DMA((chunks,)),
        ],
        compiler_params=communicating(3, True),
        name="project",
    )(turned, rest, units, small, seg_ids.reshape(length // 128, 128))


PARTS = 8
SLAB = STATE // PARTS
JOIN, DONE = 2, 4


class Exchange:
    def __init__(self, held, gathered, joined, incoming, sems):
        self.held, self.gathered, self.joined, self.incoming, self.sems = held, gathered, joined, incoming, sems
        self.me = lax.axis_index("ctx")

    def others(self):
        return [lax.rem(self.me + hop, PARTS) for hop in range(1, PARTS)]

    def greet(self, *further):
        barrier = pltpu.get_barrier_semaphore()
        peers = [{"ctx": other} for other in self.others()] + list(further)
        for peer in peers:
            pl.semaphore_signal(barrier, inc=1, device_id=peer, device_id_type=pl.DeviceIdType.MESH)
        pl.semaphore_wait(barrier, len(peers))

    def copy(self, source, target, kind, group, other):
        return pltpu.make_async_remote_copy(
            src_ref=source,
            dst_ref=target,
            send_sem=self.sems.at[2 * kind, group],
            recv_sem=self.sems.at[2 * kind + 1, group],
            device_id={"ctx": other},
            device_id_type=pl.DeviceIdType.MESH,
        )

    def all_of(self, kind, group):
        source, target = ((self.held, self.gathered), (self.joined, self.incoming))[kind]
        some = pl.ds(0, PARTS - 1)
        return self.copy(source.at[group, some], target.at[group, some], kind, group, self.others()[0])

    def spread(self, group, state):
        self.held[group] = state.astype(BF16).reshape(PARTS, SLAB, BLK)
        self.gathered[group, self.me] = self.held[group, self.me]
        for other in self.others():
            self.copy(self.held.at[group, other], self.gathered.at[group, self.me], 0, group, other).start()

    def join(self, group, kept, forward):
        self.all_of(0, group).wait_recv()
        total = jnp.zeros((SLAB, BLK), F32)
        for part in range(PARTS) if forward else range(PARTS - 1, -1, -1):
            self.joined[group, part] = total.astype(BF16)
            total = kept[part : part + 1, :] * total + self.gathered[group, part].astype(F32)
        self.incoming[group, self.me] = self.joined[group, self.me]
        for other in self.others():
            self.copy(self.joined.at[group, other], self.incoming.at[group, self.me], 1, group, other).start()

    def finish(self, group):
        self.all_of(1, group).wait_recv()
        self.all_of(0, group).wait_send()
        self.all_of(1, group).wait_send()
        return self.incoming[group].reshape(STATE, BLK)


def exchange_scratch():
    return [pltpu.VMEM((STEPS, PARTS, SLAB, BLK), BF16) for _ in range(4)] + [pltpu.SemaphoreType.DMA((4, STEPS))]


def first_rows(kept_ref):
    return jnp.concatenate([kept_ref[part, 0:1, :] for part in range(PARTS)], axis=0)


def joined_plainly(states, kept, place, forward):
    factors = jnp.repeat(kept[:, 0, :HEADS], HDIM, axis=1)[:, None, :]
    total = jnp.zeros(states.shape[1:], F32)
    result = total
    count = states.shape[0]
    for part in range(count) if forward else range(count - 1, -1, -1):
        result = jnp.where(place == part, total, result)
        total = factors[part] * total + states[part].astype(F32)
    return result.astype(BF16)


def front_kernel(
    x_ref, bc_ref, dtraw_ref, halo_ref, halo_bc_ref, taps_ref, taps_bc_ref, heads_ref, seg_ref, row_ref, shard_ref,
    xs_ref, y_ref, state_ref, b_ref, c_ref, dt_ref, run_ref, in_ref, keep_ref, whole_ref,
    ext, scores, run_t, b_t, enter, leave, *parts,
):
    step = pl.program_id(0)
    length = x_ref.shape[0]
    chunks = length // Q
    if parts:
        exchange = Exchange(*parts[:5])
        own_keep, keeps, keep_sends, keep_arrivals, gathered, loads, sends, arrivals, stores = parts[5:]
        gather = Gather(
            lambda k, s, start, size: gathered.at[k, s, pl.ds(pl.multiple_of(start, size), size)],
            gathered.shape[2],
            loads,
            sends,
            arrivals,
        )

        def store(k):
            columns = pl.ds(pl.multiple_of(k * WIDE, WIDE), WIDE)
            return pltpu.make_async_copy(gathered.at[k], whole_ref.at[:, :, columns], stores.at[k])


        def keep_copy(hop):
            return pltpu.make_async_remote_copy(
                src_ref=own_keep,
                dst_ref=keeps.at[exchange.me],
                send_sem=keep_sends.at[hop],
                recv_sem=keep_arrivals.at[hop],
                device_id={"ctx": lax.rem(exchange.me + hop + 1, PARTS)},
                device_id_type=pl.DeviceIdType.MESH,
            )

    @pl.when(step == 0)
    def _():
        ext[0:PAD, :] = halo_bc_ref[...]
        ext[PAD:, :] = bc_ref[...].astype(F32)
        lane = iota((Q, 128), 1)
        lower = (iota((Q, Q), 1) <= iota((Q, Q), 0)).astype(F32)
        offset = jnp.zeros((1, 128), F32)
        for k in range(chunks):
            rows = slice(k * Q, (k + 1) * Q)
            total = conv_rows(ext, seg_ref, taps_bc_ref, k * Q, Q)
            active = total * sigmoid(total)
            b_rows, c_rows = active[:, :STATE], active[:, STATE:].astype(BF16)
            b_t[:, rows] = b_rows.T.astype(BF16)
            b_rows = b_rows.astype(BF16)
            b_ref[rows, :] = b_rows
            c_ref[rows, :] = c_rows
            scores[rows, :] = masked_scores(seg_ref, row_ref, b_rows, c_rows, k)
            raw = jnp.where(lane < HEADS, dtraw_ref[rows, :128].astype(F32), 0.0) + heads_ref[0:1, :]
            dt = jnp.maximum(raw, 0.0) + jnp.log1p(jnp.exp(-jnp.abs(raw)))
            log_decay = -dt * jnp.exp(heads_ref[1:2, :])
            running = jnp.dot(lower, log_decay, precision=HIGHEST, preferred_element_type=F32)
            dt_ref[rows, :] = dt
            run_ref[rows, :] = running
            run_t[k] = running.T
            carry, tail = chunk_flags(seg_ref, k)
            enter[rows, :] = jnp.exp(running) * carry
            leave[rows, :] = jnp.exp(running[Q - 1 : Q, :] - running) * tail
            same = (seg_ref[PAD + k * Q : PAD + (k + 1) * Q, :] == seg_ref[PAD - 1 : PAD, :]).astype(F32)
            whole = jnp.exp(running + offset) * same
            in_ref[rows, :] = whole
            offset = offset + running[Q - 1 : Q, :]
        keep = jnp.broadcast_to(whole[Q - 1 : Q, :], (8, 128))
        if parts:
            own_keep[...] = keep
            keeps[exchange.me] = keep
            exchange.greet(gather.peers["core"], gather.peers["y"])
            for hop in range(PARTS - 1):
                keep_copy(hop).start()
            for k in range(D // WIDE):
                gather.load(k, shard_ref.at[:, k * WIDE : (k + 1) * WIDE]).start()
            for k in range(D // WIDE):
                gather.begin(k)
        else:
            keep_ref[0] = keep

    @pl.when(step < STEPS)
    def _():
        state = local_scan(
            step, x_ref, halo_ref, taps_ref, seg_ref, xs_ref, y_ref, c_ref, dt_ref, run_ref,
            ext, scores, run_t, b_t, enter, leave,
        )
        if parts:
            exchange.spread(step, state)
        else:
            state_ref[...] = state.astype(BF16)

    if parts:

        @pl.when(step == JOIN)
        def _():
            for hop in range(PARTS - 1):
                keep_copy(hop).wait()
            keep_ref[...] = keeps[...]

        @pl.when((step >= JOIN) & (step < STEPS + JOIN))
        def _():
            group = step - JOIN
            exchange.join(group, widen(first_rows(keeps), chosen(group)), True)

        @pl.when(step >= DONE)
        def _():
            state_ref[...] = exchange.finish(step - DONE)

        def complete(k):
            gather.complete(k)
            store(k).start()

        def drain(k):
            gather.drain(k)
            store(k).wait()

        for lag, advance in enumerate((gather.first, gather.second, gather.third, complete, drain)):
            k = step - 2 - 2 * lag

            @pl.when((k >= 0) & (k < D // WIDE))
            def _():
                advance(k)


def local_scan(
    step, x_ref, halo_ref, taps_ref, seg_ref, xs_ref, y_ref, c_ref, dt_ref, run_ref,
    ext, scores, run_t, b_t, enter, leave,
):
    chunks = x_ref.shape[0] // Q
    ext[0:PAD, :] = halo_ref[...]
    ext[PAD:, :] = x_ref[...].astype(F32)
    select = chosen(step)
    state = jnp.zeros((STATE, BLK), F32)
    for k in range(chunks):
        rows = slice(k * Q, (k + 1) * Q)
        total = conv_rows(ext, seg_ref, taps_ref, k * Q, Q)
        values = total * sigmoid(total)
        xs_ref[rows, :] = values.astype(BF16)
        scaled = (values * widen(dt_ref[rows, :], select)).astype(BF16)
        entering = widen(enter[rows, :], select)
        running = pltpu.roll(run_ref[rows, :], lax.rem(128 - step * GROUP, 128), 1)
        parts = []
        for pair in range(2):
            mixing = []
            for one in range(2):
                head = 2 * pair + one
                gap = running[:, head : head + 1] - run_t[k, pl.ds(step * GROUP + head, 1), :]
                mixing.append((jnp.exp(jnp.minimum(gap, 0.0)) * scores[rows, :]).astype(BF16))
            parts.append(
                dot(jnp.concatenate(mixing, axis=1), halves(scaled[:, pair * 128 : (pair + 1) * 128]))
            )
        inside = jnp.concatenate(parts, axis=1)
        y_ref[rows, :] = (inside + entering * dot(c_ref[rows, :], state.astype(BF16))).astype(BF16)
        weighted = (scaled.astype(F32) * widen(leave[rows, :], select)).astype(BF16)
        state = entering[Q - 1 : Q, :] * state + dot(b_t[:, rows], weighted)
    return state


def front(projected, halo, taps, heads, seg_lanes, seg_row, out_matrix, exchanging):
    length = projected.shape[0]
    last = STEPS - 1
    keeps = PARTS if exchanging else 1
    whole = lambda *shape: pl.BlockSpec(shape, lambda j: (0,) * len(shape))
    columns = lambda rows, at: pl.BlockSpec((rows, BLK), at)
    return pl.pallas_call(
        front_kernel,
        grid=(STEPS + DONE * exchanging,),
        in_specs=[
            columns(length, lambda j: (0, STEPS + jnp.minimum(j, last))),
            columns(length, lambda j: (0, 2 * STEPS)),
            columns(length, lambda j: (0, 2 * STEPS + 1)),
            columns(PAD, lambda j: (0, STEPS + jnp.minimum(j, last))),
            columns(PAD, lambda j: (0, 2 * STEPS)),
            columns(8, lambda j: (0, jnp.minimum(j, last))),
            columns(8, lambda j: (0, STEPS)),
            whole(8, 128),
            whole(length + 2 * PAD, 128),
            whole(8, length),
            pl.BlockSpec(memory_space=pl.ANY),
        ],
        out_specs=[
            columns(length, lambda j: (0, jnp.minimum(j, last))),
            columns(length, lambda j: (0, jnp.minimum(j, last))),
            columns(STATE, lambda j: (0, jnp.maximum(j - DONE * exchanging, 0))),
            whole(length, 128),
            whole(length, 128),
            whole(length, 128),
            whole(length, 128),
            whole(length, 128),
            whole(keeps, 8, 128),
            pl.BlockSpec(memory_space=pl.ANY),
        ],
        out_shape=[
            jax.ShapeDtypeStruct((length, INNER), BF16),
            jax.ShapeDtypeStruct((length, INNER), BF16),
            jax.ShapeDtypeStruct((STATE, INNER), BF16),
            jax.ShapeDtypeStruct((length, 128), BF16),
            jax.ShapeDtypeStruct((length, 128), BF16),
            jax.ShapeDtypeStruct((length, 128), F32),
            jax.ShapeDtypeStruct((length, 128), F32),
            jax.ShapeDtypeStruct((length, 128), F32),
            jax.ShapeDtypeStruct((keeps, 8, 128), F32),
            jax.ShapeDtypeStruct((4, *out_matrix.shape), BF16),
        ],
        scratch_shapes=[
            pltpu.VMEM((length + PAD, BLK), F32),
            pltpu.VMEM((length, Q), F32),
            pltpu.VMEM((length // Q, 128, Q), F32),
            pltpu.VMEM((128, length), BF16),
            pltpu.VMEM((length, 128), F32),
            pltpu.VMEM((length, 128), F32),
        ]
        + (
            exchange_scratch()
            + [
                pltpu.VMEM((8, 128), F32),
                pltpu.VMEM((PARTS, 8, 128), F32),
                pltpu.SemaphoreType.DMA((PARTS - 1,)),
                pltpu.SemaphoreType.DMA((PARTS - 1,)),
                pltpu.VMEM((D // WIDE, 4, 2 * SHARD, WIDE), BF16),
                *gather_sems(D // WIDE),
                pltpu.SemaphoreType.DMA((D // WIDE,)),
            ]
        )
        * exchanging,
        compiler_params=communicating(1, exchanging),
        cost_estimate=pl.CostEstimate(
            flops=6 * 10**9, bytes_accessed=16 * 10**6, transcendentals=10**7
        ),
        name="front",
    )(projected, projected, projected, halo, halo, taps, taps, heads, seg_lanes, seg_row, out_matrix)


def tail_kernel(
    y_ref, xs_ref, gate_ref, incoming_ref, kept_ref, out_ref, c_ref, in_ref, heads_ref, gain_ref, g_ref, units_ref,
    mixer_ref, dproj_ref, dy_ref, dsin_ref, sums_ref, block_ref, stats_ref,
    full, dmix, squares, products, mixed, c_t, *parts,
):
    step = pl.program_id(0)
    length = y_ref.shape[0]
    group = jnp.where(step < STEPS, step, jnp.minimum(step - STEPS, STEPS - 1))
    select = chosen(group)
    half = length // 2
    if parts:
        exchange = Exchange(*parts)

        @pl.when(step == 0)
        def _():
            exchange.greet()

    @pl.when(step == 0)
    def _():
        squares[...] = jnp.zeros_like(squares)
        products[...] = jnp.zeros_like(products)
        for k in range(length // Q):
            rows = slice(k * Q, (k + 1) * Q)
            c_t[:, rows] = c_ref[rows, :].astype(F32).T.astype(BF16)

    @pl.when(step < STEPS)
    def _():
        incoming = incoming_ref[...]
        skip = widen(heads_ref[...], select)[2:3, :]
        for k in range(2):
            rows = slice(k * half, (k + 1) * half)
            y = y_ref[rows, :].astype(F32)
            y = y + widen(in_ref[rows, :], select) * dot(c_ref[rows, :], incoming)
            y = y + skip * xs_ref[rows, :].astype(F32)
            full[step, rows, :] = y
            gate = gate_ref[rows, :].astype(F32)
            gated = y * gate * sigmoid(gate)
            d_mixer = dot_nt(g_ref[rows, :], out_ref[...])
            dmix[step, rows, :] = d_mixer
            square = gated * gated
            product = gated * d_mixer * gain_ref[0:1, :]
            squares[rows, :] += square[:, :128] + square[:, 128:]
            products[rows, :] += product[:, :128] + product[:, 128:]

    @pl.when(step == STEPS)
    def _():
        norm = lax.rsqrt(jnp.sum(squares[...], axis=1, keepdims=True) * (1.0 / INNER) + epsilon)
        mean = norm * jnp.sum(products[...], axis=1, keepdims=True) * (1.0 / INNER)
        squares[...] = jnp.broadcast_to(norm, squares.shape)
        products[...] = jnp.broadcast_to(mean, products.shape)

    @pl.when((step >= STEPS) & (step < 2 * STEPS))
    def _():
        gain = gain_ref[0:1, :]
        d_gain = jnp.zeros((1, BLK), F32)
        d_skip = jnp.zeros((1, BLK), F32)
        d_state = jnp.zeros((STATE, BLK), F32)
        for k in range(2):
            rows = slice(k * half, (k + 1) * half)
            norm, mean = both(squares[rows, :]), both(products[rows, :])
            y = full[group, rows, :]
            d_mixer = dmix[group, rows, :]
            gate = gate_ref[rows, :].astype(F32)
            sig = sigmoid(gate)
            silu = gate * sig
            unit = y * silu * norm
            low = (unit * gain).astype(BF16)
            mixer_ref[:, rows] = (unit * gain).T.astype(BF16)
            part = dot(low, out_ref[...])

            @pl.when(step == STEPS)
            def _():
                mixed[rows, :] = part

            @pl.when(step > STEPS)
            def _():
                mixed[rows, :] += part

            d_gain = d_gain + jnp.sum(d_mixer * unit, axis=0, keepdims=True)
            d_gated = norm * (d_mixer * gain - unit * mean)
            dproj_ref[rows, :] = (d_gated * y * (sig * (1.0 + gate * (1.0 - sig)))).astype(BF16)
            dy = (d_gated * silu).astype(BF16)
            dy_ref[rows, :] = dy
            dy = dy.astype(F32)
            d_skip = d_skip + jnp.sum(dy * xs_ref[rows, :].astype(F32), axis=0, keepdims=True)
            d_state = d_state + dot(c_t[:, rows], (dy * widen(in_ref[rows, :], select)).astype(BF16))
        if parts:
            exchange.spread(group, d_state)
        else:
            dsin_ref[...] = d_state.astype(BF16)
        sums_ref[...] = jnp.concatenate([d_gain, d_skip, jnp.zeros((6, BLK), F32)], axis=0)

    @pl.when(step == 2 * STEPS - 1)
    def _():
        total = units_ref[...].astype(F32) + mixed[...]
        block_ref[...] = total.astype(BF16)
        first = jnp.sum(total * total, axis=0, keepdims=True)
        second = jnp.sum(mixed[...] * mixed[...], axis=0, keepdims=True)
        stats_ref[...] = jnp.concatenate([first, second, jnp.zeros((6, D), F32)], axis=0)

    if parts:
        at = step - STEPS

        @pl.when((at >= JOIN) & (at < STEPS + JOIN))
        def _():
            done = at - JOIN
            exchange.join(done, widen(first_rows(kept_ref), chosen(done)), False)

        @pl.when(at >= DONE)
        def _():
            dsin_ref[...] = exchange.finish(at - DONE)


def tail(y, xs, projected, incoming, kept, out_whole, c_rows, entering, heads, gain, cot, units, exchanging):
    length = y.shape[0]
    group = lambda i: jnp.where(i < STEPS, i, jnp.minimum(i - STEPS, STEPS - 1))
    second = lambda i: jnp.clip(i - STEPS, 0, STEPS - 1)
    early = lambda rows: pl.BlockSpec((rows, BLK), lambda i: (0, jnp.minimum(i, STEPS - 1)))
    late = lambda rows: pl.BlockSpec((rows, BLK), lambda i: (0, second(i)))
    each = lambda rows: pl.BlockSpec((rows, BLK), lambda i: (0, group(i)))
    whole = lambda *shape: pl.BlockSpec(shape, lambda i: (0,) * len(shape))
    return pl.pallas_call(
        tail_kernel,
        grid=(2 * STEPS + DONE * exchanging,),
        in_specs=[
            early(length),
            each(length),
            each(length),
            early(STATE),
            whole(*kept.shape),
            pl.BlockSpec((BLK, D), lambda i: (group(i), 0)),
            whole(length, 128),
            whole(length, 128),
            whole(8, 128),
            each(8),
            whole(length, D),
            whole(length, D),
        ],
        out_specs=[
            pl.BlockSpec((BLK, length), lambda i: (second(i), 0)),
            late(length),
            late(length),
            pl.BlockSpec((STATE, BLK), lambda i: (0, second(i - DONE * exchanging))),
            late(8),
            whole(length, D),
            whole(8, D),
        ],
        out_shape=[
            jax.ShapeDtypeStruct((INNER, length), BF16),
            jax.ShapeDtypeStruct((length, WIDTH), BF16),
            jax.ShapeDtypeStruct((length, INNER), BF16),
            jax.ShapeDtypeStruct((STATE, INNER), BF16),
            jax.ShapeDtypeStruct((8, INNER), F32),
            jax.ShapeDtypeStruct((length, D), BF16),
            jax.ShapeDtypeStruct((8, D), F32),
        ],
        scratch_shapes=[
            pltpu.VMEM((STEPS, length, BLK), F32),
            pltpu.VMEM((STEPS, length, BLK), F32),
            pltpu.VMEM((length, 128), F32),
            pltpu.VMEM((length, 128), F32),
            pltpu.VMEM((length, D), F32),
            pltpu.VMEM((128, length), BF16),
        ]
        + exchange_scratch() * exchanging,
        compiler_params=communicating(2, exchanging),
        cost_estimate=pl.CostEstimate(
            flops=12 * 10**9, bytes_accessed=50 * 10**6, transcendentals=4 * 10**6
        ),
        name="tail",
    )(y, xs, projected, incoming, kept, out_whole, c_rows, entering, heads, gain, cot, units)


def back_steps(step, given, scratch, write, write_halo, write_taps, write_heads):
    (
        x_ref, dtraw_ref, halo_ref, taps_ref, heads_ref, seg_ref, row_ref, b_ref, c_ref, dt_ref, run_ref, dy_ref, sin_ref, dout_ref,
    ) = given
    (
        ext, pre, dact, dbuf, scores, dscores, run_t, b_t, c_t, enter, leave, d_b, d_c, suffix, prefix, d_dt, fixed, states,
    ) = scratch
    length = x_ref.shape[0]
    chunks = length // Q

    @pl.when(step == 0)
    def _():
        for k in range(chunks):
            rows = slice(k * Q, (k + 1) * Q)
            b_rows, c_rows = b_ref[rows, :], c_ref[rows, :]
            b_t[:, rows] = b_rows.astype(F32).T.astype(BF16)
            c_t[:, rows] = c_rows.astype(F32).T.astype(BF16)
            scores[rows, :] = masked_scores(seg_ref, row_ref, b_rows, c_rows, k)
            running = run_ref[rows, :]
            run_t[k] = running.T
            carry, tail = chunk_flags(seg_ref, k)
            enter[rows, :] = jnp.exp(running) * carry
            leave[rows, :] = jnp.exp(running[Q - 1 : Q, :] - running) * tail
        for each in (dscores, d_b, d_c, suffix, prefix, d_dt, fixed):
            each[...] = jnp.zeros_like(each)
        dbuf[0:PAD, :] = jnp.zeros((PAD, BLK), F32)
        dbuf[PAD + length :, :] = jnp.zeros((PAD, BLK), F32)

    @pl.when(step <= STEPS)
    def _():
        ext[0:PAD, :] = halo_ref[...]
        ext[PAD:, :] = x_ref[...].astype(F32)
        for k in range(chunks):
            pre[k * Q : (k + 1) * Q, :] = conv_rows(ext, seg_ref, taps_ref, k * Q, Q)

    @pl.when(step < STEPS)
    def _():
        select = chosen(step)
        gather = chosen_back(step)
        skip = widen(heads_ref[...], select)[2:3, :]
        state = sin_ref[...].astype(F32)
        for k in range(chunks):
            rows = slice(k * Q, (k + 1) * Q)
            states[k] = state
            if k + 1 < chunks:
                total = pre[rows, :]
                scaled = total * sigmoid(total) * widen(dt_ref[rows, :], select)
                weighted = (scaled.astype(BF16).astype(F32) * widen(leave[rows, :], select)).astype(BF16)
                last = widen(enter[rows.stop - 8 : rows.stop, :], select)[7:8, :]
                state = last * state + dot(b_t[:, rows], weighted)
        d_state = dout_ref[...].astype(F32)
        for k in range(chunks - 1, -1, -1):
            rows = slice(k * Q, (k + 1) * Q)
            total = pre[rows, :]
            values = total * sigmoid(total)
            step_size = widen(dt_ref[rows, :], select)
            entering = widen(enter[rows, :], select)
            leaving = widen(leave[rows, :], select)
            scaled = (values * step_size).astype(BF16)
            scaled_wide = scaled.astype(F32)
            dy = dy_ref[rows, :]
            dy_wide = dy.astype(F32)
            before = states[k]
            before_low = before.astype(BF16)
            d_low = d_state.astype(BF16)
            running = pltpu.roll(run_ref[rows, :], lax.rem(128 - step * GROUP, 128), 1)
            insides, backs = [], []
            d_score = dscores[rows, :]
            for pair in range(2):
                lanes = slice(pair * 128, (pair + 1) * 128)
                mixing, turned, decays = [], [], []
                for one in range(2):
                    head = 2 * pair + one
                    gap = running[:, head : head + 1] - run_t[k, pl.ds(step * GROUP + head, 1), :]
                    decay = jnp.exp(jnp.minimum(gap, 0.0))
                    mixed = decay * scores[rows, :]
                    decays.append(decay)
                    mixing.append(mixed.astype(BF16))
                    turned.append(mixed.T.astype(BF16))
                spread = halves(scaled[:, lanes])
                insides.append(dot(jnp.concatenate(mixing, axis=1), spread))
                backs.append(dot(jnp.concatenate(turned, axis=1), halves(dy[:, lanes])))
                products = dot_nt(dy[:, lanes], spread)
                d_score = d_score + decays[0] * products[:, :Q] + decays[1] * products[:, Q:]
            dscores[rows, :] = d_score
            inside = jnp.concatenate(insides, axis=1) + entering * dot(c_ref[rows, :], before_low)
            back_inside = jnp.concatenate(backs, axis=1)
            back_state = leaving * dot(b_ref[rows, :], d_low)
            high, low = in_two(dy_wide * inside - scaled_wide * back_inside)
            suffix[rows, :] += dot(high, gather) + dot(low, gather)
            prefix[rows, :] += dot((scaled_wide * back_state).astype(BF16), gather)
            back = back_inside + back_state
            d_dt[rows, :] += dot((values * back).astype(BF16), gather)
            entered = (dy_wide * entering).astype(BF16)
            d_c[rows, :] += dot_nt(entered, before_low)
            d_b[rows, :] += dot_nt((scaled_wide * leaving).astype(BF16), d_low)
            kept = entering[Q - 1 : Q, :]
            through = jnp.sum(before * d_state, axis=0, keepdims=True) * kept
            high, low = in_two(jnp.broadcast_to(through, (8, BLK)))
            fixed[k * 8 : (k + 1) * 8, :] += dot(high, gather) + dot(low, gather)
            d_state = kept * d_state + dot(c_t[:, rows], entered)
            dact[rows, :] = back * step_size + skip * dy_wide

    @pl.when(step == STEPS)
    def _():
        for k in range(chunks):
            rows = slice(k * Q, (k + 1) * Q)
            own = seg_ref[PAD + k * Q : PAD + (k + 1) * Q, :]
            keep = (own == row_ref[0:1, rows]) & (iota((Q, Q), 1) <= iota((Q, Q), 0))
            d_score = jnp.where(keep, dscores[rows, :], 0.0)
            dact[rows, STATE:] = d_c[rows, :] + dot(d_score.astype(BF16), b_ref[rows, :])
            dact[rows, :STATE] = d_b[rows, :] + dot(d_score.T.astype(BF16), c_ref[rows, :])

    @pl.when(step <= STEPS)
    def _():
        sums = [jnp.zeros((1, BLK), F32) for _ in range(CONV + 1)]
        for k in range(chunks):
            rows = slice(k * Q, (k + 1) * Q)
            total = pre[rows, :]
            sig = sigmoid(total)
            d_conv = dact[rows, :] * (sig * (1.0 + total * (1.0 - sig)))
            dbuf[PAD + k * Q : PAD + (k + 1) * Q, :] = d_conv
            sums[4] = sums[4] + jnp.sum(d_conv, axis=0, keepdims=True)
            own = seg_ref[PAD + k * Q : PAD + (k + 1) * Q, :]
            for shift in range(CONV):
                at = PAD + k * Q - shift
                term = d_conv * ext[at : at + Q, :]
                if shift:
                    term = jnp.where(both(seg_ref[at : at + Q, :] == own), term, 0.0)
                sums[3 - shift] = sums[3 - shift] + jnp.sum(term, axis=0, keepdims=True)
        write_taps(jnp.concatenate(sums + [jnp.zeros((3, BLK), F32)], axis=0))

        def returned(at, rows):
            own = seg_ref[at : at + rows, :]
            result = taps_ref[3:4, :] * dbuf[at : at + rows, :]
            for shift in range(1, CONV):
                same = both(seg_ref[at + shift : at + shift + rows, :] == own)
                result = result + jnp.where(
                    same, taps_ref[3 - shift : 4 - shift, :] * dbuf[at + shift : at + shift + rows, :], 0.0
                )
            return result

        write_halo(returned(0, PAD))
        for k in range(chunks):
            write(slice(k * Q, (k + 1) * Q), returned(PAD + k * Q, Q).astype(BF16))

    @pl.when(step == STEPS + 1)
    def _():
        lower = (iota((Q, Q), 1) < iota((Q, Q), 0)).astype(F32)
        upper = (iota((Q, Q), 1) >= iota((Q, Q), 0)).astype(F32)
        lane = iota((Q, 128), 1)
        rate = jnp.exp(heads_ref[1:2, :])
        bias_sum = jnp.zeros((1, 128), F32)
        decay_sum = jnp.zeros((1, 128), F32)
        for k in range(chunks):
            rows = slice(k * Q, (k + 1) * Q)
            d_log = jnp.dot(upper, suffix[rows, :], precision=HIGHEST, preferred_element_type=F32)
            d_log = d_log + jnp.dot(lower, prefix[rows, :], precision=HIGHEST, preferred_element_type=F32)
            d_log = d_log + fixed[k * 8 : k * 8 + 1, :]
            raw = jnp.where(lane < HEADS, dtraw_ref[rows, :128].astype(F32), 0.0) + heads_ref[0:1, :]
            d_raw = jnp.where(lane < HEADS, (d_dt[rows, :] - rate * d_log) * sigmoid(raw), 0.0)
            bias_sum = bias_sum + jnp.sum(d_raw, axis=0, keepdims=True)
            decay_sum = decay_sum - jnp.sum(d_log * dt_ref[rows, :] * rate, axis=0, keepdims=True)
            write(rows, jnp.concatenate([d_raw, jnp.zeros_like(d_raw)], axis=1).astype(BF16))
        write_heads(jnp.concatenate([bias_sum, decay_sum, jnp.zeros((6, 128), F32)], axis=0))


def back_kernel(*refs):
    given, (_, dproj_ref, dhalo_ref, dtaps_ref, dheads_ref), scratch = refs[:14], refs[14:19], refs[19:]

    def write(rows, value):
        dproj_ref[rows, :] = value

    def write_halo(value):
        dhalo_ref[...] = value

    def write_taps(value):
        dtaps_ref[...] = value

    def write_heads(value):
        dheads_ref[...] = value

    back_steps(pl.program_id(0), given, scratch, write, write_halo, write_taps, write_heads)


def back_scratch(length):
    return [
        pltpu.VMEM((length + PAD, BLK), F32),
        pltpu.VMEM((length, BLK), F32),
        pltpu.VMEM((length, BLK), F32),
        pltpu.VMEM((length + 2 * PAD, BLK), F32),
        pltpu.VMEM((length, Q), F32),
        pltpu.VMEM((length, Q), F32),
        pltpu.VMEM((length // Q, 128, Q), F32),
        pltpu.VMEM((128, length), BF16),
        pltpu.VMEM((128, length), BF16),
        *[pltpu.VMEM((length, 128), F32) for _ in range(7)],
        pltpu.VMEM((8 * (length // Q), 128), F32),
        pltpu.VMEM((length // Q, STATE, BLK), F32),
    ]


def back_inputs(length):
    whole = lambda *shape: pl.BlockSpec(shape, lambda j: (0,) * len(shape))
    upto = lambda last, first=0: lambda j: (0, first + jnp.minimum(j, last))
    return [
        pl.BlockSpec((length, BLK), upto(STEPS, STEPS)),
        pl.BlockSpec((length, BLK), lambda j: (0, 2 * STEPS + 1)),
        pl.BlockSpec((PAD, BLK), upto(STEPS, STEPS)),
        pl.BlockSpec((8, BLK), upto(STEPS)),
        whole(8, 128),
        whole(length + 2 * PAD, 128),
        whole(8, length),
        whole(length, 128),
        whole(length, 128),
        whole(length, 128),
        whole(length, 128),
        pl.BlockSpec((length, BLK), upto(STEPS - 1)),
        pl.BlockSpec((STATE, BLK), upto(STEPS - 1)),
        pl.BlockSpec((STATE, BLK), upto(STEPS - 1)),
    ]


def back(given, dproj):
    length = dproj.shape[0]
    upto = lambda last, first=0: lambda j: (0, first + jnp.minimum(j, last))
    return pl.pallas_call(
        back_kernel,
        grid=(STEPS + 2,),
        in_specs=[*back_inputs(length), pl.BlockSpec(memory_space=pl.ANY)],
        out_specs=[
            pl.BlockSpec((length, BLK), lambda j: (0, STEPS + j)),
            pl.BlockSpec((PAD, BLK), upto(STEPS)),
            pl.BlockSpec((8, BLK), upto(STEPS)),
            pl.BlockSpec((8, 128), lambda j: (0, 0)),
        ],
        out_shape=[
            jax.ShapeDtypeStruct((length, WIDTH), BF16),
            jax.ShapeDtypeStruct((PAD, XBC), F32),
            jax.ShapeDtypeStruct((8, XBC), F32),
            jax.ShapeDtypeStruct((8, 128), F32),
        ],
        scratch_shapes=back_scratch(length),
        input_output_aliases={14: 0},
        compiler_params=pltpu.CompilerParams(vmem_limit_bytes=VMEM_LIMIT),
        name="back",
    )(*given, dproj)


OUT_CHUNKS = 2 * D // WIDE
GATE_CHUNKS = INNER // WIDE
IN_CHUNKS = WIDTH // WIDE
CHUNKS = OUT_CHUNKS + IN_CHUNKS
LAGS = 8
RING = 8


def small_sums(taps, columns, input_gain, heads, stats):
    fill = lambda width: jnp.zeros((1, width), F32)
    squares = [jnp.broadcast_to(jnp.sum(stats[i : i + 1], axis=1, keepdims=True), (1, 128)) for i in range(2)]
    return jnp.concatenate(
        [
            taps[:5],
            jnp.concatenate([columns[0:1], fill(XBC - INNER)], axis=1),
            jnp.concatenate([columns[1:2], fill(XBC - INNER)], axis=1),
            jnp.concatenate([input_gain, heads[0:1], heads[1:2], *squares, fill(XBC - D - 512)], axis=1),
        ],
        axis=0,
    )


def finish_kernel(*refs):
    given, refs = refs[:14], refs[14:]
    lhs_in, lhs_out, gate_ref, weight_ref, cot_ref, units_ref, gain_ref, columns_ref, stats_ref = refs[:9]
    din_ref, dout_ref, input_grad_ref, total_ref = refs[9:13]
    scratch, refs = refs[13:31], refs[31:]
    grads, edges, halos, taps, heads, d_normed = refs[:6]
    own, core_send, core_recv, y_recv, x_recv, z_recv, w_recv, final, small_send, small_recv = refs[6:16]
    send_sems, recv_sems, small_send_sems, small_recv_sems, edge_sends, edge_arrivals = refs[16:]
    step = pl.program_id(0)
    length = cot_ref.shape[0]
    shard, part = lax.axis_index("fsdp"), lax.axis_index("ctx")
    core, y = lax.rem(shard, 2), shard // 2
    x, z = lax.rem(part, 2), part // 2
    near, far = lax.rem(z, 2), z // 2
    peers = (
        {"fsdp": flipped(shard, 1)},
        {"fsdp": flipped(shard, 2)},
        {"ctx": flipped(part, 1)},
        {"ctx": flipped(part, 2)},
        {"ctx": flipped(part, 4)},
    )
    preceding, outer = lax.rem(part + PARTS - 1, PARTS), lax.rem(part + PARTS - 1 + 2 * lax.rem(part, 2), PARTS)

    def remote(source, target, send, arrival, peer):
        return pltpu.make_async_remote_copy(
            src_ref=source,
            dst_ref=target,
            send_sem=send,
            recv_sem=arrival,
            device_id=peer,
            device_id_type=pl.DeviceIdType.MESH,
        )

    def ring(k):
        return lax.rem(k, RING)

    def sent(stage, k, source, target, peer):
        return remote(source, target, send_sems.at[stage, k], recv_sems.at[stage, k], peers[peer])

    copies = (
        lambda k: sent(0, k, core_send.at[lax.rem(k, 2)], core_recv.at[ring(k)], 0),
        lambda k: sent(1, k, core_recv.at[ring(k), 1 - y], y_recv.at[ring(k)], 1),
        lambda k: sent(2, k, y_recv.at[ring(k), 1 - x], x_recv.at[ring(k)], 2),
        lambda k: sent(3, k, x_recv.at[ring(k), 1 - near], z_recv.at[ring(k)], 3),
        lambda k: sent(4, k, z_recv.at[ring(k), 1 - far], w_recv.at[ring(k)], 4),
        lambda k: sent(5, k, final.at[ring(k), x, near, far], final.at[ring(k), x, near, far], 4),
        lambda k: sent(6, k, final.at[ring(k), x, near], final.at[ring(k), x, near], 3),
        lambda k: sent(7, k, final.at[ring(k), x], final.at[ring(k), x], 2),
    )
    arrivals = copies[:5] + (
        lambda k: sent(5, k, final.at[ring(k), x, near, 1 - far], final.at[ring(k), x, near, 1 - far], 4),
        lambda k: sent(6, k, final.at[ring(k), x, 1 - near], final.at[ring(k), x, 1 - near], 3),
        lambda k: sent(7, k, final.at[ring(k), 1 - x], final.at[ring(k), 1 - x], 2),
    )

    def small_copy(stage):
        return remote(
            small_send.at[stage], small_recv.at[stage], small_send_sems.at[stage], small_recv_sems.at[stage], peers[stage]
        )

    def edge_copy(block):
        return remote(
            edges.at[block], halos.at[block], edge_sends.at[block], edge_arrivals.at[block], {"ctx": preceding}
        )

    @pl.when(step == 0)
    def _():
        barrier = pltpu.get_barrier_semaphore()
        greeted = [*peers, {"ctx": outer}]
        for peer in greeted:
            pl.semaphore_signal(barrier, inc=1, device_id=peer, device_id_type=pl.DeviceIdType.MESH)
        pl.semaphore_wait(barrier, len(greeted))
        d_normed[...] = jnp.zeros_like(d_normed)

    def partial(lhs_of, rhs):
        for row in range(2):
            value = dot(lhs_of(2 * row + 1 - core), rhs).astype(BF16)
            core_send[lax.rem(step, 2), row] = value.reshape(2, 2, 2, PIECE, WIDE)
        copies[0](step).start()
        for row in range(2):
            own[row] = dot(lhs_of(2 * row + core), rhs).reshape(2, 2, 2, PIECE, WIDE)

    def in_chunk(rhs):
        partial(lambda s: lhs_in[s], rhs)
        d_normed[...] += dot(rhs, weight_ref[...])

    @pl.when(step < OUT_CHUNKS)
    def _():
        columns = lax.rem(step, D // WIDE) * WIDE
        rhs = cot_ref[:, pl.ds(pl.multiple_of(columns, WIDE), WIDE)]
        partial(lambda s: lhs_out[s, step // (D // WIDE)], rhs)

    @pl.when((step >= OUT_CHUNKS) & (step < OUT_CHUNKS + GATE_CHUNKS))
    def _():
        in_chunk(gate_ref[...])

    @pl.when((step >= OUT_CHUNKS + GATE_CHUNKS) & (step < CHUNKS))
    def _():
        first = 2 * (step - OUT_CHUNKS - GATE_CHUNKS)
        for block in (first, first + 1):

            @pl.when(block <= STEPS)
            def _():
                edge_copy(block).wait()
                tail = slice(length - 16, length)
                more = jnp.where(part == PARTS - 1, 0.0, halos[block])
                more = jnp.concatenate([jnp.zeros_like(more), more], axis=0)
                grads[block, tail, :] = (grads[block, tail, :].astype(F32) + more).astype(BF16)

        in_chunk(jnp.concatenate([grads[first], grads[first + 1]], axis=1))

    def write(rows, value):
        grads[step, rows, :] = value

    def write_halo(value):
        edges[step] = value
        edge_copy(step).start()

    def write_taps(value):
        taps[step] = value

    def write_heads(value):
        heads[...] = value

    back_steps(step, given, scratch, write, write_halo, write_taps, write_heads)

    @pl.when(step < CHUNKS)
    def _():
        arrivals[0](step).wait_recv()
        for row in (1 - y, y):
            core_recv[ring(step), row] = (own[row] + core_recv[ring(step), row].astype(F32)).astype(BF16)
        copies[1](step).start()

    def stage(lag):
        def decorate(body):
            k = step - lag

            @pl.when((k >= 0) & (k < CHUNKS))
            def _():
                body(k, ring(k))

        return decorate

    def summed(a, b):
        return (a.astype(F32) + b.astype(F32)).astype(BF16)

    @stage(1)
    def _(k, at):
        arrivals[1](k).wait_recv()
        y_recv[at] = summed(y_recv[at], core_recv[at, y])
        copies[2](k).start()
        copies[0](k).wait_send()

    @stage(2)
    def _(k, at):
        arrivals[2](k).wait_recv()
        x_recv[at] = summed(x_recv[at], y_recv[at, x])
        copies[3](k).start()

    @stage(3)
    def _(k, at):
        arrivals[3](k).wait_recv()
        z_recv[at] = summed(z_recv[at], x_recv[at, near])
        copies[4](k).start()
        copies[1](k).wait_send()

    @stage(4)
    def _(k, at):
        arrivals[4](k).wait_recv()
        final[at, x, near, far] = summed(w_recv[at], z_recv[at, far])
        copies[5](k).start()
        copies[2](k).wait_send()

    @stage(5)
    def _(k, at):
        arrivals[5](k).wait_recv()
        copies[6](k).start()
        copies[3](k).wait_send()

    @stage(6)
    def _(k, at):
        arrivals[6](k).wait_recv()
        copies[7](k).start()
        copies[4](k).wait_send()

    @stage(7)
    def _(k, at):
        arrivals[7](k).wait_recv()
        for one in (5, 6, 7):
            copies[one](k).wait_send()
        whole = final[at].reshape(SHARD, WIDE)

        @pl.when(k < OUT_CHUNKS)
        def _():
            dout_ref[...] = whole

        @pl.when(k >= OUT_CHUNKS)
        def _():
            din_ref[...] = whole.astype(F32).T.astype(BF16)

    @pl.when(step == CHUNKS)
    def _():
        input_gain = jnp.zeros((1, D), F32)
        for k in range(length // Q):
            rows = slice(k * Q, (k + 1) * Q)
            units = units_ref[rows, :].astype(F32)
            norm = lax.rsqrt(jnp.sum(units * units, axis=1, keepdims=True) * (1.0 / D) + epsilon)
            base = units * norm
            grad = d_normed[rows, :]
            input_gain = input_gain + jnp.sum(grad * base, axis=0, keepdims=True)
            scaled = grad * gain_ref[0:1, :]
            mean = jnp.sum(scaled * base, axis=1, keepdims=True) * (1.0 / D)
            input_grad_ref[rows, :] = (cot_ref[rows, :].astype(F32) + norm * (scaled - base * mean)).astype(BF16)
        whole = jnp.concatenate([taps[block] for block in range(STEPS + 1)], axis=1)
        small_send[0] = small_sums(whole, columns_ref[...], input_gain, heads[...], stats_ref[...])
        small_copy(0).start()

    for stage_of_small in range(5):

        @pl.when(step == CHUNKS + 1 + stage_of_small)
        def _():
            small_copy(stage_of_small).wait()
            total = small_send[stage_of_small] + small_recv[stage_of_small]
            if stage_of_small < 4:
                small_send[stage_of_small + 1] = total
                small_copy(stage_of_small + 1).start()
            else:
                total_ref[...] = total


def finish(given, normed_t, mixer_t, dproj, w_turned, cot, units, input_gain, column_sums, stats):
    length = cot.shape[0]
    per_half = D // WIDE
    once = pl.Buffered(1)
    whole = lambda *shape: pl.BlockSpec(shape, lambda t: (0,) * len(shape), pipeline_mode=once)
    in_chunk = lambda t: jnp.clip(t - OUT_CHUNKS, 0, IN_CHUNKS - 1)

    def out_block(t):
        k = jnp.clip(t - LAGS + 1, 0, OUT_CHUNKS - 1)
        return (k // per_half, lax.rem(k, per_half))

    slots = lambda *shape: pltpu.VMEM((RING, *shape, PIECE, WIDE), BF16)
    return pl.pallas_call(
        finish_kernel,
        grid=(CHUNKS + LAGS - 1,),
        in_specs=[
            *back_inputs(length),
            whole(4, SHARD, length),
            whole(4, 2, SHARD, length),
            pl.BlockSpec((length, WIDE), lambda t: (0, jnp.minimum(in_chunk(t), GATE_CHUNKS - 1))),
            pl.BlockSpec((WIDE, D), lambda t: (in_chunk(t), 0)),
            whole(length, D),
            whole(length, D),
            whole(1, D),
            whole(8, INNER),
            whole(8, D),
        ],
        out_specs=[
            pl.BlockSpec((WIDE, SHARD), lambda t: (in_chunk(t - LAGS + 1), 0)),
            pl.BlockSpec((SHARD, WIDE), out_block),
            pl.BlockSpec((length, D), lambda t: (0, 0)),
            pl.BlockSpec((8, XBC), lambda t: (0, 0)),
        ],
        out_shape=[
            jax.ShapeDtypeStruct((PROJ, SHARD), BF16),
            jax.ShapeDtypeStruct((2 * SHARD, D), BF16),
            jax.ShapeDtypeStruct((length, D), BF16),
            jax.ShapeDtypeStruct((8, XBC), F32),
        ],
        scratch_shapes=[
            *back_scratch(length),
            pltpu.VMEM((STEPS + 2, length, BLK), BF16),
            pltpu.VMEM((STEPS + 1, PAD, BLK), F32),
            pltpu.VMEM((STEPS + 1, PAD, BLK), F32),
            pltpu.VMEM((STEPS + 1, 8, BLK), F32),
            pltpu.VMEM((8, 128), F32),
            pltpu.VMEM((length, D), F32),
            pltpu.VMEM((2, 2, 2, 2, PIECE, WIDE), F32),
            pltpu.VMEM((2, 2, 2, 2, 2, PIECE, WIDE), BF16),
            slots(2, 2, 2, 2),
            slots(2, 2, 2),
            slots(2, 2),
            slots(2),
            slots(),
            slots(2, 2, 2),
            pltpu.VMEM((5, 8, XBC), F32),
            pltpu.VMEM((5, 8, XBC), F32),
            pltpu.SemaphoreType.DMA((8, CHUNKS)),
            pltpu.SemaphoreType.DMA((8, CHUNKS)),
            pltpu.SemaphoreType.DMA((5,)),
            pltpu.SemaphoreType.DMA((5,)),
            pltpu.SemaphoreType.DMA((STEPS + 1,)),
            pltpu.SemaphoreType.DMA((STEPS + 1,)),
        ],
        compiler_params=communicating(0, True),
        name="finish",
    )(*given, normed_t, mixer_t, dproj, w_turned, cot, units, input_gain, column_sums, stats)


def passed_along(block, axis, distance):
    devices = range(lax.axis_size(axis))
    route = [(i - distance, i) for i in devices if i - distance in devices]
    return lax.ppermute(block, axis, route)


def pack_small(conv_taps, conv_bias, dt_bias, decay_log, skip_scale, mixer_gain, input_gain):
    width = conv_bias.shape[0]

    def line(*parts):
        flat = jnp.concatenate(parts)
        return jnp.pad(flat, (0, width - flat.shape[0]))[None]

    rows = jnp.concatenate(
        [
            conv_taps.T,
            conv_bias[None],
            line(mixer_gain),
            line(input_gain),
            line(dt_bias, decay_log, skip_scale),
        ],
        axis=0,
    )
    return jnp.pad(rows.astype(F32), ((0, 0), (0, SMALL_WIDTH - width)))


def unpack_small(whole, width):
    shards = whole.shape[0]
    joined = jnp.swapaxes(whole, 0, 1)
    taps = jnp.pad(joined[:5, :, :width].reshape(5, shards * width).astype(F32), ((0, 3), (0, 0)))
    gain = joined[5, :, : INNER // shards].reshape(1, INNER).astype(F32)
    input_gain = joined[6, :, : D // shards].reshape(1, D).astype(F32)
    own = HEADS // shards
    heads = joined[7, :, : 3 * own].reshape(shards, 3, own).swapaxes(0, 1).reshape(3, HEADS)
    heads = jnp.pad(heads.astype(F32), ((0, 5), (0, 128 - HEADS)))
    return taps, jnp.pad(gain, ((0, 7), (0, 0))), input_gain, heads


def on_device(
    inputs,
    segment_ids,
    out_grad,
    in_matrix,
    out_matrix,
    conv_taps,
    conv_bias,
    dt_bias,
    decay_log,
    skip_scale,
    mixer_gain,
    input_gain,
):
    shards, parts = lax.axis_size("fsdp"), lax.axis_size("ctx")
    place = lax.axis_index("ctx")
    units_low, cot = inputs[0], out_grad[0]
    seg_ids = segment_ids[0]
    length = units_low.shape[0]
    here = (shards, parts) == (4, PARTS)
    small = pack_small(conv_taps, conv_bias, dt_bias, decay_log, skip_scale, mixer_gain, input_gain)
    if here:
        w_turned, projected, normed_t, smalls, halo, seg_before = project(in_matrix, units_low, small, seg_ids)
        rim_seg = seg_before.reshape(length)[length - CONV + 1 :]
        taps, gain, g_float, heads = unpack_small(smalls, conv_bias.shape[0])
    else:
        units = units_low.astype(F32)
        inv_rms = lax.rsqrt(jnp.mean(units * units, axis=-1, keepdims=True) + epsilon)
        base_rows = units * inv_rms
        w_whole = jnp.pad(in_matrix, ((0, 0), (0, WIDTH - PROJ)))
        w_whole = lax.all_gather(w_whole, "fsdp", axis=0, tiled=True)
        rim_seg = passed_along(seg_ids[length - CONV + 1 :], "ctx", 1)
        taps, gain, g_float, heads = unpack_small(lax.all_gather(small, "fsdp"), conv_bias.shape[0])
        normed = (base_rows * g_float).astype(BF16)
        normed_t = normed.T
        projected = dot(normed, w_whole).astype(BF16)
        rim_rows = passed_along(projected[length - CONV + 1 :], "ctx", 1)
        halo = jnp.pad(rim_rows, ((PAD - CONV + 1, 0), (0, 0))).astype(F32)
    seg_ext = jnp.concatenate(
        [
            jnp.full((PAD - CONV + 1,), -1, jnp.int32),
            rim_seg,
            seg_ids,
            jnp.full((PAD,), -2, jnp.int32),
        ]
    )
    seg_lanes = jnp.broadcast_to(seg_ext[:, None], (length + 2 * PAD, 128))
    seg_row = jnp.broadcast_to(seg_ids[None], (8, length))

    xs, y_local, incoming, b_rows, c_rows, dt, running, entering, kept, out_whole = front(
        projected, halo, taps, heads, seg_lanes, seg_row, out_matrix, here
    )
    out_whole = out_whole.reshape(-1, D)
    if not here:
        out_whole = lax.all_gather(out_matrix, "fsdp", axis=0, tiled=True)
        kept = lax.all_gather(kept[0], "ctx")
        incoming = joined_plainly(lax.all_gather(incoming, "ctx"), kept, place, True)
    mixer_t, dproj, dy, outgoing, column_sums, block_out, stats = tail(
        y_local, xs, projected, incoming, kept, out_whole, c_rows, entering, heads, gain, cot, units_low, here
    )
    if not here:
        outgoing = joined_plainly(lax.all_gather(outgoing, "ctx"), kept, place, False)
    given = (
        projected, projected, halo, taps, heads, seg_lanes, seg_row, b_rows, c_rows, dt, running, dy, incoming, outgoing,
    )
    if here:
        d_in, d_out, input_grad, total = finish(
            given, normed_t, mixer_t.reshape(4, 2, SHARD, length), dproj, w_turned, cot, units_low, g_float, column_sums, stats
        )
        d_in, d_out = d_in.T.astype(F32), d_out.astype(F32)
    else:
        dproj, d_halo, d_taps, d_heads = back(given, dproj)
        returned = passed_along(d_halo.astype(BF16), "ctx", -1)
        last = lax.slice(dproj, (length - PAD, INNER), (length, INNER + XBC))
        last = (last.astype(F32) + returned.astype(F32)).astype(BF16)
        dproj = lax.dynamic_update_slice(dproj, last, (length - PAD, INNER))
        d_normed = dot_nt(dproj, w_whole)
        d_input_gain = jnp.sum(d_normed * base_rows, axis=0)
        d_base = d_normed * g_float
        d_units = inv_rms * (d_base - base_rows * jnp.mean(d_base * base_rows, axis=-1, keepdims=True))
        input_grad = (cot.astype(F32) + d_units).astype(BF16)

        def scattered(grad):
            return lax.psum_scatter(grad.astype(BF16), "fsdp", scatter_dimension=0, tiled=True)

        d_in = jnp.dot(normed_t, dproj, preferred_element_type=F32)[:, :PROJ]
        d_out = jnp.dot(mixer_t, cot, preferred_element_type=F32)
        d_in = lax.psum(scattered(d_in), "ctx").astype(F32)
        d_out = lax.psum(scattered(d_out), "ctx").astype(F32)
        total = lax.psum(small_sums(d_taps, column_sums, d_input_gain[None], d_heads, stats), ("fsdp", "ctx"))
    me = lax.axis_index("fsdp")

    def own(flat):
        size = flat.shape[-1] // shards
        return lax.dynamic_slice_in_dim(flat, me * size, size, flat.ndim - 1)

    skip_sums = jnp.sum(total[6, :INNER].reshape(HEADS, HDIM), axis=1)
    at = D + 256
    stat_sums = jnp.stack([total[7, at], total[7, at + 128]])
    rms_stats = jnp.sqrt(stat_sums / (length * shards * parts * D))
    return (
        block_out[None],
        input_grad[None],
        d_in,
        d_out,
        own(total[:4]).T,
        own(total[4]),
        own(total[7, D : D + HEADS]),
        own(total[7, D + 128 : D + 128 + HEADS]),
        own(skip_sums),
        own(total[5, :INNER]),
        own(total[7, :D]),
        rms_stats,
    )


def solution(mesh):
    return jax.shard_map(
        on_device,
        mesh=mesh,
        in_specs=(
            P("fsdp", "ctx", None),
            P("fsdp", "ctx"),
            P("fsdp", "ctx", None),
            P("fsdp", None),
            P("fsdp", None),
            P("fsdp", None),
            P("fsdp"),
            P("fsdp"),
            P("fsdp"),
            P("fsdp"),
            P("fsdp"),
            P("fsdp"),
        ),
        out_specs=(
            P("fsdp", "ctx", None),
            P("fsdp", "ctx", None),
            P("fsdp", None),
            P("fsdp", None),
            P("fsdp", None),
            P("fsdp"),
            P("fsdp"),
            P("fsdp"),
            P("fsdp"),
            P("fsdp"),
            P("fsdp"),
            P(),
        ),
        check_vma=False,
    )
```

```python
import functools

import jax
import jax.numpy as jnp
from jax import lax
from jax.experimental import pallas as pl
from jax.experimental.pallas import tpu as pltpu
from jax.sharding import PartitionSpec as P

D = 1536
HEADS = 48
HDIM = 64
STATE = 128
CONV = 4
INNER = 3072
XBC = 3328
PROJ = 6448
WIDTH = 6656

BLK = 256
GROUP = BLK // HDIM
STEPS = INNER // BLK
Q = 128
PAD = 8
WIDE = 512
SHARD = D // 4
PIECE = SHARD // 8
SMALL_WIDTH = 896
AHEAD = 2

epsilon = 1e-05
F32, BF16 = jnp.float32, jnp.bfloat16
HIGHEST = lax.Precision.HIGHEST
VMEM_LIMIT = 60 * 1024 * 1024


def communicating(number):
    return pltpu.CompilerParams(
        vmem_limit_bytes=VMEM_LIMIT, collective_id=number, has_side_effects=True
    )


def dot(a, b):
    return jnp.dot(a, b, preferred_element_type=F32)


def dot_nt(a, b):
    return lax.dot_general(a, b, (((1,), (1,)), ((), ())), preferred_element_type=F32)


def iota(shape, dim):
    return lax.broadcasted_iota(jnp.int32, shape, dim)


def sigmoid(v):
    return 1.0 / (1.0 + jnp.exp(-v))


def in_two(a):
    high = a.astype(BF16)
    return high, (a - high.astype(F32)).astype(BF16)


def chosen(step):
    columns = step * GROUP + lax.shift_right_logical(iota((128, BLK), 1), 6)
    return (iota((128, BLK), 0) == columns).astype(BF16)


def chosen_back(step):
    heads = step * GROUP + lax.shift_right_logical(iota((BLK, 128), 0), 6)
    return (iota((BLK, 128), 1) == heads).astype(BF16)


def widen(per_head, select):
    high, low = in_two(per_head)
    return dot(high, select) + dot(low, select)


def halves(pair):
    first = iota(pair.shape, 1) < HDIM
    zero = jnp.zeros_like(pair)
    return jnp.concatenate([jnp.where(first, pair, zero), jnp.where(first, zero, pair)], axis=0)


def both(mask):
    return jnp.concatenate([mask, mask], axis=1)


def conv_rows(ext_ref, seg_ref, taps_ref, start, rows):
    own = seg_ref[start + PAD : start + PAD + rows, :]
    total = taps_ref[4:5, :] + taps_ref[3:4, :] * ext_ref[start + PAD : start + PAD + rows, :]
    for back in range(1, CONV):
        at = start + PAD - back
        same = both(seg_ref[at : at + rows, :] == own)
        total = total + jnp.where(
            same, taps_ref[3 - back : 4 - back, :] * ext_ref[at : at + rows, :], 0.0
        )
    return total


def chunk_flags(seg_ref, k):
    own = seg_ref[PAD + k * Q : PAD + (k + 1) * Q, :]
    before = seg_ref[PAD + k * Q - 1 : PAD + k * Q, :]
    last = seg_ref[PAD + (k + 1) * Q - 1 : PAD + (k + 1) * Q, :]
    return (own == before).astype(F32), (own == last).astype(F32)


def masked_scores(seg_ref, row_ref, b_rows, c_rows, k):
    own = seg_ref[PAD + k * Q : PAD + (k + 1) * Q, :]
    row = row_ref[0:1, k * Q : (k + 1) * Q]
    keep = (own == row) & (iota((Q, Q), 1) <= iota((Q, Q), 0))
    return jnp.where(keep, dot_nt(c_rows, b_rows), 0.0)


def remote(source, target, send, arrival, peer):
    return pltpu.make_async_remote_copy(
        src_ref=source,
        dst_ref=target,
        send_sem=send,
        recv_sem=arrival,
        device_id=peer,
        device_id_type=pl.DeviceIdType.MESH,
    )


def flipped(index, bit):
    return index + bit - 2 * bit * lax.rem(index // bit, 2)


class Gather:
    def __init__(self, locate, rows, loads, sends, arrivals):
        self.locate, self.rows = locate, rows
        self.loads, self.sends, self.arrivals = loads, sends, arrivals
        shard, part = lax.axis_index("fsdp"), lax.axis_index("ctx")
        self.own, self.other = shard, flipped(shard, 2)
        self.sibling, self.opposite = flipped(shard, 1), flipped(flipped(shard, 2), 1)
        x, near = lax.rem(part, 2), lax.rem(part // 2, 2)
        self.mine, self.over_x, self.over_z = 2 * x + near, 2 * (1 - x) + near, 2 * x + 1 - near
        self.across = 2 * (1 - x) + 1 - near
        self.peers = {
            "core": {"fsdp": flipped(shard, 1)},
            "y": {"fsdp": flipped(shard, 2)},
            "x": {"ctx": flipped(part, 1)},
            "z": {"ctx": flipped(part, 2)},
        }

    def whole(self, shard, k):
        return self.locate(k, shard, 0, self.rows)

    def quarter(self, shard, k, which):
        return self.locate(k, shard, which * (self.rows // 4), self.rows // 4)

    def half(self, shard, k, which, second):
        return self.locate(k, shard, (2 * which + second) * (self.rows // 8), self.rows // 8)

    def copy(self, place, kind, k, peer):
        return pltpu.make_async_remote_copy(
            src_ref=place,
            dst_ref=place,
            send_sem=self.sends.at[kind, k],
            recv_sem=self.arrivals.at[kind, k],
            device_id=self.peers[peer],
            device_id_type=pl.DeviceIdType.MESH,
        )

    def outgoing(self, kind, k):
        own, other = self.own, self.other
        if kind == 0:
            return self.copy(self.whole(own, k), kind, k, "core")
        if kind == 1:
            return self.copy(self.quarter(own, k, self.mine), kind, k, "y")
        if kind == 2:
            return self.copy(self.quarter(other, k, self.mine), kind, k, "x")
        if kind == 3:
            return self.copy(self.quarter(other, k, self.mine), kind, k, "z")
        if kind == 4:
            return self.copy(self.half(other, k, self.over_x, 0), kind, k, "z")
        if kind == 5:
            return self.copy(self.half(other, k, self.over_z, 1), kind, k, "x")
        which = (self.mine, self.over_x, self.over_z, self.across)[kind - 6]
        return self.copy(self.quarter(other, k, which), kind, k, "core")

    def arrived(self, kind, k):
        other, opposite = self.other, self.opposite
        if kind == 0:
            place = self.whole(self.sibling, k)
        elif kind < 4:
            place = self.quarter(other, k, (self.mine, self.over_x, self.over_z)[kind - 1])
        elif kind < 6:
            place = self.half(other, k, self.across, kind - 4)
        else:
            place = self.quarter(opposite, k, (self.mine, self.over_x, self.over_z, self.across)[kind - 6])
        self.copy(place, kind, k, "core").wait_recv()

    def load(self, k, source):
        return pltpu.make_async_copy(source, self.whole(self.own, k), self.loads.at[k])

    def begin(self, k):
        self.load(k, self.whole(self.own, k)).wait()
        self.outgoing(1, k).start()
        self.outgoing(0, k).start()

    def first(self, k):
        self.arrived(1, k)
        for kind in (2, 3, 6):
            self.outgoing(kind, k).start()

    def second(self, k):
        self.arrived(2, k)
        self.outgoing(4, k).start()
        self.outgoing(7, k).start()
        self.arrived(3, k)
        self.outgoing(5, k).start()
        self.outgoing(8, k).start()

    def third(self, k):
        self.arrived(4, k)
        self.arrived(5, k)
        self.outgoing(9, k).start()

    def complete(self, k):
        for kind in (0, 6, 7, 8, 9):
            self.arrived(kind, k)

    def drain(self, k):
        for kind in range(10):
            self.outgoing(kind, k).wait_send()


def gather_sems(chunks):
    return [
        pltpu.SemaphoreType.DMA((chunks,)),
        pltpu.SemaphoreType.DMA((10, chunks)),
        pltpu.SemaphoreType.DMA((10, chunks)),
    ]


PARTS = 8
SLAB = STATE // PARTS
JOIN, DONE = 2, 4


class Exchange:
    def __init__(self, held, gathered, joined, incoming, sems):
        self.held, self.gathered, self.joined, self.incoming, self.sems = held, gathered, joined, incoming, sems
        self.me = lax.axis_index("ctx")

    def others(self):
        return [lax.rem(self.me + hop, PARTS) for hop in range(1, PARTS)]

    def greet(self, *further):
        barrier = pltpu.get_barrier_semaphore()
        peers = [{"ctx": other} for other in self.others()] + list(further)
        for peer in peers:
            pl.semaphore_signal(barrier, inc=1, device_id=peer, device_id_type=pl.DeviceIdType.MESH)
        pl.semaphore_wait(barrier, len(peers))

    def copy(self, source, target, kind, group, other):
        return pltpu.make_async_remote_copy(
            src_ref=source,
            dst_ref=target,
            send_sem=self.sems.at[2 * kind, group],
            recv_sem=self.sems.at[2 * kind + 1, group],
            device_id={"ctx": other},
            device_id_type=pl.DeviceIdType.MESH,
        )

    def all_of(self, kind, group):
        source, target = ((self.held, self.gathered), (self.joined, self.incoming))[kind]
        some = pl.ds(0, PARTS - 1)
        return self.copy(source.at[group, some], target.at[group, some], kind, group, self.others()[0])

    def spread(self, group, state):
        self.held[group] = state.astype(BF16).reshape(PARTS, SLAB, BLK)
        self.gathered[group, self.me] = self.held[group, self.me]
        for other in self.others():
            self.copy(self.held.at[group, other], self.gathered.at[group, self.me], 0, group, other).start()

    def join(self, group, kept, forward):
        self.all_of(0, group).wait_recv()
        total = jnp.zeros((SLAB, BLK), F32)
        for part in range(PARTS) if forward else range(PARTS - 1, -1, -1):
            self.joined[group, part] = total.astype(BF16)
            total = kept[part : part + 1, :] * total + self.gathered[group, part].astype(F32)
        self.incoming[group, self.me] = self.joined[group, self.me]
        for other in self.others():
            self.copy(self.joined.at[group, other], self.incoming.at[group, self.me], 1, group, other).start()

    def finish(self, group):
        self.all_of(1, group).wait_recv()
        self.all_of(0, group).wait_send()
        self.all_of(1, group).wait_send()
        return self.incoming[group].reshape(STATE, BLK)


def exchange_scratch():
    return [pltpu.VMEM((STEPS, PARTS, SLAB, BLK), BF16) for _ in range(4)] + [pltpu.SemaphoreType.DMA((4, STEPS))]


def first_rows(kept_ref):
    return jnp.concatenate([kept_ref[part, 0:1, :] for part in range(PARTS)], axis=0)


def joined_plainly(states, kept, place, forward):
    factors = jnp.repeat(kept[:, 0, :HEADS], HDIM, axis=1)[:, None, :]
    total = jnp.zeros(states.shape[1:], F32)
    result = total
    count = states.shape[0]
    for part in range(count) if forward else range(count - 1, -1, -1):
        result = jnp.where(place == part, total, result)
        total = factors[part] * total + states[part].astype(F32)
    return result.astype(BF16)


def prepare(
    bc_ref, dt_raw, halo_bc_ref, taps_bc_ref, heads_ref, seg_ref, row_ref, b_ref, c_ref, dt_ref, run_ref, in_ref,
    ext, scores, run_t, b_t, enter, leave,
):
    chunks = bc_ref.shape[0] // Q
    ext[0:PAD, :] = halo_bc_ref[...]
    ext[PAD:, :] = bc_ref[...].astype(F32)
    lane = iota((Q, 128), 1)
    lower = (iota((Q, Q), 1) <= iota((Q, Q), 0)).astype(F32)
    offset = jnp.zeros((1, 128), F32)
    for k in range(chunks):
        rows = slice(k * Q, (k + 1) * Q)
        total = conv_rows(ext, seg_ref, taps_bc_ref, k * Q, Q)
        active = total * sigmoid(total)
        b_rows, c_rows = active[:, :STATE], active[:, STATE:].astype(BF16)
        b_t[:, rows] = b_rows.T.astype(BF16)
        b_rows = b_rows.astype(BF16)
        b_ref[rows, :] = b_rows
        c_ref[rows, :] = c_rows
        scores[rows, :] = masked_scores(seg_ref, row_ref, b_rows, c_rows, k)
        raw = jnp.where(lane < HEADS, dt_raw(rows).astype(F32), 0.0) + heads_ref[0:1, :]
        dt = jnp.maximum(raw, 0.0) + jnp.log1p(jnp.exp(-jnp.abs(raw)))
        log_decay = -dt * jnp.exp(heads_ref[1:2, :])
        running = jnp.dot(lower, log_decay, precision=HIGHEST, preferred_element_type=F32)
        dt_ref[rows, :] = dt
        run_ref[rows, :] = running
        run_t[k] = running.T
        carry, tail = chunk_flags(seg_ref, k)
        enter[rows, :] = jnp.exp(running) * carry
        leave[rows, :] = jnp.exp(running[Q - 1 : Q, :] - running) * tail
        same = (seg_ref[PAD + k * Q : PAD + (k + 1) * Q, :] == seg_ref[PAD - 1 : PAD, :]).astype(F32)
        whole = jnp.exp(running + offset) * same
        in_ref[rows, :] = whole
        offset = offset + running[Q - 1 : Q, :]
    return jnp.broadcast_to(whole[Q - 1 : Q, :], (8, 128))


def front_kernel(
    x_ref, bc_ref, dtraw_ref, halo_ref, halo_bc_ref, taps_ref, taps_bc_ref, heads_ref, seg_ref, row_ref,
    xs_ref, y_ref, state_ref, b_ref, c_ref, dt_ref, run_ref, in_ref, keep_ref,
    ext, scores, run_t, b_t, enter, leave,
):
    step = pl.program_id(0)

    @pl.when(step == 0)
    def _():
        keep_ref[...] = prepare(
            bc_ref, lambda rows: dtraw_ref[rows, :128], halo_bc_ref, taps_bc_ref, heads_ref, seg_ref, row_ref,
            b_ref, c_ref, dt_ref, run_ref, in_ref, ext, scores, run_t, b_t, enter, leave,
        )

    state = local_scan(
        step, x_ref, halo_ref, taps_ref, seg_ref, xs_ref, y_ref, c_ref, dt_ref, run_ref,
        ext, scores, run_t, b_t, enter, leave,
    )
    state_ref[...] = state.astype(BF16)


def local_scan(
    step, x_ref, halo_ref, taps_ref, seg_ref, xs_ref, y_ref, c_ref, dt_ref, run_ref,
    ext, scores, run_t, b_t, enter, leave,
):
    chunks = x_ref.shape[0] // Q
    ext[0:PAD, :] = halo_ref[...]
    ext[PAD:, :] = x_ref[...].astype(F32)
    select = chosen(step)
    state = jnp.zeros((STATE, BLK), F32)
    for k in range(chunks):
        rows = slice(k * Q, (k + 1) * Q)
        total = conv_rows(ext, seg_ref, taps_ref, k * Q, Q)
        values = total * sigmoid(total)
        xs_ref[rows, :] = values.astype(BF16)
        scaled = (values * widen(dt_ref[rows, :], select)).astype(BF16)
        entering = widen(enter[rows, :], select)
        running = pltpu.roll(run_ref[rows, :], lax.rem(128 - step * GROUP, 128), 1)
        parts = []
        for pair in range(2):
            mixing = []
            for one in range(2):
                head = 2 * pair + one
                gap = running[:, head : head + 1] - run_t[k, pl.ds(step * GROUP + head, 1), :]
                mixing.append((jnp.exp(jnp.minimum(gap, 0.0)) * scores[rows, :]).astype(BF16))
            parts.append(
                dot(jnp.concatenate(mixing, axis=1), halves(scaled[:, pair * 128 : (pair + 1) * 128]))
            )
        inside = jnp.concatenate(parts, axis=1)
        y_ref[rows, :] = (inside + entering * dot(c_ref[rows, :], state.astype(BF16))).astype(BF16)
        weighted = (scaled.astype(F32) * widen(leave[rows, :], select)).astype(BF16)
        state = entering[Q - 1 : Q, :] * state + dot(b_t[:, rows], weighted)
    return state


def front_outputs(length, column, state_at):
    whole = lambda *shape: (pl.BlockSpec(shape, lambda j: (0, 0)), shape)
    columns = lambda rows, at: (pl.BlockSpec((rows, BLK), at), (rows, INNER))
    specs = [
        (columns(length, column), BF16),
        (columns(length, column), BF16),
        (columns(STATE, state_at), BF16),
        (whole(length, 128), BF16),
        (whole(length, 128), BF16),
        (whole(length, 128), F32),
        (whole(length, 128), F32),
        (whole(length, 128), F32),
    ]
    return [spec for (spec, _), _ in specs], [jax.ShapeDtypeStruct(shape, kind) for (_, shape), kind in specs]


def front_scratch(length):
    return [
        pltpu.VMEM((length + PAD, BLK), F32),
        pltpu.VMEM((length, Q), F32),
        pltpu.VMEM((length // Q, 128, Q), F32),
        pltpu.VMEM((128, length), BF16),
        pltpu.VMEM((length, 128), F32),
        pltpu.VMEM((length, 128), F32),
    ]


def front(projected, halo, taps, heads, seg_lanes, seg_row):
    length = projected.shape[0]
    whole = lambda *shape: pl.BlockSpec(shape, lambda j: (0,) * len(shape))
    columns = lambda rows, at: pl.BlockSpec((rows, BLK), at)
    out_specs, out_shape = front_outputs(length, lambda j: (0, j), lambda j: (0, j))
    return pl.pallas_call(
        front_kernel,
        grid=(STEPS,),
        in_specs=[
            columns(length, lambda j: (0, STEPS + j)),
            columns(length, lambda j: (0, 2 * STEPS)),
            columns(length, lambda j: (0, 2 * STEPS + 1)),
            columns(PAD, lambda j: (0, STEPS + j)),
            columns(PAD, lambda j: (0, 2 * STEPS)),
            columns(8, lambda j: (0, j)),
            columns(8, lambda j: (0, STEPS)),
            whole(8, 128),
            whole(length + 2 * PAD, 128),
            whole(8, length),
        ],
        out_specs=[*out_specs, whole(8, 128)],
        out_shape=[*out_shape, jax.ShapeDtypeStruct((8, 128), F32)],
        scratch_shapes=front_scratch(length),
        compiler_params=pltpu.CompilerParams(vmem_limit_bytes=VMEM_LIMIT),
        name="front",
    )(projected, projected, projected, halo, halo, taps, taps, heads, seg_lanes, seg_row)


ORDER = (2 * INNER // WIDE, *range(INNER // WIDE, 2 * INNER // WIDE), *range(INNER // WIDE))
MULTIPLY = 3
SCAN = MULTIPLY + 2
OUT_PIECES = D // WIDE
SLOTS = SCAN + STEPS + DONE


def chunk_at(position):
    half = INNER // WIDE
    return jnp.where(position == 0, 2 * half, jnp.where(position <= half, position - 1 + half, position - 1 - half))


def forward_kernel(*refs):
    main_ref, rest_ref, shard_ref, units_ref, small_ref, seg_own_ref, row_ref = refs[:7]
    xs_ref, y_ref, state_ref, b_ref, c_ref, dt_ref, run_ref, in_ref = refs[7:15]
    keep_ref, weight_ref, whole_ref, projected_ref, normed_t_ref = refs[15:20]
    halo_ref, taps_ref, heads_ref, gain_ref, input_gain_ref, seg_ref = refs[20:26]
    ext, scores, run_t, b_t, enter, leave = refs[26:32]
    exchange = Exchange(*refs[32:37])
    own_keep, keeps, keep_sends, keep_arrivals = refs[37:41]
    gathered, loads, sends, arrivals, stores = refs[41:46]
    out_gathered, out_loads, out_sends, out_arrivals, out_stores = refs[46:51]
    normed, blocks, taps, own_small, smalls, seg_tail, seg_head = refs[51:58]
    edges, halos, small_sends, small_arrivals, edge_sends, edge_arrivals = refs[58:]
    step = pl.program_id(0)
    length = units_ref.shape[0]
    shard, part = lax.axis_index("fsdp"), lax.axis_index("ctx")
    others = ({"fsdp": flipped(shard, 1)}, {"fsdp": flipped(shard, 2)}, {"fsdp": flipped(flipped(shard, 1), 2)})
    following = {"ctx": lax.rem(part + 1, PARTS)}

    def place_in(k, s, start, size):
        rows, columns = pl.multiple_of(start, size), pl.multiple_of(s * SHARD, SHARD)
        return gathered.at[k, pl.ds(rows, size), pl.ds(columns, SHARD)]

    def place_out(k, s, start, size):
        return out_gathered.at[k, s, pl.ds(pl.multiple_of(start, size), size)]

    gather = Gather(place_in, WIDE, loads, sends, arrivals)
    gather_out = Gather(place_out, 2 * SHARD, out_loads, out_sends, out_arrivals)

    def small_copy(hop):
        return remote(own_small, smalls.at[shard], small_sends.at[hop], small_arrivals.at[hop], others[hop])

    def seg_copy():
        return remote(seg_tail, seg_head, small_sends.at[3], small_arrivals.at[3], following)

    def edge_copy(k):
        return remote(edges.at[k], halos.at[k], edge_sends.at[k], edge_arrivals.at[k], following)

    def keep_copy(hop):
        peer = {"ctx": lax.rem(part + hop + 1, PARTS)}
        return remote(own_keep, keeps.at[part], keep_sends.at[hop], keep_arrivals.at[hop], peer)

    def store(k):
        rows = pl.ds(pl.multiple_of(chunk_at(k) * WIDE, WIDE), WIDE)
        return pltpu.make_async_copy(gathered.at[k], weight_ref.at[rows], stores.at[k])

    def store_out(k):
        columns = pl.ds(pl.multiple_of(k * WIDE, WIDE), WIDE)
        return pltpu.make_async_copy(out_gathered.at[k], whole_ref.at[:, :, columns], out_stores.at[k])

    @pl.when(step == 0)
    def _():
        for k, chunk in enumerate(ORDER):
            source = rest_ref if (chunk + 1) * WIDE > PROJ else main_ref.at[chunk * WIDE : (chunk + 1) * WIDE, :]
            gather.load(k, source).start()
        for k in range(OUT_PIECES):
            gather_out.load(k, shard_ref.at[:, k * WIDE : (k + 1) * WIDE]).start()
        own_small[...] = small_ref[...]
        smalls[shard] = small_ref[...]
        seg_tail[...] = seg_own_ref[length - PAD :, :]
        exchange.greet(*others)
        for hop in range(3):
            small_copy(hop).start()
        seg_copy().start()
        for k in range(AHEAD):
            gather.begin(k)
        for hop in range(3):
            small_copy(hop).wait()
        seg_copy().wait()
        seg_ref[0:PAD, :] = jnp.where(part == 0, -1, seg_head[...])
        seg_ref[PAD : PAD + length, :] = seg_own_ref[...]
        seg_ref[PAD + length :, :] = jnp.full((PAD, 128), -2, jnp.int32)
        gain = jnp.concatenate([smalls[s, 6:7, :SHARD] for s in range(4)], axis=1)
        input_gain_ref[...] = gain
        for k in range(length // Q):
            rows = slice(k * Q, (k + 1) * Q)
            units = units_ref[rows, :].astype(F32)
            norm = lax.rsqrt(jnp.sum(units * units, axis=1, keepdims=True) * (1.0 / D) + epsilon)
            normed[rows, :] = (units * norm * gain).astype(BF16)

    @pl.when(step == 1)
    def _():
        mixer_gain = jnp.concatenate([smalls[s, 5:6, : INNER // 4] for s in range(4)], axis=1)
        gain_ref[...] = jnp.broadcast_to(mixer_gain, (8, INNER))
        whole = jnp.zeros((8, XBC), F32)
        heads = jnp.zeros((8, 128), F32)
        row, lane = iota((8, 128), 0), iota((8, 128), 1)
        own = HEADS // 4
        for s in range(4):
            padded = jnp.concatenate([smalls[s], jnp.zeros((8, XBC - SMALL_WIDTH), F32)], axis=1)
            padded = jnp.where(iota((8, XBC), 1) < XBC // 4, padded, 0.0)
            whole = whole + (pltpu.roll(padded, s * (XBC // 4), 1) if s else padded)
            line = jnp.broadcast_to(smalls[s, 7:8, :128], (8, 128))
            inside = (lane >= s * own) & (lane < (s + 1) * own)
            for kind in range(3):
                shift = (s - kind) * own % 128
                moved = pltpu.roll(line, shift, 1) if shift else line
                heads = jnp.where(inside & (row == kind), moved, heads)
        taps_ref[...] = whole
        heads_ref[...] = heads
        for block in range(STEPS + 1):
            taps[block] = whole[:, block * BLK : (block + 1) * BLK]

    def stage(lag, count=len(ORDER)):
        def decorate(body):
            k = step - lag

            @pl.when((k >= 0) & (k < count))
            def _():
                body(k)

        return decorate

    stage(-AHEAD)(lambda k: pl.when(k >= AHEAD)(lambda: gather.begin(k)))
    stage(6, OUT_PIECES)(gather_out.begin)
    stage(0)(gather.first)
    stage(1)(gather.second)
    stage(2)(gather.third)
    stage(12, OUT_PIECES)(gather_out.first)
    stage(13, OUT_PIECES)(gather_out.second)
    stage(14, OUT_PIECES)(gather_out.third)

    @stage(MULTIPLY)
    def _(k):
        gather.complete(k)
        store(k).start()
        low = dot_nt(normed[...], gathered[k]).astype(BF16)
        projected_ref[...] = low
        edge = low[length - 16 :, :].astype(F32)[8:, :]
        for half in range(2):
            columns = slice(half * BLK, (half + 1) * BLK)
            blocks[2 * chunk_at(k) + half] = low[:, columns]
            edges[k, half] = edge[:, columns]
        edge_copy(k).start()

    @stage(MULTIPLY + 1)
    def _(k):
        edge_copy(k).wait()
        gather.drain(k)
        store(k).wait()
        for half in range(2):
            columns = slice(half * BLK, (half + 1) * BLK)
            halos[k, half] = jnp.where(part == 0, 0.0, halos[k, half])
            halo_ref[:, columns] = halos[k, half]

    @pl.when(step == SCAN - 1)
    def _():
        keep = prepare(
            blocks.at[2 * STEPS], lambda rows: blocks[2 * STEPS + 1, rows, :128], halos.at[0, 0], taps.at[STEPS], heads_ref,
            seg_ref, row_ref, b_ref, c_ref, dt_ref, run_ref, in_ref, ext, scores, run_t, b_t, enter, leave,
        )
        own_keep[...] = keep
        keeps[part] = keep
        for hop in range(PARTS - 1):
            keep_copy(hop).start()

    @stage(SCAN, STEPS)
    def _(j):
        state = local_scan(
            j, blocks.at[STEPS + j], halos.at[1 + j // 2, lax.rem(j, 2)], taps.at[j], seg_ref,
            xs_ref, y_ref, c_ref, dt_ref, run_ref, ext, scores, run_t, b_t, enter, leave,
        )
        exchange.spread(j, state)

    @pl.when(step == SCAN + JOIN)
    def _():
        for hop in range(PARTS - 1):
            keep_copy(hop).wait()
        keep_ref[...] = keeps[...]

    @stage(SCAN + JOIN, STEPS)
    def _(j):
        exchange.join(j, widen(first_rows(keeps), chosen(j)), True)

    @stage(SCAN + DONE, STEPS)
    def _(j):
        state_ref[...] = exchange.finish(j)

    @stage(16, OUT_PIECES)
    def _(k):
        gather_out.complete(k)
        store_out(k).start()

    @stage(18, OUT_PIECES)
    def _(k):
        gather_out.drain(k)
        store_out(k).wait()

    @pl.when(step == SLOTS - 1)
    def _():
        for s in range(4):
            columns = slice(s * SHARD, (s + 1) * SHARD)
            normed_t_ref[s] = normed[:, columns].astype(F32).T.astype(BF16)


def forward(in_matrix, out_matrix, units, small, seg_own, seg_row):
    length = units.shape[0]
    chunks = len(ORDER)
    turned = in_matrix.T
    rest = jnp.pad(turned[(chunks - 1) * WIDE :], ((0, WIDTH - PROJ), (0, 0)))
    whole = lambda *shape: pl.BlockSpec(shape, lambda t: (0,) * len(shape))
    once = lambda *shape: pl.BlockSpec(shape, lambda t: (0,) * len(shape), pipeline_mode=pl.Buffered(1))
    anywhere = pl.BlockSpec(memory_space=pl.ANY)
    chunk = lambda rows, lag: pl.BlockSpec((rows, WIDE), lambda t: (0, chunk_at(jnp.clip(t - lag, 0, chunks - 1))))
    group = lambda lag: lambda t: (0, jnp.clip(t - lag, 0, STEPS - 1))
    out_specs, out_shape = front_outputs(length, group(SCAN), group(SCAN + DONE))
    shape = jax.ShapeDtypeStruct
    return pl.pallas_call(
        forward_kernel,
        grid=(SLOTS,),
        in_specs=[
            anywhere,
            anywhere,
            anywhere,
            once(length, D),
            once(8, SMALL_WIDTH),
            once(length, 128),
            once(8, length),
        ],
        out_specs=[
            *out_specs,
            whole(PARTS, 8, 128),
            anywhere,
            anywhere,
            chunk(length, MULTIPLY),
            once(4, SHARD, length),
            chunk(PAD, MULTIPLY + 1),
            whole(8, XBC),
            whole(8, 128),
            whole(8, INNER),
            whole(1, D),
            whole(length + 2 * PAD, 128),
        ],
        out_shape=[
            *out_shape,
            shape((PARTS, 8, 128), F32),
            shape((WIDTH, D), BF16),
            shape((4, 2 * SHARD, D), BF16),
            shape((length, WIDTH), BF16),
            shape((4, SHARD, length), BF16),
            shape((PAD, WIDTH), F32),
            shape((8, XBC), F32),
            shape((8, 128), F32),
            shape((8, INNER), F32),
            shape((1, D), F32),
            shape((length + 2 * PAD, 128), jnp.int32),
        ],
        scratch_shapes=[
            *front_scratch(length),
            *exchange_scratch(),
            pltpu.VMEM((8, 128), F32),
            pltpu.VMEM((PARTS, 8, 128), F32),
            pltpu.SemaphoreType.DMA((PARTS - 1,)),
            pltpu.SemaphoreType.DMA((PARTS - 1,)),
            pltpu.VMEM((chunks, WIDE, D), BF16),
            *gather_sems(chunks),
            pltpu.SemaphoreType.DMA((chunks,)),
            pltpu.VMEM((OUT_PIECES, 4, 2 * SHARD, WIDE), BF16),
            *gather_sems(OUT_PIECES),
            pltpu.SemaphoreType.DMA((OUT_PIECES,)),
            pltpu.VMEM((length, D), BF16),
            pltpu.VMEM((2 * chunks, length, BLK), BF16),
            pltpu.VMEM((STEPS + 1, 8, BLK), F32),
            pltpu.VMEM((8, SMALL_WIDTH), F32),
            pltpu.VMEM((4, 8, SMALL_WIDTH), F32),
            pltpu.VMEM((PAD, 128), jnp.int32),
            pltpu.VMEM((PAD, 128), jnp.int32),
            pltpu.VMEM((chunks, 2, PAD, BLK), F32),
            pltpu.VMEM((chunks, 2, PAD, BLK), F32),
            pltpu.SemaphoreType.DMA((4,)),
            pltpu.SemaphoreType.DMA((4,)),
            pltpu.SemaphoreType.DMA((chunks,)),
            pltpu.SemaphoreType.DMA((chunks,)),
        ],
        compiler_params=communicating(1),
        name="forward",
    )(turned, rest, out_matrix, units, small, seg_own, seg_row)


def tail_kernel(
    y_ref, xs_ref, gate_ref, incoming_ref, out_ref, c_ref, in_ref, heads_ref, gain_ref, g_ref, units_ref,
    mixer_ref, dproj_ref, dy_ref, dsin_ref, sums_ref, block_ref, stats_ref,
    full, dmix, squares, products, mixed, c_t,
):
    step = pl.program_id(0)
    length = y_ref.shape[0]
    group = jnp.where(step < STEPS, step, jnp.minimum(step - STEPS, STEPS - 1))
    select = chosen(group)
    half = length // 2
    @pl.when(step == 0)
    def _():
        squares[...] = jnp.zeros_like(squares)
        products[...] = jnp.zeros_like(products)
        for k in range(length // Q):
            rows = slice(k * Q, (k + 1) * Q)
            c_t[:, rows] = c_ref[rows, :].astype(F32).T.astype(BF16)

    @pl.when(step < STEPS)
    def _():
        incoming = incoming_ref[...]
        skip = widen(heads_ref[...], select)[2:3, :]
        for k in range(2):
            rows = slice(k * half, (k + 1) * half)
            y = y_ref[rows, :].astype(F32)
            y = y + widen(in_ref[rows, :], select) * dot(c_ref[rows, :], incoming)
            y = y + skip * xs_ref[rows, :].astype(F32)
            full[step, rows, :] = y
            gate = gate_ref[rows, :].astype(F32)
            gated = y * gate * sigmoid(gate)
            d_mixer = dot_nt(g_ref[rows, :], out_ref[...])
            dmix[step, rows, :] = d_mixer
            square = gated * gated
            product = gated * d_mixer * gain_ref[0:1, :]
            squares[rows, :] += square[:, :128] + square[:, 128:]
            products[rows, :] += product[:, :128] + product[:, 128:]

    @pl.when(step == STEPS)
    def _():
        norm = lax.rsqrt(jnp.sum(squares[...], axis=1, keepdims=True) * (1.0 / INNER) + epsilon)
        mean = norm * jnp.sum(products[...], axis=1, keepdims=True) * (1.0 / INNER)
        squares[...] = jnp.broadcast_to(norm, squares.shape)
        products[...] = jnp.broadcast_to(mean, products.shape)

    @pl.when((step >= STEPS) & (step < 2 * STEPS))
    def _():
        gain = gain_ref[0:1, :]
        d_gain = jnp.zeros((1, BLK), F32)
        d_skip = jnp.zeros((1, BLK), F32)
        d_state = jnp.zeros((STATE, BLK), F32)
        for k in range(2):
            rows = slice(k * half, (k + 1) * half)
            norm, mean = both(squares[rows, :]), both(products[rows, :])
            y = full[group, rows, :]
            d_mixer = dmix[group, rows, :]
            gate = gate_ref[rows, :].astype(F32)
            sig = sigmoid(gate)
            silu = gate * sig
            unit = y * silu * norm
            low = (unit * gain).astype(BF16)
            mixer_ref[:, rows] = (unit * gain).T.astype(BF16)
            part = dot(low, out_ref[...])

            @pl.when(step == STEPS)
            def _():
                mixed[rows, :] = part

            @pl.when(step > STEPS)
            def _():
                mixed[rows, :] += part

            d_gain = d_gain + jnp.sum(d_mixer * unit, axis=0, keepdims=True)
            d_gated = norm * (d_mixer * gain - unit * mean)
            dproj_ref[rows, :] = (d_gated * y * (sig * (1.0 + gate * (1.0 - sig)))).astype(BF16)
            dy = (d_gated * silu).astype(BF16)
            dy_ref[rows, :] = dy
            dy = dy.astype(F32)
            d_skip = d_skip + jnp.sum(dy * xs_ref[rows, :].astype(F32), axis=0, keepdims=True)
            d_state = d_state + dot(c_t[:, rows], (dy * widen(in_ref[rows, :], select)).astype(BF16))
        dsin_ref[...] = d_state.astype(BF16)
        sums_ref[...] = jnp.concatenate([d_gain, d_skip, jnp.zeros((6, BLK), F32)], axis=0)

    @pl.when(step == 2 * STEPS - 1)
    def _():
        total = units_ref[...].astype(F32) + mixed[...]
        block_ref[...] = total.astype(BF16)
        first = jnp.sum(total * total, axis=0, keepdims=True)
        second = jnp.sum(mixed[...] * mixed[...], axis=0, keepdims=True)
        stats_ref[...] = jnp.concatenate([first, second, jnp.zeros((6, D), F32)], axis=0)


def tail(y, xs, projected, incoming, out_whole, c_rows, entering, heads, gain, cot, units):
    length = y.shape[0]
    group = lambda i: jnp.where(i < STEPS, i, jnp.minimum(i - STEPS, STEPS - 1))
    second = lambda i: jnp.clip(i - STEPS, 0, STEPS - 1)
    early = lambda rows: pl.BlockSpec((rows, BLK), lambda i: (0, jnp.minimum(i, STEPS - 1)))
    late = lambda rows: pl.BlockSpec((rows, BLK), lambda i: (0, second(i)))
    each = lambda rows: pl.BlockSpec((rows, BLK), lambda i: (0, group(i)))
    whole = lambda *shape: pl.BlockSpec(shape, lambda i: (0,) * len(shape))
    return pl.pallas_call(
        tail_kernel,
        grid=(2 * STEPS,),
        in_specs=[
            early(length),
            each(length),
            each(length),
            early(STATE),
            pl.BlockSpec((BLK, D), lambda i: (group(i), 0)),
            whole(length, 128),
            whole(length, 128),
            whole(8, 128),
            each(8),
            whole(length, D),
            whole(length, D),
        ],
        out_specs=[
            pl.BlockSpec((BLK, length), lambda i: (second(i), 0)),
            late(length),
            late(length),
            pl.BlockSpec((STATE, BLK), lambda i: (0, second(i))),
            late(8),
            whole(length, D),
            whole(8, D),
        ],
        out_shape=[
            jax.ShapeDtypeStruct((INNER, length), BF16),
            jax.ShapeDtypeStruct((length, WIDTH), BF16),
            jax.ShapeDtypeStruct((length, INNER), BF16),
            jax.ShapeDtypeStruct((STATE, INNER), BF16),
            jax.ShapeDtypeStruct((8, INNER), F32),
            jax.ShapeDtypeStruct((length, D), BF16),
            jax.ShapeDtypeStruct((8, D), F32),
        ],
        scratch_shapes=[
            pltpu.VMEM((STEPS, length, BLK), F32),
            pltpu.VMEM((STEPS, length, BLK), F32),
            pltpu.VMEM((length, 128), F32),
            pltpu.VMEM((length, 128), F32),
            pltpu.VMEM((length, D), F32),
            pltpu.VMEM((128, length), BF16),
        ],
        compiler_params=pltpu.CompilerParams(vmem_limit_bytes=VMEM_LIMIT),
        cost_estimate=pl.CostEstimate(
            flops=12 * 10**9, bytes_accessed=50 * 10**6, transcendentals=4 * 10**6
        ),
        name="tail",
    )(y, xs, projected, incoming, out_whole, c_rows, entering, heads, gain, cot, units)


def back_steps(step, given, scratch, write, write_halo, write_taps, write_heads):
    (
        x_ref, dtraw_ref, halo_ref, taps_ref, heads_ref, seg_ref, row_ref, b_ref, c_ref, dt_ref, run_ref, dy_ref, sin_ref, dout_ref,
    ) = given
    (
        ext, pre, dact, dbuf, scores, dscores, run_t, b_t, c_t, enter, leave, d_b, d_c, suffix, prefix, d_dt, fixed, states,
    ) = scratch
    length = x_ref.shape[0]
    chunks = length // Q

    @pl.when(step == 0)
    def _():
        for k in range(chunks):
            rows = slice(k * Q, (k + 1) * Q)
            b_rows, c_rows = b_ref[rows, :], c_ref[rows, :]
            b_t[:, rows] = b_rows.astype(F32).T.astype(BF16)
            c_t[:, rows] = c_rows.astype(F32).T.astype(BF16)
            scores[rows, :] = masked_scores(seg_ref, row_ref, b_rows, c_rows, k)
            running = run_ref[rows, :]
            run_t[k] = running.T
            carry, tail = chunk_flags(seg_ref, k)
            enter[rows, :] = jnp.exp(running) * carry
            leave[rows, :] = jnp.exp(running[Q - 1 : Q, :] - running) * tail
        for each in (dscores, d_b, d_c, suffix, prefix, d_dt, fixed):
            each[...] = jnp.zeros_like(each)
        dbuf[0:PAD, :] = jnp.zeros((PAD, BLK), F32)
        dbuf[PAD + length :, :] = jnp.zeros((PAD, BLK), F32)

    @pl.when(step <= STEPS)
    def _():
        ext[0:PAD, :] = halo_ref[...]
        ext[PAD:, :] = x_ref[...].astype(F32)
        for k in range(chunks):
            pre[k * Q : (k + 1) * Q, :] = conv_rows(ext, seg_ref, taps_ref, k * Q, Q)

    @pl.when(step < STEPS)
    def _():
        select = chosen(step)
        gather = chosen_back(step)
        skip = widen(heads_ref[...], select)[2:3, :]
        state = sin_ref[...].astype(F32)
        for k in range(chunks):
            rows = slice(k * Q, (k + 1) * Q)
            states[k] = state
            if k + 1 < chunks:
                total = pre[rows, :]
                scaled = total * sigmoid(total) * widen(dt_ref[rows, :], select)
                weighted = (scaled.astype(BF16).astype(F32) * widen(leave[rows, :], select)).astype(BF16)
                last = widen(enter[rows.stop - 8 : rows.stop, :], select)[7:8, :]
                state = last * state + dot(b_t[:, rows], weighted)
        d_state = dout_ref[...].astype(F32)
        for k in range(chunks - 1, -1, -1):
            rows = slice(k * Q, (k + 1) * Q)
            total = pre[rows, :]
            values = total * sigmoid(total)
            step_size = widen(dt_ref[rows, :], select)
            entering = widen(enter[rows, :], select)
            leaving = widen(leave[rows, :], select)
            scaled = (values * step_size).astype(BF16)
            scaled_wide = scaled.astype(F32)
            dy = dy_ref[rows, :]
            dy_wide = dy.astype(F32)
            before = states[k]
            before_low = before.astype(BF16)
            d_low = d_state.astype(BF16)
            running = pltpu.roll(run_ref[rows, :], lax.rem(128 - step * GROUP, 128), 1)
            insides, backs = [], []
            d_score = dscores[rows, :]
            for pair in range(2):
                lanes = slice(pair * 128, (pair + 1) * 128)
                mixing, turned, decays = [], [], []
                for one in range(2):
                    head = 2 * pair + one
                    gap = running[:, head : head + 1] - run_t[k, pl.ds(step * GROUP + head, 1), :]
                    decay = jnp.exp(jnp.minimum(gap, 0.0))
                    mixed = decay * scores[rows, :]
                    decays.append(decay)
                    mixing.append(mixed.astype(BF16))
                    turned.append(mixed.T.astype(BF16))
                spread = halves(scaled[:, lanes])
                insides.append(dot(jnp.concatenate(mixing, axis=1), spread))
                backs.append(dot(jnp.concatenate(turned, axis=1), halves(dy[:, lanes])))
                products = dot_nt(dy[:, lanes], spread)
                d_score = d_score + decays[0] * products[:, :Q] + decays[1] * products[:, Q:]
            dscores[rows, :] = d_score
            inside = jnp.concatenate(insides, axis=1) + entering * dot(c_ref[rows, :], before_low)
            back_inside = jnp.concatenate(backs, axis=1)
            back_state = leaving * dot(b_ref[rows, :], d_low)
            high, low = in_two(dy_wide * inside - scaled_wide * back_inside)
            suffix[rows, :] += dot(high, gather) + dot(low, gather)
            prefix[rows, :] += dot((scaled_wide * back_state).astype(BF16), gather)
            back = back_inside + back_state
            d_dt[rows, :] += dot((values * back).astype(BF16), gather)
            entered = (dy_wide * entering).astype(BF16)
            d_c[rows, :] += dot_nt(entered, before_low)
            d_b[rows, :] += dot_nt((scaled_wide * leaving).astype(BF16), d_low)
            kept = entering[Q - 1 : Q, :]
            through = jnp.sum(before * d_state, axis=0, keepdims=True) * kept
            high, low = in_two(jnp.broadcast_to(through, (8, BLK)))
            fixed[k * 8 : (k + 1) * 8, :] += dot(high, gather) + dot(low, gather)
            d_state = kept * d_state + dot(c_t[:, rows], entered)
            dact[rows, :] = back * step_size + skip * dy_wide

    @pl.when(step == STEPS)
    def _():
        for k in range(chunks):
            rows = slice(k * Q, (k + 1) * Q)
            own = seg_ref[PAD + k * Q : PAD + (k + 1) * Q, :]
            keep = (own == row_ref[0:1, rows]) & (iota((Q, Q), 1) <= iota((Q, Q), 0))
            d_score = jnp.where(keep, dscores[rows, :], 0.0)
            dact[rows, STATE:] = d_c[rows, :] + dot(d_score.astype(BF16), b_ref[rows, :])
            dact[rows, :STATE] = d_b[rows, :] + dot(d_score.T.astype(BF16), c_ref[rows, :])

    @pl.when(step <= STEPS)
    def _():
        sums = [jnp.zeros((1, BLK), F32) for _ in range(CONV + 1)]
        for k in range(chunks):
            rows = slice(k * Q, (k + 1) * Q)
            total = pre[rows, :]
            sig = sigmoid(total)
            d_conv = dact[rows, :] * (sig * (1.0 + total * (1.0 - sig)))
            dbuf[PAD + k * Q : PAD + (k + 1) * Q, :] = d_conv
            sums[4] = sums[4] + jnp.sum(d_conv, axis=0, keepdims=True)
            own = seg_ref[PAD + k * Q : PAD + (k + 1) * Q, :]
            for shift in range(CONV):
                at = PAD + k * Q - shift
                term = d_conv * ext[at : at + Q, :]
                if shift:
                    term = jnp.where(both(seg_ref[at : at + Q, :] == own), term, 0.0)
                sums[3 - shift] = sums[3 - shift] + jnp.sum(term, axis=0, keepdims=True)
        write_taps(jnp.concatenate(sums + [jnp.zeros((3, BLK), F32)], axis=0))

        def returned(at, rows):
            own = seg_ref[at : at + rows, :]
            result = taps_ref[3:4, :] * dbuf[at : at + rows, :]
            for shift in range(1, CONV):
                same = both(seg_ref[at + shift : at + shift + rows, :] == own)
                result = result + jnp.where(
                    same, taps_ref[3 - shift : 4 - shift, :] * dbuf[at + shift : at + shift + rows, :], 0.0
                )
            return result

        write_halo(returned(0, PAD))
        for k in range(chunks):
            write(slice(k * Q, (k + 1) * Q), returned(PAD + k * Q, Q).astype(BF16))

    @pl.when(step == STEPS + 1)
    def _():
        lower = (iota((Q, Q), 1) < iota((Q, Q), 0)).astype(F32)
        upper = (iota((Q, Q), 1) >= iota((Q, Q), 0)).astype(F32)
        lane = iota((Q, 128), 1)
        rate = jnp.exp(heads_ref[1:2, :])
        bias_sum = jnp.zeros((1, 128), F32)
        decay_sum = jnp.zeros((1, 128), F32)
        for k in range(chunks):
            rows = slice(k * Q, (k + 1) * Q)
            d_log = jnp.dot(upper, suffix[rows, :], precision=HIGHEST, preferred_element_type=F32)
            d_log = d_log + jnp.dot(lower, prefix[rows, :], precision=HIGHEST, preferred_element_type=F32)
            d_log = d_log + fixed[k * 8 : k * 8 + 1, :]
            raw = jnp.where(lane < HEADS, dtraw_ref[rows, :128].astype(F32), 0.0) + heads_ref[0:1, :]
            d_raw = jnp.where(lane < HEADS, (d_dt[rows, :] - rate * d_log) * sigmoid(raw), 0.0)
            bias_sum = bias_sum + jnp.sum(d_raw, axis=0, keepdims=True)
            decay_sum = decay_sum - jnp.sum(d_log * dt_ref[rows, :] * rate, axis=0, keepdims=True)
            write(rows, jnp.concatenate([d_raw, jnp.zeros_like(d_raw)], axis=1).astype(BF16))
        write_heads(jnp.concatenate([bias_sum, decay_sum, jnp.zeros((6, 128), F32)], axis=0))


def back_kernel(*refs):
    given, (_, dproj_ref, dhalo_ref, dtaps_ref, dheads_ref), scratch = refs[:14], refs[14:19], refs[19:]

    def write(rows, value):
        dproj_ref[rows, :] = value

    def write_halo(value):
        dhalo_ref[...] = value

    def write_taps(value):
        dtaps_ref[...] = value

    def write_heads(value):
        dheads_ref[...] = value

    back_steps(pl.program_id(0), given, scratch, write, write_halo, write_taps, write_heads)


def back_scratch(length):
    return [
        pltpu.VMEM((length + PAD, BLK), F32),
        pltpu.VMEM((length, BLK), F32),
        pltpu.VMEM((length, BLK), F32),
        pltpu.VMEM((length + 2 * PAD, BLK), F32),
        pltpu.VMEM((length, Q), F32),
        pltpu.VMEM((length, Q), F32),
        pltpu.VMEM((length // Q, 128, Q), F32),
        pltpu.VMEM((128, length), BF16),
        pltpu.VMEM((128, length), BF16),
        *[pltpu.VMEM((length, 128), F32) for _ in range(7)],
        pltpu.VMEM((8 * (length // Q), 128), F32),
        pltpu.VMEM((length // Q, STATE, BLK), F32),
    ]


def back_inputs(length, late=0):
    whole = lambda *shape: pl.BlockSpec(shape, lambda j: (0,) * len(shape))
    upto = lambda last, first=0: lambda j: (0, first + jnp.clip(j - late, 0, last))
    return [
        pl.BlockSpec((length, BLK), upto(STEPS, STEPS)),
        pl.BlockSpec((length, BLK), lambda j: (0, 2 * STEPS + 1)),
        pl.BlockSpec((PAD, BLK), upto(STEPS, STEPS)),
        pl.BlockSpec((8, BLK), upto(STEPS)),
        whole(8, 128),
        whole(length + 2 * PAD, 128),
        whole(8, length),
        whole(length, 128),
        whole(length, 128),
        whole(length, 128),
        whole(length, 128),
        pl.BlockSpec((length, BLK), upto(STEPS - 1)),
        pl.BlockSpec((STATE, BLK), upto(STEPS - 1)),
        whole(STATE, INNER) if late else pl.BlockSpec((STATE, BLK), upto(STEPS - 1)),
    ]


def back(given, dproj):
    length = dproj.shape[0]
    upto = lambda last, first=0: lambda j: (0, first + jnp.minimum(j, last))
    return pl.pallas_call(
        back_kernel,
        grid=(STEPS + 2,),
        in_specs=[*back_inputs(length), pl.BlockSpec(memory_space=pl.ANY)],
        out_specs=[
            pl.BlockSpec((length, BLK), lambda j: (0, STEPS + j)),
            pl.BlockSpec((PAD, BLK), upto(STEPS)),
            pl.BlockSpec((8, BLK), upto(STEPS)),
            pl.BlockSpec((8, 128), lambda j: (0, 0)),
        ],
        out_shape=[
            jax.ShapeDtypeStruct((length, WIDTH), BF16),
            jax.ShapeDtypeStruct((PAD, XBC), F32),
            jax.ShapeDtypeStruct((8, XBC), F32),
            jax.ShapeDtypeStruct((8, 128), F32),
        ],
        scratch_shapes=back_scratch(length),
        input_output_aliases={14: 0},
        compiler_params=pltpu.CompilerParams(vmem_limit_bytes=VMEM_LIMIT),
        name="back",
    )(*given, dproj)


OUT_CHUNKS = 2 * D // WIDE
GATE_CHUNKS = INNER // WIDE
IN_CHUNKS = WIDTH // WIDE
CHUNKS = OUT_CHUNKS + IN_CHUNKS
LAGS = 8
RING = 8
LATE = 3


def small_sums(taps, columns, input_gain, heads, stats):
    fill = lambda width: jnp.zeros((1, width), F32)
    squares = [jnp.broadcast_to(jnp.sum(stats[i : i + 1], axis=1, keepdims=True), (1, 128)) for i in range(2)]
    return jnp.concatenate(
        [
            taps[:5],
            jnp.concatenate([columns[0:1], fill(XBC - INNER)], axis=1),
            jnp.concatenate([columns[1:2], fill(XBC - INNER)], axis=1),
            jnp.concatenate([input_gain, heads[0:1], heads[1:2], *squares, fill(XBC - D - 512)], axis=1),
        ],
        axis=0,
    )


def finish_kernel(*refs):
    given, refs = refs[:14], refs[14:]
    lhs_in, lhs_out, gate_ref, weight_ref, cot_ref, units_ref, gain_ref, columns_ref, stats_ref, kept_ref = refs[:10]
    din_ref, dout_ref, input_grad_ref, total_ref = refs[10:14]
    scratch, refs = refs[14:32], refs[32:]
    exchange, outgoing, refs = Exchange(*refs[:5]), refs[5], refs[6:]
    grads, edges, halos, taps, heads, d_normed = refs[:6]
    own, core_send, core_recv, y_recv, x_recv, z_recv, w_recv, final, small_send, small_recv = refs[6:16]
    send_sems, recv_sems, small_send_sems, small_recv_sems, edge_sends, edge_arrivals = refs[16:]
    step = pl.program_id(0)
    length = cot_ref.shape[0]
    shard, part = lax.axis_index("fsdp"), lax.axis_index("ctx")
    core, y = lax.rem(shard, 2), shard // 2
    x, z = lax.rem(part, 2), part // 2
    near, far = lax.rem(z, 2), z // 2
    peers = (
        {"fsdp": flipped(shard, 1)},
        {"fsdp": flipped(shard, 2)},
        {"ctx": flipped(part, 1)},
        {"ctx": flipped(part, 2)},
        {"ctx": flipped(part, 4)},
    )
    preceding = lax.rem(part + PARTS - 1, PARTS)

    def ring(k):
        return lax.rem(k, RING)

    def sent(stage, k, source, target, peer):
        return remote(source, target, send_sems.at[stage, k], recv_sems.at[stage, k], peers[peer])

    copies = (
        lambda k: sent(0, k, core_send.at[lax.rem(k, 2)], core_recv.at[ring(k)], 0),
        lambda k: sent(1, k, core_recv.at[ring(k), 1 - y], y_recv.at[ring(k)], 1),
        lambda k: sent(2, k, y_recv.at[ring(k), 1 - x], x_recv.at[ring(k)], 2),
        lambda k: sent(3, k, x_recv.at[ring(k), 1 - near], z_recv.at[ring(k)], 3),
        lambda k: sent(4, k, z_recv.at[ring(k), 1 - far], w_recv.at[ring(k)], 4),
        lambda k: sent(5, k, final.at[ring(k), x, near, far], final.at[ring(k), x, near, far], 4),
        lambda k: sent(6, k, final.at[ring(k), x, near], final.at[ring(k), x, near], 3),
        lambda k: sent(7, k, final.at[ring(k), x], final.at[ring(k), x], 2),
    )
    arrivals = copies[:5] + (
        lambda k: sent(5, k, final.at[ring(k), x, near, 1 - far], final.at[ring(k), x, near, 1 - far], 4),
        lambda k: sent(6, k, final.at[ring(k), x, 1 - near], final.at[ring(k), x, 1 - near], 3),
        lambda k: sent(7, k, final.at[ring(k), 1 - x], final.at[ring(k), 1 - x], 2),
    )

    def small_copy(stage):
        return remote(
            small_send.at[stage], small_recv.at[stage], small_send_sems.at[stage], small_recv_sems.at[stage], peers[stage]
        )

    def edge_copy(block):
        return remote(
            edges.at[block], halos.at[block], edge_sends.at[block], edge_arrivals.at[block], {"ctx": preceding}
        )

    @pl.when(step == 0)
    def _():
        exchange.greet(peers[0], peers[1])
        for group in range(STEPS):
            exchange.spread(group, given[13][:, group * BLK : (group + 1) * BLK])
        d_normed[...] = jnp.zeros_like(d_normed)

    def partial(lhs_of, rhs):
        for row in range(2):
            value = dot(lhs_of(2 * row + 1 - core), rhs).astype(BF16)
            core_send[lax.rem(step, 2), row] = value.reshape(2, 2, 2, PIECE, WIDE)
        copies[0](step).start()
        for row in range(2):
            own[row] = dot(lhs_of(2 * row + core), rhs).reshape(2, 2, 2, PIECE, WIDE)

    def in_chunk(rhs):
        partial(lambda s: lhs_in[s], rhs)
        d_normed[...] += dot(rhs, weight_ref[...])

    @pl.when(step < OUT_CHUNKS)
    def _():
        columns = lax.rem(step, D // WIDE) * WIDE
        rhs = cot_ref[:, pl.ds(pl.multiple_of(columns, WIDE), WIDE)]
        partial(lambda s: lhs_out[s, step // (D // WIDE)], rhs)

    @pl.when((step >= OUT_CHUNKS) & (step < OUT_CHUNKS + GATE_CHUNKS))
    def _():
        in_chunk(gate_ref[...])

    @pl.when((step >= OUT_CHUNKS + GATE_CHUNKS) & (step < CHUNKS))
    def _():
        first = 2 * (step - OUT_CHUNKS - GATE_CHUNKS)
        for done in (first, first + 1):

            @pl.when(done <= STEPS)
            def _():
                edge_copy(done).wait()
                tail = slice(length - 16, length)
                more = jnp.where(part == PARTS - 1, 0.0, halos[done])
                more = jnp.concatenate([jnp.zeros_like(more), more], axis=0)
                grads[done, tail, :] = (grads[done, tail, :].astype(F32) + more).astype(BF16)

        in_chunk(jnp.concatenate([grads[first], grads[first + 1]], axis=1))

    for half in range(2):

        @pl.when(step == 1 + half)
        def _():
            for group in range(half * STEPS // 2, (half + 1) * STEPS // 2):
                exchange.join(group, widen(first_rows(kept_ref), chosen(group)), False)

    block = step - LATE

    def write(rows, value):
        grads[block, rows, :] = value

    def write_halo(value):
        edges[block] = value
        edge_copy(block).start()

    def write_taps(value):
        taps[block] = value

    def write_heads(value):
        heads[...] = value

    @pl.when((block >= 0) & (block < STEPS))
    def _():
        outgoing[...] = exchange.finish(block)

    @pl.when(block >= 0)
    def _():
        back_steps(block, (*given[:13], outgoing), scratch, write, write_halo, write_taps, write_heads)

    @pl.when(step < CHUNKS)
    def _():
        arrivals[0](step).wait_recv()
        for row in (1 - y, y):
            core_recv[ring(step), row] = (own[row] + core_recv[ring(step), row].astype(F32)).astype(BF16)
        copies[1](step).start()

    def stage(lag):
        def decorate(body):
            k = step - lag

            @pl.when((k >= 0) & (k < CHUNKS))
            def _():
                body(k, ring(k))

        return decorate

    def summed(a, b):
        return (a.astype(F32) + b.astype(F32)).astype(BF16)

    @stage(1)
    def _(k, at):
        arrivals[1](k).wait_recv()
        y_recv[at] = summed(y_recv[at], core_recv[at, y])
        copies[2](k).start()
        copies[0](k).wait_send()

    @stage(2)
    def _(k, at):
        arrivals[2](k).wait_recv()
        x_recv[at] = summed(x_recv[at], y_recv[at, x])
        copies[3](k).start()

    @stage(3)
    def _(k, at):
        arrivals[3](k).wait_recv()
        z_recv[at] = summed(z_recv[at], x_recv[at, near])
        copies[4](k).start()
        copies[1](k).wait_send()

    @stage(4)
    def _(k, at):
        arrivals[4](k).wait_recv()
        final[at, x, near, far] = summed(w_recv[at], z_recv[at, far])
        copies[5](k).start()
        copies[2](k).wait_send()

    @stage(5)
    def _(k, at):
        arrivals[5](k).wait_recv()
        copies[6](k).start()
        copies[3](k).wait_send()

    @stage(6)
    def _(k, at):
        arrivals[6](k).wait_recv()
        copies[7](k).start()
        copies[4](k).wait_send()

    @stage(7)
    def _(k, at):
        arrivals[7](k).wait_recv()
        for one in (5, 6, 7):
            copies[one](k).wait_send()
        whole = final[at].reshape(SHARD, WIDE)

        @pl.when(k < OUT_CHUNKS)
        def _():
            dout_ref[...] = whole

        @pl.when(k >= OUT_CHUNKS)
        def _():
            din_ref[...] = whole.astype(F32).T.astype(BF16)

    @pl.when(step == CHUNKS)
    def _():
        input_gain = jnp.zeros((1, D), F32)
        for k in range(length // Q):
            rows = slice(k * Q, (k + 1) * Q)
            units = units_ref[rows, :].astype(F32)
            norm = lax.rsqrt(jnp.sum(units * units, axis=1, keepdims=True) * (1.0 / D) + epsilon)
            base = units * norm
            grad = d_normed[rows, :]
            input_gain = input_gain + jnp.sum(grad * base, axis=0, keepdims=True)
            scaled = grad * gain_ref[0:1, :]
            mean = jnp.sum(scaled * base, axis=1, keepdims=True) * (1.0 / D)
            input_grad_ref[rows, :] = (cot_ref[rows, :].astype(F32) + norm * (scaled - base * mean)).astype(BF16)
        whole = jnp.concatenate([taps[one] for one in range(STEPS + 1)], axis=1)
        small_send[0] = small_sums(whole, columns_ref[...], input_gain, heads[...], stats_ref[...])
        small_copy(0).start()

    for stage_of_small in range(5):

        @pl.when(step == CHUNKS + 1 + stage_of_small)
        def _():
            small_copy(stage_of_small).wait()
            total = small_send[stage_of_small] + small_recv[stage_of_small]
            if stage_of_small < 4:
                small_send[stage_of_small + 1] = total
                small_copy(stage_of_small + 1).start()
            else:
                total_ref[...] = total


def finish(given, normed_t, mixer_t, dproj, w_turned, cot, units, input_gain, column_sums, stats, kept):
    length = cot.shape[0]
    per_half = D // WIDE
    once = pl.Buffered(1)
    whole = lambda *shape: pl.BlockSpec(shape, lambda t: (0,) * len(shape), pipeline_mode=once)
    in_chunk = lambda t: jnp.clip(t - OUT_CHUNKS, 0, IN_CHUNKS - 1)

    def out_block(t):
        k = jnp.clip(t - LAGS + 1, 0, OUT_CHUNKS - 1)
        return (k // per_half, lax.rem(k, per_half))

    slots = lambda *shape: pltpu.VMEM((RING, *shape, PIECE, WIDE), BF16)
    return pl.pallas_call(
        finish_kernel,
        grid=(CHUNKS + LAGS - 1,),
        in_specs=[
            *back_inputs(length, LATE),
            whole(4, SHARD, length),
            whole(4, 2, SHARD, length),
            pl.BlockSpec((length, WIDE), lambda t: (0, jnp.minimum(in_chunk(t), GATE_CHUNKS - 1))),
            pl.BlockSpec((WIDE, D), lambda t: (in_chunk(t), 0)),
            whole(length, D),
            whole(length, D),
            whole(1, D),
            whole(8, INNER),
            whole(8, D),
            whole(PARTS, 8, 128),
        ],
        out_specs=[
            pl.BlockSpec((WIDE, SHARD), lambda t: (in_chunk(t - LAGS + 1), 0)),
            pl.BlockSpec((SHARD, WIDE), out_block),
            pl.BlockSpec((length, D), lambda t: (0, 0)),
            pl.BlockSpec((8, XBC), lambda t: (0, 0)),
        ],
        out_shape=[
            jax.ShapeDtypeStruct((PROJ, SHARD), BF16),
            jax.ShapeDtypeStruct((2 * SHARD, D), BF16),
            jax.ShapeDtypeStruct((length, D), BF16),
            jax.ShapeDtypeStruct((8, XBC), F32),
        ],
        scratch_shapes=[
            *back_scratch(length),
            *exchange_scratch(),
            pltpu.VMEM((STATE, BLK), BF16),
            pltpu.VMEM((STEPS + 2, length, BLK), BF16),
            pltpu.VMEM((STEPS + 1, PAD, BLK), F32),
            pltpu.VMEM((STEPS + 1, PAD, BLK), F32),
            pltpu.VMEM((STEPS + 1, 8, BLK), F32),
            pltpu.VMEM((8, 128), F32),
            pltpu.VMEM((length, D), F32),
            pltpu.VMEM((2, 2, 2, 2, PIECE, WIDE), F32),
            pltpu.VMEM((2, 2, 2, 2, 2, PIECE, WIDE), BF16),
            slots(2, 2, 2, 2),
            slots(2, 2, 2),
            slots(2, 2),
            slots(2),
            slots(),
            slots(2, 2, 2),
            pltpu.VMEM((5, 8, XBC), F32),
            pltpu.VMEM((5, 8, XBC), F32),
            pltpu.SemaphoreType.DMA((8, CHUNKS)),
            pltpu.SemaphoreType.DMA((8, CHUNKS)),
            pltpu.SemaphoreType.DMA((5,)),
            pltpu.SemaphoreType.DMA((5,)),
            pltpu.SemaphoreType.DMA((STEPS + 1,)),
            pltpu.SemaphoreType.DMA((STEPS + 1,)),
        ],
        compiler_params=communicating(0),
        name="finish",
    )(*given, normed_t, mixer_t, dproj, w_turned, cot, units, input_gain, column_sums, stats, kept)


def passed_along(block, axis, distance):
    devices = range(lax.axis_size(axis))
    route = [(i - distance, i) for i in devices if i - distance in devices]
    return lax.ppermute(block, axis, route)


def pack_small(conv_taps, conv_bias, dt_bias, decay_log, skip_scale, mixer_gain, input_gain):
    width = conv_bias.shape[0]

    def line(*parts):
        flat = jnp.concatenate(parts)
        return jnp.pad(flat, (0, width - flat.shape[0]))[None]

    rows = jnp.concatenate(
        [
            conv_taps.T,
            conv_bias[None],
            line(mixer_gain),
            line(input_gain),
            line(dt_bias, decay_log, skip_scale),
        ],
        axis=0,
    )
    return jnp.pad(rows.astype(F32), ((0, 0), (0, SMALL_WIDTH - width)))


def unpack_small(whole, width):
    shards = whole.shape[0]
    joined = jnp.swapaxes(whole, 0, 1)
    taps = jnp.pad(joined[:5, :, :width].reshape(5, shards * width).astype(F32), ((0, 3), (0, 0)))
    gain = joined[5, :, : INNER // shards].reshape(1, INNER).astype(F32)
    input_gain = joined[6, :, : D // shards].reshape(1, D).astype(F32)
    own = HEADS // shards
    heads = joined[7, :, : 3 * own].reshape(shards, 3, own).swapaxes(0, 1).reshape(3, HEADS)
    heads = jnp.pad(heads.astype(F32), ((0, 5), (0, 128 - HEADS)))
    return taps, jnp.pad(gain, ((0, 7), (0, 0))), input_gain, heads


def on_device(
    inputs,
    segment_ids,
    out_grad,
    in_matrix,
    out_matrix,
    conv_taps,
    conv_bias,
    dt_bias,
    decay_log,
    skip_scale,
    mixer_gain,
    input_gain,
):
    shards, parts = lax.axis_size("fsdp"), lax.axis_size("ctx")
    place = lax.axis_index("ctx")
    units_low, cot = inputs[0], out_grad[0]
    seg_ids = segment_ids[0]
    length = units_low.shape[0]
    here = (shards, parts) == (4, PARTS)
    small = pack_small(conv_taps, conv_bias, dt_bias, decay_log, skip_scale, mixer_gain, input_gain)
    seg_row = jnp.broadcast_to(seg_ids[None], (8, length))
    if here:
        seg_own = jnp.broadcast_to(seg_ids[:, None], (length, 128))
        (
            xs, y_local, incoming, b_rows, c_rows, dt, running, entering,
            kept, w_turned, out_whole, projected, normed_t, halo, taps, heads, gain, g_float, seg_lanes,
        ) = forward(in_matrix, out_matrix, units_low, small, seg_own, seg_row)
        out_whole = out_whole.reshape(-1, D)
    else:
        units = units_low.astype(F32)
        inv_rms = lax.rsqrt(jnp.mean(units * units, axis=-1, keepdims=True) + epsilon)
        base_rows = units * inv_rms
        w_whole = jnp.pad(in_matrix, ((0, 0), (0, WIDTH - PROJ)))
        w_whole = lax.all_gather(w_whole, "fsdp", axis=0, tiled=True)
        out_whole = lax.all_gather(out_matrix, "fsdp", axis=0, tiled=True)
        rim_seg = passed_along(seg_ids[length - CONV + 1 :], "ctx", 1)
        taps, gain, g_float, heads = unpack_small(lax.all_gather(small, "fsdp"), conv_bias.shape[0])
        normed = (base_rows * g_float).astype(BF16)
        normed_t = normed.T
        projected = dot(normed, w_whole).astype(BF16)
        rim_rows = passed_along(projected[length - CONV + 1 :], "ctx", 1)
        halo = jnp.pad(rim_rows, ((PAD - CONV + 1, 0), (0, 0))).astype(F32)
        seg_ext = jnp.concatenate(
            [
                jnp.full((PAD - CONV + 1,), -1, jnp.int32),
                rim_seg,
                seg_ids,
                jnp.full((PAD,), -2, jnp.int32),
            ]
        )
        seg_lanes = jnp.broadcast_to(seg_ext[:, None], (length + 2 * PAD, 128))
        xs, y_local, state, b_rows, c_rows, dt, running, entering, keep = front(
            projected, halo, taps, heads, seg_lanes, seg_row
        )
        kept = lax.all_gather(keep, "ctx")
        incoming = joined_plainly(lax.all_gather(state, "ctx"), kept, place, True)
    mixer_t, dproj, dy, outgoing, column_sums, block_out, stats = tail(
        y_local, xs, projected, incoming, out_whole, c_rows, entering, heads, gain, cot, units_low
    )
    if not here:
        outgoing = joined_plainly(lax.all_gather(outgoing, "ctx"), kept, place, False)
    given = (
        projected, projected, halo, taps, heads, seg_lanes, seg_row, b_rows, c_rows, dt, running, dy, incoming, outgoing,
    )
    if here:
        d_in, d_out, input_grad, total = finish(
            given, normed_t, mixer_t.reshape(4, 2, SHARD, length), dproj, w_turned, cot, units_low, g_float, column_sums, stats, kept
        )
        d_in, d_out = d_in.T.astype(F32), d_out.astype(F32)
    else:
        dproj, d_halo, d_taps, d_heads = back(given, dproj)
        returned = passed_along(d_halo.astype(BF16), "ctx", -1)
        last = lax.slice(dproj, (length - PAD, INNER), (length, INNER + XBC))
        last = (last.astype(F32) + returned.astype(F32)).astype(BF16)
        dproj = lax.dynamic_update_slice(dproj, last, (length - PAD, INNER))
        d_normed = dot_nt(dproj, w_whole)
        d_input_gain = jnp.sum(d_normed * base_rows, axis=0)
        d_base = d_normed * g_float
        d_units = inv_rms * (d_base - base_rows * jnp.mean(d_base * base_rows, axis=-1, keepdims=True))
        input_grad = (cot.astype(F32) + d_units).astype(BF16)

        def scattered(grad):
            return lax.psum_scatter(grad.astype(BF16), "fsdp", scatter_dimension=0, tiled=True)

        d_in = jnp.dot(normed_t, dproj, preferred_element_type=F32)[:, :PROJ]
        d_out = jnp.dot(mixer_t, cot, preferred_element_type=F32)
        d_in = lax.psum(scattered(d_in), "ctx").astype(F32)
        d_out = lax.psum(scattered(d_out), "ctx").astype(F32)
        total = lax.psum(small_sums(d_taps, column_sums, d_input_gain[None], d_heads, stats), ("fsdp", "ctx"))
    me = lax.axis_index("fsdp")

    def own(flat):
        size = flat.shape[-1] // shards
        return lax.dynamic_slice_in_dim(flat, me * size, size, flat.ndim - 1)

    skip_sums = jnp.sum(total[6, :INNER].reshape(HEADS, HDIM), axis=1)
    at = D + 256
    stat_sums = jnp.stack([total[7, at], total[7, at + 128]])
    rms_stats = jnp.sqrt(stat_sums / (length * shards * parts * D))
    return (
        block_out[None],
        input_grad[None],
        d_in,
        d_out,
        own(total[:4]).T,
        own(total[4]),
        own(total[7, D : D + HEADS]),
        own(total[7, D + 128 : D + 128 + HEADS]),
        own(skip_sums),
        own(total[5, :INNER]),
        own(total[7, :D]),
        rms_stats,
    )


def solution(mesh):
    return jax.shard_map(
        on_device,
        mesh=mesh,
        in_specs=(
            P("fsdp", "ctx", None),
            P("fsdp", "ctx"),
            P("fsdp", "ctx", None),
            P("fsdp", None),
            P("fsdp", None),
            P("fsdp", None),
            P("fsdp"),
            P("fsdp"),
            P("fsdp"),
            P("fsdp"),
            P("fsdp"),
            P("fsdp"),
        ),
        out_specs=(
            P("fsdp", "ctx", None),
            P("fsdp", "ctx", None),
            P("fsdp", None),
            P("fsdp", None),
            P("fsdp", None),
            P("fsdp"),
            P("fsdp"),
            P("fsdp"),
            P("fsdp"),
            P("fsdp"),
            P("fsdp"),
            P(),
        ),
        check_vma=False,
    )
```

```python
import functools

import jax
import jax.numpy as jnp
from jax import lax
from jax.experimental import pallas as pl
from jax.experimental.pallas import tpu as pltpu
from jax.sharding import PartitionSpec as P

D = 1536
HEADS = 48
HDIM = 64
STATE = 128
CONV = 4
INNER = 3072
XBC = 3328
PROJ = 6448
WIDTH = 6656

BLK = 256
GROUP = BLK // HDIM
STEPS = INNER // BLK
Q = 128
PAD = 8
WIDE = 512
SHARD = D // 4
PIECE = SHARD // 8
SMALL_WIDTH = 896
AHEAD = 2

epsilon = 1e-05
F32, BF16 = jnp.float32, jnp.bfloat16
HIGHEST = lax.Precision.HIGHEST
VMEM_LIMIT = 60 * 1024 * 1024


def communicating(number):
    return pltpu.CompilerParams(
        vmem_limit_bytes=VMEM_LIMIT, collective_id=number, has_side_effects=True
    )


def dot(a, b):
    return jnp.dot(a, b, preferred_element_type=F32)


def dot_nt(a, b):
    return lax.dot_general(a, b, (((1,), (1,)), ((), ())), preferred_element_type=F32)


def iota(shape, dim):
    return lax.broadcasted_iota(jnp.int32, shape, dim)


def sigmoid(v):
    return 1.0 / (1.0 + jnp.exp(-v))


def in_two(a):
    high = a.astype(BF16)
    return high, (a - high.astype(F32)).astype(BF16)


def chosen(step):
    columns = step * GROUP + lax.shift_right_logical(iota((128, BLK), 1), 6)
    return (iota((128, BLK), 0) == columns).astype(BF16)


def chosen_back(step):
    heads = step * GROUP + lax.shift_right_logical(iota((BLK, 128), 0), 6)
    return (iota((BLK, 128), 1) == heads).astype(BF16)


def widen(per_head, select):
    high, low = in_two(per_head)
    return dot(high, select) + dot(low, select)


def halves(pair):
    first = iota(pair.shape, 1) < HDIM
    zero = jnp.zeros_like(pair)
    return jnp.concatenate([jnp.where(first, pair, zero), jnp.where(first, zero, pair)], axis=0)


def both(mask):
    return jnp.concatenate([mask, mask], axis=1)


def conv_rows(ext_ref, seg_ref, taps_ref, start, rows):
    own = seg_ref[start + PAD : start + PAD + rows, :]
    total = taps_ref[4:5, :] + taps_ref[3:4, :] * ext_ref[start + PAD : start + PAD + rows, :]
    for back in range(1, CONV):
        at = start + PAD - back
        same = both(seg_ref[at : at + rows, :] == own)
        total = total + jnp.where(
            same, taps_ref[3 - back : 4 - back, :] * ext_ref[at : at + rows, :], 0.0
        )
    return total


def chunk_flags(seg_ref, k):
    own = seg_ref[PAD + k * Q : PAD + (k + 1) * Q, :]
    before = seg_ref[PAD + k * Q - 1 : PAD + k * Q, :]
    last = seg_ref[PAD + (k + 1) * Q - 1 : PAD + (k + 1) * Q, :]
    return (own == before).astype(F32), (own == last).astype(F32)


def masked_scores(seg_ref, row_ref, b_rows, c_rows, k):
    own = seg_ref[PAD + k * Q : PAD + (k + 1) * Q, :]
    row = row_ref[0:1, k * Q : (k + 1) * Q]
    keep = (own == row) & (iota((Q, Q), 1) <= iota((Q, Q), 0))
    return jnp.where(keep, dot_nt(c_rows, b_rows), 0.0)


def remote(source, target, send, arrival, peer):
    return pltpu.make_async_remote_copy(
        src_ref=source,
        dst_ref=target,
        send_sem=send,
        recv_sem=arrival,
        device_id=peer,
        device_id_type=pl.DeviceIdType.MESH,
    )


def flipped(index, bit):
    return index + bit - 2 * bit * lax.rem(index // bit, 2)


class Gather:
    def __init__(self, locate, several, rows, loads, sends, arrivals):
        self.locate, self.several, self.rows = locate, several, rows
        self.loads, self.sends, self.arrivals = loads, sends, arrivals
        shard, part = lax.axis_index("fsdp"), lax.axis_index("ctx")
        self.own, self.other = shard, flipped(shard, 2)
        x, near = lax.rem(part, 2), lax.rem(part // 2, 2)
        self.mine, self.over_x, self.over_z = 2 * x + near, 2 * (1 - x) + near, 2 * x + 1 - near
        self.across = 2 * (1 - x) + 1 - near
        self.core, self.y = {"fsdp": flipped(shard, 1)}, {"fsdp": flipped(shard, 2)}
        self.to_x, self.to_z = {"ctx": flipped(part, 1)}, {"ctx": flipped(part, 2)}

    def whole(self, shard, k):
        return self.locate(k, shard, 0, self.rows)

    def quarter(self, shard, k, which):
        return self.locate(k, shard, which * (self.rows // 4), self.rows // 4)

    def half(self, shard, k, which, second):
        return self.locate(k, shard, (2 * which + second) * (self.rows // 8), self.rows // 8)

    def copy(self, place, kind, k, peer):
        return remote(place, place, self.sends.at[k], self.arrivals.at[kind, k], peer)

    def load(self, k, source):
        return pltpu.make_async_copy(source, self.whole(self.own, k), self.loads.at[k])

    def begin(self, k):
        self.load(k, self.whole(self.own, k)).wait()
        self.send_own(k)

    def send_own(self, k):
        self.copy(self.quarter(self.own, k, self.mine), 1, k, self.y).start()
        self.copy(self.whole(self.own, k), 0, k, self.core).start()

    def first(self, k):
        quarter = self.quarter(self.other, k, self.mine)
        self.copy(quarter, 1, k, self.y).wait_recv()
        self.copy(quarter, 2, k, self.to_x).start()
        self.copy(quarter, 3, k, self.to_z).start()

    def second(self, k):
        self.copy(self.quarter(self.other, k, self.over_x), 2, k, self.to_x).wait_recv()
        self.copy(self.half(self.other, k, self.over_x, 0), 4, k, self.to_z).start()
        self.copy(self.quarter(self.other, k, self.over_z), 3, k, self.to_z).wait_recv()
        self.copy(self.half(self.other, k, self.over_z, 1), 4, k, self.to_x).start()

    def third(self, k):
        self.copy(self.quarter(self.other, k, self.across), 4, k, self.to_x).wait_recv()
        self.copy(self.whole(self.other, k), 0, k, self.core).start()

    def complete(self, k):
        self.copy(self.several(k, 2), 0, k, self.core).wait_recv()

    def drain(self, k):
        self.copy(self.several(k, 3), 0, k, self.core).wait_send()


class PlainGather(Gather):
    def direct(self, shard, k):
        return self.locate(k, shard, 0, DIRECT * self.rows // 6)

    def part_of(self, shard, k, which):
        size = (6 - DIRECT) * self.rows // 12
        return self.locate(k, shard, DIRECT * self.rows // 6 + which * size, size)

    def send_own(self, k):
        self.copy(self.direct(self.own, k), 3, k, self.y).start()
        self.copy(self.part_of(self.own, k, self.mine // 2), 1, k, self.y).start()
        self.copy(self.whole(self.own, k), 0, k, self.core).start()

    def first(self, k):
        part = self.part_of(self.other, k, self.mine // 2)
        self.copy(part, 1, k, self.y).wait_recv()
        self.copy(part, 2, k, self.to_x).start()

    def second(self, k):
        self.copy(self.direct(self.other, k), 3, k, self.y).wait_recv()
        self.copy(self.part_of(self.other, k, self.over_x // 2), 2, k, self.to_x).wait_recv()
        self.copy(self.whole(self.other, k), 0, k, self.core).start()


def gather_sems(chunks):
    return [
        pltpu.SemaphoreType.DMA((chunks,)),
        pltpu.SemaphoreType.DMA((chunks,)),
        pltpu.SemaphoreType.DMA((5, chunks)),
    ]


PARTS = 8
SLAB = STATE // PARTS
UNIT = 2 * BLK
UNITS = INNER // UNIT


class Exchange:
    def __init__(self, held, gathered, joined, incoming, sems):
        self.held, self.gathered, self.joined, self.incoming, self.sems = held, gathered, joined, incoming, sems
        self.me = lax.axis_index("ctx")

    def others(self):
        return [lax.rem(self.me + hop, PARTS) for hop in range(1, PARTS)]

    def greet(self, *further):
        barrier = pltpu.get_barrier_semaphore()
        peers = [{"ctx": other} for other in self.others()] + list(further)
        for peer in peers:
            pl.semaphore_signal(barrier, inc=1, device_id=peer, device_id_type=pl.DeviceIdType.MESH)
        pl.semaphore_wait(barrier, len(peers))

    def copy(self, source, target, kind, group, other):
        return pltpu.make_async_remote_copy(
            src_ref=source,
            dst_ref=target,
            send_sem=self.sems.at[2 * kind, group],
            recv_sem=self.sems.at[2 * kind + 1, group],
            device_id={"ctx": other},
            device_id_type=pl.DeviceIdType.MESH,
        )

    def all_of(self, kind, group):
        source, target = ((self.held, self.gathered), (self.joined, self.incoming))[kind]
        some = pl.ds(0, PARTS - 1)
        return self.copy(source.at[group, some], target.at[group, some], kind, group, self.others()[0])

    def hold(self, group, half, state):
        self.held[group, :, :, half * BLK : (half + 1) * BLK] = state.astype(BF16).reshape(PARTS, SLAB, BLK)

    def spread(self, group):
        self.gathered[group, self.me] = self.held[group, self.me]
        for other in self.others():
            self.copy(self.held.at[group, other], self.gathered.at[group, self.me], 0, group, other).start()

    def join(self, group, kept, forward):
        self.all_of(0, group).wait_recv()
        total = jnp.zeros((SLAB, UNIT), F32)
        for part in range(PARTS) if forward else range(PARTS - 1, -1, -1):
            self.joined[group, part] = total.astype(BF16)
            total = kept[part : part + 1, :] * total + self.gathered[group, part].astype(F32)
        self.incoming[group, self.me] = self.joined[group, self.me]
        for other in self.others():
            self.copy(self.joined.at[group, other], self.incoming.at[group, self.me], 1, group, other).start()

    def finish(self, group):
        self.all_of(1, group).wait_recv()
        self.all_of(0, group).wait_send()
        self.all_of(1, group).wait_send()
        return self.incoming[group].reshape(STATE, UNIT)


def exchange_scratch():
    return [pltpu.VMEM((UNITS, PARTS, SLAB, UNIT), BF16) for _ in range(4)] + [pltpu.SemaphoreType.DMA((4, UNITS))]


def kept_of(kept_ref, unit):
    rows = jnp.concatenate([kept_ref[part, 0:1, :] for part in range(PARTS)], axis=0)
    return jnp.concatenate([widen(rows, chosen(2 * unit)), widen(rows, chosen(2 * unit + 1))], axis=1)


def joined_plainly(states, kept, place, forward):
    factors = jnp.repeat(kept[:, 0, :HEADS], HDIM, axis=1)[:, None, :]
    total = jnp.zeros(states.shape[1:], F32)
    result = total
    count = states.shape[0]
    for part in range(count) if forward else range(count - 1, -1, -1):
        result = jnp.where(place == part, total, result)
        total = factors[part] * total + states[part].astype(F32)
    return result.astype(BF16)


def prepare(
    bc_ref, dt_raw, halo_bc_ref, taps_bc_ref, heads_ref, seg_ref, row_ref, b_ref, c_ref, dt_ref, run_ref, in_ref,
    ext, scores, run_t, b_t, enter, leave,
):
    chunks = bc_ref.shape[0] // Q
    ext[0:PAD, :] = halo_bc_ref[...]
    ext[PAD:, :] = bc_ref[...].astype(F32)
    lane = iota((Q, 128), 1)
    lower = (iota((Q, Q), 1) <= iota((Q, Q), 0)).astype(F32)
    offset = jnp.zeros((1, 128), F32)
    for k in range(chunks):
        rows = slice(k * Q, (k + 1) * Q)
        total = conv_rows(ext, seg_ref, taps_bc_ref, k * Q, Q)
        active = total * sigmoid(total)
        b_rows, c_rows = active[:, :STATE], active[:, STATE:].astype(BF16)
        b_t[:, rows] = b_rows.T.astype(BF16)
        b_rows = b_rows.astype(BF16)
        b_ref[rows, :] = b_rows
        c_ref[rows, :] = c_rows
        scores[rows, :] = masked_scores(seg_ref, row_ref, b_rows, c_rows, k)
        raw = jnp.where(lane < HEADS, dt_raw(rows).astype(F32), 0.0) + heads_ref[0:1, :]
        dt = jnp.maximum(raw, 0.0) + jnp.log1p(jnp.exp(-jnp.abs(raw)))
        log_decay = -dt * jnp.exp(heads_ref[1:2, :])
        running = jnp.dot(lower, log_decay, precision=HIGHEST, preferred_element_type=F32)
        dt_ref[rows, :] = dt
        run_ref[rows, :] = running
        run_t[k] = running.T
        carry, tail = chunk_flags(seg_ref, k)
        enter[rows, :] = jnp.exp(running) * carry
        leave[rows, :] = jnp.exp(running[Q - 1 : Q, :] - running) * tail
        same = (seg_ref[PAD + k * Q : PAD + (k + 1) * Q, :] == seg_ref[PAD - 1 : PAD, :]).astype(F32)
        whole = jnp.exp(running + offset) * same
        in_ref[rows, :] = whole
        offset = offset + running[Q - 1 : Q, :]
    return jnp.broadcast_to(whole[Q - 1 : Q, :], (8, 128))


def front_kernel(
    x_ref, bc_ref, dtraw_ref, halo_ref, halo_bc_ref, taps_ref, taps_bc_ref, heads_ref, seg_ref, row_ref,
    xs_ref, y_ref, state_ref, b_ref, c_ref, dt_ref, run_ref, in_ref, keep_ref,
    ext, scores, run_t, b_t, enter, leave,
):
    step = pl.program_id(0)

    @pl.when(step == 0)
    def _():
        keep_ref[...] = prepare(
            bc_ref, lambda rows: dtraw_ref[rows, :128], halo_bc_ref, taps_bc_ref, heads_ref, seg_ref, row_ref,
            b_ref, c_ref, dt_ref, run_ref, in_ref, ext, scores, run_t, b_t, enter, leave,
        )

    state = local_scan(
        step, x_ref, halo_ref, taps_ref, seg_ref, xs_ref, y_ref, c_ref, dt_ref, run_ref,
        ext, scores, run_t, b_t, enter, leave,
    )
    state_ref[...] = state.astype(BF16)


def local_scan(
    step, x_ref, halo_ref, taps_ref, seg_ref, xs_ref, y_ref, c_ref, dt_ref, run_ref,
    ext, scores, run_t, b_t, enter, leave,
):
    chunks = x_ref.shape[0] // Q
    ext[0:PAD, :] = halo_ref[...]
    ext[PAD:, :] = x_ref[...].astype(F32)
    select = chosen(step)
    state = jnp.zeros((STATE, BLK), F32)
    for k in range(chunks):
        rows = slice(k * Q, (k + 1) * Q)
        total = conv_rows(ext, seg_ref, taps_ref, k * Q, Q)
        values = total * sigmoid(total)
        xs_ref[rows, :] = values.astype(BF16)
        scaled = (values * widen(dt_ref[rows, :], select)).astype(BF16)
        entering = widen(enter[rows, :], select)
        running = pltpu.roll(run_ref[rows, :], lax.rem(128 - step * GROUP, 128), 1)
        parts = []
        for pair in range(2):
            mixing = []
            for one in range(2):
                head = 2 * pair + one
                gap = running[:, head : head + 1] - run_t[k, pl.ds(step * GROUP + head, 1), :]
                mixing.append((jnp.exp(jnp.minimum(gap, 0.0)) * scores[rows, :]).astype(BF16))
            parts.append(
                dot(jnp.concatenate(mixing, axis=1), halves(scaled[:, pair * 128 : (pair + 1) * 128]))
            )
        inside = jnp.concatenate(parts, axis=1)
        y_ref[rows, :] = (inside + entering * dot(c_ref[rows, :], state.astype(BF16))).astype(BF16)
        weighted = (scaled.astype(F32) * widen(leave[rows, :], select)).astype(BF16)
        state = entering[Q - 1 : Q, :] * state + dot(b_t[:, rows], weighted)
    return state


def front_outputs(length, column, state_at, width=BLK):
    whole = lambda *shape: (pl.BlockSpec(shape, lambda j: (0, 0)), shape)
    columns = lambda rows, at: (pl.BlockSpec((rows, width), at), (rows, INNER))
    specs = [
        (columns(length, column), BF16),
        (columns(length, column), BF16),
        (columns(STATE, state_at), BF16),
        (whole(length, 128), BF16),
        (whole(length, 128), BF16),
        (whole(length, 128), F32),
        (whole(length, 128), F32),
        (whole(length, 128), F32),
    ]
    return [spec for (spec, _), _ in specs], [jax.ShapeDtypeStruct(shape, kind) for (_, shape), kind in specs]


def front_scratch(length):
    return [
        pltpu.VMEM((length + PAD, BLK), F32),
        pltpu.VMEM((length, Q), F32),
        pltpu.VMEM((length // Q, 128, Q), F32),
        pltpu.VMEM((128, length), BF16),
        pltpu.VMEM((length, 128), F32),
        pltpu.VMEM((length, 128), F32),
    ]


def front(projected, halo, taps, heads, seg_lanes, seg_row):
    length = projected.shape[0]
    whole = lambda *shape: pl.BlockSpec(shape, lambda j: (0,) * len(shape))
    columns = lambda rows, at: pl.BlockSpec((rows, BLK), at)
    out_specs, out_shape = front_outputs(length, lambda j: (0, j), lambda j: (0, j))
    return pl.pallas_call(
        front_kernel,
        grid=(STEPS,),
        in_specs=[
            columns(length, lambda j: (0, STEPS + j)),
            columns(length, lambda j: (0, 2 * STEPS)),
            columns(length, lambda j: (0, 2 * STEPS + 1)),
            columns(PAD, lambda j: (0, STEPS + j)),
            columns(PAD, lambda j: (0, 2 * STEPS)),
            columns(8, lambda j: (0, j)),
            columns(8, lambda j: (0, STEPS)),
            whole(8, 128),
            whole(length + 2 * PAD, 128),
            whole(1, length),
        ],
        out_specs=[*out_specs, whole(8, 128)],
        out_shape=[*out_shape, jax.ShapeDtypeStruct((8, 128), F32)],
        scratch_shapes=front_scratch(length),
        compiler_params=pltpu.CompilerParams(vmem_limit_bytes=VMEM_LIMIT),
        name="front",
    )(projected, projected, projected, halo, halo, taps, taps, heads, seg_lanes, seg_row)


ORDER = (2 * INNER // WIDE, *range(INNER // WIDE, 2 * INNER // WIDE), *range(INNER // WIDE))
MULTIPLY = 3
SCAN = MULTIPLY + 2
OUT_WIDE = 128
OUT_PIECES = D // OUT_WIDE
OUT_BEGIN, DIRECT = 4, 4
JOIN, DONE = 2, 4
SLOTS = MULTIPLY + len(ORDER)
EDGES = 1 + INNER // WIDE


def chunk_at(position):
    half = INNER // WIDE
    return jnp.where(position == 0, 2 * half, jnp.where(position <= half, position - 1 + half, position - 1 - half))


def forward_kernel(*refs):
    main_ref, shard_ref, units_ref, small_ref, row_ref = refs[:5]
    xs_ref, y_ref, state_ref, b_ref, c_ref, dt_ref, run_ref, in_ref = refs[5:13]
    keep_ref, weight_ref, whole_ref, projected_ref, normed_t_ref = refs[13:18]
    halo_ref, taps_ref, heads_ref, gain_ref, input_gain_ref, seg_ref = refs[18:24]
    ext, scores, run_t, b_t, enter, leave = refs[24:30]
    exchange = Exchange(*refs[30:35])
    own_keep, keeps, keep_sends, keep_arrivals = refs[35:39]
    gathered, loads, sends, arrivals, stores = refs[39:44]
    out_gathered, out_loads, out_sends, out_arrivals, out_stores = refs[44:49]
    normed, blocks, taps, own_small, smalls, seg_tail, seg_head = refs[49:56]
    edges, halos, small_sends, small_arrivals, edge_sends, edge_arrivals = refs[56:]
    step = pl.program_id(0)
    length = units_ref.shape[0]
    shard, part = lax.axis_index("fsdp"), lax.axis_index("ctx")
    others = ({"fsdp": flipped(shard, 1)}, {"fsdp": flipped(shard, 2)}, {"fsdp": flipped(flipped(shard, 1), 2)})
    following = {"ctx": lax.rem(part + 1, PARTS)}

    def place_in(k, s, start, size):
        rows, columns = pl.multiple_of(start, size), pl.multiple_of(s * SHARD, SHARD)
        return gathered.at[k, pl.ds(rows, size), pl.ds(columns, SHARD)]

    def place_out(k, s, start, size):
        return out_gathered.at[k, s, pl.ds(pl.multiple_of(start, size), size)]

    several_in = lambda k, count: gathered.at[k, :, pl.ds(0, count * SHARD)]
    several_out = lambda k, count: out_gathered.at[k, pl.ds(0, count)]
    gather = Gather(place_in, several_in, WIDE, loads, sends, arrivals)
    gather_out = PlainGather(place_out, several_out, 2 * SHARD, out_loads, out_sends, out_arrivals)
    rest = PROJ % WIDE

    def load_rest():
        columns = pl.ds(pl.multiple_of(shard * SHARD, SHARD), SHARD)
        return pltpu.make_async_copy(
            main_ref.at[PROJ - rest : PROJ, :], gathered.at[0, pl.ds(0, rest), columns], loads.at[0]
        )

    def small_copy(hop):
        return remote(own_small, smalls.at[shard], small_sends.at[hop], small_arrivals.at[hop], others[hop])

    def seg_copy():
        return remote(seg_tail, seg_head, small_sends.at[3], small_arrivals.at[3], following)

    def edge_copy(k):
        return remote(edges.at[k], halos.at[k], edge_sends.at[k], edge_arrivals.at[k], following)

    def keep_copy(hop):
        peer = {"ctx": lax.rem(part + hop + 1, PARTS)}
        return remote(own_keep, keeps.at[part], keep_sends.at[hop], keep_arrivals.at[hop], peer)

    def store(k):
        rows = pl.ds(pl.multiple_of(chunk_at(k) * WIDE, WIDE), WIDE)
        return pltpu.make_async_copy(gathered.at[k], weight_ref.at[rows], stores.at[k])

    def store_out(k):
        columns = pl.ds(pl.multiple_of(k * OUT_WIDE, OUT_WIDE), OUT_WIDE)
        return pltpu.make_async_copy(out_gathered.at[k], whole_ref.at[:, :, columns], out_stores.at[k])

    @pl.when(step == 0)
    def _():
        load_rest().start()
        for k, chunk in enumerate(ORDER):
            if k:
                gather.load(k, main_ref.at[chunk * WIDE : (chunk + 1) * WIDE, :]).start()
        for k in range(OUT_PIECES):
            gather_out.load(k, shard_ref.at[:, k * OUT_WIDE : (k + 1) * OUT_WIDE]).start()
        own_small[...] = small_ref[...]
        smalls[shard] = small_ref[...]
        columns = pl.ds(pl.multiple_of(shard * SHARD, SHARD), SHARD)
        gathered[0, rest:, columns] = jnp.zeros((WIDE - rest, SHARD), BF16)
        for k in range(length // 128):
            ids = jnp.broadcast_to(row_ref[0:1, k * 128 : (k + 1) * 128].astype(F32), (128, 128))
            seg_ref[PAD + k * 128 : PAD + (k + 1) * 128, :] = ids.T.astype(jnp.int32)
        seg_tail[...] = seg_ref[length : length + PAD, :]
        exchange.greet(*others)
        for hop in range(3):
            small_copy(hop).start()
        seg_copy().start()
        load_rest().wait()
        gather.send_own(0)
        for k in range(1, AHEAD):
            gather.begin(k)

    def take_small():
        for hop in range(3):
            small_copy(hop).wait()
        seg_copy().wait()
        seg_ref[0:PAD, :] = jnp.where(part == 0, -1, seg_head[...])
        seg_ref[PAD + length :, :] = jnp.full((PAD, 128), -2, jnp.int32)

    def normalise():
        gain = jnp.concatenate([smalls[s, 6:7, :SHARD] for s in range(4)], axis=1)
        input_gain_ref[...] = gain
        for k in range(length // Q):
            rows = slice(k * Q, (k + 1) * Q)
            units = units_ref[rows, :].astype(F32)
            norm = lax.rsqrt(jnp.sum(units * units, axis=1, keepdims=True) * (1.0 / D) + epsilon)
            normed[rows, :] = (units * norm * gain).astype(BF16)

    def take_taps():
        mixer_gain = jnp.concatenate([smalls[s, 5:6, : INNER // 4] for s in range(4)], axis=1)
        gain_ref[...] = jnp.broadcast_to(mixer_gain, (8, INNER))
        whole = jnp.zeros((8, XBC), F32)
        heads = jnp.zeros((8, 128), F32)
        row, lane = iota((8, 128), 0), iota((8, 128), 1)
        own = HEADS // 4
        for s in range(4):
            padded = jnp.concatenate([smalls[s], jnp.zeros((8, XBC - SMALL_WIDTH), F32)], axis=1)
            padded = jnp.where(iota((8, XBC), 1) < XBC // 4, padded, 0.0)
            whole = whole + (pltpu.roll(padded, s * (XBC // 4), 1) if s else padded)
            line = jnp.broadcast_to(smalls[s, 7:8, :128], (8, 128))
            inside = (lane >= s * own) & (lane < (s + 1) * own)
            for kind in range(3):
                shift = (s - kind) * own % 128
                moved = pltpu.roll(line, shift, 1) if shift else line
                heads = jnp.where(inside & (row == kind), moved, heads)
        taps_ref[...] = whole
        heads_ref[...] = heads
        for block in range(STEPS + 1):
            taps[block] = whole[:, block * BLK : (block + 1) * BLK]

    def complete_out(k):
        gather_out.complete(k)
        store_out(k).start()

    def stage(lag, count=len(ORDER)):
        def decorate(body):
            k = step - lag

            @pl.when((k >= 0) & (k < count))
            def _():
                body(k)

        return decorate

    def advance(tick):
        def at(lag, body, first=0, count=len(ORDER)):
            k = tick - lag

            @pl.when((k >= first) & (k < count))
            def _():
                body(k)

        def complete(k):
            gather.complete(k)
            store(k).start()

        at(-AHEAD, gather.begin, AHEAD)
        at(0, gather.first)
        at(1, gather.second)
        at(2, gather.third)
        at(3, complete)
        at(OUT_BEGIN, gather_out.begin, 0, OUT_PIECES)
        at(OUT_BEGIN + 2, gather_out.first, 0, OUT_PIECES)
        at(OUT_BEGIN + 4, gather_out.second, 0, OUT_PIECES)
        at(OUT_BEGIN + 6, complete_out, 0, OUT_PIECES)

    tick = jnp.where(step < SCAN, step, 2 * step - SCAN)
    advance(tick)
    pl.when(step == 0)(take_small)
    pl.when(step == 1)(normalise)
    pl.when(step == 2)(take_taps)

    @stage(MULTIPLY)
    def _(k):
        low = dot_nt(normed[...], gathered[k]).astype(BF16)
        projected_ref[...] = low

        @pl.when(k < EDGES)
        def _():
            edge = low[length - 16 :, :].astype(F32)[8:, :]
            for half in range(2):
                columns = slice(half * BLK, (half + 1) * BLK)
                blocks[2 * k + half] = low[:, columns]
                edges[k, half] = edge[:, columns]
            edge_copy(k).start()

    @stage(SCAN - 1, EDGES)
    def _(k):
        edge_copy(k).wait()
        for half in range(2):
            columns = slice(half * BLK, (half + 1) * BLK)
            halos[k, half] = jnp.where(part == 0, 0.0, halos[k, half])
            halo_ref[:, columns] = halos[k, half]

    @pl.when(step == SCAN - 1)
    def _():
        keep = prepare(
            blocks.at[0], lambda rows: blocks[1, rows, :128], halos.at[0, 0], taps.at[STEPS], heads_ref,
            seg_ref, row_ref, b_ref, c_ref, dt_ref, run_ref, in_ref, ext, scores, run_t, b_t, enter, leave,
        )
        own_keep[...] = keep
        keeps[part] = keep
        for hop in range(PARTS - 1):
            keep_copy(hop).start()

    for half in range(2):

        @stage(SCAN, UNITS)
        def _(unit):
            columns = pl.ds(half * BLK, BLK)
            group = 2 * unit + half
            state = local_scan(
                group, blocks.at[2 + group], halos.at[1 + unit, half], taps.at[group], seg_ref,
                xs_ref.at[:, columns], y_ref.at[:, columns], c_ref, dt_ref, run_ref, ext, scores, run_t, b_t, enter, leave,
            )
            exchange.hold(unit, half, state)

        if half == 0:

            @pl.when(step >= SCAN)
            def _():
                advance(tick + 1)

    stage(SCAN, UNITS)(exchange.spread)

    @pl.when(step == SCAN + JOIN)
    def _():
        for hop in range(PARTS - 1):
            keep_copy(hop).wait()
        keep_ref[...] = keeps[...]

    @stage(SCAN + JOIN, UNITS)
    def _(unit):
        exchange.join(unit, kept_of(keeps, unit), True)

    @stage(SCAN + DONE, UNITS)
    def _(unit):
        state_ref[...] = exchange.finish(unit)

    @pl.when(step == SLOTS - 1)
    def _():
        for k in range(len(ORDER)):
            gather.drain(k)
            store(k).wait()
        for k in range(OUT_PIECES):
            gather_out.drain(k)
            store_out(k).wait()
        for s in range(4):
            columns = slice(s * SHARD, (s + 1) * SHARD)
            normed_t_ref[s] = normed[:, columns].astype(F32).T.astype(BF16)


def forward(in_matrix, out_matrix, units, small, seg_row):
    length = units.shape[0]
    chunks = len(ORDER)
    whole = lambda *shape: pl.BlockSpec(shape, lambda t: (0,) * len(shape))
    once = lambda *shape: pl.BlockSpec(shape, lambda t: (0,) * len(shape), pipeline_mode=pl.Buffered(1))
    anywhere = pl.BlockSpec(memory_space=pl.ANY)
    chunk = lambda rows, lag: pl.BlockSpec((rows, WIDE), lambda t: (0, chunk_at(jnp.clip(t - lag, 0, chunks - 1))))
    unit = lambda lag: lambda t: (0, jnp.clip(t - lag, 0, UNITS - 1))
    out_specs, out_shape = front_outputs(length, unit(SCAN), unit(SCAN + DONE), UNIT)
    shape = jax.ShapeDtypeStruct
    return pl.pallas_call(
        forward_kernel,
        grid=(SLOTS,),
        in_specs=[
            anywhere,
            anywhere,
            once(length, D),
            once(8, SMALL_WIDTH),
            once(1, length),
        ],
        out_specs=[
            *out_specs,
            whole(PARTS, 8, 128),
            anywhere,
            anywhere,
            chunk(length, MULTIPLY),
            once(4, SHARD, length),
            pl.BlockSpec((PAD, WIDE), lambda t: (0, chunk_at(jnp.clip(t - SCAN + 1, 0, EDGES - 1)))),
            whole(8, XBC),
            whole(8, 128),
            whole(8, INNER),
            whole(1, D),
            whole(length + 2 * PAD, 128),
        ],
        out_shape=[
            *out_shape,
            shape((PARTS, 8, 128), F32),
            shape((WIDTH, D), BF16),
            shape((4, 2 * SHARD, D), BF16),
            shape((length, WIDTH), BF16),
            shape((4, SHARD, length), BF16),
            shape((PAD, WIDTH), F32),
            shape((8, XBC), F32),
            shape((8, 128), F32),
            shape((8, INNER), F32),
            shape((1, D), F32),
            shape((length + 2 * PAD, 128), jnp.int32),
        ],
        scratch_shapes=[
            *front_scratch(length),
            *exchange_scratch(),
            pltpu.VMEM((8, 128), F32),
            pltpu.VMEM((PARTS, 8, 128), F32),
            pltpu.SemaphoreType.DMA((PARTS - 1,)),
            pltpu.SemaphoreType.DMA((PARTS - 1,)),
            pltpu.VMEM((chunks, WIDE, D), BF16),
            *gather_sems(chunks),
            pltpu.SemaphoreType.DMA((chunks,)),
            pltpu.VMEM((OUT_PIECES, 4, 2 * SHARD, OUT_WIDE), BF16),
            *gather_sems(OUT_PIECES),
            pltpu.SemaphoreType.DMA((OUT_PIECES,)),
            pltpu.VMEM((length, D), BF16),
            pltpu.VMEM((2 * EDGES, length, BLK), BF16),
            pltpu.VMEM((STEPS + 1, 8, BLK), F32),
            pltpu.VMEM((8, SMALL_WIDTH), F32),
            pltpu.VMEM((4, 8, SMALL_WIDTH), F32),
            pltpu.VMEM((PAD, 128), jnp.int32),
            pltpu.VMEM((PAD, 128), jnp.int32),
            pltpu.VMEM((EDGES, 2, PAD, BLK), F32),
            pltpu.VMEM((EDGES, 2, PAD, BLK), F32),
            pltpu.SemaphoreType.DMA((4,)),
            pltpu.SemaphoreType.DMA((4,)),
            pltpu.SemaphoreType.DMA((EDGES,)),
            pltpu.SemaphoreType.DMA((EDGES,)),
        ],
        compiler_params=communicating(1),
        name="forward",
    )(in_matrix.T, out_matrix, units, small, seg_row)


def tail_kernel(
    y_ref, xs_ref, gate_ref, incoming_ref, out_ref, c_ref, in_ref, heads_ref, gain_ref, g_ref, units_ref,
    mixer_ref, dproj_ref, dy_ref, dsin_ref, sums_ref, block_ref, stats_ref,
    full, dmix, squares, products, mixed, c_t,
):
    step = pl.program_id(0)
    length = y_ref.shape[0]
    group = jnp.where(step < STEPS, step, jnp.minimum(step - STEPS, STEPS - 1))
    select = chosen(group)
    half = length // 2
    @pl.when(step == 0)
    def _():
        squares[...] = jnp.zeros_like(squares)
        products[...] = jnp.zeros_like(products)
        for k in range(length // Q):
            rows = slice(k * Q, (k + 1) * Q)
            c_t[:, rows] = c_ref[rows, :].astype(F32).T.astype(BF16)

    @pl.when(step < STEPS)
    def _():
        incoming = incoming_ref[...]
        skip = widen(heads_ref[...], select)[2:3, :]
        for k in range(2):
            rows = slice(k * half, (k + 1) * half)
            y = y_ref[rows, :].astype(F32)
            y = y + widen(in_ref[rows, :], select) * dot(c_ref[rows, :], incoming)
            y = y + skip * xs_ref[rows, :].astype(F32)
            full[step, rows, :] = y
            gate = gate_ref[rows, :].astype(F32)
            gated = y * gate * sigmoid(gate)
            d_mixer = dot_nt(g_ref[rows, :], out_ref[...])
            dmix[step, rows, :] = d_mixer
            square = gated * gated
            product = gated * d_mixer * gain_ref[0:1, :]
            squares[rows, :] += square[:, :128] + square[:, 128:]
            products[rows, :] += product[:, :128] + product[:, 128:]

    @pl.when(step == STEPS)
    def _():
        norm = lax.rsqrt(jnp.sum(squares[...], axis=1, keepdims=True) * (1.0 / INNER) + epsilon)
        mean = norm * jnp.sum(products[...], axis=1, keepdims=True) * (1.0 / INNER)
        squares[...] = jnp.broadcast_to(norm, squares.shape)
        products[...] = jnp.broadcast_to(mean, products.shape)

    @pl.when((step >= STEPS) & (step < 2 * STEPS))
    def _():
        gain = gain_ref[0:1, :]
        d_gain = jnp.zeros((1, BLK), F32)
        d_skip = jnp.zeros((1, BLK), F32)
        d_state = jnp.zeros((STATE, BLK), F32)
        for k in range(2):
            rows = slice(k * half, (k + 1) * half)
            norm, mean = both(squares[rows, :]), both(products[rows, :])
            y = full[group, rows, :]
            d_mixer = dmix[group, rows, :]
            gate = gate_ref[rows, :].astype(F32)
            sig = sigmoid(gate)
            silu = gate * sig
            unit = y * silu * norm
            low = (unit * gain).astype(BF16)
            mixer_ref[:, rows] = (unit * gain).T.astype(BF16)
            part = dot(low, out_ref[...])

            @pl.when(step == STEPS)
            def _():
                mixed[rows, :] = part

            @pl.when(step > STEPS)
            def _():
                mixed[rows, :] += part

            d_gain = d_gain + jnp.sum(d_mixer * unit, axis=0, keepdims=True)
            d_gated = norm * (d_mixer * gain - unit * mean)
            dproj_ref[rows, :] = (d_gated * y * (sig * (1.0 + gate * (1.0 - sig)))).astype(BF16)
            dy = (d_gated * silu).astype(BF16)
            dy_ref[rows, :] = dy
            dy = dy.astype(F32)
            d_skip = d_skip + jnp.sum(dy * xs_ref[rows, :].astype(F32), axis=0, keepdims=True)
            d_state = d_state + dot(c_t[:, rows], (dy * widen(in_ref[rows, :], select)).astype(BF16))
        dsin_ref[...] = d_state.astype(BF16)
        sums_ref[...] = jnp.concatenate([d_gain, d_skip, jnp.zeros((6, BLK), F32)], axis=0)

    @pl.when(step == 2 * STEPS - 1)
    def _():
        total = units_ref[...].astype(F32) + mixed[...]
        block_ref[...] = total.astype(BF16)
        first = jnp.sum(total * total, axis=0, keepdims=True)
        second = jnp.sum(mixed[...] * mixed[...], axis=0, keepdims=True)
        stats_ref[...] = jnp.concatenate([first, second, jnp.zeros((6, D), F32)], axis=0)


def tail(y, xs, projected, incoming, out_whole, c_rows, entering, heads, gain, cot, units):
    length = y.shape[0]
    group = lambda i: jnp.where(i < STEPS, i, jnp.minimum(i - STEPS, STEPS - 1))
    second = lambda i: jnp.clip(i - STEPS, 0, STEPS - 1)
    early = lambda rows: pl.BlockSpec((rows, BLK), lambda i: (0, jnp.minimum(i, STEPS - 1)))
    late = lambda rows: pl.BlockSpec((rows, BLK), lambda i: (0, second(i)))
    each = lambda rows: pl.BlockSpec((rows, BLK), lambda i: (0, group(i)))
    whole = lambda *shape: pl.BlockSpec(shape, lambda i: (0,) * len(shape))
    return pl.pallas_call(
        tail_kernel,
        grid=(2 * STEPS,),
        in_specs=[
            early(length),
            each(length),
            each(length),
            early(STATE),
            pl.BlockSpec((BLK, D), lambda i: (group(i), 0)),
            whole(length, 128),
            whole(length, 128),
            whole(8, 128),
            each(8),
            whole(length, D),
            whole(length, D),
        ],
        out_specs=[
            pl.BlockSpec((BLK, length), lambda i: (second(i), 0)),
            late(length),
            late(length),
            pl.BlockSpec((STATE, BLK), lambda i: (0, second(i))),
            late(8),
            whole(length, D),
            whole(8, D),
        ],
        out_shape=[
            jax.ShapeDtypeStruct((INNER, length), BF16),
            jax.ShapeDtypeStruct((length, WIDTH), BF16),
            jax.ShapeDtypeStruct((length, INNER), BF16),
            jax.ShapeDtypeStruct((STATE, INNER), BF16),
            jax.ShapeDtypeStruct((8, INNER), F32),
            jax.ShapeDtypeStruct((length, D), BF16),
            jax.ShapeDtypeStruct((8, D), F32),
        ],
        scratch_shapes=[
            pltpu.VMEM((STEPS, length, BLK), F32),
            pltpu.VMEM((STEPS, length, BLK), F32),
            pltpu.VMEM((length, 128), F32),
            pltpu.VMEM((length, 128), F32),
            pltpu.VMEM((length, D), F32),
            pltpu.VMEM((128, length), BF16),
        ],
        compiler_params=pltpu.CompilerParams(vmem_limit_bytes=VMEM_LIMIT),
        cost_estimate=pl.CostEstimate(
            flops=12 * 10**9, bytes_accessed=50 * 10**6, transcendentals=4 * 10**6
        ),
        name="tail",
    )(y, xs, projected, incoming, out_whole, c_rows, entering, heads, gain, cot, units)


def back_steps(step, given, scratch, write, write_halo, write_taps, write_heads):
    (
        x_ref, dtraw_ref, halo_ref, taps_ref, heads_ref, seg_ref, row_ref, b_ref, c_ref, dt_ref, run_ref, dy_ref, sin_ref, dout_ref,
    ) = given
    (
        ext, pre, dact, dbuf, scores, dscores, run_t, b_t, c_t, enter, leave, d_b, d_c, suffix, prefix, d_dt, fixed, states,
    ) = scratch
    length = x_ref.shape[0]
    chunks = length // Q

    @pl.when(step == 0)
    def _():
        for k in range(chunks):
            rows = slice(k * Q, (k + 1) * Q)
            b_rows, c_rows = b_ref[rows, :], c_ref[rows, :]
            b_t[:, rows] = b_rows.astype(F32).T.astype(BF16)
            c_t[:, rows] = c_rows.astype(F32).T.astype(BF16)
            scores[rows, :] = masked_scores(seg_ref, row_ref, b_rows, c_rows, k)
            running = run_ref[rows, :]
            run_t[k] = running.T
            carry, tail = chunk_flags(seg_ref, k)
            enter[rows, :] = jnp.exp(running) * carry
            leave[rows, :] = jnp.exp(running[Q - 1 : Q, :] - running) * tail
        for each in (dscores, d_b, d_c, suffix, prefix, d_dt, fixed):
            each[...] = jnp.zeros_like(each)
        dbuf[0:PAD, :] = jnp.zeros((PAD, BLK), F32)
        dbuf[PAD + length :, :] = jnp.zeros((PAD, BLK), F32)

    @pl.when(step <= STEPS)
    def _():
        ext[0:PAD, :] = halo_ref[...]
        ext[PAD:, :] = x_ref[...].astype(F32)
        for k in range(chunks):
            pre[k * Q : (k + 1) * Q, :] = conv_rows(ext, seg_ref, taps_ref, k * Q, Q)

    @pl.when(step < STEPS)
    def _():
        select = chosen(step)
        gather = chosen_back(step)
        skip = widen(heads_ref[...], select)[2:3, :]
        state = sin_ref[...].astype(F32)
        for k in range(chunks):
            rows = slice(k * Q, (k + 1) * Q)
            states[k] = state
            if k + 1 < chunks:
                total = pre[rows, :]
                scaled = total * sigmoid(total) * widen(dt_ref[rows, :], select)
                weighted = (scaled.astype(BF16).astype(F32) * widen(leave[rows, :], select)).astype(BF16)
                last = widen(enter[rows.stop - 8 : rows.stop, :], select)[7:8, :]
                state = last * state + dot(b_t[:, rows], weighted)
        d_state = dout_ref[...].astype(F32)
        for k in range(chunks - 1, -1, -1):
            rows = slice(k * Q, (k + 1) * Q)
            total = pre[rows, :]
            values = total * sigmoid(total)
            step_size = widen(dt_ref[rows, :], select)
            entering = widen(enter[rows, :], select)
            leaving = widen(leave[rows, :], select)
            scaled = (values * step_size).astype(BF16)
            scaled_wide = scaled.astype(F32)
            dy = dy_ref[rows, :]
            dy_wide = dy.astype(F32)
            before = states[k]
            before_low = before.astype(BF16)
            d_low = d_state.astype(BF16)
            running = pltpu.roll(run_ref[rows, :], lax.rem(128 - step * GROUP, 128), 1)
            insides, backs = [], []
            d_score = dscores[rows, :]
            for pair in range(2):
                lanes = slice(pair * 128, (pair + 1) * 128)
                mixing, turned, decays = [], [], []
                for one in range(2):
                    head = 2 * pair + one
                    gap = running[:, head : head + 1] - run_t[k, pl.ds(step * GROUP + head, 1), :]
                    decay = jnp.exp(jnp.minimum(gap, 0.0))
                    mixed = decay * scores[rows, :]
                    decays.append(decay)
                    mixing.append(mixed.astype(BF16))
                    turned.append(mixed.T.astype(BF16))
                spread = halves(scaled[:, lanes])
                insides.append(dot(jnp.concatenate(mixing, axis=1), spread))
                backs.append(dot(jnp.concatenate(turned, axis=1), halves(dy[:, lanes])))
                products = dot_nt(dy[:, lanes], spread)
                d_score = d_score + decays[0] * products[:, :Q] + decays[1] * products[:, Q:]
            dscores[rows, :] = d_score
            inside = jnp.concatenate(insides, axis=1) + entering * dot(c_ref[rows, :], before_low)
            back_inside = jnp.concatenate(backs, axis=1)
            back_state = leaving * dot(b_ref[rows, :], d_low)
            high, low = in_two(dy_wide * inside - scaled_wide * back_inside)
            suffix[rows, :] += dot(high, gather) + dot(low, gather)
            prefix[rows, :] += dot((scaled_wide * back_state).astype(BF16), gather)
            back = back_inside + back_state
            d_dt[rows, :] += dot((values * back).astype(BF16), gather)
            entered = (dy_wide * entering).astype(BF16)
            d_c[rows, :] += dot_nt(entered, before_low)
            d_b[rows, :] += dot_nt((scaled_wide * leaving).astype(BF16), d_low)
            kept = entering[Q - 1 : Q, :]
            through = jnp.sum(before * d_state, axis=0, keepdims=True) * kept
            high, low = in_two(jnp.broadcast_to(through, (8, BLK)))
            fixed[k * 8 : (k + 1) * 8, :] += dot(high, gather) + dot(low, gather)
            d_state = kept * d_state + dot(c_t[:, rows], entered)
            dact[rows, :] = back * step_size + skip * dy_wide

    @pl.when(step == STEPS)
    def _():
        for k in range(chunks):
            rows = slice(k * Q, (k + 1) * Q)
            own = seg_ref[PAD + k * Q : PAD + (k + 1) * Q, :]
            keep = (own == row_ref[0:1, rows]) & (iota((Q, Q), 1) <= iota((Q, Q), 0))
            d_score = jnp.where(keep, dscores[rows, :], 0.0)
            dact[rows, STATE:] = d_c[rows, :] + dot(d_score.astype(BF16), b_ref[rows, :])
            dact[rows, :STATE] = d_b[rows, :] + dot(d_score.T.astype(BF16), c_ref[rows, :])

    @pl.when(step <= STEPS)
    def _():
        sums = [jnp.zeros((1, BLK), F32) for _ in range(CONV + 1)]
        for k in range(chunks):
            rows = slice(k * Q, (k + 1) * Q)
            total = pre[rows, :]
            sig = sigmoid(total)
            d_conv = dact[rows, :] * (sig * (1.0 + total * (1.0 - sig)))
            dbuf[PAD + k * Q : PAD + (k + 1) * Q, :] = d_conv
            sums[4] = sums[4] + jnp.sum(d_conv, axis=0, keepdims=True)
            own = seg_ref[PAD + k * Q : PAD + (k + 1) * Q, :]
            for shift in range(CONV):
                at = PAD + k * Q - shift
                term = d_conv * ext[at : at + Q, :]
                if shift:
                    term = jnp.where(both(seg_ref[at : at + Q, :] == own), term, 0.0)
                sums[3 - shift] = sums[3 - shift] + jnp.sum(term, axis=0, keepdims=True)
        write_taps(jnp.concatenate(sums + [jnp.zeros((3, BLK), F32)], axis=0))

        def returned(at, rows):
            own = seg_ref[at : at + rows, :]
            result = taps_ref[3:4, :] * dbuf[at : at + rows, :]
            for shift in range(1, CONV):
                same = both(seg_ref[at + shift : at + shift + rows, :] == own)
                result = result + jnp.where(
                    same, taps_ref[3 - shift : 4 - shift, :] * dbuf[at + shift : at + shift + rows, :], 0.0
                )
            return result

        write_halo(returned(0, PAD))
        for k in range(chunks):
            write(slice(k * Q, (k + 1) * Q), returned(PAD + k * Q, Q).astype(BF16))

    @pl.when(step == STEPS + 1)
    def _():
        lower = (iota((Q, Q), 1) < iota((Q, Q), 0)).astype(F32)
        upper = (iota((Q, Q), 1) >= iota((Q, Q), 0)).astype(F32)
        lane = iota((Q, 128), 1)
        rate = jnp.exp(heads_ref[1:2, :])
        bias_sum = jnp.zeros((1, 128), F32)
        decay_sum = jnp.zeros((1, 128), F32)
        for k in range(chunks):
            rows = slice(k * Q, (k + 1) * Q)
            d_log = jnp.dot(upper, suffix[rows, :], precision=HIGHEST, preferred_element_type=F32)
            d_log = d_log + jnp.dot(lower, prefix[rows, :], precision=HIGHEST, preferred_element_type=F32)
            d_log = d_log + fixed[k * 8 : k * 8 + 1, :]
            raw = jnp.where(lane < HEADS, dtraw_ref[rows, :128].astype(F32), 0.0) + heads_ref[0:1, :]
            d_raw = jnp.where(lane < HEADS, (d_dt[rows, :] - rate * d_log) * sigmoid(raw), 0.0)
            bias_sum = bias_sum + jnp.sum(d_raw, axis=0, keepdims=True)
            decay_sum = decay_sum - jnp.sum(d_log * dt_ref[rows, :] * rate, axis=0, keepdims=True)
            write(rows, jnp.concatenate([d_raw, jnp.zeros_like(d_raw)], axis=1).astype(BF16))
        write_heads(jnp.concatenate([bias_sum, decay_sum, jnp.zeros((6, 128), F32)], axis=0))


def back_kernel(*refs):
    given, (_, dproj_ref, dhalo_ref, dtaps_ref, dheads_ref), scratch = refs[:14], refs[14:19], refs[19:]

    def write(rows, value):
        dproj_ref[rows, :] = value

    def write_halo(value):
        dhalo_ref[...] = value

    def write_taps(value):
        dtaps_ref[...] = value

    def write_heads(value):
        dheads_ref[...] = value

    back_steps(pl.program_id(0), given, scratch, write, write_halo, write_taps, write_heads)


def back_scratch(length):
    return [
        pltpu.VMEM((length + PAD, BLK), F32),
        pltpu.VMEM((length, BLK), F32),
        pltpu.VMEM((length, BLK), F32),
        pltpu.VMEM((length + 2 * PAD, BLK), F32),
        pltpu.VMEM((length, Q), F32),
        pltpu.VMEM((length, Q), F32),
        pltpu.VMEM((length // Q, 128, Q), F32),
        pltpu.VMEM((128, length), BF16),
        pltpu.VMEM((128, length), BF16),
        *[pltpu.VMEM((length, 128), F32) for _ in range(7)],
        pltpu.VMEM((8 * (length // Q), 128), F32),
        pltpu.VMEM((length // Q, STATE, BLK), F32),
    ]


def back_inputs(length, late=0):
    whole = lambda *shape: pl.BlockSpec(shape, lambda j: (0,) * len(shape))
    upto = lambda last, first=0: lambda j: (0, first + jnp.clip(j - late, 0, last))
    return [
        pl.BlockSpec((length, BLK), upto(STEPS, STEPS)),
        pl.BlockSpec((length, BLK), lambda j: (0, 2 * STEPS + 1)),
        pl.BlockSpec((PAD, BLK), upto(STEPS, STEPS)),
        pl.BlockSpec((8, BLK), upto(STEPS)),
        whole(8, 128),
        whole(length + 2 * PAD, 128),
        whole(1, length),
        whole(length, 128),
        whole(length, 128),
        whole(length, 128),
        whole(length, 128),
        pl.BlockSpec((length, BLK), upto(STEPS - 1)),
        pl.BlockSpec((STATE, BLK), upto(STEPS - 1)),
        whole(STATE, INNER) if late else pl.BlockSpec((STATE, BLK), upto(STEPS - 1)),
    ]


def back(given, dproj):
    length = dproj.shape[0]
    upto = lambda last, first=0: lambda j: (0, first + jnp.minimum(j, last))
    return pl.pallas_call(
        back_kernel,
        grid=(STEPS + 2,),
        in_specs=[*back_inputs(length), pl.BlockSpec(memory_space=pl.ANY)],
        out_specs=[
            pl.BlockSpec((length, BLK), lambda j: (0, STEPS + j)),
            pl.BlockSpec((PAD, BLK), upto(STEPS)),
            pl.BlockSpec((8, BLK), upto(STEPS)),
            pl.BlockSpec((8, 128), lambda j: (0, 0)),
        ],
        out_shape=[
            jax.ShapeDtypeStruct((length, WIDTH), BF16),
            jax.ShapeDtypeStruct((PAD, XBC), F32),
            jax.ShapeDtypeStruct((8, XBC), F32),
            jax.ShapeDtypeStruct((8, 128), F32),
        ],
        scratch_shapes=back_scratch(length),
        input_output_aliases={14: 0},
        compiler_params=pltpu.CompilerParams(vmem_limit_bytes=VMEM_LIMIT),
        name="back",
    )(*given, dproj)


OUT_CHUNKS = 2 * D // WIDE
GATE_CHUNKS = INNER // WIDE
IN_CHUNKS = WIDTH // WIDE
CHUNKS = OUT_CHUNKS + IN_CHUNKS
LAGS = 8
RING = 8
LATE = 3


def small_sums(taps, columns, input_gain, heads, stats):
    fill = lambda width: jnp.zeros((1, width), F32)
    squares = [jnp.broadcast_to(jnp.sum(stats[i : i + 1], axis=1, keepdims=True), (1, 128)) for i in range(2)]
    return jnp.concatenate(
        [
            taps[:5],
            jnp.concatenate([columns[0:1], fill(XBC - INNER)], axis=1),
            jnp.concatenate([columns[1:2], fill(XBC - INNER)], axis=1),
            jnp.concatenate([input_gain, heads[0:1], heads[1:2], *squares, fill(XBC - D - 512)], axis=1),
        ],
        axis=0,
    )


def finish_kernel(*refs):
    given, refs = refs[:14], refs[14:]
    lhs_in, lhs_out, gate_ref, weight_ref, cot_ref, units_ref, gain_ref, columns_ref, stats_ref, kept_ref = refs[:10]
    din_ref, dout_ref, input_grad_ref, total_ref = refs[10:14]
    scratch, refs = refs[14:32], refs[32:]
    exchange, outgoing, refs = Exchange(*refs[:5]), refs[5], refs[6:]
    grads, edges, halos, taps, heads, d_normed = refs[:6]
    own, core_send, core_recv, y_recv, x_recv, z_recv, w_recv, final, small_send, small_recv = refs[6:16]
    send_sems, recv_sems, small_send_sems, small_recv_sems, edge_sends, edge_arrivals = refs[16:]
    step = pl.program_id(0)
    length = cot_ref.shape[0]
    shard, part = lax.axis_index("fsdp"), lax.axis_index("ctx")
    core, y = lax.rem(shard, 2), shard // 2
    x, z = lax.rem(part, 2), part // 2
    near, far = lax.rem(z, 2), z // 2
    peers = (
        {"fsdp": flipped(shard, 1)},
        {"fsdp": flipped(shard, 2)},
        {"ctx": flipped(part, 1)},
        {"ctx": flipped(part, 2)},
        {"ctx": flipped(part, 4)},
    )
    preceding = lax.rem(part + PARTS - 1, PARTS)

    def ring(k):
        return lax.rem(k, RING)

    def sent(stage, k, source, target, peer):
        return remote(source, target, send_sems.at[stage, k], recv_sems.at[stage, k], peers[peer])

    copies = (
        lambda k: sent(0, k, core_send.at[lax.rem(k, 2)], core_recv.at[ring(k)], 0),
        lambda k: sent(1, k, core_recv.at[ring(k), 1 - y], y_recv.at[ring(k)], 1),
        lambda k: sent(2, k, y_recv.at[ring(k), 1 - x], x_recv.at[ring(k)], 2),
        lambda k: sent(3, k, x_recv.at[ring(k), 1 - near], z_recv.at[ring(k)], 3),
        lambda k: sent(4, k, z_recv.at[ring(k), 1 - far], w_recv.at[ring(k)], 4),
        lambda k: sent(5, k, final.at[ring(k), x, near, far], final.at[ring(k), x, near, far], 4),
        lambda k: sent(6, k, final.at[ring(k), x, near], final.at[ring(k), x, near], 3),
        lambda k: sent(7, k, final.at[ring(k), x], final.at[ring(k), x], 2),
    )
    arrivals = copies[:5] + (
        lambda k: sent(5, k, final.at[ring(k), x, near, 1 - far], final.at[ring(k), x, near, 1 - far], 4),
        lambda k: sent(6, k, final.at[ring(k), x, 1 - near], final.at[ring(k), x, 1 - near], 3),
        lambda k: sent(7, k, final.at[ring(k), 1 - x], final.at[ring(k), 1 - x], 2),
    )

    def small_copy(stage):
        return remote(
            small_send.at[stage], small_recv.at[stage], small_send_sems.at[stage], small_recv_sems.at[stage], peers[stage]
        )

    def edge_copy(block):
        return remote(
            edges.at[block], halos.at[block], edge_sends.at[block], edge_arrivals.at[block], {"ctx": preceding}
        )

    @pl.when(step == 0)
    def _():
        exchange.greet(peers[0], peers[1])
        for group in range(STEPS):
            exchange.hold(group // 2, group % 2, given[13][:, group * BLK : (group + 1) * BLK])
            if group % 2:
                exchange.spread(group // 2)
        d_normed[...] = jnp.zeros_like(d_normed)

    def partial(lhs_of, rhs):
        for row in range(2):
            value = dot(lhs_of(2 * row + 1 - core), rhs).astype(BF16)
            core_send[lax.rem(step, 2), row] = value.reshape(2, 2, 2, PIECE, WIDE)
        copies[0](step).start()
        for row in range(2):
            own[row] = dot(lhs_of(2 * row + core), rhs).reshape(2, 2, 2, PIECE, WIDE)

    def in_chunk(rhs):
        partial(lambda s: lhs_in[s], rhs)
        d_normed[...] += dot(rhs, weight_ref[...])

    @pl.when(step < OUT_CHUNKS)
    def _():
        columns = lax.rem(step, D // WIDE) * WIDE
        rhs = cot_ref[:, pl.ds(pl.multiple_of(columns, WIDE), WIDE)]
        partial(lambda s: lhs_out[s, step // (D // WIDE)], rhs)

    @pl.when((step >= OUT_CHUNKS) & (step < OUT_CHUNKS + GATE_CHUNKS))
    def _():
        in_chunk(gate_ref[...])

    @pl.when((step >= OUT_CHUNKS + GATE_CHUNKS) & (step < CHUNKS))
    def _():
        first = 2 * (step - OUT_CHUNKS - GATE_CHUNKS)
        for done in (first, first + 1):

            @pl.when(done <= STEPS)
            def _():
                edge_copy(done).wait()
                tail = slice(length - 16, length)
                more = jnp.where(part == PARTS - 1, 0.0, halos[done])
                more = jnp.concatenate([jnp.zeros_like(more), more], axis=0)
                grads[done, tail, :] = (grads[done, tail, :].astype(F32) + more).astype(BF16)

        in_chunk(jnp.concatenate([grads[first], grads[first + 1]], axis=1))

    for half in range(2):

        @pl.when(step == 1 + half)
        def _():
            for unit in range(half * UNITS // 2, (half + 1) * UNITS // 2):
                exchange.join(unit, kept_of(kept_ref, unit), False)

    block = step - LATE

    def write(rows, value):
        grads[block, rows, :] = value

    def write_halo(value):
        edges[block] = value
        edge_copy(block).start()

    def write_taps(value):
        taps[block] = value

    def write_heads(value):
        heads[...] = value

    @pl.when((block >= 0) & (block < STEPS) & (lax.rem(block, 2) == 0))
    def _():
        both_groups = exchange.finish(block // 2)
        outgoing[0] = both_groups[:, :BLK]
        outgoing[1] = both_groups[:, BLK:]

    @pl.when(block >= 0)
    def _():
        back_steps(block, (*given[:13], outgoing.at[lax.rem(block, 2)]), scratch, write, write_halo, write_taps, write_heads)

    @pl.when(step < CHUNKS)
    def _():
        arrivals[0](step).wait_recv()
        for row in (1 - y, y):
            core_recv[ring(step), row] = (own[row] + core_recv[ring(step), row].astype(F32)).astype(BF16)
        copies[1](step).start()

    def stage(lag):
        def decorate(body):
            k = step - lag

            @pl.when((k >= 0) & (k < CHUNKS))
            def _():
                body(k, ring(k))

        return decorate

    def summed(a, b):
        return (a.astype(F32) + b.astype(F32)).astype(BF16)

    @stage(1)
    def _(k, at):
        arrivals[1](k).wait_recv()
        y_recv[at] = summed(y_recv[at], core_recv[at, y])
        copies[2](k).start()
        copies[0](k).wait_send()

    @stage(2)
    def _(k, at):
        arrivals[2](k).wait_recv()
        x_recv[at] = summed(x_recv[at], y_recv[at, x])
        copies[3](k).start()

    @stage(3)
    def _(k, at):
        arrivals[3](k).wait_recv()
        z_recv[at] = summed(z_recv[at], x_recv[at, near])
        copies[4](k).start()
        copies[1](k).wait_send()

    @stage(4)
    def _(k, at):
        arrivals[4](k).wait_recv()
        final[at, x, near, far] = summed(w_recv[at], z_recv[at, far])
        copies[5](k).start()
        copies[2](k).wait_send()

    @stage(5)
    def _(k, at):
        arrivals[5](k).wait_recv()
        copies[6](k).start()
        copies[3](k).wait_send()

    @stage(6)
    def _(k, at):
        arrivals[6](k).wait_recv()
        copies[7](k).start()
        copies[4](k).wait_send()

    @stage(7)
    def _(k, at):
        arrivals[7](k).wait_recv()
        for one in (5, 6, 7):
            copies[one](k).wait_send()
        whole = final[at].reshape(SHARD, WIDE)

        @pl.when(k < OUT_CHUNKS)
        def _():
            dout_ref[...] = whole

        @pl.when(k >= OUT_CHUNKS)
        def _():
            din_ref[...] = whole.astype(F32).T.astype(BF16)

    @pl.when(step == CHUNKS)
    def _():
        input_gain = jnp.zeros((1, D), F32)
        for k in range(length // Q):
            rows = slice(k * Q, (k + 1) * Q)
            units = units_ref[rows, :].astype(F32)
            norm = lax.rsqrt(jnp.sum(units * units, axis=1, keepdims=True) * (1.0 / D) + epsilon)
            base = units * norm
            grad = d_normed[rows, :]
            input_gain = input_gain + jnp.sum(grad * base, axis=0, keepdims=True)
            scaled = grad * gain_ref[0:1, :]
            mean = jnp.sum(scaled * base, axis=1, keepdims=True) * (1.0 / D)
            input_grad_ref[rows, :] = (cot_ref[rows, :].astype(F32) + norm * (scaled - base * mean)).astype(BF16)
        whole = jnp.concatenate([taps[one] for one in range(STEPS + 1)], axis=1)
        small_send[0] = small_sums(whole, columns_ref[...], input_gain, heads[...], stats_ref[...])
        small_copy(0).start()

    for stage_of_small in range(5):

        @pl.when(step == CHUNKS + 1 + stage_of_small)
        def _():
            small_copy(stage_of_small).wait()
            total = small_send[stage_of_small] + small_recv[stage_of_small]
            if stage_of_small < 4:
                small_send[stage_of_small + 1] = total
                small_copy(stage_of_small + 1).start()
            else:
                total_ref[...] = total


def finish(given, normed_t, mixer_t, dproj, w_turned, cot, units, input_gain, column_sums, stats, kept):
    length = cot.shape[0]
    per_half = D // WIDE
    once = pl.Buffered(1)
    whole = lambda *shape: pl.BlockSpec(shape, lambda t: (0,) * len(shape), pipeline_mode=once)
    in_chunk = lambda t: jnp.clip(t - OUT_CHUNKS, 0, IN_CHUNKS - 1)

    def out_block(t):
        k = jnp.clip(t - LAGS + 1, 0, OUT_CHUNKS - 1)
        return (k // per_half, lax.rem(k, per_half))

    slots = lambda *shape: pltpu.VMEM((RING, *shape, PIECE, WIDE), BF16)
    return pl.pallas_call(
        finish_kernel,
        grid=(CHUNKS + LAGS - 1,),
        in_specs=[
            *back_inputs(length, LATE),
            whole(4, SHARD, length),
            whole(4, 2, SHARD, length),
            pl.BlockSpec((length, WIDE), lambda t: (0, jnp.minimum(in_chunk(t), GATE_CHUNKS - 1))),
            pl.BlockSpec((WIDE, D), lambda t: (in_chunk(t), 0)),
            whole(length, D),
            whole(length, D),
            whole(1, D),
            whole(8, INNER),
            whole(8, D),
            whole(PARTS, 8, 128),
        ],
        out_specs=[
            pl.BlockSpec((WIDE, SHARD), lambda t: (in_chunk(t - LAGS + 1), 0)),
            pl.BlockSpec((SHARD, WIDE), out_block),
            pl.BlockSpec((length, D), lambda t: (0, 0)),
            pl.BlockSpec((8, XBC), lambda t: (0, 0)),
        ],
        out_shape=[
            jax.ShapeDtypeStruct((PROJ, SHARD), BF16),
            jax.ShapeDtypeStruct((2 * SHARD, D), BF16),
            jax.ShapeDtypeStruct((length, D), BF16),
            jax.ShapeDtypeStruct((8, XBC), F32),
        ],
        scratch_shapes=[
            *back_scratch(length),
            *exchange_scratch(),
            pltpu.VMEM((2, STATE, BLK), BF16),
            pltpu.VMEM((STEPS + 2, length, BLK), BF16),
            pltpu.VMEM((STEPS + 1, PAD, BLK), F32),
            pltpu.VMEM((STEPS + 1, PAD, BLK), F32),
            pltpu.VMEM((STEPS + 1, 8, BLK), F32),
            pltpu.VMEM((8, 128), F32),
            pltpu.VMEM((length, D), F32),
            pltpu.VMEM((2, 2, 2, 2, PIECE, WIDE), F32),
            pltpu.VMEM((2, 2, 2, 2, 2, PIECE, WIDE), BF16),
            slots(2, 2, 2, 2),
            slots(2, 2, 2),
            slots(2, 2),
            slots(2),
            slots(),
            slots(2, 2, 2),
            pltpu.VMEM((5, 8, XBC), F32),
            pltpu.VMEM((5, 8, XBC), F32),
            pltpu.SemaphoreType.DMA((8, CHUNKS)),
            pltpu.SemaphoreType.DMA((8, CHUNKS)),
            pltpu.SemaphoreType.DMA((5,)),
            pltpu.SemaphoreType.DMA((5,)),
            pltpu.SemaphoreType.DMA((STEPS + 1,)),
            pltpu.SemaphoreType.DMA((STEPS + 1,)),
        ],
        compiler_params=communicating(0),
        name="finish",
    )(*given, normed_t, mixer_t, dproj, w_turned, cot, units, input_gain, column_sums, stats, kept)


def passed_along(block, axis, distance):
    devices = range(lax.axis_size(axis))
    route = [(i - distance, i) for i in devices if i - distance in devices]
    return lax.ppermute(block, axis, route)


def pack_small(conv_taps, conv_bias, dt_bias, decay_log, skip_scale, mixer_gain, input_gain):
    width = conv_bias.shape[0]

    def line(*parts):
        flat = jnp.concatenate(parts)
        return jnp.pad(flat, (0, width - flat.shape[0]))[None]

    rows = jnp.concatenate(
        [
            conv_taps.T,
            conv_bias[None],
            line(mixer_gain),
            line(input_gain),
            line(dt_bias, decay_log, skip_scale),
        ],
        axis=0,
    )
    return jnp.pad(rows.astype(F32), ((0, 0), (0, SMALL_WIDTH - width)))


def unpack_small(whole, width):
    shards = whole.shape[0]
    joined = jnp.swapaxes(whole, 0, 1)
    taps = jnp.pad(joined[:5, :, :width].reshape(5, shards * width).astype(F32), ((0, 3), (0, 0)))
    gain = joined[5, :, : INNER // shards].reshape(1, INNER).astype(F32)
    input_gain = joined[6, :, : D // shards].reshape(1, D).astype(F32)
    own = HEADS // shards
    heads = joined[7, :, : 3 * own].reshape(shards, 3, own).swapaxes(0, 1).reshape(3, HEADS)
    heads = jnp.pad(heads.astype(F32), ((0, 5), (0, 128 - HEADS)))
    return taps, jnp.pad(gain, ((0, 7), (0, 0))), input_gain, heads


def on_device(
    inputs,
    segment_ids,
    out_grad,
    in_matrix,
    out_matrix,
    conv_taps,
    conv_bias,
    dt_bias,
    decay_log,
    skip_scale,
    mixer_gain,
    input_gain,
):
    shards, parts = lax.axis_size("fsdp"), lax.axis_size("ctx")
    place = lax.axis_index("ctx")
    units_low, cot = inputs[0], out_grad[0]
    seg_ids = segment_ids[0]
    length = units_low.shape[0]
    here = (shards, parts) == (4, PARTS)
    small = pack_small(conv_taps, conv_bias, dt_bias, decay_log, skip_scale, mixer_gain, input_gain)
    seg_row = segment_ids
    if here:
        (
            xs, y_local, incoming, b_rows, c_rows, dt, running, entering,
            kept, w_turned, out_whole, projected, normed_t, halo, taps, heads, gain, g_float, seg_lanes,
        ) = forward(in_matrix, out_matrix, units_low, small, seg_row)
        out_whole = out_whole.reshape(-1, D)
    else:
        units = units_low.astype(F32)
        inv_rms = lax.rsqrt(jnp.mean(units * units, axis=-1, keepdims=True) + epsilon)
        base_rows = units * inv_rms
        w_whole = jnp.pad(in_matrix, ((0, 0), (0, WIDTH - PROJ)))
        w_whole = lax.all_gather(w_whole, "fsdp", axis=0, tiled=True)
        out_whole = lax.all_gather(out_matrix, "fsdp", axis=0, tiled=True)
        rim_seg = passed_along(seg_ids[length - CONV + 1 :], "ctx", 1)
        taps, gain, g_float, heads = unpack_small(lax.all_gather(small, "fsdp"), conv_bias.shape[0])
        normed = (base_rows * g_float).astype(BF16)
        normed_t = normed.T
        projected = dot(normed, w_whole).astype(BF16)
        rim_rows = passed_along(projected[length - CONV + 1 :], "ctx", 1)
        halo = jnp.pad(rim_rows, ((PAD - CONV + 1, 0), (0, 0))).astype(F32)
        seg_ext = jnp.concatenate(
            [
                jnp.full((PAD - CONV + 1,), -1, jnp.int32),
                rim_seg,
                seg_ids,
                jnp.full((PAD,), -2, jnp.int32),
            ]
        )
        seg_lanes = jnp.broadcast_to(seg_ext[:, None], (length + 2 * PAD, 128))
        xs, y_local, state, b_rows, c_rows, dt, running, entering, keep = front(
            projected, halo, taps, heads, seg_lanes, seg_row
        )
        kept = lax.all_gather(keep, "ctx")
        incoming = joined_plainly(lax.all_gather(state, "ctx"), kept, place, True)
    mixer_t, dproj, dy, outgoing, column_sums, block_out, stats = tail(
        y_local, xs, projected, incoming, out_whole, c_rows, entering, heads, gain, cot, units_low
    )
    if not here:
        outgoing = joined_plainly(lax.all_gather(outgoing, "ctx"), kept, place, False)
    given = (
        projected, projected, halo, taps, heads, seg_lanes, seg_row, b_rows, c_rows, dt, running, dy, incoming, outgoing,
    )
    if here:
        d_in, d_out, input_grad, total = finish(
            given, normed_t, mixer_t.reshape(4, 2, SHARD, length), dproj, w_turned, cot, units_low, g_float, column_sums, stats, kept
        )
        d_in, d_out = d_in.T.astype(F32), d_out.astype(F32)
    else:
        dproj, d_halo, d_taps, d_heads = back(given, dproj)
        returned = passed_along(d_halo.astype(BF16), "ctx", -1)
        last = lax.slice(dproj, (length - PAD, INNER), (length, INNER + XBC))
        last = (last.astype(F32) + returned.astype(F32)).astype(BF16)
        dproj = lax.dynamic_update_slice(dproj, last, (length - PAD, INNER))
        d_normed = dot_nt(dproj, w_whole)
        d_input_gain = jnp.sum(d_normed * base_rows, axis=0)
        d_base = d_normed * g_float
        d_units = inv_rms * (d_base - base_rows * jnp.mean(d_base * base_rows, axis=-1, keepdims=True))
        input_grad = (cot.astype(F32) + d_units).astype(BF16)

        def scattered(grad):
            return lax.psum_scatter(grad.astype(BF16), "fsdp", scatter_dimension=0, tiled=True)

        d_in = jnp.dot(normed_t, dproj, preferred_element_type=F32)[:, :PROJ]
        d_out = jnp.dot(mixer_t, cot, preferred_element_type=F32)
        d_in = lax.psum(scattered(d_in), "ctx").astype(F32)
        d_out = lax.psum(scattered(d_out), "ctx").astype(F32)
        total = lax.psum(small_sums(d_taps, column_sums, d_input_gain[None], d_heads, stats), ("fsdp", "ctx"))
    me = lax.axis_index("fsdp")

    def own(flat):
        size = flat.shape[-1] // shards
        return lax.dynamic_slice_in_dim(flat, me * size, size, flat.ndim - 1)

    skip_sums = jnp.sum(total[6, :INNER].reshape(HEADS, HDIM), axis=1)
    at = D + 256
    stat_sums = jnp.stack([total[7, at], total[7, at + 128]])
    rms_stats = jnp.sqrt(stat_sums / (length * shards * parts * D))
    return (
        block_out[None],
        input_grad[None],
        d_in,
        d_out,
        own(total[:4]).T,
        own(total[4]),
        own(total[7, D : D + HEADS]),
        own(total[7, D + 128 : D + 128 + HEADS]),
        own(skip_sums),
        own(total[5, :INNER]),
        own(total[7, :D]),
        rms_stats,
    )


def solution(mesh):
    return jax.shard_map(
        on_device,
        mesh=mesh,
        in_specs=(
            P("fsdp", "ctx", None),
            P("fsdp", "ctx"),
            P("fsdp", "ctx", None),
            P("fsdp", None),
            P("fsdp", None),
            P("fsdp", None),
            P("fsdp"),
            P("fsdp"),
            P("fsdp"),
            P("fsdp"),
            P("fsdp"),
            P("fsdp"),
        ),
        out_specs=(
            P("fsdp", "ctx", None),
            P("fsdp", "ctx", None),
            P("fsdp", None),
            P("fsdp", None),
            P("fsdp", None),
            P("fsdp"),
            P("fsdp"),
            P("fsdp"),
            P("fsdp"),
            P("fsdp"),
            P("fsdp"),
            P(),
        ),
        check_vma=False,
    )
```

```python
import functools

import jax
import jax.numpy as jnp
from jax import lax
from jax.experimental import pallas as pl
from jax.experimental.pallas import tpu as pltpu
from jax.sharding import PartitionSpec as P

D = 1536
HEADS = 48
HDIM = 64
STATE = 128
CONV = 4
INNER = 3072
XBC = 3328
PROJ = 6448
WIDTH = 6656

BLK = 256
GROUP = BLK // HDIM
STEPS = INNER // BLK
Q = 128
PAD = 8
WIDE = 512
SHARD = D // 4
PIECE = SHARD // 8
SMALL_WIDTH = 896
AHEAD = 2

epsilon = 1e-05
F32, BF16 = jnp.float32, jnp.bfloat16
HIGHEST = lax.Precision.HIGHEST
VMEM_LIMIT = 60 * 1024 * 1024


def communicating(number):
    return pltpu.CompilerParams(
        vmem_limit_bytes=VMEM_LIMIT, collective_id=number, has_side_effects=True
    )


def dot(a, b):
    return jnp.dot(a, b, preferred_element_type=F32)


def dot_nt(a, b):
    return lax.dot_general(a, b, (((1,), (1,)), ((), ())), preferred_element_type=F32)


def iota(shape, dim):
    return lax.broadcasted_iota(jnp.int32, shape, dim)


def sigmoid(v):
    return 0.5 + 0.5 * jnp.tanh(0.5 * v)


def in_two(a):
    high = a.astype(BF16)
    return high, (a - high.astype(F32)).astype(BF16)


def chosen(step):
    columns = step * GROUP + lax.shift_right_logical(iota((128, BLK), 1), 6)
    return (iota((128, BLK), 0) == columns).astype(BF16)


def chosen_back(step):
    heads = step * GROUP + lax.shift_right_logical(iota((BLK, 128), 0), 6)
    return (iota((BLK, 128), 1) == heads).astype(BF16)


def widen(per_head, select):
    high, low = in_two(per_head)
    return dot(high, select) + dot(low, select)


def halves(pair):
    first = iota(pair.shape, 1) < HDIM
    zero = jnp.zeros_like(pair)
    return jnp.concatenate([jnp.where(first, pair, zero), jnp.where(first, zero, pair)], axis=0)


def both(mask):
    return jnp.concatenate([mask, mask], axis=1)


def conv_rows(ext_ref, seg_ref, taps_ref, start, rows):
    own = seg_ref[start + PAD : start + PAD + rows, :]
    total = taps_ref[4:5, :] + taps_ref[3:4, :] * ext_ref[start + PAD : start + PAD + rows, :]
    for back in range(1, CONV):
        at = start + PAD - back
        same = both(seg_ref[at : at + rows, :] == own)
        total = total + jnp.where(
            same, taps_ref[3 - back : 4 - back, :] * ext_ref[at : at + rows, :], 0.0
        )
    return total


def chunk_flags(seg_ref, k):
    own = seg_ref[PAD + k * Q : PAD + (k + 1) * Q, :]
    before = seg_ref[PAD + k * Q - 1 : PAD + k * Q, :]
    last = seg_ref[PAD + (k + 1) * Q - 1 : PAD + (k + 1) * Q, :]
    return (own == before).astype(F32), (own == last).astype(F32)


def masked_scores(seg_ref, row_ref, b_rows, c_rows, k):
    own = seg_ref[PAD + k * Q : PAD + (k + 1) * Q, :]
    row = row_ref[0:1, k * Q : (k + 1) * Q]
    keep = (own == row) & (iota((Q, Q), 1) <= iota((Q, Q), 0))
    return jnp.where(keep, dot_nt(c_rows, b_rows), 0.0)


def remote(source, target, send, arrival, peer):
    return pltpu.make_async_remote_copy(
        src_ref=source,
        dst_ref=target,
        send_sem=send,
        recv_sem=arrival,
        device_id=peer,
        device_id_type=pl.DeviceIdType.MESH,
    )


def flipped(index, bit):
    return index + bit - 2 * bit * lax.rem(index // bit, 2)


class Gather:
    def __init__(self, locate, several, rows, loads, sends, arrivals):
        self.locate, self.several, self.rows = locate, several, rows
        self.loads, self.sends, self.arrivals = loads, sends, arrivals
        shard, part = lax.axis_index("fsdp"), lax.axis_index("ctx")
        self.own, self.other = shard, flipped(shard, 2)
        x, near = lax.rem(part, 2), lax.rem(part // 2, 2)
        self.mine, self.over_x, self.over_z = 2 * x + near, 2 * (1 - x) + near, 2 * x + 1 - near
        self.across = 2 * (1 - x) + 1 - near
        self.core, self.y = {"fsdp": flipped(shard, 1)}, {"fsdp": flipped(shard, 2)}
        self.to_x, self.to_z = {"ctx": flipped(part, 1)}, {"ctx": flipped(part, 2)}

    def whole(self, shard, k):
        return self.locate(k, shard, 0, self.rows)

    def quarter(self, shard, k, which):
        return self.locate(k, shard, which * (self.rows // 4), self.rows // 4)

    def half(self, shard, k, which, second):
        return self.locate(k, shard, (2 * which + second) * (self.rows // 8), self.rows // 8)

    def copy(self, place, kind, k, peer):
        return remote(place, place, self.sends.at[k], self.arrivals.at[kind, k], peer)

    def load(self, k, source):
        return pltpu.make_async_copy(source, self.whole(self.own, k), self.loads.at[k])

    def begin(self, k):
        self.load(k, self.whole(self.own, k)).wait()
        self.send_own(k)

    def send_own(self, k):
        self.copy(self.quarter(self.own, k, self.mine), 1, k, self.y).start()
        self.copy(self.whole(self.own, k), 0, k, self.core).start()

    def first(self, k):
        quarter = self.quarter(self.other, k, self.mine)
        self.copy(quarter, 1, k, self.y).wait_recv()
        self.copy(quarter, 2, k, self.to_x).start()
        self.copy(quarter, 3, k, self.to_z).start()

    def second(self, k):
        self.copy(self.quarter(self.other, k, self.over_x), 2, k, self.to_x).wait_recv()
        self.copy(self.half(self.other, k, self.over_x, 0), 4, k, self.to_z).start()
        self.copy(self.quarter(self.other, k, self.over_z), 3, k, self.to_z).wait_recv()
        self.copy(self.half(self.other, k, self.over_z, 1), 4, k, self.to_x).start()

    def third(self, k):
        self.copy(self.quarter(self.other, k, self.across), 4, k, self.to_x).wait_recv()
        self.copy(self.whole(self.other, k), 0, k, self.core).start()

    def complete(self, k):
        self.copy(self.several(k, 2), 0, k, self.core).wait_recv()

    def drain(self, k):
        self.copy(self.several(k, 3), 0, k, self.core).wait_send()


class PlainGather(Gather):
    def direct(self, shard, k):
        return self.locate(k, shard, 0, DIRECT * self.rows // 6)

    def part_of(self, shard, k, which):
        size = (6 - DIRECT) * self.rows // 12
        return self.locate(k, shard, DIRECT * self.rows // 6 + which * size, size)

    def send_own(self, k):
        self.copy(self.direct(self.own, k), 3, k, self.y).start()
        self.copy(self.part_of(self.own, k, self.mine // 2), 1, k, self.y).start()
        self.copy(self.whole(self.own, k), 0, k, self.core).start()

    def first(self, k):
        part = self.part_of(self.other, k, self.mine // 2)
        self.copy(part, 1, k, self.y).wait_recv()
        self.copy(part, 2, k, self.to_x).start()

    def second(self, k):
        self.copy(self.direct(self.other, k), 3, k, self.y).wait_recv()
        self.copy(self.part_of(self.other, k, self.over_x // 2), 2, k, self.to_x).wait_recv()
        self.copy(self.whole(self.other, k), 0, k, self.core).start()


def gather_sems(chunks):
    return [
        pltpu.SemaphoreType.DMA((chunks,)),
        pltpu.SemaphoreType.DMA((chunks,)),
        pltpu.SemaphoreType.DMA((5, chunks)),
    ]


PARTS = 8
SLAB = STATE // PARTS
UNIT = 2 * BLK
UNITS = INNER // UNIT


class Exchange:
    def __init__(self, held, gathered, joined, incoming, sems):
        self.held, self.gathered, self.joined, self.incoming, self.sems = held, gathered, joined, incoming, sems
        self.me = lax.axis_index("ctx")

    def others(self):
        return [lax.rem(self.me + hop, PARTS) for hop in range(1, PARTS)]

    def greet(self, *further):
        barrier = pltpu.get_barrier_semaphore()
        peers = [{"ctx": other} for other in self.others()] + list(further)
        for peer in peers:
            pl.semaphore_signal(barrier, inc=1, device_id=peer, device_id_type=pl.DeviceIdType.MESH)
        pl.semaphore_wait(barrier, len(peers))

    def copy(self, source, target, kind, group, other):
        return pltpu.make_async_remote_copy(
            src_ref=source,
            dst_ref=target,
            send_sem=self.sems.at[2 * kind, group],
            recv_sem=self.sems.at[2 * kind + 1, group],
            device_id={"ctx": other},
            device_id_type=pl.DeviceIdType.MESH,
        )

    def all_of(self, kind, group):
        source, target = ((self.held, self.gathered), (self.joined, self.incoming))[kind]
        some = pl.ds(0, PARTS - 1)
        return self.copy(source.at[group, some], target.at[group, some], kind, group, self.others()[0])

    def hold(self, group, half, state):
        self.held[group, :, :, half * BLK : (half + 1) * BLK] = state.astype(BF16).reshape(PARTS, SLAB, BLK)

    def spread(self, group):
        self.gathered[group, self.me] = self.held[group, self.me]
        for other in self.others():
            self.copy(self.held.at[group, other], self.gathered.at[group, self.me], 0, group, other).start()

    def join(self, group, kept, forward):
        self.all_of(0, group).wait_recv()
        total = jnp.zeros((SLAB, UNIT), F32)
        for part in range(PARTS) if forward else range(PARTS - 1, -1, -1):
            self.joined[group, part] = total.astype(BF16)
            total = kept[part : part + 1, :] * total + self.gathered[group, part].astype(F32)
        self.incoming[group, self.me] = self.joined[group, self.me]
        for other in self.others():
            self.copy(self.joined.at[group, other], self.incoming.at[group, self.me], 1, group, other).start()

    def finish(self, group):
        self.all_of(1, group).wait_recv()
        self.all_of(0, group).wait_send()
        self.all_of(1, group).wait_send()
        return self.incoming[group].reshape(STATE, UNIT)


def exchange_scratch():
    return [pltpu.VMEM((UNITS, PARTS, SLAB, UNIT), BF16) for _ in range(4)] + [pltpu.SemaphoreType.DMA((4, UNITS))]


def kept_of(kept_ref, unit):
    rows = jnp.concatenate([kept_ref[part, 0:1, :] for part in range(PARTS)], axis=0)
    return jnp.concatenate([widen(rows, chosen(2 * unit)), widen(rows, chosen(2 * unit + 1))], axis=1)


def joined_plainly(states, kept, place, forward):
    factors = jnp.repeat(kept[:, 0, :HEADS], HDIM, axis=1)[:, None, :]
    total = jnp.zeros(states.shape[1:], F32)
    result = total
    count = states.shape[0]
    for part in range(count) if forward else range(count - 1, -1, -1):
        result = jnp.where(place == part, total, result)
        total = factors[part] * total + states[part].astype(F32)
    return result.astype(BF16)


def prepare(
    bc_ref, dt_raw, halo_bc_ref, taps_bc_ref, heads_ref, seg_ref, row_ref, b_ref, c_ref, dt_ref, run_ref, in_ref,
    ext, scores, run_t, b_t, enter, leave,
):
    chunks = bc_ref.shape[0] // Q
    ext[0:PAD, :] = halo_bc_ref[...]
    ext[PAD:, :] = bc_ref[...].astype(F32)
    lane = iota((Q, 128), 1)
    lower = (iota((Q, Q), 1) <= iota((Q, Q), 0)).astype(F32)
    offset = jnp.zeros((1, 128), F32)
    for k in range(chunks):
        rows = slice(k * Q, (k + 1) * Q)
        total = conv_rows(ext, seg_ref, taps_bc_ref, k * Q, Q)
        active = total * sigmoid(total)
        b_rows, c_rows = active[:, :STATE], active[:, STATE:].astype(BF16)
        b_t[:, rows] = b_rows.T.astype(BF16)
        b_rows = b_rows.astype(BF16)
        b_ref[rows, :] = b_rows
        c_ref[rows, :] = c_rows
        scores[rows, :] = masked_scores(seg_ref, row_ref, b_rows, c_rows, k)
        raw = jnp.where(lane < HEADS, dt_raw(rows).astype(F32), 0.0) + heads_ref[0:1, :]
        dt = jnp.maximum(raw, 0.0) + jnp.log1p(jnp.exp(-jnp.abs(raw)))
        log_decay = -dt * jnp.exp(heads_ref[1:2, :])
        running = jnp.dot(lower, log_decay, precision=HIGHEST, preferred_element_type=F32)
        dt_ref[rows, :] = dt
        run_ref[rows, :] = running
        run_t[k] = running.T
        carry, tail = chunk_flags(seg_ref, k)
        enter[rows, :] = jnp.exp(running) * carry
        leave[rows, :] = jnp.exp(running[Q - 1 : Q, :] - running) * tail
        same = (seg_ref[PAD + k * Q : PAD + (k + 1) * Q, :] == seg_ref[PAD - 1 : PAD, :]).astype(F32)
        whole = jnp.exp(running + offset) * same
        in_ref[rows, :] = whole
        offset = offset + running[Q - 1 : Q, :]
    return jnp.broadcast_to(whole[Q - 1 : Q, :], (8, 128))


def front_kernel(
    x_ref, bc_ref, dtraw_ref, halo_ref, halo_bc_ref, taps_ref, taps_bc_ref, heads_ref, seg_ref, row_ref,
    xs_ref, y_ref, state_ref, b_ref, c_ref, dt_ref, run_ref, in_ref, keep_ref,
    ext, scores, run_t, b_t, enter, leave,
):
    step = pl.program_id(0)

    @pl.when(step == 0)
    def _():
        keep_ref[...] = prepare(
            bc_ref, lambda rows: dtraw_ref[rows, :128], halo_bc_ref, taps_bc_ref, heads_ref, seg_ref, row_ref,
            b_ref, c_ref, dt_ref, run_ref, in_ref, ext, scores, run_t, b_t, enter, leave,
        )

    state = local_scan(
        step, x_ref, halo_ref, taps_ref, seg_ref, xs_ref, y_ref, c_ref, dt_ref, run_ref,
        ext, scores, run_t, b_t, enter, leave,
    )
    state_ref[...] = state.astype(BF16)


def local_scan(
    step, x_ref, halo_ref, taps_ref, seg_ref, xs_ref, y_ref, c_ref, dt_ref, run_ref,
    ext, scores, run_t, b_t, enter, leave,
):
    chunks = x_ref.shape[0] // Q
    ext[0:PAD, :] = halo_ref[...]
    ext[PAD:, :] = x_ref[...].astype(F32)
    select = chosen(step)
    state = jnp.zeros((STATE, BLK), F32)
    for k in range(chunks):
        rows = slice(k * Q, (k + 1) * Q)
        total = conv_rows(ext, seg_ref, taps_ref, k * Q, Q)
        values = total * sigmoid(total)
        xs_ref[rows, :] = values.astype(BF16)
        scaled = (values * widen(dt_ref[rows, :], select)).astype(BF16)
        entering = widen(enter[rows, :], select)
        running = pltpu.roll(run_ref[rows, :], lax.rem(128 - step * GROUP, 128), 1)
        parts = []
        for pair in range(2):
            mixing = []
            for one in range(2):
                head = 2 * pair + one
                gap = running[:, head : head + 1] - run_t[k, pl.ds(step * GROUP + head, 1), :]
                mixing.append((jnp.exp(jnp.minimum(gap, 0.0)) * scores[rows, :]).astype(BF16))
            parts.append(
                dot(jnp.concatenate(mixing, axis=1), halves(scaled[:, pair * 128 : (pair + 1) * 128]))
            )
        inside = jnp.concatenate(parts, axis=1)
        y_ref[rows, :] = (inside + entering * dot(c_ref[rows, :], state.astype(BF16))).astype(BF16)
        weighted = (scaled.astype(F32) * widen(leave[rows, :], select)).astype(BF16)
        state = entering[Q - 1 : Q, :] * state + dot(b_t[:, rows], weighted)
    return state


def front_outputs(length, column, state_at, width=BLK):
    whole = lambda *shape: (pl.BlockSpec(shape, lambda j: (0, 0)), shape)
    columns = lambda rows, at: (pl.BlockSpec((rows, width), at), (rows, INNER))
    specs = [
        (columns(length, column), BF16),
        (columns(length, column), BF16),
        (columns(STATE, state_at), BF16),
        (whole(length, 128), BF16),
        (whole(length, 128), BF16),
        (whole(length, 128), F32),
        (whole(length, 128), F32),
        (whole(length, 128), F32),
    ]
    return [spec for (spec, _), _ in specs], [jax.ShapeDtypeStruct(shape, kind) for (_, shape), kind in specs]


def front_scratch(length):
    return [
        pltpu.VMEM((length + PAD, BLK), F32),
        pltpu.VMEM((length, Q), F32),
        pltpu.VMEM((length // Q, 128, Q), F32),
        pltpu.VMEM((128, length), BF16),
        pltpu.VMEM((length, 128), F32),
        pltpu.VMEM((length, 128), F32),
    ]


def front(projected, halo, taps, heads, seg_lanes, seg_row):
    length = projected.shape[0]
    whole = lambda *shape: pl.BlockSpec(shape, lambda j: (0,) * len(shape))
    columns = lambda rows, at: pl.BlockSpec((rows, BLK), at)
    out_specs, out_shape = front_outputs(length, lambda j: (0, j), lambda j: (0, j))
    return pl.pallas_call(
        front_kernel,
        grid=(STEPS,),
        in_specs=[
            columns(length, lambda j: (0, STEPS + j)),
            columns(length, lambda j: (0, 2 * STEPS)),
            columns(length, lambda j: (0, 2 * STEPS + 1)),
            columns(PAD, lambda j: (0, STEPS + j)),
            columns(PAD, lambda j: (0, 2 * STEPS)),
            columns(8, lambda j: (0, j)),
            columns(8, lambda j: (0, STEPS)),
            whole(8, 128),
            whole(length + 2 * PAD, 128),
            whole(1, length),
        ],
        out_specs=[*out_specs, whole(8, 128)],
        out_shape=[*out_shape, jax.ShapeDtypeStruct((8, 128), F32)],
        scratch_shapes=front_scratch(length),
        compiler_params=pltpu.CompilerParams(vmem_limit_bytes=VMEM_LIMIT),
        name="front",
    )(projected, projected, projected, halo, halo, taps, taps, heads, seg_lanes, seg_row)


ORDER = (2 * INNER // WIDE, *range(INNER // WIDE, 2 * INNER // WIDE), *range(INNER // WIDE))
MULTIPLY = 3
SCAN = MULTIPLY + 2
OUT_WIDE = 128
OUT_PIECES = D // OUT_WIDE
OUT_BEGIN, DIRECT = 4, 4
JOIN, DONE = 2, 4
SLOTS = MULTIPLY + len(ORDER)
EDGES = 1 + INNER // WIDE


def chunk_at(position):
    half = INNER // WIDE
    return jnp.where(position == 0, 2 * half, jnp.where(position <= half, position - 1 + half, position - 1 - half))


def forward_kernel(*refs):
    main_ref, shard_ref, units_ref, row_ref = refs[:4]
    conv_ref, bias_ref, mixer_ref, input_ref, *head_refs = refs[4:11]
    refs = refs[6:]
    xs_ref, y_ref, state_ref, b_ref, c_ref, dt_ref, run_ref, in_ref = refs[5:13]
    keep_ref, weight_ref, whole_ref, projected_ref, normed_t_ref = refs[13:18]
    halo_ref, taps_ref, heads_ref, gain_ref, input_gain_ref, seg_ref = refs[18:24]
    ext, scores, run_t, b_t, enter, leave = refs[24:30]
    exchange = Exchange(*refs[30:35])
    own_keep, keeps, keep_sends, keep_arrivals = refs[35:39]
    gathered, loads, sends, arrivals, stores = refs[39:44]
    out_gathered, out_loads, out_sends, out_arrivals, out_stores = refs[44:49]
    normed, blocks, taps, own_small, smalls, seg_tail, seg_head = refs[49:56]
    edges, halos, small_sends, small_arrivals, edge_sends, edge_arrivals = refs[56:]
    step = pl.program_id(0)
    length = units_ref.shape[0]
    shard, part = lax.axis_index("fsdp"), lax.axis_index("ctx")
    others = ({"fsdp": flipped(shard, 1)}, {"fsdp": flipped(shard, 2)}, {"fsdp": flipped(flipped(shard, 1), 2)})
    following = {"ctx": lax.rem(part + 1, PARTS)}

    def place_in(k, s, start, size):
        rows, columns = pl.multiple_of(start, size), pl.multiple_of(s * SHARD, SHARD)
        return gathered.at[k, pl.ds(rows, size), pl.ds(columns, SHARD)]

    def place_out(k, s, start, size):
        return out_gathered.at[k, s, pl.ds(pl.multiple_of(start, size), size)]

    several_in = lambda k, count: gathered.at[k, :, pl.ds(0, count * SHARD)]
    several_out = lambda k, count: out_gathered.at[k, pl.ds(0, count)]
    gather = Gather(place_in, several_in, WIDE, loads, sends, arrivals)
    gather_out = PlainGather(place_out, several_out, 2 * SHARD, out_loads, out_sends, out_arrivals)
    rest = PROJ % WIDE

    def load_rest():
        columns = pl.ds(pl.multiple_of(shard * SHARD, SHARD), SHARD)
        return pltpu.make_async_copy(
            main_ref.at[PROJ - rest : PROJ, :], gathered.at[0, pl.ds(0, rest), columns], loads.at[0]
        )

    def small_copy(hop):
        return remote(own_small, smalls.at[shard], small_sends.at[hop], small_arrivals.at[hop], others[hop])

    def seg_copy():
        return remote(seg_tail, seg_head, small_sends.at[3], small_arrivals.at[3], following)

    def edge_copy(k):
        return remote(edges.at[k], halos.at[k], edge_sends.at[k], edge_arrivals.at[k], following)

    def keep_copy(hop):
        peer = {"ctx": lax.rem(part + hop + 1, PARTS)}
        return remote(own_keep, keeps.at[part], keep_sends.at[hop], keep_arrivals.at[hop], peer)

    def store(k):
        rows = pl.ds(pl.multiple_of(chunk_at(k) * WIDE, WIDE), WIDE)
        return pltpu.make_async_copy(gathered.at[k], weight_ref.at[rows], stores.at[k])

    def store_out(k):
        columns = pl.ds(pl.multiple_of(k * OUT_WIDE, OUT_WIDE), OUT_WIDE)
        return pltpu.make_async_copy(out_gathered.at[k], whole_ref.at[:, :, columns], out_stores.at[k])

    @pl.when(step == 0)
    def _():
        load_rest().start()
        for k, chunk in enumerate(ORDER):
            if k:
                gather.load(k, main_ref.at[chunk * WIDE : (chunk + 1) * WIDE, :]).start()
        for k in range(OUT_PIECES):
            gather_out.load(k, shard_ref.at[:, k * OUT_WIDE : (k + 1) * OUT_WIDE]).start()
        own_small[...] = jnp.zeros((8, SMALL_WIDTH), F32)
        own_small[0:4, : XBC // 4] = conv_ref[...].astype(F32)
        for row, ref in ((4, bias_ref), (5, mixer_ref), (6, input_ref)):
            own_small[row : row + 1, : ref.shape[0]] = ref[...].astype(F32).reshape(1, ref.shape[0])
        for kind, ref in enumerate(head_refs):
            own_small[7:8, kind * 128 : kind * 128 + HEADS // 4] = ref[...].astype(F32).reshape(1, HEADS // 4)
        smalls[shard] = own_small[...]
        columns = pl.ds(pl.multiple_of(shard * SHARD, SHARD), SHARD)
        gathered[0, rest:, columns] = jnp.zeros((WIDE - rest, SHARD), BF16)
        for k in range(length // 128):
            ids = jnp.broadcast_to(row_ref[0:1, k * 128 : (k + 1) * 128].astype(F32), (128, 128))
            seg_ref[PAD + k * 128 : PAD + (k + 1) * 128, :] = ids.T.astype(jnp.int32)
        seg_tail[...] = seg_ref[length : length + PAD, :]
        exchange.greet(*others)
        for hop in range(3):
            small_copy(hop).start()
        seg_copy().start()
        load_rest().wait()
        gather.send_own(0)
        for k in range(1, AHEAD):
            gather.begin(k)

    def take_small():
        for hop in range(3):
            small_copy(hop).wait()
        seg_copy().wait()
        seg_ref[0:PAD, :] = jnp.where(part == 0, -1, seg_head[...])
        seg_ref[PAD + length :, :] = jnp.full((PAD, 128), -2, jnp.int32)

    def normalise():
        gain = jnp.concatenate([smalls[s, 6:7, :SHARD] for s in range(4)], axis=1)
        input_gain_ref[...] = gain
        for k in range(length // Q):
            rows = slice(k * Q, (k + 1) * Q)
            units = units_ref[rows, :].astype(F32)
            norm = lax.rsqrt(jnp.sum(units * units, axis=1, keepdims=True) * (1.0 / D) + epsilon)
            normed[rows, :] = (units * norm * gain).astype(BF16)

    def take_taps():
        mixer_gain = jnp.concatenate([smalls[s, 5:6, : INNER // 4] for s in range(4)], axis=1)
        gain_ref[...] = jnp.broadcast_to(mixer_gain, (8, INNER))
        whole = jnp.zeros((8, XBC), F32)
        heads = jnp.zeros((8, 128), F32)
        row, lane = iota((8, 128), 0), iota((8, 128), 1)
        own = HEADS // 4
        for s in range(4):
            padded = jnp.concatenate([smalls[s], jnp.zeros((8, XBC - SMALL_WIDTH), F32)], axis=1)
            padded = jnp.where(iota((8, XBC), 1) < XBC // 4, padded, 0.0)
            whole = whole + (pltpu.roll(padded, s * (XBC // 4), 1) if s else padded)
            inside = (lane >= s * own) & (lane < (s + 1) * own)
            for kind in range(3):
                moved = jnp.broadcast_to(smalls[s, 7:8, kind * 128 : (kind + 1) * 128], (8, 128))
                moved = pltpu.roll(moved, s * own, 1) if s else moved
                heads = jnp.where(inside & (row == kind), moved, heads)
        taps_ref[...] = whole
        heads_ref[...] = heads
        for block in range(STEPS + 1):
            taps[block] = whole[:, block * BLK : (block + 1) * BLK]

    def complete_out(k):
        gather_out.complete(k)
        store_out(k).start()

    def stage(lag, count=len(ORDER)):
        def decorate(body):
            k = step - lag

            @pl.when((k >= 0) & (k < count))
            def _():
                body(k)

        return decorate

    def advance(tick):
        def at(lag, body, first=0, count=len(ORDER)):
            k = tick - lag

            @pl.when((k >= first) & (k < count))
            def _():
                body(k)

        def complete(k):
            gather.complete(k)
            store(k).start()

        at(-AHEAD, gather.begin, AHEAD)
        at(0, gather.first)
        at(1, gather.second)
        at(2, gather.third)
        at(3, complete)
        at(OUT_BEGIN, gather_out.begin, 0, OUT_PIECES)
        at(OUT_BEGIN + 2, gather_out.first, 0, OUT_PIECES)
        at(OUT_BEGIN + 4, gather_out.second, 0, OUT_PIECES)
        at(OUT_BEGIN + 6, complete_out, 0, OUT_PIECES)

    tick = jnp.where(step < SCAN, step, 2 * step - SCAN)
    advance(tick)
    pl.when(step == 0)(take_small)
    pl.when(step == 1)(normalise)
    pl.when(step == 2)(take_taps)

    @stage(MULTIPLY)
    def _(k):
        low = dot_nt(normed[...], gathered[k]).astype(BF16)
        projected_ref[...] = low

        @pl.when(k < EDGES)
        def _():
            edge = low[length - 16 :, :].astype(F32)[8:, :]
            for half in range(2):
                columns = slice(half * BLK, (half + 1) * BLK)
                blocks[2 * k + half] = low[:, columns]
                edges[k, half] = edge[:, columns]
            edge_copy(k).start()

    @stage(SCAN - 1, EDGES)
    def _(k):
        edge_copy(k).wait()
        for half in range(2):
            columns = slice(half * BLK, (half + 1) * BLK)
            halos[k, half] = jnp.where(part == 0, 0.0, halos[k, half])
            halo_ref[:, columns] = halos[k, half]

    @pl.when(step == SCAN - 1)
    def _():
        keep = prepare(
            blocks.at[0], lambda rows: blocks[1, rows, :128], halos.at[0, 0], taps.at[STEPS], heads_ref,
            seg_ref, row_ref, b_ref, c_ref, dt_ref, run_ref, in_ref, ext, scores, run_t, b_t, enter, leave,
        )
        own_keep[...] = keep
        keeps[part] = keep
        for hop in range(PARTS - 1):
            keep_copy(hop).start()

    for half in range(2):

        @stage(SCAN, UNITS)
        def _(unit):
            columns = pl.ds(half * BLK, BLK)
            group = 2 * unit + half
            state = local_scan(
                group, blocks.at[2 + group], halos.at[1 + unit, half], taps.at[group], seg_ref,
                xs_ref.at[:, columns], y_ref.at[:, columns], c_ref, dt_ref, run_ref, ext, scores, run_t, b_t, enter, leave,
            )
            exchange.hold(unit, half, state)

        if half == 0:

            @pl.when(step >= SCAN)
            def _():
                advance(tick + 1)

    stage(SCAN, UNITS)(exchange.spread)

    @pl.when(step == SCAN + JOIN)
    def _():
        for hop in range(PARTS - 1):
            keep_copy(hop).wait()
        keep_ref[...] = keeps[...]

    @stage(SCAN + JOIN, UNITS)
    def _(unit):
        exchange.join(unit, kept_of(keeps, unit), True)

    @stage(SCAN + DONE, UNITS)
    def _(unit):
        state_ref[...] = exchange.finish(unit)

    @pl.when(step == SLOTS - 1)
    def _():
        for k in range(len(ORDER)):
            gather.drain(k)
            store(k).wait()
        for k in range(OUT_PIECES):
            gather_out.drain(k)
            store_out(k).wait()
        for s in range(4):
            columns = slice(s * SHARD, (s + 1) * SHARD)
            normed_t_ref[s] = normed[:, columns].astype(F32).T.astype(BF16)


def forward(in_matrix, out_matrix, units, seg_row, *small):
    length = units.shape[0]
    chunks = len(ORDER)
    whole = lambda *shape: pl.BlockSpec(shape, lambda t: (0,) * len(shape))
    once = lambda *shape: pl.BlockSpec(shape, lambda t: (0,) * len(shape), pipeline_mode=pl.Buffered(1))
    anywhere = pl.BlockSpec(memory_space=pl.ANY)
    chunk = lambda rows, lag: pl.BlockSpec((rows, WIDE), lambda t: (0, chunk_at(jnp.clip(t - lag, 0, chunks - 1))))
    unit = lambda lag: lambda t: (0, jnp.clip(t - lag, 0, UNITS - 1))
    out_specs, out_shape = front_outputs(length, unit(SCAN), unit(SCAN + DONE), UNIT)
    shape = jax.ShapeDtypeStruct
    return pl.pallas_call(
        forward_kernel,
        grid=(SLOTS,),
        in_specs=[
            anywhere,
            anywhere,
            once(length, D),
            once(1, length),
            *[once(*each.shape) for each in small],
        ],
        out_specs=[
            *out_specs,
            whole(PARTS, 8, 128),
            anywhere,
            anywhere,
            chunk(length, MULTIPLY),
            once(4, SHARD, length),
            pl.BlockSpec((PAD, WIDE), lambda t: (0, chunk_at(jnp.clip(t - SCAN + 1, 0, EDGES - 1)))),
            whole(8, XBC),
            whole(8, 128),
            whole(8, INNER),
            whole(1, D),
            whole(length + 2 * PAD, 128),
        ],
        out_shape=[
            *out_shape,
            shape((PARTS, 8, 128), F32),
            shape((WIDTH, D), BF16),
            shape((4, 2 * SHARD, D), BF16),
            shape((length, WIDTH), BF16),
            shape((4, SHARD, length), BF16),
            shape((PAD, WIDTH), F32),
            shape((8, XBC), F32),
            shape((8, 128), F32),
            shape((8, INNER), F32),
            shape((1, D), F32),
            shape((length + 2 * PAD, 128), jnp.int32),
        ],
        scratch_shapes=[
            *front_scratch(length),
            *exchange_scratch(),
            pltpu.VMEM((8, 128), F32),
            pltpu.VMEM((PARTS, 8, 128), F32),
            pltpu.SemaphoreType.DMA((PARTS - 1,)),
            pltpu.SemaphoreType.DMA((PARTS - 1,)),
            pltpu.VMEM((chunks, WIDE, D), BF16),
            *gather_sems(chunks),
            pltpu.SemaphoreType.DMA((chunks,)),
            pltpu.VMEM((OUT_PIECES, 4, 2 * SHARD, OUT_WIDE), BF16),
            *gather_sems(OUT_PIECES),
            pltpu.SemaphoreType.DMA((OUT_PIECES,)),
            pltpu.VMEM((length, D), BF16),
            pltpu.VMEM((2 * EDGES, length, BLK), BF16),
            pltpu.VMEM((STEPS + 1, 8, BLK), F32),
            pltpu.VMEM((8, SMALL_WIDTH), F32),
            pltpu.VMEM((4, 8, SMALL_WIDTH), F32),
            pltpu.VMEM((PAD, 128), jnp.int32),
            pltpu.VMEM((PAD, 128), jnp.int32),
            pltpu.VMEM((EDGES, 2, PAD, BLK), F32),
            pltpu.VMEM((EDGES, 2, PAD, BLK), F32),
            pltpu.SemaphoreType.DMA((4,)),
            pltpu.SemaphoreType.DMA((4,)),
            pltpu.SemaphoreType.DMA((EDGES,)),
            pltpu.SemaphoreType.DMA((EDGES,)),
        ],
        compiler_params=communicating(1),
        name="forward",
    )(in_matrix.T, out_matrix, units, seg_row, *small)


def tail_kernel(
    y_ref, xs_ref, gate_ref, incoming_ref, out_ref, c_ref, in_ref, heads_ref, gain_ref, g_ref, units_ref,
    mixer_ref, dproj_ref, dy_ref, dsin_ref, sums_ref, block_ref, stats_ref,
    full, dmix, squares, products, mixed, c_t,
):
    step = pl.program_id(0)
    length = y_ref.shape[0]
    unit = lax.rem(step, UNITS)
    half = length // 2

    @pl.when(step == 0)
    def _():
        squares[...] = jnp.zeros_like(squares)
        products[...] = jnp.zeros_like(products)
        mixed[...] = jnp.zeros_like(mixed)
        for k in range(length // Q):
            rows = slice(k * Q, (k + 1) * Q)
            c_t[:, rows] = c_ref[rows, :].astype(F32).T.astype(BF16)

    def earlier(one):
        columns = slice(one * BLK, (one + 1) * BLK)
        group = 2 * unit + one
        select = chosen(group)
        incoming = incoming_ref[:, columns]
        skip = widen(heads_ref[...], select)[2:3, :]
        for k in range(2):
            rows = slice(k * half, (k + 1) * half)
            y = y_ref[rows, columns].astype(F32)
            y = y + widen(in_ref[rows, :], select) * dot(c_ref[rows, :], incoming)
            y = y + skip * xs_ref[rows, columns].astype(F32)
            full[group, rows, :] = y
            gate = gate_ref[rows, columns].astype(F32)
            gated = y * gate * sigmoid(gate)
            d_mixer = dot_nt(g_ref[rows, :], out_ref[columns, :])
            dmix[group, rows, :] = d_mixer
            square = gated * gated
            product = gated * d_mixer * gain_ref[0:1, columns]
            squares[rows, :] += square[:, :128] + square[:, 128:]
            products[rows, :] += product[:, :128] + product[:, 128:]

    def later(one):
        columns = slice(one * BLK, (one + 1) * BLK)
        group = 2 * unit + one
        select = chosen(group)
        gain = gain_ref[0:1, columns]
        d_gain = jnp.zeros((1, BLK), F32)
        d_skip = jnp.zeros((1, BLK), F32)
        d_state = jnp.zeros((STATE, BLK), F32)
        for k in range(2):
            rows = slice(k * half, (k + 1) * half)
            norm, mean = both(squares[rows, :]), both(products[rows, :])
            y = full[group, rows, :]
            d_mixer = dmix[group, rows, :]
            gate = gate_ref[rows, columns].astype(F32)
            sig = sigmoid(gate)
            silu = gate * sig
            unscaled = y * silu * norm
            value = unscaled * gain
            mixer_ref[columns, rows] = value.T.astype(BF16)
            mixed[rows, :] += dot(value.astype(BF16), out_ref[columns, :])
            d_gain = d_gain + jnp.sum(d_mixer * unscaled, axis=0, keepdims=True)
            d_gated = norm * (d_mixer * gain - unscaled * mean)
            dproj_ref[rows, columns] = (d_gated * y * (sig * (1.0 + gate * (1.0 - sig)))).astype(BF16)
            dy = (d_gated * silu).astype(BF16)
            dy_ref[rows, columns] = dy
            dy = dy.astype(F32)
            d_skip = d_skip + jnp.sum(dy * xs_ref[rows, columns].astype(F32), axis=0, keepdims=True)
            d_state = d_state + dot(c_t[:, rows], (dy * widen(in_ref[rows, :], select)).astype(BF16))
        dsin_ref[:, columns] = d_state.astype(BF16)
        sums_ref[:, columns] = jnp.concatenate([d_gain, d_skip, jnp.zeros((6, BLK), F32)], axis=0)

    @pl.when(step < UNITS)
    def _():
        earlier(0)
        earlier(1)

    @pl.when(step == UNITS)
    def _():
        norm = lax.rsqrt(jnp.sum(squares[...], axis=1, keepdims=True) * (1.0 / INNER) + epsilon)
        mean = norm * jnp.sum(products[...], axis=1, keepdims=True) * (1.0 / INNER)
        squares[...] = jnp.broadcast_to(norm, squares.shape)
        products[...] = jnp.broadcast_to(mean, products.shape)

    @pl.when(step >= UNITS)
    def _():
        later(0)
        later(1)

    @pl.when(step == 2 * UNITS - 1)
    def _():
        total = units_ref[...].astype(F32) + mixed[...]
        block_ref[...] = total.astype(BF16)
        first = jnp.sum(total * total, axis=0, keepdims=True)
        second = jnp.sum(mixed[...] * mixed[...], axis=0, keepdims=True)
        stats_ref[...] = jnp.concatenate([first, second, jnp.zeros((6, D), F32)], axis=0)


def tail(y, xs, projected, incoming, out_whole, c_rows, entering, heads, gain, cot, units):
    length = y.shape[0]
    unit = lambda i: lax.rem(i, UNITS)
    second = lambda i: jnp.maximum(i - UNITS, 0)
    early = lambda rows: pl.BlockSpec((rows, UNIT), lambda i: (0, jnp.minimum(i, UNITS - 1)))
    late = lambda rows: pl.BlockSpec((rows, UNIT), lambda i: (0, second(i)))
    each = lambda rows: pl.BlockSpec((rows, UNIT), lambda i: (0, unit(i)))
    whole = lambda *shape: pl.BlockSpec(shape, lambda i: (0,) * len(shape))
    return pl.pallas_call(
        tail_kernel,
        grid=(2 * UNITS,),
        in_specs=[
            early(length),
            each(length),
            each(length),
            early(STATE),
            pl.BlockSpec((UNIT, D), lambda i: (unit(i), 0)),
            whole(length, 128),
            whole(length, 128),
            whole(8, 128),
            each(8),
            whole(length, D),
            whole(length, D),
        ],
        out_specs=[
            pl.BlockSpec((UNIT, length), lambda i: (second(i), 0)),
            late(length),
            late(length),
            pl.BlockSpec((STATE, UNIT), lambda i: (0, second(i))),
            late(8),
            whole(length, D),
            whole(8, D),
        ],
        out_shape=[
            jax.ShapeDtypeStruct((INNER, length), BF16),
            jax.ShapeDtypeStruct((length, WIDTH), BF16),
            jax.ShapeDtypeStruct((length, INNER), BF16),
            jax.ShapeDtypeStruct((STATE, INNER), BF16),
            jax.ShapeDtypeStruct((8, INNER), F32),
            jax.ShapeDtypeStruct((length, D), BF16),
            jax.ShapeDtypeStruct((8, D), F32),
        ],
        scratch_shapes=[
            pltpu.VMEM((STEPS, length, BLK), F32),
            pltpu.VMEM((STEPS, length, BLK), F32),
            pltpu.VMEM((length, 128), F32),
            pltpu.VMEM((length, 128), F32),
            pltpu.VMEM((length, D), F32),
            pltpu.VMEM((128, length), BF16),
        ],
        compiler_params=pltpu.CompilerParams(vmem_limit_bytes=VMEM_LIMIT),
        cost_estimate=pl.CostEstimate(
            flops=12 * 10**9, bytes_accessed=50 * 10**6, transcendentals=4 * 10**6
        ),
        name="tail",
    )(y, xs, projected, incoming, out_whole, c_rows, entering, heads, gain, cot, units)


def back_steps(step, given, scratch, write, write_halo, write_taps, write_heads):
    (
        x_ref, dtraw_ref, halo_ref, taps_ref, heads_ref, seg_ref, row_ref, b_ref, c_ref, dt_ref, run_ref, dy_ref, sin_ref, dout_ref,
    ) = given
    (
        ext, pre, dact, dbuf, scores, dscores, run_t, b_t, c_t, enter, leave, d_b, d_c, suffix, prefix, d_dt, fixed, states,
    ) = scratch
    length = x_ref.shape[0]
    chunks = length // Q

    @pl.when(step == 0)
    def _():
        for k in range(chunks):
            rows = slice(k * Q, (k + 1) * Q)
            b_rows, c_rows = b_ref[rows, :], c_ref[rows, :]
            b_t[:, rows] = b_rows.astype(F32).T.astype(BF16)
            c_t[:, rows] = c_rows.astype(F32).T.astype(BF16)
            scores[rows, :] = masked_scores(seg_ref, row_ref, b_rows, c_rows, k)
            running = run_ref[rows, :]
            run_t[k] = running.T
            carry, tail = chunk_flags(seg_ref, k)
            enter[rows, :] = jnp.exp(running) * carry
            leave[rows, :] = jnp.exp(running[Q - 1 : Q, :] - running) * tail
        for each in (dscores, d_b, d_c, suffix, prefix, d_dt, fixed):
            each[...] = jnp.zeros_like(each)
        dbuf[0:PAD, :] = jnp.zeros((PAD, BLK), F32)
        dbuf[PAD + length :, :] = jnp.zeros((PAD, BLK), F32)

    @pl.when(step <= STEPS)
    def _():
        ext[0:PAD, :] = halo_ref[...]
        ext[PAD:, :] = x_ref[...].astype(F32)
        for k in range(chunks):
            pre[k * Q : (k + 1) * Q, :] = conv_rows(ext, seg_ref, taps_ref, k * Q, Q)

    @pl.when(step < STEPS)
    def _():
        select = chosen(step)
        gather = chosen_back(step)
        skip = widen(heads_ref[...], select)[2:3, :]
        state = sin_ref[...].astype(F32)
        for k in range(chunks):
            rows = slice(k * Q, (k + 1) * Q)
            states[k] = state
            if k + 1 < chunks:
                total = pre[rows, :]
                scaled = total * sigmoid(total) * widen(dt_ref[rows, :], select)
                weighted = (scaled.astype(BF16).astype(F32) * widen(leave[rows, :], select)).astype(BF16)
                last = widen(enter[rows.stop - 8 : rows.stop, :], select)[7:8, :]
                state = last * state + dot(b_t[:, rows], weighted)
        d_state = dout_ref[...].astype(F32)
        for k in range(chunks - 1, -1, -1):
            rows = slice(k * Q, (k + 1) * Q)
            total = pre[rows, :]
            values = total * sigmoid(total)
            step_size = widen(dt_ref[rows, :], select)
            entering = widen(enter[rows, :], select)
            leaving = widen(leave[rows, :], select)
            scaled = (values * step_size).astype(BF16)
            scaled_wide = scaled.astype(F32)
            dy = dy_ref[rows, :]
            dy_wide = dy.astype(F32)
            before = states[k]
            before_low = before.astype(BF16)
            d_low = d_state.astype(BF16)
            running = pltpu.roll(run_ref[rows, :], lax.rem(128 - step * GROUP, 128), 1)
            insides, backs = [], []
            d_score = dscores[rows, :]
            for pair in range(2):
                lanes = slice(pair * 128, (pair + 1) * 128)
                mixing, turned, decays = [], [], []
                for one in range(2):
                    head = 2 * pair + one
                    gap = running[:, head : head + 1] - run_t[k, pl.ds(step * GROUP + head, 1), :]
                    decay = jnp.exp(jnp.minimum(gap, 0.0))
                    mixed = decay * scores[rows, :]
                    decays.append(decay)
                    mixing.append(mixed.astype(BF16))
                    turned.append(mixed.T.astype(BF16))
                spread = halves(scaled[:, lanes])
                insides.append(dot(jnp.concatenate(mixing, axis=1), spread))
                backs.append(dot(jnp.concatenate(turned, axis=1), halves(dy[:, lanes])))
                products = dot_nt(dy[:, lanes], spread)
                d_score = d_score + decays[0] * products[:, :Q] + decays[1] * products[:, Q:]
            dscores[rows, :] = d_score
            inside = jnp.concatenate(insides, axis=1) + entering * dot(c_ref[rows, :], before_low)
            back_inside = jnp.concatenate(backs, axis=1)
            back_state = leaving * dot(b_ref[rows, :], d_low)
            high, low = in_two(dy_wide * inside - scaled_wide * back_inside)
            suffix[rows, :] += dot(high, gather) + dot(low, gather)
            prefix[rows, :] += dot((scaled_wide * back_state).astype(BF16), gather)
            back = back_inside + back_state
            d_dt[rows, :] += dot((values * back).astype(BF16), gather)
            entered = (dy_wide * entering).astype(BF16)
            d_c[rows, :] += dot_nt(entered, before_low)
            d_b[rows, :] += dot_nt((scaled_wide * leaving).astype(BF16), d_low)
            kept = entering[Q - 1 : Q, :]
            through = jnp.sum(before * d_state, axis=0, keepdims=True) * kept
            high, low = in_two(jnp.broadcast_to(through, (8, BLK)))
            fixed[k * 8 : (k + 1) * 8, :] += dot(high, gather) + dot(low, gather)
            d_state = kept * d_state + dot(c_t[:, rows], entered)
            dact[rows, :] = back * step_size + skip * dy_wide

    @pl.when(step == STEPS)
    def _():
        for k in range(chunks):
            rows = slice(k * Q, (k + 1) * Q)
            own = seg_ref[PAD + k * Q : PAD + (k + 1) * Q, :]
            keep = (own == row_ref[0:1, rows]) & (iota((Q, Q), 1) <= iota((Q, Q), 0))
            d_score = jnp.where(keep, dscores[rows, :], 0.0)
            dact[rows, STATE:] = d_c[rows, :] + dot(d_score.astype(BF16), b_ref[rows, :])
            dact[rows, :STATE] = d_b[rows, :] + dot(d_score.T.astype(BF16), c_ref[rows, :])

    @pl.when(step <= STEPS)
    def _():
        sums = [jnp.zeros((1, BLK), F32) for _ in range(CONV + 1)]
        for k in range(chunks):
            rows = slice(k * Q, (k + 1) * Q)
            total = pre[rows, :]
            sig = sigmoid(total)
            d_conv = dact[rows, :] * (sig * (1.0 + total * (1.0 - sig)))
            dbuf[PAD + k * Q : PAD + (k + 1) * Q, :] = d_conv
            sums[4] = sums[4] + jnp.sum(d_conv, axis=0, keepdims=True)
            own = seg_ref[PAD + k * Q : PAD + (k + 1) * Q, :]
            for shift in range(CONV):
                at = PAD + k * Q - shift
                term = d_conv * ext[at : at + Q, :]
                if shift:
                    term = jnp.where(both(seg_ref[at : at + Q, :] == own), term, 0.0)
                sums[3 - shift] = sums[3 - shift] + jnp.sum(term, axis=0, keepdims=True)
        write_taps(jnp.concatenate(sums + [jnp.zeros((3, BLK), F32)], axis=0))

        def returned(at, rows):
            own = seg_ref[at : at + rows, :]
            result = taps_ref[3:4, :] * dbuf[at : at + rows, :]
            for shift in range(1, CONV):
                same = both(seg_ref[at + shift : at + shift + rows, :] == own)
                result = result + jnp.where(
                    same, taps_ref[3 - shift : 4 - shift, :] * dbuf[at + shift : at + shift + rows, :], 0.0
                )
            return result

        write_halo(returned(0, PAD))
        for k in range(chunks):
            write(slice(k * Q, (k + 1) * Q), returned(PAD + k * Q, Q).astype(BF16))

    @pl.when(step == STEPS + 1)
    def _():
        lower = (iota((Q, Q), 1) < iota((Q, Q), 0)).astype(F32)
        upper = (iota((Q, Q), 1) >= iota((Q, Q), 0)).astype(F32)
        lane = iota((Q, 128), 1)
        rate = jnp.exp(heads_ref[1:2, :])
        bias_sum = jnp.zeros((1, 128), F32)
        decay_sum = jnp.zeros((1, 128), F32)
        for k in range(chunks):
            rows = slice(k * Q, (k + 1) * Q)
            d_log = jnp.dot(upper, suffix[rows, :], precision=HIGHEST, preferred_element_type=F32)
            d_log = d_log + jnp.dot(lower, prefix[rows, :], precision=HIGHEST, preferred_element_type=F32)
            d_log = d_log + fixed[k * 8 : k * 8 + 1, :]
            raw = jnp.where(lane < HEADS, dtraw_ref[rows, :128].astype(F32), 0.0) + heads_ref[0:1, :]
            d_raw = jnp.where(lane < HEADS, (d_dt[rows, :] - rate * d_log) * sigmoid(raw), 0.0)
            bias_sum = bias_sum + jnp.sum(d_raw, axis=0, keepdims=True)
            decay_sum = decay_sum - jnp.sum(d_log * dt_ref[rows, :] * rate, axis=0, keepdims=True)
            write(rows, jnp.concatenate([d_raw, jnp.zeros_like(d_raw)], axis=1).astype(BF16))
        write_heads(jnp.concatenate([bias_sum, decay_sum, jnp.zeros((6, 128), F32)], axis=0))


def back_kernel(*refs):
    given, (_, dproj_ref, dhalo_ref, dtaps_ref, dheads_ref), scratch = refs[:14], refs[14:19], refs[19:]

    def write(rows, value):
        dproj_ref[rows, :] = value

    def write_halo(value):
        dhalo_ref[...] = value

    def write_taps(value):
        dtaps_ref[...] = value

    def write_heads(value):
        dheads_ref[...] = value

    back_steps(pl.program_id(0), given, scratch, write, write_halo, write_taps, write_heads)


def back_scratch(length):
    return [
        pltpu.VMEM((length + PAD, BLK), F32),
        pltpu.VMEM((length, BLK), F32),
        pltpu.VMEM((length, BLK), F32),
        pltpu.VMEM((length + 2 * PAD, BLK), F32),
        pltpu.VMEM((length, Q), F32),
        pltpu.VMEM((length, Q), F32),
        pltpu.VMEM((length // Q, 128, Q), F32),
        pltpu.VMEM((128, length), BF16),
        pltpu.VMEM((128, length), BF16),
        *[pltpu.VMEM((length, 128), F32) for _ in range(7)],
        pltpu.VMEM((8 * (length // Q), 128), F32),
        pltpu.VMEM((length // Q, STATE, BLK), F32),
    ]


def back_inputs(length, late=0):
    whole = lambda *shape: pl.BlockSpec(shape, lambda j: (0,) * len(shape))
    upto = lambda last, first=0: lambda j: (0, first + jnp.clip(j - late, 0, last))
    return [
        pl.BlockSpec((length, BLK), upto(STEPS, STEPS)),
        pl.BlockSpec((length, BLK), lambda j: (0, 2 * STEPS + 1)),
        pl.BlockSpec((PAD, BLK), upto(STEPS, STEPS)),
        pl.BlockSpec((8, BLK), upto(STEPS)),
        whole(8, 128),
        whole(length + 2 * PAD, 128),
        whole(1, length),
        whole(length, 128),
        whole(length, 128),
        whole(length, 128),
        whole(length, 128),
        pl.BlockSpec((length, BLK), upto(STEPS - 1)),
        pl.BlockSpec((STATE, BLK), upto(STEPS - 1)),
        whole(STATE, INNER) if late else pl.BlockSpec((STATE, BLK), upto(STEPS - 1)),
    ]


def back(given, dproj):
    length = dproj.shape[0]
    upto = lambda last, first=0: lambda j: (0, first + jnp.minimum(j, last))
    return pl.pallas_call(
        back_kernel,
        grid=(STEPS + 2,),
        in_specs=[*back_inputs(length), pl.BlockSpec(memory_space=pl.ANY)],
        out_specs=[
            pl.BlockSpec((length, BLK), lambda j: (0, STEPS + j)),
            pl.BlockSpec((PAD, BLK), upto(STEPS)),
            pl.BlockSpec((8, BLK), upto(STEPS)),
            pl.BlockSpec((8, 128), lambda j: (0, 0)),
        ],
        out_shape=[
            jax.ShapeDtypeStruct((length, WIDTH), BF16),
            jax.ShapeDtypeStruct((PAD, XBC), F32),
            jax.ShapeDtypeStruct((8, XBC), F32),
            jax.ShapeDtypeStruct((8, 128), F32),
        ],
        scratch_shapes=back_scratch(length),
        input_output_aliases={14: 0},
        compiler_params=pltpu.CompilerParams(vmem_limit_bytes=VMEM_LIMIT),
        name="back",
    )(*given, dproj)


OUT_CHUNKS = 2 * D // WIDE
GATE_CHUNKS = INNER // WIDE
IN_CHUNKS = WIDTH // WIDE
CHUNKS = OUT_CHUNKS + IN_CHUNKS
LAGS = 8
RING = 8
LATE = 3


def small_sums(taps, columns, input_gain, heads, stats):
    fill = lambda width: jnp.zeros((1, width), F32)
    squares = [jnp.broadcast_to(jnp.sum(stats[i : i + 1], axis=1, keepdims=True), (1, 128)) for i in range(2)]
    return jnp.concatenate(
        [
            taps[:5],
            jnp.concatenate([columns[0:1], fill(XBC - INNER)], axis=1),
            jnp.concatenate([columns[1:2], fill(XBC - INNER)], axis=1),
            jnp.concatenate([input_gain, heads[0:1], heads[1:2], *squares, fill(XBC - D - 512)], axis=1),
        ],
        axis=0,
    )


def finish_kernel(*refs):
    given, refs = refs[:14], refs[14:]
    lhs_in, lhs_out, gate_ref, weight_ref, cot_ref, units_ref, gain_ref, columns_ref, stats_ref, kept_ref = refs[:10]
    din_ref, dout_ref, input_grad_ref, total_ref = refs[10:14]
    scratch, refs = refs[14:32], refs[32:]
    exchange, outgoing, refs = Exchange(*refs[:5]), refs[5], refs[6:]
    grads, edges, halos, taps, heads, d_normed = refs[:6]
    own, core_send, core_recv, y_recv, x_recv, z_recv, w_recv, final, small_send, small_recv = refs[6:16]
    send_sems, recv_sems, small_send_sems, small_recv_sems, edge_sends, edge_arrivals = refs[16:]
    step = pl.program_id(0)
    length = cot_ref.shape[0]
    shard, part = lax.axis_index("fsdp"), lax.axis_index("ctx")
    core, y = lax.rem(shard, 2), shard // 2
    x, z = lax.rem(part, 2), part // 2
    near, far = lax.rem(z, 2), z // 2
    peers = (
        {"fsdp": flipped(shard, 1)},
        {"fsdp": flipped(shard, 2)},
        {"ctx": flipped(part, 1)},
        {"ctx": flipped(part, 2)},
        {"ctx": flipped(part, 4)},
    )
    preceding = lax.rem(part + PARTS - 1, PARTS)

    def ring(k):
        return lax.rem(k, RING)

    def sent(stage, k, source, target, peer):
        return remote(source, target, send_sems.at[stage, k], recv_sems.at[stage, k], peers[peer])

    copies = (
        lambda k: sent(0, k, core_send.at[lax.rem(k, 2)], core_recv.at[ring(k)], 0),
        lambda k: sent(1, k, core_recv.at[ring(k), 1 - y], y_recv.at[ring(k)], 1),
        lambda k: sent(2, k, y_recv.at[ring(k), 1 - x], x_recv.at[ring(k)], 2),
        lambda k: sent(3, k, x_recv.at[ring(k), 1 - near], z_recv.at[ring(k)], 3),
        lambda k: sent(4, k, z_recv.at[ring(k), 1 - far], w_recv.at[ring(k)], 4),
        lambda k: sent(5, k, final.at[ring(k), x, near, far], final.at[ring(k), x, near, far], 4),
        lambda k: sent(6, k, final.at[ring(k), x, near], final.at[ring(k), x, near], 3),
        lambda k: sent(7, k, final.at[ring(k), x], final.at[ring(k), x], 2),
    )
    arrivals = copies[:5] + (
        lambda k: sent(5, k, final.at[ring(k), x, near, 1 - far], final.at[ring(k), x, near, 1 - far], 4),
        lambda k: sent(6, k, final.at[ring(k), x, 1 - near], final.at[ring(k), x, 1 - near], 3),
        lambda k: sent(7, k, final.at[ring(k), 1 - x], final.at[ring(k), 1 - x], 2),
    )

    def small_copy(stage):
        return remote(
            small_send.at[stage], small_recv.at[stage], small_send_sems.at[stage], small_recv_sems.at[stage], peers[stage]
        )

    def edge_copy(block):
        return remote(
            edges.at[block], halos.at[block], edge_sends.at[block], edge_arrivals.at[block], {"ctx": preceding}
        )

    @pl.when(step == 0)
    def _():
        exchange.greet(peers[0], peers[1])
        for group in range(STEPS):
            exchange.hold(group // 2, group % 2, given[13][:, group * BLK : (group + 1) * BLK])
            if group % 2:
                exchange.spread(group // 2)
        d_normed[...] = jnp.zeros_like(d_normed)

    def partial(lhs_of, rhs):
        for row in range(2):
            value = dot(lhs_of(2 * row + 1 - core), rhs).astype(BF16)
            core_send[lax.rem(step, 2), row] = value.reshape(2, 2, 2, PIECE, WIDE)
        copies[0](step).start()
        for row in range(2):
            own[row] = dot(lhs_of(2 * row + core), rhs).reshape(2, 2, 2, PIECE, WIDE)

    def in_chunk(rhs):
        partial(lambda s: lhs_in[s], rhs)
        d_normed[...] += dot(rhs, weight_ref[...])

    @pl.when(step < OUT_CHUNKS)
    def _():
        columns = lax.rem(step, D // WIDE) * WIDE
        rhs = cot_ref[:, pl.ds(pl.multiple_of(columns, WIDE), WIDE)]
        partial(lambda s: lhs_out[s, step // (D // WIDE)], rhs)

    @pl.when((step >= OUT_CHUNKS) & (step < OUT_CHUNKS + GATE_CHUNKS))
    def _():
        in_chunk(gate_ref[...])

    @pl.when((step >= OUT_CHUNKS + GATE_CHUNKS) & (step < CHUNKS))
    def _():
        first = 2 * (step - OUT_CHUNKS - GATE_CHUNKS)
        for done in (first, first + 1):

            @pl.when(done <= STEPS)
            def _():
                edge_copy(done).wait()
                tail = slice(length - 16, length)
                more = jnp.where(part == PARTS - 1, 0.0, halos[done])
                more = jnp.concatenate([jnp.zeros_like(more), more], axis=0)
                grads[done, tail, :] = (grads[done, tail, :].astype(F32) + more).astype(BF16)

        in_chunk(jnp.concatenate([grads[first], grads[first + 1]], axis=1))

    for half in range(2):

        @pl.when(step == 1 + half)
        def _():
            for unit in range(half * UNITS // 2, (half + 1) * UNITS // 2):
                exchange.join(unit, kept_of(kept_ref, unit), False)

    block = step - LATE

    def write(rows, value):
        grads[block, rows, :] = value

    def write_halo(value):
        edges[block] = value
        edge_copy(block).start()

    def write_taps(value):
        taps[block] = value

    def write_heads(value):
        heads[...] = value

    @pl.when((block >= 0) & (block < STEPS) & (lax.rem(block, 2) == 0))
    def _():
        both_groups = exchange.finish(block // 2)
        outgoing[0] = both_groups[:, :BLK]
        outgoing[1] = both_groups[:, BLK:]

    @pl.when(block >= 0)
    def _():
        back_steps(block, (*given[:13], outgoing.at[lax.rem(block, 2)]), scratch, write, write_halo, write_taps, write_heads)

    @pl.when(step < CHUNKS)
    def _():
        arrivals[0](step).wait_recv()
        for row in (1 - y, y):
            core_recv[ring(step), row] = (own[row] + core_recv[ring(step), row].astype(F32)).astype(BF16)
        copies[1](step).start()

    def stage(lag):
        def decorate(body):
            k = step - lag

            @pl.when((k >= 0) & (k < CHUNKS))
            def _():
                body(k, ring(k))

        return decorate

    def summed(a, b):
        return (a.astype(F32) + b.astype(F32)).astype(BF16)

    @stage(1)
    def _(k, at):
        arrivals[1](k).wait_recv()
        y_recv[at] = summed(y_recv[at], core_recv[at, y])
        copies[2](k).start()
        copies[0](k).wait_send()

    @stage(2)
    def _(k, at):
        arrivals[2](k).wait_recv()
        x_recv[at] = summed(x_recv[at], y_recv[at, x])
        copies[3](k).start()

    @stage(3)
    def _(k, at):
        arrivals[3](k).wait_recv()
        z_recv[at] = summed(z_recv[at], x_recv[at, near])
        copies[4](k).start()
        copies[1](k).wait_send()

    @stage(4)
    def _(k, at):
        arrivals[4](k).wait_recv()
        final[at, x, near, far] = summed(w_recv[at], z_recv[at, far])
        copies[5](k).start()
        copies[2](k).wait_send()

    @stage(5)
    def _(k, at):
        arrivals[5](k).wait_recv()
        copies[6](k).start()
        copies[3](k).wait_send()

    @stage(6)
    def _(k, at):
        arrivals[6](k).wait_recv()
        copies[7](k).start()
        copies[4](k).wait_send()

    @stage(7)
    def _(k, at):
        arrivals[7](k).wait_recv()
        for one in (5, 6, 7):
            copies[one](k).wait_send()
        whole = final[at].reshape(SHARD, WIDE)

        @pl.when(k < OUT_CHUNKS)
        def _():
            dout_ref[...] = whole

        @pl.when(k >= OUT_CHUNKS)
        def _():
            din_ref[...] = whole.astype(F32).T.astype(BF16)

    @pl.when(step == CHUNKS)
    def _():
        input_gain = jnp.zeros((1, D), F32)
        for k in range(length // Q):
            rows = slice(k * Q, (k + 1) * Q)
            units = units_ref[rows, :].astype(F32)
            norm = lax.rsqrt(jnp.sum(units * units, axis=1, keepdims=True) * (1.0 / D) + epsilon)
            base = units * norm
            grad = d_normed[rows, :]
            input_gain = input_gain + jnp.sum(grad * base, axis=0, keepdims=True)
            scaled = grad * gain_ref[0:1, :]
            mean = jnp.sum(scaled * base, axis=1, keepdims=True) * (1.0 / D)
            input_grad_ref[rows, :] = (cot_ref[rows, :].astype(F32) + norm * (scaled - base * mean)).astype(BF16)
        whole = jnp.concatenate([taps[one] for one in range(STEPS + 1)], axis=1)
        small_send[0] = small_sums(whole, columns_ref[...], input_gain, heads[...], stats_ref[...])
        small_copy(0).start()

    for stage_of_small in range(5):

        @pl.when(step == CHUNKS + 1 + stage_of_small)
        def _():
            small_copy(stage_of_small).wait()
            total = small_send[stage_of_small] + small_recv[stage_of_small]
            if stage_of_small < 4:
                small_send[stage_of_small + 1] = total
                small_copy(stage_of_small + 1).start()
            else:
                total_ref[...] = total


def finish(given, normed_t, mixer_t, dproj, w_turned, cot, units, input_gain, column_sums, stats, kept):
    length = cot.shape[0]
    per_half = D // WIDE
    once = pl.Buffered(1)
    whole = lambda *shape: pl.BlockSpec(shape, lambda t: (0,) * len(shape), pipeline_mode=once)
    in_chunk = lambda t: jnp.clip(t - OUT_CHUNKS, 0, IN_CHUNKS - 1)

    def out_block(t):
        k = jnp.clip(t - LAGS + 1, 0, OUT_CHUNKS - 1)
        return (k // per_half, lax.rem(k, per_half))

    slots = lambda *shape: pltpu.VMEM((RING, *shape, PIECE, WIDE), BF16)
    return pl.pallas_call(
        finish_kernel,
        grid=(CHUNKS + LAGS - 1,),
        in_specs=[
            *back_inputs(length, LATE),
            whole(4, SHARD, length),
            whole(4, 2, SHARD, length),
            pl.BlockSpec((length, WIDE), lambda t: (0, jnp.minimum(in_chunk(t), GATE_CHUNKS - 1))),
            pl.BlockSpec((WIDE, D), lambda t: (in_chunk(t), 0)),
            whole(length, D),
            whole(length, D),
            whole(1, D),
            whole(8, INNER),
            whole(8, D),
            whole(PARTS, 8, 128),
        ],
        out_specs=[
            pl.BlockSpec((WIDE, SHARD), lambda t: (in_chunk(t - LAGS + 1), 0)),
            pl.BlockSpec((SHARD, WIDE), out_block),
            pl.BlockSpec((length, D), lambda t: (0, 0)),
            pl.BlockSpec((8, XBC), lambda t: (0, 0)),
        ],
        out_shape=[
            jax.ShapeDtypeStruct((PROJ, SHARD), BF16),
            jax.ShapeDtypeStruct((2 * SHARD, D), BF16),
            jax.ShapeDtypeStruct((length, D), BF16),
            jax.ShapeDtypeStruct((8, XBC), F32),
        ],
        scratch_shapes=[
            *back_scratch(length),
            *exchange_scratch(),
            pltpu.VMEM((2, STATE, BLK), BF16),
            pltpu.VMEM((STEPS + 2, length, BLK), BF16),
            pltpu.VMEM((STEPS + 1, PAD, BLK), F32),
            pltpu.VMEM((STEPS + 1, PAD, BLK), F32),
            pltpu.VMEM((STEPS + 1, 8, BLK), F32),
            pltpu.VMEM((8, 128), F32),
            pltpu.VMEM((length, D), F32),
            pltpu.VMEM((2, 2, 2, 2, PIECE, WIDE), F32),
            pltpu.VMEM((2, 2, 2, 2, 2, PIECE, WIDE), BF16),
            slots(2, 2, 2, 2),
            slots(2, 2, 2),
            slots(2, 2),
            slots(2),
            slots(),
            slots(2, 2, 2),
            pltpu.VMEM((5, 8, XBC), F32),
            pltpu.VMEM((5, 8, XBC), F32),
            pltpu.SemaphoreType.DMA((8, CHUNKS)),
            pltpu.SemaphoreType.DMA((8, CHUNKS)),
            pltpu.SemaphoreType.DMA((5,)),
            pltpu.SemaphoreType.DMA((5,)),
            pltpu.SemaphoreType.DMA((STEPS + 1,)),
            pltpu.SemaphoreType.DMA((STEPS + 1,)),
        ],
        compiler_params=communicating(0),
        name="finish",
    )(*given, normed_t, mixer_t, dproj, w_turned, cot, units, input_gain, column_sums, stats, kept)


def settle_kernel(din_ref, dout_ref, total_ref, *outs, entries):
    (
        din_out, dout_out, taps_out, bias_out, step_bias_out, decay_out, skip_out, gain_out, input_gain_out, rms_out,
    ) = outs
    din_out[...] = din_ref[...].astype(F32)
    dout_out[...] = dout_ref[...].astype(F32)

    @pl.when(pl.program_id(0) == 0)
    def _():
        shard = lax.axis_index("fsdp")
        own = HEADS // 4
        width = XBC // 4

        def mine(pieces):
            result = pieces[0]
            for s in range(1, 4):
                result = jnp.where(shard == s, pieces[s], result)
            return result

        def flat(ref, row):
            ref[...] = row.reshape(ref.shape)

        total = total_ref[...]
        columns = mine([pltpu.roll(total, (XBC - s * width) % XBC, 1) if s else total for s in range(4)])
        taps_out[...] = columns[:4, :width]
        flat(bias_out, columns[4:5, :width])

        def heads(row):
            rows = jnp.broadcast_to(row, (8, 128))
            rows = mine([pltpu.roll(rows, (128 - s * own) % 128, 1) if s else rows for s in range(4)])
            return rows[:1, :own]

        flat(step_bias_out, heads(total[7:8, D : D + 128]))
        flat(decay_out, heads(total[7:8, D + 128 : D + 256]))
        skip = jnp.zeros((8, 128), F32)
        for group in range(STEPS):
            high, low = in_two(jnp.broadcast_to(total[6:7, group * BLK : (group + 1) * BLK], (8, BLK)))
            skip = skip + dot(high, chosen_back(group)) + dot(low, chosen_back(group))
        flat(skip_out, heads(skip[:1]))
        flat(gain_out, mine([total[5:6, s * (INNER // 4) : (s + 1) * (INNER // 4)] for s in range(4)]))
        flat(input_gain_out, mine([total[7:8, s * SHARD : (s + 1) * SHARD] for s in range(4)]))
        squares = jnp.concatenate([total[7:8, D + 256 : D + 257], total[7:8, D + 384 : D + 385]], axis=1)
        flat(rms_out, jnp.sqrt(squares * (1.0 / entries)))


def settle(d_in, d_out, total, entries):
    steps = 6
    shapes = [
        (4, XBC // 4),
        (XBC // 4,),
        (HEADS // 4,),
        (HEADS // 4,),
        (HEADS // 4,),
        (INNER // 4,),
        (SHARD,),
        (2,),
    ]
    rows = -(-PROJ // steps // 16) * 16
    whole = lambda shape: pl.BlockSpec(shape, lambda i: (0,) * len(shape))
    blocks = [
        pl.BlockSpec((rows, SHARD), lambda i: (i, 0)),
        pl.BlockSpec((2 * SHARD // steps, D), lambda i: (i, 0)),
    ]
    d_in, d_out, taps, *rest = pl.pallas_call(
        functools.partial(settle_kernel, entries=entries),
        grid=(steps,),
        in_specs=[*blocks, whole((8, XBC))],
        out_specs=[*blocks, *[whole(shape) for shape in shapes]],
        out_shape=[
            jax.ShapeDtypeStruct((PROJ, SHARD), F32),
            jax.ShapeDtypeStruct((2 * SHARD, D), F32),
            *[jax.ShapeDtypeStruct(shape, F32) for shape in shapes],
        ],
        compiler_params=pltpu.CompilerParams(vmem_limit_bytes=VMEM_LIMIT),
        name="settle",
    )(d_in, d_out, total)
    return (d_in.T, d_out, taps.T, *[each.reshape(-1) for each in rest])


def passed_along(block, axis, distance):
    devices = range(lax.axis_size(axis))
    route = [(i - distance, i) for i in devices if i - distance in devices]
    return lax.ppermute(block, axis, route)


def pack_small(conv_taps, conv_bias, dt_bias, decay_log, skip_scale, mixer_gain, input_gain):
    width = conv_bias.shape[0]

    def line(*parts):
        flat = jnp.concatenate(parts)
        return jnp.pad(flat, (0, width - flat.shape[0]))[None]

    rows = jnp.concatenate(
        [
            conv_taps.T,
            conv_bias[None],
            line(mixer_gain),
            line(input_gain),
            line(dt_bias, decay_log, skip_scale),
        ],
        axis=0,
    )
    return jnp.pad(rows.astype(F32), ((0, 0), (0, SMALL_WIDTH - width)))


def unpack_small(whole, width):
    shards = whole.shape[0]
    joined = jnp.swapaxes(whole, 0, 1)
    taps = jnp.pad(joined[:5, :, :width].reshape(5, shards * width).astype(F32), ((0, 3), (0, 0)))
    gain = joined[5, :, : INNER // shards].reshape(1, INNER).astype(F32)
    input_gain = joined[6, :, : D // shards].reshape(1, D).astype(F32)
    own = HEADS // shards
    heads = joined[7, :, : 3 * own].reshape(shards, 3, own).swapaxes(0, 1).reshape(3, HEADS)
    heads = jnp.pad(heads.astype(F32), ((0, 5), (0, 128 - HEADS)))
    return taps, jnp.pad(gain, ((0, 7), (0, 0))), input_gain, heads


def on_device(
    inputs,
    segment_ids,
    out_grad,
    in_matrix,
    out_matrix,
    conv_taps,
    conv_bias,
    dt_bias,
    decay_log,
    skip_scale,
    mixer_gain,
    input_gain,
):
    shards, parts = lax.axis_size("fsdp"), lax.axis_size("ctx")
    place = lax.axis_index("ctx")
    units_low, cot = inputs[0], out_grad[0]
    seg_ids = segment_ids[0]
    length = units_low.shape[0]
    here = (shards, parts) == (4, PARTS)
    seg_row = segment_ids
    if here:
        (
            xs, y_local, incoming, b_rows, c_rows, dt, running, entering,
            kept, w_turned, out_whole, projected, normed_t, halo, taps, heads, gain, g_float, seg_lanes,
        ) = forward(
            in_matrix, out_matrix, units_low, seg_row,
            conv_taps.T, conv_bias, mixer_gain, input_gain, dt_bias, decay_log, skip_scale,
        )
        out_whole = out_whole.reshape(-1, D)
    else:
        units = units_low.astype(F32)
        inv_rms = lax.rsqrt(jnp.mean(units * units, axis=-1, keepdims=True) + epsilon)
        base_rows = units * inv_rms
        w_whole = jnp.pad(in_matrix, ((0, 0), (0, WIDTH - PROJ)))
        w_whole = lax.all_gather(w_whole, "fsdp", axis=0, tiled=True)
        out_whole = lax.all_gather(out_matrix, "fsdp", axis=0, tiled=True)
        rim_seg = passed_along(seg_ids[length - CONV + 1 :], "ctx", 1)
        small = pack_small(conv_taps, conv_bias, dt_bias, decay_log, skip_scale, mixer_gain, input_gain)
        taps, gain, g_float, heads = unpack_small(lax.all_gather(small, "fsdp"), conv_bias.shape[0])
        normed = (base_rows * g_float).astype(BF16)
        normed_t = normed.T
        projected = dot(normed, w_whole).astype(BF16)
        rim_rows = passed_along(projected[length - CONV + 1 :], "ctx", 1)
        halo = jnp.pad(rim_rows, ((PAD - CONV + 1, 0), (0, 0))).astype(F32)
        seg_ext = jnp.concatenate(
            [
                jnp.full((PAD - CONV + 1,), -1, jnp.int32),
                rim_seg,
                seg_ids,
                jnp.full((PAD,), -2, jnp.int32),
            ]
        )
        seg_lanes = jnp.broadcast_to(seg_ext[:, None], (length + 2 * PAD, 128))
        xs, y_local, state, b_rows, c_rows, dt, running, entering, keep = front(
            projected, halo, taps, heads, seg_lanes, seg_row
        )
        kept = lax.all_gather(keep, "ctx")
        incoming = joined_plainly(lax.all_gather(state, "ctx"), kept, place, True)
    mixer_t, dproj, dy, outgoing, column_sums, block_out, stats = tail(
        y_local, xs, projected, incoming, out_whole, c_rows, entering, heads, gain, cot, units_low
    )
    if not here:
        outgoing = joined_plainly(lax.all_gather(outgoing, "ctx"), kept, place, False)
    given = (
        projected, projected, halo, taps, heads, seg_lanes, seg_row, b_rows, c_rows, dt, running, dy, incoming, outgoing,
    )
    if here:
        d_in, d_out, input_grad, total = finish(
            given, normed_t, mixer_t.reshape(4, 2, SHARD, length), dproj, w_turned, cot, units_low, g_float, column_sums, stats, kept
        )
        sums = settle(d_in, d_out, total, length * shards * parts * D)
        return (block_out[None], input_grad[None], *sums)
    else:
        dproj, d_halo, d_taps, d_heads = back(given, dproj)
        returned = passed_along(d_halo.astype(BF16), "ctx", -1)
        last = lax.slice(dproj, (length - PAD, INNER), (length, INNER + XBC))
        last = (last.astype(F32) + returned.astype(F32)).astype(BF16)
        dproj = lax.dynamic_update_slice(dproj, last, (length - PAD, INNER))
        d_normed = dot_nt(dproj, w_whole)
        d_input_gain = jnp.sum(d_normed * base_rows, axis=0)
        d_base = d_normed * g_float
        d_units = inv_rms * (d_base - base_rows * jnp.mean(d_base * base_rows, axis=-1, keepdims=True))
        input_grad = (cot.astype(F32) + d_units).astype(BF16)

        def scattered(grad):
            return lax.psum_scatter(grad.astype(BF16), "fsdp", scatter_dimension=0, tiled=True)

        d_in = jnp.dot(normed_t, dproj, preferred_element_type=F32)[:, :PROJ]
        d_out = jnp.dot(mixer_t, cot, preferred_element_type=F32)
        d_in = lax.psum(scattered(d_in), "ctx").astype(F32)
        d_out = lax.psum(scattered(d_out), "ctx").astype(F32)
        total = lax.psum(small_sums(d_taps, column_sums, d_input_gain[None], d_heads, stats), ("fsdp", "ctx"))
    me = lax.axis_index("fsdp")

    def own(flat):
        size = flat.shape[-1] // shards
        return lax.dynamic_slice_in_dim(flat, me * size, size, flat.ndim - 1)

    skip_sums = jnp.sum(total[6, :INNER].reshape(HEADS, HDIM), axis=1)
    at = D + 256
    stat_sums = jnp.stack([total[7, at], total[7, at + 128]])
    rms_stats = jnp.sqrt(stat_sums / (length * shards * parts * D))
    return (
        block_out[None],
        input_grad[None],
        d_in,
        d_out,
        own(total[:4]).T,
        own(total[4]),
        own(total[7, D : D + HEADS]),
        own(total[7, D + 128 : D + 128 + HEADS]),
        own(skip_sums),
        own(total[5, :INNER]),
        own(total[7, :D]),
        rms_stats,
    )


def solution(mesh):
    return jax.shard_map(
        on_device,
        mesh=mesh,
        in_specs=(
            P("fsdp", "ctx", None),
            P("fsdp", "ctx"),
            P("fsdp", "ctx", None),
            P("fsdp", None),
            P("fsdp", None),
            P("fsdp", None),
            P("fsdp"),
            P("fsdp"),
            P("fsdp"),
            P("fsdp"),
            P("fsdp"),
            P("fsdp"),
        ),
        out_specs=(
            P("fsdp", "ctx", None),
            P("fsdp", "ctx", None),
            P("fsdp", None),
            P("fsdp", None),
            P("fsdp", None),
            P("fsdp"),
            P("fsdp"),
            P("fsdp"),
            P("fsdp"),
            P("fsdp"),
            P("fsdp"),
            P(),
        ),
        check_vma=False,
    )
```

```python
import functools

import jax
import jax.numpy as jnp
from jax import lax
from jax.experimental import pallas as pl
from jax.experimental.pallas import tpu as pltpu
from jax.sharding import PartitionSpec as P

D = 1536
HEADS = 48
HDIM = 64
STATE = 128
CONV = 4
INNER = 3072
XBC = 3328
PROJ = 6448
WIDTH = 6656

BLK = 256
GROUP = BLK // HDIM
STEPS = INNER // BLK
Q = 128
PAD = 8
WIDE = 512
SHARD = D // 4
PIECE = SHARD // 8
SMALL_WIDTH = 896
AHEAD = 2

epsilon = 1e-05
F32, BF16 = jnp.float32, jnp.bfloat16
HIGHEST = lax.Precision.HIGHEST
VMEM_LIMIT = 60 * 1024 * 1024


def communicating(number):
    return pltpu.CompilerParams(
        vmem_limit_bytes=VMEM_LIMIT, collective_id=number, has_side_effects=True
    )


def dot(a, b):
    return jnp.dot(a, b, preferred_element_type=F32)


def dot_nt(a, b):
    return lax.dot_general(a, b, (((1,), (1,)), ((), ())), preferred_element_type=F32)


def iota(shape, dim):
    return lax.broadcasted_iota(jnp.int32, shape, dim)


def sigmoid(v):
    return 0.5 + 0.5 * jnp.tanh(0.5 * v)


def in_two(a):
    high = a.astype(BF16)
    return high, (a - high.astype(F32)).astype(BF16)


def chosen(step):
    columns = step * GROUP + lax.shift_right_logical(iota((128, BLK), 1), 6)
    return (iota((128, BLK), 0) == columns).astype(BF16)


def chosen_back(step):
    heads = step * GROUP + lax.shift_right_logical(iota((BLK, 128), 0), 6)
    return (iota((BLK, 128), 1) == heads).astype(BF16)


def widen(per_head, select):
    high, low = in_two(per_head)
    return dot(high, select) + dot(low, select)


def halves(pair):
    first = iota(pair.shape, 1) < HDIM
    zero = jnp.zeros_like(pair)
    return jnp.concatenate([jnp.where(first, pair, zero), jnp.where(first, zero, pair)], axis=0)


def both(mask):
    return jnp.concatenate([mask, mask], axis=1)


def conv_rows(ext_ref, seg_ref, taps_ref, start, rows):
    own = seg_ref[start + PAD : start + PAD + rows, :]
    total = taps_ref[4:5, :] + taps_ref[3:4, :] * ext_ref[start + PAD : start + PAD + rows, :]
    for back in range(1, CONV):
        at = start + PAD - back
        same = both(seg_ref[at : at + rows, :] == own)
        total = total + jnp.where(
            same, taps_ref[3 - back : 4 - back, :] * ext_ref[at : at + rows, :], 0.0
        )
    return total


def chunk_flags(seg_ref, k):
    own = seg_ref[PAD + k * Q : PAD + (k + 1) * Q, :]
    before = seg_ref[PAD + k * Q - 1 : PAD + k * Q, :]
    last = seg_ref[PAD + (k + 1) * Q - 1 : PAD + (k + 1) * Q, :]
    return (own == before).astype(F32), (own == last).astype(F32)


def masked_scores(seg_ref, row_ref, b_rows, c_rows, k):
    own = seg_ref[PAD + k * Q : PAD + (k + 1) * Q, :]
    row = row_ref[0:1, k * Q : (k + 1) * Q]
    keep = (own == row) & (iota((Q, Q), 1) <= iota((Q, Q), 0))
    return jnp.where(keep, dot_nt(c_rows, b_rows), 0.0)


def remote(source, target, send, arrival, peer):
    return pltpu.make_async_remote_copy(
        src_ref=source,
        dst_ref=target,
        send_sem=send,
        recv_sem=arrival,
        device_id=peer,
        device_id_type=pl.DeviceIdType.MESH,
    )


def flipped(index, bit):
    return index + bit - 2 * bit * lax.rem(index // bit, 2)


class Gather:
    def __init__(self, locate, several, rows, loads, sends, arrivals):
        self.locate, self.several, self.rows = locate, several, rows
        self.loads, self.sends, self.arrivals = loads, sends, arrivals
        shard, part = lax.axis_index("fsdp"), lax.axis_index("ctx")
        self.own, self.other = shard, flipped(shard, 2)
        x, near = lax.rem(part, 2), lax.rem(part // 2, 2)
        self.mine, self.over_x, self.over_z = 2 * x + near, 2 * (1 - x) + near, 2 * x + 1 - near
        self.across = 2 * (1 - x) + 1 - near
        self.core, self.y = {"fsdp": flipped(shard, 1)}, {"fsdp": flipped(shard, 2)}
        self.to_x, self.to_z = {"ctx": flipped(part, 1)}, {"ctx": flipped(part, 2)}

    def whole(self, shard, k):
        return self.locate(k, shard, 0, self.rows)

    def quarter(self, shard, k, which):
        return self.locate(k, shard, which * (self.rows // 4), self.rows // 4)

    def half(self, shard, k, which, second):
        return self.locate(k, shard, (2 * which + second) * (self.rows // 8), self.rows // 8)

    def copy(self, place, kind, k, peer):
        return remote(place, place, self.sends.at[k], self.arrivals.at[kind, k], peer)

    def load(self, k, source):
        return pltpu.make_async_copy(source, self.whole(self.own, k), self.loads.at[k])

    def begin(self, k):
        self.load(k, self.whole(self.own, k)).wait()
        self.send_own(k)

    def send_own(self, k):
        self.copy(self.quarter(self.own, k, self.mine), 1, k, self.y).start()
        self.copy(self.whole(self.own, k), 0, k, self.core).start()

    def first(self, k):
        quarter = self.quarter(self.other, k, self.mine)
        self.copy(quarter, 1, k, self.y).wait_recv()
        self.copy(quarter, 2, k, self.to_x).start()
        self.copy(quarter, 3, k, self.to_z).start()

    def second(self, k):
        self.copy(self.quarter(self.other, k, self.over_x), 2, k, self.to_x).wait_recv()
        self.copy(self.half(self.other, k, self.over_x, 0), 4, k, self.to_z).start()
        self.copy(self.quarter(self.other, k, self.over_z), 3, k, self.to_z).wait_recv()
        self.copy(self.half(self.other, k, self.over_z, 1), 4, k, self.to_x).start()

    def third(self, k):
        self.copy(self.quarter(self.other, k, self.across), 4, k, self.to_x).wait_recv()
        self.copy(self.whole(self.other, k), 0, k, self.core).start()

    def complete(self, k):
        self.copy(self.several(k, 2), 0, k, self.core).wait_recv()

    def drain(self, k):
        self.copy(self.several(k, 3), 0, k, self.core).wait_send()


class PlainGather(Gather):
    def direct(self, shard, k):
        return self.locate(k, shard, 0, DIRECT * self.rows // 6)

    def part_of(self, shard, k, which):
        size = (6 - DIRECT) * self.rows // 12
        return self.locate(k, shard, DIRECT * self.rows // 6 + which * size, size)

    def send_own(self, k):
        self.copy(self.direct(self.own, k), 3, k, self.y).start()
        self.copy(self.part_of(self.own, k, self.mine // 2), 1, k, self.y).start()
        self.copy(self.whole(self.own, k), 0, k, self.core).start()

    def first(self, k):
        part = self.part_of(self.other, k, self.mine // 2)
        self.copy(part, 1, k, self.y).wait_recv()
        self.copy(part, 2, k, self.to_x).start()

    def second(self, k):
        self.copy(self.direct(self.other, k), 3, k, self.y).wait_recv()
        self.copy(self.part_of(self.other, k, self.over_x // 2), 2, k, self.to_x).wait_recv()
        self.copy(self.whole(self.other, k), 0, k, self.core).start()


def gather_sems(chunks):
    return [
        pltpu.SemaphoreType.DMA((chunks,)),
        pltpu.SemaphoreType.DMA((chunks,)),
        pltpu.SemaphoreType.DMA((5, chunks)),
    ]


PARTS = 8
SLAB = STATE // PARTS
UNIT = 2 * BLK
UNITS = INNER // UNIT


class Exchange:
    def __init__(self, held, gathered, joined, incoming, sems):
        self.held, self.gathered, self.joined, self.incoming, self.sems = held, gathered, joined, incoming, sems
        self.me = lax.axis_index("ctx")

    def others(self):
        return [lax.rem(self.me + hop, PARTS) for hop in range(1, PARTS)]

    def greet(self, *further):
        barrier = pltpu.get_barrier_semaphore()
        peers = [{"ctx": other} for other in self.others()] + list(further)
        for peer in peers:
            pl.semaphore_signal(barrier, inc=1, device_id=peer, device_id_type=pl.DeviceIdType.MESH)
        pl.semaphore_wait(barrier, len(peers))

    def copy(self, source, target, kind, group, other):
        return pltpu.make_async_remote_copy(
            src_ref=source,
            dst_ref=target,
            send_sem=self.sems.at[2 * kind, group],
            recv_sem=self.sems.at[2 * kind + 1, group],
            device_id={"ctx": other},
            device_id_type=pl.DeviceIdType.MESH,
        )

    def all_of(self, kind, group):
        source, target = ((self.held, self.gathered), (self.joined, self.incoming))[kind]
        some = pl.ds(0, PARTS - 1)
        return self.copy(source.at[group, some], target.at[group, some], kind, group, self.others()[0])

    def hold(self, group, half, state):
        self.held[group, :, :, half * BLK : (half + 1) * BLK] = state.astype(BF16).reshape(PARTS, SLAB, BLK)

    def spread(self, group):
        self.gathered[group, self.me] = self.held[group, self.me]
        for other in self.others():
            self.copy(self.held.at[group, other], self.gathered.at[group, self.me], 0, group, other).start()

    def join(self, group, kept, forward):
        self.all_of(0, group).wait_recv()
        total = jnp.zeros((SLAB, UNIT), F32)
        for part in range(PARTS) if forward else range(PARTS - 1, -1, -1):
            self.joined[group, part] = total.astype(BF16)
            total = kept[part : part + 1, :] * total + self.gathered[group, part].astype(F32)
        self.incoming[group, self.me] = self.joined[group, self.me]
        for other in self.others():
            self.copy(self.joined.at[group, other], self.incoming.at[group, self.me], 1, group, other).start()

    def finish(self, group):
        self.all_of(1, group).wait_recv()
        self.all_of(0, group).wait_send()
        self.all_of(1, group).wait_send()
        return self.incoming[group].reshape(STATE, UNIT)


def exchange_scratch():
    return [pltpu.VMEM((UNITS, PARTS, SLAB, UNIT), BF16) for _ in range(4)] + [pltpu.SemaphoreType.DMA((4, UNITS))]


def kept_of(kept_ref, unit):
    rows = jnp.concatenate([kept_ref[part, 0:1, :] for part in range(PARTS)], axis=0)
    return jnp.concatenate([widen(rows, chosen(2 * unit)), widen(rows, chosen(2 * unit + 1))], axis=1)


def joined_plainly(states, kept, place, forward):
    factors = jnp.repeat(kept[:, 0, :HEADS], HDIM, axis=1)[:, None, :]
    total = jnp.zeros(states.shape[1:], F32)
    result = total
    count = states.shape[0]
    for part in range(count) if forward else range(count - 1, -1, -1):
        result = jnp.where(place == part, total, result)
        total = factors[part] * total + states[part].astype(F32)
    return result.astype(BF16)


def prepare(
    bc_ref, dt_raw, halo_bc_ref, taps_bc_ref, heads_ref, seg_ref, row_ref, b_ref, c_ref, dt_ref, run_ref, in_ref,
    ext, scores, run_t, b_t, enter, leave,
):
    chunks = bc_ref.shape[0] // Q
    ext[0:PAD, :] = halo_bc_ref[...]
    ext[PAD:, :] = bc_ref[...].astype(F32)
    lane = iota((Q, 128), 1)
    lower = (iota((Q, Q), 1) <= iota((Q, Q), 0)).astype(F32)
    offset = jnp.zeros((1, 128), F32)
    for k in range(chunks):
        rows = slice(k * Q, (k + 1) * Q)
        total = conv_rows(ext, seg_ref, taps_bc_ref, k * Q, Q)
        active = total * sigmoid(total)
        b_rows, c_rows = active[:, :STATE], active[:, STATE:].astype(BF16)
        b_t[:, rows] = b_rows.T.astype(BF16)
        b_rows = b_rows.astype(BF16)
        b_ref[rows, :] = b_rows
        c_ref[rows, :] = c_rows
        scores[rows, :] = masked_scores(seg_ref, row_ref, b_rows, c_rows, k)
        raw = jnp.where(lane < HEADS, dt_raw(rows).astype(F32), 0.0) + heads_ref[0:1, :]
        dt = jnp.maximum(raw, 0.0) + jnp.log1p(jnp.exp(-jnp.abs(raw)))
        log_decay = -dt * jnp.exp(heads_ref[1:2, :])
        running = jnp.dot(lower, log_decay, precision=HIGHEST, preferred_element_type=F32)
        dt_ref[rows, :] = dt
        run_ref[rows, :] = running
        run_t[k] = running.T
        carry, tail = chunk_flags(seg_ref, k)
        enter[rows, :] = jnp.exp(running) * carry
        leave[rows, :] = jnp.exp(running[Q - 1 : Q, :] - running) * tail
        same = (seg_ref[PAD + k * Q : PAD + (k + 1) * Q, :] == seg_ref[PAD - 1 : PAD, :]).astype(F32)
        whole = jnp.exp(running + offset) * same
        in_ref[rows, :] = whole
        offset = offset + running[Q - 1 : Q, :]
    return jnp.broadcast_to(whole[Q - 1 : Q, :], (8, 128))


def front_kernel(
    x_ref, bc_ref, dtraw_ref, halo_ref, halo_bc_ref, taps_ref, taps_bc_ref, heads_ref, seg_ref, row_ref,
    xs_ref, y_ref, state_ref, b_ref, c_ref, dt_ref, run_ref, in_ref, keep_ref,
    ext, scores, run_t, b_t, enter, leave,
):
    step = pl.program_id(0)

    @pl.when(step == 0)
    def _():
        keep_ref[...] = prepare(
            bc_ref, lambda rows: dtraw_ref[rows, :128], halo_bc_ref, taps_bc_ref, heads_ref, seg_ref, row_ref,
            b_ref, c_ref, dt_ref, run_ref, in_ref, ext, scores, run_t, b_t, enter, leave,
        )

    state = local_scan(
        step, x_ref, halo_ref, taps_ref, seg_ref, xs_ref, y_ref, c_ref, dt_ref, run_ref,
        ext, scores, run_t, b_t, enter, leave,
    )
    state_ref[...] = state.astype(BF16)


def local_scan(
    step, x_ref, halo_ref, taps_ref, seg_ref, xs_ref, y_ref, c_ref, dt_ref, run_ref,
    ext, scores, run_t, b_t, enter, leave,
):
    chunks = x_ref.shape[0] // Q
    ext[0:PAD, :] = halo_ref[...]
    ext[PAD:, :] = x_ref[...].astype(F32)
    select = chosen(step)
    state = jnp.zeros((STATE, BLK), F32)
    for k in range(chunks):
        rows = slice(k * Q, (k + 1) * Q)
        total = conv_rows(ext, seg_ref, taps_ref, k * Q, Q)
        values = total * sigmoid(total)
        xs_ref[rows, :] = values.astype(BF16)
        scaled = (values * widen(dt_ref[rows, :], select)).astype(BF16)
        entering = widen(enter[rows, :], select)
        running = pltpu.roll(run_ref[rows, :], lax.rem(128 - step * GROUP, 128), 1)
        parts = []
        for pair in range(2):
            mixing = []
            for one in range(2):
                head = 2 * pair + one
                gap = running[:, head : head + 1] - run_t[k, pl.ds(step * GROUP + head, 1), :]
                mixing.append((jnp.exp(jnp.minimum(gap, 0.0)) * scores[rows, :]).astype(BF16))
            parts.append(
                dot(jnp.concatenate(mixing, axis=1), halves(scaled[:, pair * 128 : (pair + 1) * 128]))
            )
        inside = jnp.concatenate(parts, axis=1)
        y_ref[rows, :] = (inside + entering * dot(c_ref[rows, :], state.astype(BF16))).astype(BF16)
        weighted = (scaled.astype(F32) * widen(leave[rows, :], select)).astype(BF16)
        state = entering[Q - 1 : Q, :] * state + dot(b_t[:, rows], weighted)
    return state


def front_outputs(length, column, state_at, width=BLK):
    whole = lambda *shape: (pl.BlockSpec(shape, lambda j: (0, 0)), shape)
    columns = lambda rows, at: (pl.BlockSpec((rows, width), at), (rows, INNER))
    specs = [
        (columns(length, column), BF16),
        (columns(length, column), BF16),
        (columns(STATE, state_at), BF16),
        (whole(length, 128), BF16),
        (whole(length, 128), BF16),
        (whole(length, 128), F32),
        (whole(length, 128), F32),
        (whole(length, 128), F32),
    ]
    return [spec for (spec, _), _ in specs], [jax.ShapeDtypeStruct(shape, kind) for (_, shape), kind in specs]


def front_scratch(length):
    return [
        pltpu.VMEM((length + PAD, BLK), F32),
        pltpu.VMEM((length, Q), F32),
        pltpu.VMEM((length // Q, 128, Q), F32),
        pltpu.VMEM((128, length), BF16),
        pltpu.VMEM((length, 128), F32),
        pltpu.VMEM((length, 128), F32),
    ]


def front(projected, halo, taps, heads, seg_lanes, seg_row):
    length = projected.shape[0]
    whole = lambda *shape: pl.BlockSpec(shape, lambda j: (0,) * len(shape))
    columns = lambda rows, at: pl.BlockSpec((rows, BLK), at)
    out_specs, out_shape = front_outputs(length, lambda j: (0, j), lambda j: (0, j))
    return pl.pallas_call(
        front_kernel,
        grid=(STEPS,),
        in_specs=[
            columns(length, lambda j: (0, STEPS + j)),
            columns(length, lambda j: (0, 2 * STEPS)),
            columns(length, lambda j: (0, 2 * STEPS + 1)),
            columns(PAD, lambda j: (0, STEPS + j)),
            columns(PAD, lambda j: (0, 2 * STEPS)),
            columns(8, lambda j: (0, j)),
            columns(8, lambda j: (0, STEPS)),
            whole(8, 128),
            whole(length + 2 * PAD, 128),
            whole(1, length),
        ],
        out_specs=[*out_specs, whole(8, 128)],
        out_shape=[*out_shape, jax.ShapeDtypeStruct((8, 128), F32)],
        scratch_shapes=front_scratch(length),
        compiler_params=pltpu.CompilerParams(vmem_limit_bytes=VMEM_LIMIT),
        name="front",
    )(projected, projected, projected, halo, halo, taps, taps, heads, seg_lanes, seg_row)


ORDER = (2 * INNER // WIDE, *range(INNER // WIDE, 2 * INNER // WIDE), *range(INNER // WIDE))
MULTIPLY = 3
SCAN = MULTIPLY + 2
OUT_WIDE = 128
OUT_PIECES = D // OUT_WIDE
OUT_BEGIN, DIRECT = 4, 4
JOIN, DONE = 2, 4
SLOTS = MULTIPLY + len(ORDER)
EDGES = 1 + INNER // WIDE


def chunk_at(position):
    half = INNER // WIDE
    return jnp.where(position == 0, 2 * half, jnp.where(position <= half, position - 1 + half, position - 1 - half))


def forward_kernel(*refs):
    main_ref, shard_ref, units_ref, row_ref = refs[:4]
    conv_ref, bias_ref, mixer_ref, input_ref, *head_refs = refs[4:11]
    refs = refs[6:]
    xs_ref, y_ref, state_ref, b_ref, c_ref, dt_ref, run_ref, in_ref = refs[5:13]
    keep_ref, weight_ref, whole_ref, projected_ref, normed_t_ref = refs[13:18]
    halo_ref, taps_ref, heads_ref, gain_ref, input_gain_ref, seg_ref = refs[18:24]
    ext, scores, run_t, b_t, enter, leave = refs[24:30]
    exchange = Exchange(*refs[30:35])
    own_keep, keeps, keep_sends, keep_arrivals = refs[35:39]
    gathered, loads, sends, arrivals, stores = refs[39:44]
    out_gathered, out_loads, out_sends, out_arrivals, out_stores = refs[44:49]
    normed, blocks, taps, own_small, smalls, seg_tail, seg_head = refs[49:56]
    edges, halos, small_sends, small_arrivals, edge_sends, edge_arrivals = refs[56:]
    step = pl.program_id(0)
    length = units_ref.shape[0]
    shard, part = lax.axis_index("fsdp"), lax.axis_index("ctx")
    others = ({"fsdp": flipped(shard, 1)}, {"fsdp": flipped(shard, 2)}, {"fsdp": flipped(flipped(shard, 1), 2)})
    following = {"ctx": lax.rem(part + 1, PARTS)}

    def place_in(k, s, start, size):
        rows, columns = pl.multiple_of(start, size), pl.multiple_of(s * SHARD, SHARD)
        return gathered.at[k, pl.ds(rows, size), pl.ds(columns, SHARD)]

    def place_out(k, s, start, size):
        return out_gathered.at[k, s, pl.ds(pl.multiple_of(start, size), size)]

    several_in = lambda k, count: gathered.at[k, :, pl.ds(0, count * SHARD)]
    several_out = lambda k, count: out_gathered.at[k, pl.ds(0, count)]
    gather = Gather(place_in, several_in, WIDE, loads, sends, arrivals)
    gather_out = PlainGather(place_out, several_out, 2 * SHARD, out_loads, out_sends, out_arrivals)
    rest = PROJ % WIDE

    def load_rest():
        columns = pl.ds(pl.multiple_of(shard * SHARD, SHARD), SHARD)
        return pltpu.make_async_copy(
            main_ref.at[PROJ - rest : PROJ, :], gathered.at[0, pl.ds(0, rest), columns], loads.at[0]
        )

    def small_copy(hop):
        return remote(own_small, smalls.at[shard], small_sends.at[hop], small_arrivals.at[hop], others[hop])

    def seg_copy():
        return remote(seg_tail, seg_head, small_sends.at[3], small_arrivals.at[3], following)

    def edge_copy(k):
        return remote(edges.at[k], halos.at[k], edge_sends.at[k], edge_arrivals.at[k], following)

    def keep_copy(hop):
        peer = {"ctx": lax.rem(part + hop + 1, PARTS)}
        return remote(own_keep, keeps.at[part], keep_sends.at[hop], keep_arrivals.at[hop], peer)

    def store(k):
        rows = pl.ds(pl.multiple_of(chunk_at(k) * WIDE, WIDE), WIDE)
        return pltpu.make_async_copy(gathered.at[k], weight_ref.at[rows], stores.at[k])

    def store_out(k):
        columns = pl.ds(pl.multiple_of(k * OUT_WIDE, OUT_WIDE), OUT_WIDE)
        return pltpu.make_async_copy(out_gathered.at[k], whole_ref.at[:, :, columns], out_stores.at[k])

    @pl.when(step == 0)
    def _():
        barrier = pltpu.get_barrier_semaphore()
        greeted = [*[{"ctx": other} for other in exchange.others()], *others]
        for peer in greeted:
            pl.semaphore_signal(barrier, inc=1, device_id=peer, device_id_type=pl.DeviceIdType.MESH)
        load_rest().start()
        for k, chunk in enumerate(ORDER):
            if k:
                gather.load(k, main_ref.at[chunk * WIDE : (chunk + 1) * WIDE, :]).start()
        for k in range(OUT_PIECES):
            gather_out.load(k, shard_ref.at[:, k * OUT_WIDE : (k + 1) * OUT_WIDE]).start()
        own_small[...] = jnp.zeros((8, SMALL_WIDTH), F32)
        own_small[0:4, : XBC // 4] = conv_ref[...].astype(F32)
        for row, ref in ((4, bias_ref), (5, mixer_ref), (6, input_ref)):
            own_small[row : row + 1, : ref.shape[0]] = ref[...].astype(F32).reshape(1, ref.shape[0])
        for kind, ref in enumerate(head_refs):
            own_small[7:8, kind * 128 : kind * 128 + HEADS // 4] = ref[...].astype(F32).reshape(1, HEADS // 4)
        smalls[shard] = own_small[...]
        columns = pl.ds(pl.multiple_of(shard * SHARD, SHARD), SHARD)
        gathered[0, rest:, columns] = jnp.zeros((WIDE - rest, SHARD), BF16)
        for k in range(length // 128):
            ids = jnp.broadcast_to(row_ref[0:1, k * 128 : (k + 1) * 128].astype(F32), (128, 128))
            seg_ref[PAD + k * 128 : PAD + (k + 1) * 128, :] = ids.T.astype(jnp.int32)
        seg_tail[...] = seg_ref[length : length + PAD, :]
        pl.semaphore_wait(barrier, len(greeted))
        for hop in range(3):
            small_copy(hop).start()
        seg_copy().start()
        load_rest().wait()
        gather.send_own(0)
        for k in range(1, AHEAD):
            gather.begin(k)

    def take_small():
        for hop in range(3):
            small_copy(hop).wait()
        seg_copy().wait()
        seg_ref[0:PAD, :] = jnp.where(part == 0, -1, seg_head[...])
        seg_ref[PAD + length :, :] = jnp.full((PAD, 128), -2, jnp.int32)

    def normalise():
        gain = jnp.concatenate([smalls[s, 6:7, :SHARD] for s in range(4)], axis=1)
        input_gain_ref[...] = gain
        for k in range(length // Q):
            rows = slice(k * Q, (k + 1) * Q)
            units = units_ref[rows, :].astype(F32)
            norm = lax.rsqrt(jnp.sum(units * units, axis=1, keepdims=True) * (1.0 / D) + epsilon)
            normed[rows, :] = (units * norm * gain).astype(BF16)

    def take_taps():
        mixer_gain = jnp.concatenate([smalls[s, 5:6, : INNER // 4] for s in range(4)], axis=1)
        gain_ref[...] = jnp.broadcast_to(mixer_gain, (8, INNER))
        whole = jnp.zeros((8, XBC), F32)
        heads = jnp.zeros((8, 128), F32)
        row, lane = iota((8, 128), 0), iota((8, 128), 1)
        own = HEADS // 4
        for s in range(4):
            padded = jnp.concatenate([smalls[s], jnp.zeros((8, XBC - SMALL_WIDTH), F32)], axis=1)
            padded = jnp.where(iota((8, XBC), 1) < XBC // 4, padded, 0.0)
            whole = whole + (pltpu.roll(padded, s * (XBC // 4), 1) if s else padded)
            inside = (lane >= s * own) & (lane < (s + 1) * own)
            for kind in range(3):
                moved = jnp.broadcast_to(smalls[s, 7:8, kind * 128 : (kind + 1) * 128], (8, 128))
                moved = pltpu.roll(moved, s * own, 1) if s else moved
                heads = jnp.where(inside & (row == kind), moved, heads)
        taps_ref[...] = whole
        heads_ref[...] = heads
        for block in range(STEPS + 1):
            taps[block] = whole[:, block * BLK : (block + 1) * BLK]

    def complete_out(k):
        gather_out.complete(k)
        store_out(k).start()

    def stage(lag, count=len(ORDER)):
        def decorate(body):
            k = step - lag

            @pl.when((k >= 0) & (k < count))
            def _():
                body(k)

        return decorate

    def advance(tick):
        def at(lag, body, first=0, count=len(ORDER)):
            k = tick - lag

            @pl.when((k >= first) & (k < count))
            def _():
                body(k)

        def complete(k):
            gather.complete(k)
            store(k).start()

        at(-AHEAD, gather.begin, AHEAD)
        at(0, gather.first)
        at(1, gather.second)
        at(2, gather.third)
        at(3, complete)
        at(OUT_BEGIN, gather_out.begin, 0, OUT_PIECES)
        at(OUT_BEGIN + 2, gather_out.first, 0, OUT_PIECES)
        at(OUT_BEGIN + 4, gather_out.second, 0, OUT_PIECES)
        at(OUT_BEGIN + 6, complete_out, 0, OUT_PIECES)

    tick = jnp.where(step < SCAN, step, 2 * step - SCAN)
    advance(tick)
    pl.when(step == 0)(take_small)
    pl.when(step == 1)(normalise)
    pl.when(step == 2)(take_taps)

    for s in range(4):

        @pl.when(step == 2 + s // 2)
        def _():
            columns = slice(s * SHARD, (s + 1) * SHARD)
            normed_t_ref[s] = normed[:, columns].astype(F32).T.astype(BF16)

    @stage(MULTIPLY)
    def _(k):
        low = dot_nt(normed[...], gathered[k]).astype(BF16)
        projected_ref[...] = low

        @pl.when(k < EDGES)
        def _():
            edge = low[length - 16 :, :].astype(F32)[8:, :]
            for half in range(2):
                columns = slice(half * BLK, (half + 1) * BLK)
                blocks[2 * k + half] = low[:, columns]
                edges[k, half] = edge[:, columns]
            edge_copy(k).start()

    @stage(SCAN - 1, EDGES)
    def _(k):
        edge_copy(k).wait()
        for half in range(2):
            columns = slice(half * BLK, (half + 1) * BLK)
            halos[k, half] = jnp.where(part == 0, 0.0, halos[k, half])
            halo_ref[:, columns] = halos[k, half]

    @pl.when(step == SCAN - 1)
    def _():
        keep = prepare(
            blocks.at[0], lambda rows: blocks[1, rows, :128], halos.at[0, 0], taps.at[STEPS], heads_ref,
            seg_ref, row_ref, b_ref, c_ref, dt_ref, run_ref, in_ref, ext, scores, run_t, b_t, enter, leave,
        )
        own_keep[...] = keep
        keeps[part] = keep
        for hop in range(PARTS - 1):
            keep_copy(hop).start()

    for half in range(2):

        @stage(SCAN, UNITS)
        def _(unit):
            columns = pl.ds(half * BLK, BLK)
            group = 2 * unit + half
            state = local_scan(
                group, blocks.at[2 + group], halos.at[1 + unit, half], taps.at[group], seg_ref,
                xs_ref.at[:, columns], y_ref.at[:, columns], c_ref, dt_ref, run_ref, ext, scores, run_t, b_t, enter, leave,
            )
            exchange.hold(unit, half, state)

        if half == 0:

            @pl.when(step >= SCAN)
            def _():
                advance(tick + 1)

    stage(SCAN, UNITS)(exchange.spread)

    @pl.when(step == SCAN + JOIN)
    def _():
        for hop in range(PARTS - 1):
            keep_copy(hop).wait()
        keep_ref[...] = keeps[...]

    @stage(SCAN + JOIN, UNITS)
    def _(unit):
        exchange.join(unit, kept_of(keeps, unit), True)

    @stage(SCAN + DONE, UNITS)
    def _(unit):
        state_ref[...] = exchange.finish(unit)

    @pl.when(step == SLOTS - 1)
    def _():
        for k in range(len(ORDER)):
            gather.drain(k)
            store(k).wait()
        for k in range(OUT_PIECES):
            gather_out.drain(k)
            store_out(k).wait()


def forward(in_matrix, out_matrix, units, seg_row, *small):
    length = units.shape[0]
    chunks = len(ORDER)
    whole = lambda *shape: pl.BlockSpec(shape, lambda t: (0,) * len(shape))
    once = lambda *shape: pl.BlockSpec(shape, lambda t: (0,) * len(shape), pipeline_mode=pl.Buffered(1))
    anywhere = pl.BlockSpec(memory_space=pl.ANY)
    chunk = lambda rows, lag: pl.BlockSpec((rows, WIDE), lambda t: (0, chunk_at(jnp.clip(t - lag, 0, chunks - 1))))
    unit = lambda lag: lambda t: (0, jnp.clip(t - lag, 0, UNITS - 1))
    out_specs, out_shape = front_outputs(length, unit(SCAN), unit(SCAN + DONE), UNIT)
    shape = jax.ShapeDtypeStruct
    return pl.pallas_call(
        forward_kernel,
        grid=(SLOTS,),
        in_specs=[
            anywhere,
            anywhere,
            once(length, D),
            once(1, length),
            *[once(*each.shape) for each in small],
        ],
        out_specs=[
            *out_specs,
            whole(PARTS, 8, 128),
            anywhere,
            anywhere,
            chunk(length, MULTIPLY),
            once(4, SHARD, length),
            pl.BlockSpec((PAD, WIDE), lambda t: (0, chunk_at(jnp.clip(t - SCAN + 1, 0, EDGES - 1)))),
            whole(8, XBC),
            whole(8, 128),
            whole(8, INNER),
            whole(1, D),
            whole(length + 2 * PAD, 128),
        ],
        out_shape=[
            *out_shape,
            shape((PARTS, 8, 128), F32),
            shape((WIDTH, D), BF16),
            shape((4, 2 * SHARD, D), BF16),
            shape((length, WIDTH), BF16),
            shape((4, SHARD, length), BF16),
            shape((PAD, WIDTH), F32),
            shape((8, XBC), F32),
            shape((8, 128), F32),
            shape((8, INNER), F32),
            shape((1, D), F32),
            shape((length + 2 * PAD, 128), jnp.int32),
        ],
        scratch_shapes=[
            *front_scratch(length),
            *exchange_scratch(),
            pltpu.VMEM((8, 128), F32),
            pltpu.VMEM((PARTS, 8, 128), F32),
            pltpu.SemaphoreType.DMA((PARTS - 1,)),
            pltpu.SemaphoreType.DMA((PARTS - 1,)),
            pltpu.VMEM((chunks, WIDE, D), BF16),
            *gather_sems(chunks),
            pltpu.SemaphoreType.DMA((chunks,)),
            pltpu.VMEM((OUT_PIECES, 4, 2 * SHARD, OUT_WIDE), BF16),
            *gather_sems(OUT_PIECES),
            pltpu.SemaphoreType.DMA((OUT_PIECES,)),
            pltpu.VMEM((length, D), BF16),
            pltpu.VMEM((2 * EDGES, length, BLK), BF16),
            pltpu.VMEM((STEPS + 1, 8, BLK), F32),
            pltpu.VMEM((8, SMALL_WIDTH), F32),
            pltpu.VMEM((4, 8, SMALL_WIDTH), F32),
            pltpu.VMEM((PAD, 128), jnp.int32),
            pltpu.VMEM((PAD, 128), jnp.int32),
            pltpu.VMEM((EDGES, 2, PAD, BLK), F32),
            pltpu.VMEM((EDGES, 2, PAD, BLK), F32),
            pltpu.SemaphoreType.DMA((4,)),
            pltpu.SemaphoreType.DMA((4,)),
            pltpu.SemaphoreType.DMA((EDGES,)),
            pltpu.SemaphoreType.DMA((EDGES,)),
        ],
        compiler_params=communicating(1),
        name="forward",
    )(in_matrix.T, out_matrix, units, seg_row, *small)


TAIL_GROUPS = 4
TAIL_STEPS = STEPS // TAIL_GROUPS


def tail_kernel(
    y_ref, xs_ref, gate_ref, incoming_ref, out_ref, c_ref, in_ref, heads_ref, gain_ref, g_ref, units_ref,
    mixer_ref, dproj_ref, dy_ref, dsin_ref, sums_ref, block_ref, stats_ref,
    full, dmix, squares, products, mixed, c_t,
):
    step = pl.program_id(0)
    length = y_ref.shape[0]
    unit = lax.rem(step, TAIL_STEPS)
    half = length // 2

    @pl.when(step == 0)
    def _():
        squares[...] = jnp.zeros_like(squares)
        products[...] = jnp.zeros_like(products)
        mixed[...] = jnp.zeros_like(mixed)
        for k in range(length // Q):
            rows = slice(k * Q, (k + 1) * Q)
            c_t[:, rows] = c_ref[rows, :].astype(F32).T.astype(BF16)

    def earlier(one):
        columns = slice(one * BLK, (one + 1) * BLK)
        group = TAIL_GROUPS * unit + one
        select = chosen(group)
        incoming = incoming_ref[:, columns]
        skip = widen(heads_ref[...], select)[2:3, :]
        for k in range(2):
            rows = slice(k * half, (k + 1) * half)
            y = y_ref[rows, columns].astype(F32)
            y = y + widen(in_ref[rows, :], select) * dot(c_ref[rows, :], incoming)
            y = y + skip * xs_ref[rows, columns].astype(F32)
            full[group, rows, :] = y
            gate = gate_ref[rows, columns].astype(F32)
            gated = y * gate * sigmoid(gate)
            d_mixer = dot_nt(g_ref[rows, :], out_ref[columns, :])
            dmix[group, rows, :] = d_mixer
            square = gated * gated
            product = gated * d_mixer * gain_ref[0:1, columns]
            squares[rows, :] += square[:, :128] + square[:, 128:]
            products[rows, :] += product[:, :128] + product[:, 128:]

    def later(one):
        columns = slice(one * BLK, (one + 1) * BLK)
        group = TAIL_GROUPS * unit + one
        select = chosen(group)
        gain = gain_ref[0:1, columns]
        d_gain = jnp.zeros((1, BLK), F32)
        d_skip = jnp.zeros((1, BLK), F32)
        d_state = jnp.zeros((STATE, BLK), F32)
        for k in range(2):
            rows = slice(k * half, (k + 1) * half)
            norm, mean = both(squares[rows, :]), both(products[rows, :])
            y = full[group, rows, :]
            d_mixer = dmix[group, rows, :]
            gate = gate_ref[rows, columns].astype(F32)
            sig = sigmoid(gate)
            silu = gate * sig
            unscaled = y * silu * norm
            value = unscaled * gain
            mixer_ref[columns, rows] = value.T.astype(BF16)
            mixed[rows, :] += dot(value.astype(BF16), out_ref[columns, :])
            d_gain = d_gain + jnp.sum(d_mixer * unscaled, axis=0, keepdims=True)
            d_gated = norm * (d_mixer * gain - unscaled * mean)
            dproj_ref[rows, columns] = (d_gated * y * (sig * (1.0 + gate * (1.0 - sig)))).astype(BF16)
            dy = (d_gated * silu).astype(BF16)
            dy_ref[rows, columns] = dy
            dy = dy.astype(F32)
            d_skip = d_skip + jnp.sum(dy * xs_ref[rows, columns].astype(F32), axis=0, keepdims=True)
            d_state = d_state + dot(c_t[:, rows], (dy * widen(in_ref[rows, :], select)).astype(BF16))
        dsin_ref[:, columns] = d_state.astype(BF16)
        sums_ref[:, columns] = jnp.concatenate([d_gain, d_skip, jnp.zeros((6, BLK), F32)], axis=0)

    @pl.when(step < TAIL_STEPS)
    def _():
        for one in range(TAIL_GROUPS):
            earlier(one)

    @pl.when(step == TAIL_STEPS)
    def _():
        norm = lax.rsqrt(jnp.sum(squares[...], axis=1, keepdims=True) * (1.0 / INNER) + epsilon)
        mean = norm * jnp.sum(products[...], axis=1, keepdims=True) * (1.0 / INNER)
        squares[...] = jnp.broadcast_to(norm, squares.shape)
        products[...] = jnp.broadcast_to(mean, products.shape)

    @pl.when(step >= TAIL_STEPS)
    def _():
        for one in range(TAIL_GROUPS):
            later(one)

    @pl.when(step == 2 * TAIL_STEPS - 1)
    def _():
        total = units_ref[...].astype(F32) + mixed[...]
        block_ref[...] = total.astype(BF16)
        first = jnp.sum(total * total, axis=0, keepdims=True)
        second = jnp.sum(mixed[...] * mixed[...], axis=0, keepdims=True)
        stats_ref[...] = jnp.concatenate([first, second, jnp.zeros((6, D), F32)], axis=0)


def tail(y, xs, projected, incoming, out_whole, c_rows, entering, heads, gain, cot, units):
    length = y.shape[0]
    unit = lambda i: lax.rem(i, TAIL_STEPS)
    second = lambda i: jnp.maximum(i - TAIL_STEPS, 0)
    early = lambda rows: pl.BlockSpec((rows, TAIL_GROUPS * BLK), lambda i: (0, jnp.minimum(i, TAIL_STEPS - 1)))
    late = lambda rows: pl.BlockSpec((rows, TAIL_GROUPS * BLK), lambda i: (0, second(i)))
    each = lambda rows: pl.BlockSpec((rows, TAIL_GROUPS * BLK), lambda i: (0, unit(i)))
    whole = lambda *shape: pl.BlockSpec(shape, lambda i: (0,) * len(shape))
    return pl.pallas_call(
        tail_kernel,
        grid=(2 * TAIL_STEPS,),
        in_specs=[
            early(length),
            each(length),
            each(length),
            early(STATE),
            pl.BlockSpec((TAIL_GROUPS * BLK, D), lambda i: (unit(i), 0)),
            whole(length, 128),
            whole(length, 128),
            whole(8, 128),
            each(8),
            whole(length, D),
            whole(length, D),
        ],
        out_specs=[
            pl.BlockSpec((TAIL_GROUPS * BLK, length), lambda i: (second(i), 0)),
            late(length),
            late(length),
            pl.BlockSpec((STATE, TAIL_GROUPS * BLK), lambda i: (0, second(i))),
            late(8),
            whole(length, D),
            whole(8, D),
        ],
        out_shape=[
            jax.ShapeDtypeStruct((INNER, length), BF16),
            jax.ShapeDtypeStruct((length, WIDTH), BF16),
            jax.ShapeDtypeStruct((length, INNER), BF16),
            jax.ShapeDtypeStruct((STATE, INNER), BF16),
            jax.ShapeDtypeStruct((8, INNER), F32),
            jax.ShapeDtypeStruct((length, D), BF16),
            jax.ShapeDtypeStruct((8, D), F32),
        ],
        scratch_shapes=[
            pltpu.VMEM((STEPS, length, BLK), F32),
            pltpu.VMEM((STEPS, length, BLK), F32),
            pltpu.VMEM((length, 128), F32),
            pltpu.VMEM((length, 128), F32),
            pltpu.VMEM((length, D), F32),
            pltpu.VMEM((128, length), BF16),
        ],
        compiler_params=pltpu.CompilerParams(vmem_limit_bytes=VMEM_LIMIT),
        cost_estimate=pl.CostEstimate(
            flops=12 * 10**9, bytes_accessed=50 * 10**6, transcendentals=4 * 10**6
        ),
        name="tail",
    )(y, xs, projected, incoming, out_whole, c_rows, entering, heads, gain, cot, units)


def back_steps(step, given, scratch, write, write_halo, write_taps, write_heads):
    (
        x_ref, dtraw_ref, halo_ref, taps_ref, heads_ref, seg_ref, row_ref, b_ref, c_ref, dt_ref, run_ref, dy_ref, sin_ref, dout_ref,
    ) = given
    (
        ext, pre, dact, dbuf, scores, dscores, run_t, b_t, c_t, enter, leave, d_b, d_c, suffix, prefix, d_dt, fixed, states,
    ) = scratch
    length = x_ref.shape[0]
    chunks = length // Q

    @pl.when(step == 0)
    def _():
        for k in range(chunks):
            rows = slice(k * Q, (k + 1) * Q)
            b_rows, c_rows = b_ref[rows, :], c_ref[rows, :]
            b_t[:, rows] = b_rows.astype(F32).T.astype(BF16)
            c_t[:, rows] = c_rows.astype(F32).T.astype(BF16)
            scores[rows, :] = masked_scores(seg_ref, row_ref, b_rows, c_rows, k)
            running = run_ref[rows, :]
            run_t[k] = running.T
            carry, tail = chunk_flags(seg_ref, k)
            enter[rows, :] = jnp.exp(running) * carry
            leave[rows, :] = jnp.exp(running[Q - 1 : Q, :] - running) * tail
        for each in (dscores, d_b, d_c, suffix, prefix, d_dt, fixed):
            each[...] = jnp.zeros_like(each)
        dbuf[0:PAD, :] = jnp.zeros((PAD, BLK), F32)
        dbuf[PAD + length :, :] = jnp.zeros((PAD, BLK), F32)

    @pl.when(step <= STEPS)
    def _():
        ext[0:PAD, :] = halo_ref[...]
        ext[PAD:, :] = x_ref[...].astype(F32)
        for k in range(chunks):
            pre[k * Q : (k + 1) * Q, :] = conv_rows(ext, seg_ref, taps_ref, k * Q, Q)

    @pl.when(step < STEPS)
    def _():
        select = chosen(step)
        gather = chosen_back(step)
        skip = widen(heads_ref[...], select)[2:3, :]
        state = sin_ref[...].astype(F32)
        for k in range(chunks):
            rows = slice(k * Q, (k + 1) * Q)
            states[k] = state
            if k + 1 < chunks:
                total = pre[rows, :]
                scaled = total * sigmoid(total) * widen(dt_ref[rows, :], select)
                weighted = (scaled.astype(BF16).astype(F32) * widen(leave[rows, :], select)).astype(BF16)
                last = widen(enter[rows.stop - 8 : rows.stop, :], select)[7:8, :]
                state = last * state + dot(b_t[:, rows], weighted)
        d_state = dout_ref[...].astype(F32)
        for k in range(chunks - 1, -1, -1):
            rows = slice(k * Q, (k + 1) * Q)
            total = pre[rows, :]
            values = total * sigmoid(total)
            step_size = widen(dt_ref[rows, :], select)
            entering = widen(enter[rows, :], select)
            leaving = widen(leave[rows, :], select)
            scaled = (values * step_size).astype(BF16)
            scaled_wide = scaled.astype(F32)
            dy = dy_ref[rows, :]
            dy_wide = dy.astype(F32)
            before = states[k]
            before_low = before.astype(BF16)
            d_low = d_state.astype(BF16)
            running = pltpu.roll(run_ref[rows, :], lax.rem(128 - step * GROUP, 128), 1)
            insides, backs = [], []
            d_score = dscores[rows, :]
            for pair in range(2):
                lanes = slice(pair * 128, (pair + 1) * 128)
                mixing, turned, decays = [], [], []
                for one in range(2):
                    head = 2 * pair + one
                    gap = running[:, head : head + 1] - run_t[k, pl.ds(step * GROUP + head, 1), :]
                    decay = jnp.exp(jnp.minimum(gap, 0.0))
                    mixed = decay * scores[rows, :]
                    decays.append(decay)
                    mixing.append(mixed.astype(BF16))
                    turned.append(mixed.T.astype(BF16))
                spread = halves(scaled[:, lanes])
                insides.append(dot(jnp.concatenate(mixing, axis=1), spread))
                backs.append(dot(jnp.concatenate(turned, axis=1), halves(dy[:, lanes])))
                products = dot_nt(dy[:, lanes], spread)
                d_score = d_score + decays[0] * products[:, :Q] + decays[1] * products[:, Q:]
            dscores[rows, :] = d_score
            inside = jnp.concatenate(insides, axis=1) + entering * dot(c_ref[rows, :], before_low)
            back_inside = jnp.concatenate(backs, axis=1)
            back_state = leaving * dot(b_ref[rows, :], d_low)
            high, low = in_two(dy_wide * inside - scaled_wide * back_inside)
            suffix[rows, :] += dot(high, gather) + dot(low, gather)
            prefix[rows, :] += dot((scaled_wide * back_state).astype(BF16), gather)
            back = back_inside + back_state
            d_dt[rows, :] += dot((values * back).astype(BF16), gather)
            entered = (dy_wide * entering).astype(BF16)
            d_c[rows, :] += dot_nt(entered, before_low)
            d_b[rows, :] += dot_nt((scaled_wide * leaving).astype(BF16), d_low)
            kept = entering[Q - 1 : Q, :]
            through = jnp.sum(before * d_state, axis=0, keepdims=True) * kept
            high, low = in_two(jnp.broadcast_to(through, (8, BLK)))
            fixed[k * 8 : (k + 1) * 8, :] += dot(high, gather) + dot(low, gather)
            d_state = kept * d_state + dot(c_t[:, rows], entered)
            dact[rows, :] = back * step_size + skip * dy_wide

    @pl.when(step == STEPS)
    def _():
        for k in range(chunks):
            rows = slice(k * Q, (k + 1) * Q)
            own = seg_ref[PAD + k * Q : PAD + (k + 1) * Q, :]
            keep = (own == row_ref[0:1, rows]) & (iota((Q, Q), 1) <= iota((Q, Q), 0))
            d_score = jnp.where(keep, dscores[rows, :], 0.0)
            dact[rows, STATE:] = d_c[rows, :] + dot(d_score.astype(BF16), b_ref[rows, :])
            dact[rows, :STATE] = d_b[rows, :] + dot(d_score.T.astype(BF16), c_ref[rows, :])

    @pl.when(step <= STEPS)
    def _():
        sums = [jnp.zeros((1, BLK), F32) for _ in range(CONV + 1)]
        for k in range(chunks):
            rows = slice(k * Q, (k + 1) * Q)
            total = pre[rows, :]
            sig = sigmoid(total)
            d_conv = dact[rows, :] * (sig * (1.0 + total * (1.0 - sig)))
            dbuf[PAD + k * Q : PAD + (k + 1) * Q, :] = d_conv
            sums[4] = sums[4] + jnp.sum(d_conv, axis=0, keepdims=True)
            own = seg_ref[PAD + k * Q : PAD + (k + 1) * Q, :]
            for shift in range(CONV):
                at = PAD + k * Q - shift
                term = d_conv * ext[at : at + Q, :]
                if shift:
                    term = jnp.where(both(seg_ref[at : at + Q, :] == own), term, 0.0)
                sums[3 - shift] = sums[3 - shift] + jnp.sum(term, axis=0, keepdims=True)
        write_taps(jnp.concatenate(sums + [jnp.zeros((3, BLK), F32)], axis=0))

        def returned(at, rows):
            own = seg_ref[at : at + rows, :]
            result = taps_ref[3:4, :] * dbuf[at : at + rows, :]
            for shift in range(1, CONV):
                same = both(seg_ref[at + shift : at + shift + rows, :] == own)
                result = result + jnp.where(
                    same, taps_ref[3 - shift : 4 - shift, :] * dbuf[at + shift : at + shift + rows, :], 0.0
                )
            return result

        write_halo(returned(0, PAD))
        for k in range(chunks):
            write(slice(k * Q, (k + 1) * Q), returned(PAD + k * Q, Q).astype(BF16))

    @pl.when(step == STEPS + 1)
    def _():
        lower = (iota((Q, Q), 1) < iota((Q, Q), 0)).astype(F32)
        upper = (iota((Q, Q), 1) >= iota((Q, Q), 0)).astype(F32)
        lane = iota((Q, 128), 1)
        rate = jnp.exp(heads_ref[1:2, :])
        bias_sum = jnp.zeros((1, 128), F32)
        decay_sum = jnp.zeros((1, 128), F32)
        for k in range(chunks):
            rows = slice(k * Q, (k + 1) * Q)
            d_log = jnp.dot(upper, suffix[rows, :], precision=HIGHEST, preferred_element_type=F32)
            d_log = d_log + jnp.dot(lower, prefix[rows, :], precision=HIGHEST, preferred_element_type=F32)
            d_log = d_log + fixed[k * 8 : k * 8 + 1, :]
            raw = jnp.where(lane < HEADS, dtraw_ref[rows, :128].astype(F32), 0.0) + heads_ref[0:1, :]
            d_raw = jnp.where(lane < HEADS, (d_dt[rows, :] - rate * d_log) * sigmoid(raw), 0.0)
            bias_sum = bias_sum + jnp.sum(d_raw, axis=0, keepdims=True)
            decay_sum = decay_sum - jnp.sum(d_log * dt_ref[rows, :] * rate, axis=0, keepdims=True)
            write(rows, jnp.concatenate([d_raw, jnp.zeros_like(d_raw)], axis=1).astype(BF16))
        write_heads(jnp.concatenate([bias_sum, decay_sum, jnp.zeros((6, 128), F32)], axis=0))


def back_kernel(*refs):
    given, (_, dproj_ref, dhalo_ref, dtaps_ref, dheads_ref), scratch = refs[:14], refs[14:19], refs[19:]

    def write(rows, value):
        dproj_ref[rows, :] = value

    def write_halo(value):
        dhalo_ref[...] = value

    def write_taps(value):
        dtaps_ref[...] = value

    def write_heads(value):
        dheads_ref[...] = value

    back_steps(pl.program_id(0), given, scratch, write, write_halo, write_taps, write_heads)


def back_scratch(length):
    return [
        pltpu.VMEM((length + PAD, BLK), F32),
        pltpu.VMEM((length, BLK), F32),
        pltpu.VMEM((length, BLK), F32),
        pltpu.VMEM((length + 2 * PAD, BLK), F32),
        pltpu.VMEM((length, Q), F32),
        pltpu.VMEM((length, Q), F32),
        pltpu.VMEM((length // Q, 128, Q), F32),
        pltpu.VMEM((128, length), BF16),
        pltpu.VMEM((128, length), BF16),
        *[pltpu.VMEM((length, 128), F32) for _ in range(7)],
        pltpu.VMEM((8 * (length // Q), 128), F32),
        pltpu.VMEM((length // Q, STATE, BLK), F32),
    ]


def back_inputs(length, late=0):
    whole = lambda *shape: pl.BlockSpec(shape, lambda j: (0,) * len(shape))
    upto = lambda last, first=0: lambda j: (0, first + jnp.clip(j - late, 0, last))
    return [
        pl.BlockSpec((length, BLK), upto(STEPS, STEPS)),
        pl.BlockSpec((length, BLK), lambda j: (0, 2 * STEPS + 1)),
        pl.BlockSpec((PAD, BLK), upto(STEPS, STEPS)),
        pl.BlockSpec((8, BLK), upto(STEPS)),
        whole(8, 128),
        whole(length + 2 * PAD, 128),
        whole(1, length),
        whole(length, 128),
        whole(length, 128),
        whole(length, 128),
        whole(length, 128),
        pl.BlockSpec((length, BLK), upto(STEPS - 1)),
        pl.BlockSpec((STATE, BLK), upto(STEPS - 1)),
        whole(STATE, INNER) if late else pl.BlockSpec((STATE, BLK), upto(STEPS - 1)),
    ]


def back(given, dproj):
    length = dproj.shape[0]
    upto = lambda last, first=0: lambda j: (0, first + jnp.minimum(j, last))
    return pl.pallas_call(
        back_kernel,
        grid=(STEPS + 2,),
        in_specs=[*back_inputs(length), pl.BlockSpec(memory_space=pl.ANY)],
        out_specs=[
            pl.BlockSpec((length, BLK), lambda j: (0, STEPS + j)),
            pl.BlockSpec((PAD, BLK), upto(STEPS)),
            pl.BlockSpec((8, BLK), upto(STEPS)),
            pl.BlockSpec((8, 128), lambda j: (0, 0)),
        ],
        out_shape=[
            jax.ShapeDtypeStruct((length, WIDTH), BF16),
            jax.ShapeDtypeStruct((PAD, XBC), F32),
            jax.ShapeDtypeStruct((8, XBC), F32),
            jax.ShapeDtypeStruct((8, 128), F32),
        ],
        scratch_shapes=back_scratch(length),
        input_output_aliases={14: 0},
        compiler_params=pltpu.CompilerParams(vmem_limit_bytes=VMEM_LIMIT),
        name="back",
    )(*given, dproj)


OUT_CHUNKS = 2 * D // WIDE
GATE_CHUNKS = INNER // WIDE
IN_CHUNKS = WIDTH // WIDE
CHUNKS = OUT_CHUNKS + IN_CHUNKS
LAGS = 8
RING = 8
LATE = 3
LAST_WIDE = 384


def small_sums(taps, columns, input_gain, heads, stats):
    fill = lambda width: jnp.zeros((1, width), F32)
    squares = [jnp.broadcast_to(jnp.sum(stats[i : i + 1], axis=1, keepdims=True), (1, 128)) for i in range(2)]
    return jnp.concatenate(
        [
            taps[:5],
            jnp.concatenate([columns[0:1], fill(XBC - INNER)], axis=1),
            jnp.concatenate([columns[1:2], fill(XBC - INNER)], axis=1),
            jnp.concatenate([input_gain, heads[0:1], heads[1:2], *squares, fill(XBC - D - 512)], axis=1),
        ],
        axis=0,
    )


def finish_kernel(*refs):
    given, refs = refs[:14], refs[14:]
    lhs_in, lhs_out, gate_ref, weight_ref, cot_ref, units_ref, gain_ref, columns_ref, stats_ref, kept_ref = refs[:10]
    din_ref, dout_ref, input_grad_ref, total_ref = refs[10:14]
    scratch, refs = refs[14:32], refs[32:]
    exchange, outgoing, refs = Exchange(*refs[:5]), refs[5], refs[6:]
    grads, edges, halos, taps, heads, d_normed = refs[:6]
    own, core_send, core_recv, y_recv, x_recv, z_recv, w_recv, final, small_send, small_recv = refs[6:16]
    send_sems, recv_sems, small_send_sems, small_recv_sems, edge_sends, edge_arrivals = refs[16:]
    step = pl.program_id(0)
    length = cot_ref.shape[0]
    shard, part = lax.axis_index("fsdp"), lax.axis_index("ctx")
    core, y = lax.rem(shard, 2), shard // 2
    x, z = lax.rem(part, 2), part // 2
    near, far = lax.rem(z, 2), z // 2
    peers = (
        {"fsdp": flipped(shard, 1)},
        {"fsdp": flipped(shard, 2)},
        {"ctx": flipped(part, 1)},
        {"ctx": flipped(part, 2)},
        {"ctx": flipped(part, 4)},
    )
    preceding = lax.rem(part + PARTS - 1, PARTS)

    def ring(k):
        return lax.rem(k, RING)

    class Sent:
        def __init__(self, stage, k, source, target, peer):
            self.given = stage, k, source, target, peer

        def act(self, name):
            stage, k, source, target, peer = self.given
            for last in range(2):

                @pl.when((k == CHUNKS - 1) == bool(last))
                def _():
                    ends = source, target
                    if last:
                        columns = (*[slice(None)] * (len(source.shape) - 1), pl.ds(0, LAST_WIDE))
                        ends = source.at[columns], target.at[columns]
                    copy = remote(*ends, send_sems.at[stage, k], recv_sems.at[stage, k], peers[peer])
                    getattr(copy, name)()

        def start(self):
            self.act("start")

        def wait_send(self):
            self.act("wait_send")

        def wait_recv(self):
            self.act("wait_recv")

    sent = Sent

    copies = (
        lambda k: sent(0, k, core_send.at[lax.rem(k, 2)], core_recv.at[ring(k)], 0),
        lambda k: sent(1, k, core_recv.at[ring(k), 1 - y], y_recv.at[ring(k)], 1),
        lambda k: sent(2, k, y_recv.at[ring(k), 1 - x], x_recv.at[ring(k)], 2),
        lambda k: sent(3, k, x_recv.at[ring(k), 1 - near], z_recv.at[ring(k)], 3),
        lambda k: sent(4, k, z_recv.at[ring(k), 1 - far], w_recv.at[ring(k)], 4),
        lambda k: sent(5, k, final.at[ring(k), x, near, far], final.at[ring(k), x, near, far], 4),
        lambda k: sent(6, k, final.at[ring(k), x, near], final.at[ring(k), x, near], 3),
        lambda k: sent(7, k, final.at[ring(k), x], final.at[ring(k), x], 2),
    )
    arrivals = copies[:5] + (
        lambda k: sent(5, k, final.at[ring(k), x, near, 1 - far], final.at[ring(k), x, near, 1 - far], 4),
        lambda k: sent(6, k, final.at[ring(k), x, 1 - near], final.at[ring(k), x, 1 - near], 3),
        lambda k: sent(7, k, final.at[ring(k), 1 - x], final.at[ring(k), 1 - x], 2),
    )

    def small_copy(stage):
        return remote(
            small_send.at[stage], small_recv.at[stage], small_send_sems.at[stage], small_recv_sems.at[stage], peers[stage]
        )

    def edge_copy(block):
        return remote(
            edges.at[block], halos.at[block], edge_sends.at[block], edge_arrivals.at[block], {"ctx": preceding}
        )

    @pl.when(step == 0)
    def _():
        exchange.greet(peers[0], peers[1])
        for group in range(STEPS):
            exchange.hold(group // 2, group % 2, given[13][:, group * BLK : (group + 1) * BLK])
            if group % 2:
                exchange.spread(group // 2)
        d_normed[...] = jnp.zeros_like(d_normed)

    def partial(lhs_of, rhs):
        for row in range(2):
            value = dot(lhs_of(2 * row + 1 - core), rhs).astype(BF16)
            core_send[lax.rem(step, 2), row] = value.reshape(2, 2, 2, PIECE, WIDE)
        copies[0](step).start()
        for row in range(2):
            own[row] = dot(lhs_of(2 * row + core), rhs).reshape(2, 2, 2, PIECE, WIDE)

    def in_chunk(rhs):
        partial(lambda s: lhs_in[s], rhs)
        d_normed[...] += dot(rhs, weight_ref[...])

    @pl.when(step < OUT_CHUNKS)
    def _():
        columns = lax.rem(step, D // WIDE) * WIDE
        rhs = cot_ref[:, pl.ds(pl.multiple_of(columns, WIDE), WIDE)]
        partial(lambda s: lhs_out[s, step // (D // WIDE)], rhs)

    @pl.when((step >= OUT_CHUNKS) & (step < OUT_CHUNKS + GATE_CHUNKS))
    def _():
        in_chunk(gate_ref[...])

    @pl.when((step >= OUT_CHUNKS + GATE_CHUNKS) & (step < CHUNKS))
    def _():
        first = 2 * (step - OUT_CHUNKS - GATE_CHUNKS)
        for done in (first, first + 1):

            @pl.when(done <= STEPS)
            def _():
                edge_copy(done).wait()
                tail = slice(length - 16, length)
                more = jnp.where(part == PARTS - 1, 0.0, halos[done])
                more = jnp.concatenate([jnp.zeros_like(more), more], axis=0)
                grads[done, tail, :] = (grads[done, tail, :].astype(F32) + more).astype(BF16)

        in_chunk(jnp.concatenate([grads[first], grads[first + 1]], axis=1))

    for half in range(2):

        @pl.when(step == 1 + half)
        def _():
            for unit in range(half * UNITS // 2, (half + 1) * UNITS // 2):
                exchange.join(unit, kept_of(kept_ref, unit), False)

    block = step - LATE

    def write(rows, value):
        grads[block, rows, :] = value

    def write_halo(value):
        edges[block] = value
        edge_copy(block).start()

    def write_taps(value):
        taps[block] = value

    def write_heads(value):
        heads[...] = value

    @pl.when((block >= 0) & (block < STEPS) & (lax.rem(block, 2) == 0))
    def _():
        both_groups = exchange.finish(block // 2)
        outgoing[0] = both_groups[:, :BLK]
        outgoing[1] = both_groups[:, BLK:]

    @pl.when(block >= 0)
    def _():
        back_steps(block, (*given[:13], outgoing.at[lax.rem(block, 2)]), scratch, write, write_halo, write_taps, write_heads)

    @pl.when(step < CHUNKS)
    def _():
        arrivals[0](step).wait_recv()
        for row in (1 - y, y):
            core_recv[ring(step), row] = (own[row] + core_recv[ring(step), row].astype(F32)).astype(BF16)
        copies[1](step).start()

    def stage(lag):
        def decorate(body):
            k = step - lag

            @pl.when((k >= 0) & (k < CHUNKS))
            def _():
                body(k, ring(k))

        return decorate

    def summed(a, b):
        return (a.astype(F32) + b.astype(F32)).astype(BF16)

    @stage(1)
    def _(k, at):
        arrivals[1](k).wait_recv()
        y_recv[at] = summed(y_recv[at], core_recv[at, y])
        copies[2](k).start()
        copies[0](k).wait_send()

    @stage(2)
    def _(k, at):
        arrivals[2](k).wait_recv()
        x_recv[at] = summed(x_recv[at], y_recv[at, x])
        copies[3](k).start()

    @stage(3)
    def _(k, at):
        arrivals[3](k).wait_recv()
        z_recv[at] = summed(z_recv[at], x_recv[at, near])
        copies[4](k).start()
        copies[1](k).wait_send()

    @stage(4)
    def _(k, at):
        arrivals[4](k).wait_recv()
        final[at, x, near, far] = summed(w_recv[at], z_recv[at, far])
        copies[5](k).start()
        copies[2](k).wait_send()

    @stage(5)
    def _(k, at):
        arrivals[5](k).wait_recv()
        copies[6](k).start()
        copies[3](k).wait_send()

    @stage(6)
    def _(k, at):
        arrivals[6](k).wait_recv()
        copies[7](k).start()
        copies[4](k).wait_send()

    @stage(7)
    def _(k, at):
        arrivals[7](k).wait_recv()
        for one in (5, 6, 7):
            copies[one](k).wait_send()
        whole = final[at].reshape(SHARD, WIDE)

        @pl.when(k < OUT_CHUNKS)
        def _():
            dout_ref[...] = whole

        @pl.when(k >= OUT_CHUNKS)
        def _():
            din_ref[...] = whole.astype(F32).T.astype(BF16)

    @pl.when(step == CHUNKS)
    def _():
        input_gain = jnp.zeros((1, D), F32)
        for k in range(length // Q):
            rows = slice(k * Q, (k + 1) * Q)
            units = units_ref[rows, :].astype(F32)
            norm = lax.rsqrt(jnp.sum(units * units, axis=1, keepdims=True) * (1.0 / D) + epsilon)
            base = units * norm
            grad = d_normed[rows, :]
            input_gain = input_gain + jnp.sum(grad * base, axis=0, keepdims=True)
            scaled = grad * gain_ref[0:1, :]
            mean = jnp.sum(scaled * base, axis=1, keepdims=True) * (1.0 / D)
            input_grad_ref[rows, :] = (cot_ref[rows, :].astype(F32) + norm * (scaled - base * mean)).astype(BF16)
        whole = jnp.concatenate([taps[one] for one in range(STEPS + 1)], axis=1)
        small_send[0] = small_sums(whole, columns_ref[...], input_gain, heads[...], stats_ref[...])
        small_copy(0).start()

    for stage_of_small in range(5):

        @pl.when(step == CHUNKS + 1 + stage_of_small)
        def _():
            small_copy(stage_of_small).wait()
            total = small_send[stage_of_small] + small_recv[stage_of_small]
            if stage_of_small < 4:
                small_send[stage_of_small + 1] = total
                small_copy(stage_of_small + 1).start()
            else:
                total_ref[...] = total


def finish(given, normed_t, mixer_t, dproj, w_turned, cot, units, input_gain, column_sums, stats, kept):
    length = cot.shape[0]
    per_half = D // WIDE
    once = pl.Buffered(1)
    whole = lambda *shape: pl.BlockSpec(shape, lambda t: (0,) * len(shape), pipeline_mode=once)
    in_chunk = lambda t: jnp.clip(t - OUT_CHUNKS, 0, IN_CHUNKS - 1)

    def out_block(t):
        k = jnp.clip(t - LAGS + 1, 0, OUT_CHUNKS - 1)
        return (k // per_half, lax.rem(k, per_half))

    slots = lambda *shape: pltpu.VMEM((RING, *shape, PIECE, WIDE), BF16)
    return pl.pallas_call(
        finish_kernel,
        grid=(CHUNKS + LAGS - 1,),
        in_specs=[
            *back_inputs(length, LATE),
            whole(4, SHARD, length),
            whole(4, 2, SHARD, length),
            pl.BlockSpec((length, WIDE), lambda t: (0, jnp.minimum(in_chunk(t), GATE_CHUNKS - 1))),
            pl.BlockSpec((WIDE, D), lambda t: (in_chunk(t), 0)),
            whole(length, D),
            whole(length, D),
            whole(1, D),
            whole(8, INNER),
            whole(8, D),
            whole(PARTS, 8, 128),
        ],
        out_specs=[
            pl.BlockSpec((WIDE, SHARD), lambda t: (in_chunk(t - LAGS + 1), 0)),
            pl.BlockSpec((SHARD, WIDE), out_block),
            pl.BlockSpec((length, D), lambda t: (0, 0)),
            pl.BlockSpec((8, XBC), lambda t: (0, 0)),
        ],
        out_shape=[
            jax.ShapeDtypeStruct((PROJ, SHARD), BF16),
            jax.ShapeDtypeStruct((2 * SHARD, D), BF16),
            jax.ShapeDtypeStruct((length, D), BF16),
            jax.ShapeDtypeStruct((8, XBC), F32),
        ],
        scratch_shapes=[
            *back_scratch(length),
            *exchange_scratch(),
            pltpu.VMEM((2, STATE, BLK), BF16),
            pltpu.VMEM((STEPS + 2, length, BLK), BF16),
            pltpu.VMEM((STEPS + 1, PAD, BLK), F32),
            pltpu.VMEM((STEPS + 1, PAD, BLK), F32),
            pltpu.VMEM((STEPS + 1, 8, BLK), F32),
            pltpu.VMEM((8, 128), F32),
            pltpu.VMEM((length, D), F32),
            pltpu.VMEM((2, 2, 2, 2, PIECE, WIDE), F32),
            pltpu.VMEM((2, 2, 2, 2, 2, PIECE, WIDE), BF16),
            slots(2, 2, 2, 2),
            slots(2, 2, 2),
            slots(2, 2),
            slots(2),
            slots(),
            slots(2, 2, 2),
            pltpu.VMEM((5, 8, XBC), F32),
            pltpu.VMEM((5, 8, XBC), F32),
            pltpu.SemaphoreType.DMA((8, CHUNKS)),
            pltpu.SemaphoreType.DMA((8, CHUNKS)),
            pltpu.SemaphoreType.DMA((5,)),
            pltpu.SemaphoreType.DMA((5,)),
            pltpu.SemaphoreType.DMA((STEPS + 1,)),
            pltpu.SemaphoreType.DMA((STEPS + 1,)),
        ],
        compiler_params=communicating(0),
        name="finish",
    )(*given, normed_t, mixer_t, dproj, w_turned, cot, units, input_gain, column_sums, stats, kept)


def settle_kernel(din_ref, dout_ref, total_ref, *outs, entries):
    (
        din_out, dout_out, taps_out, bias_out, step_bias_out, decay_out, skip_out, gain_out, input_gain_out, rms_out,
    ) = outs
    din_out[...] = din_ref[...].astype(F32)
    dout_out[...] = dout_ref[...].astype(F32)

    @pl.when(pl.program_id(0) == 0)
    def _():
        shard = lax.axis_index("fsdp")
        own = HEADS // 4
        width = XBC // 4

        def mine(pieces):
            result = pieces[0]
            for s in range(1, 4):
                result = jnp.where(shard == s, pieces[s], result)
            return result

        def flat(ref, row):
            ref[...] = row.reshape(ref.shape)

        total = total_ref[...]
        columns = mine([pltpu.roll(total, (XBC - s * width) % XBC, 1) if s else total for s in range(4)])
        taps_out[...] = columns[:4, :width]
        flat(bias_out, columns[4:5, :width])

        def heads(row):
            rows = jnp.broadcast_to(row, (8, 128))
            rows = mine([pltpu.roll(rows, (128 - s * own) % 128, 1) if s else rows for s in range(4)])
            return rows[:1, :own]

        flat(step_bias_out, heads(total[7:8, D : D + 128]))
        flat(decay_out, heads(total[7:8, D + 128 : D + 256]))
        skip = jnp.zeros((8, 128), F32)
        for group in range(STEPS):
            high, low = in_two(jnp.broadcast_to(total[6:7, group * BLK : (group + 1) * BLK], (8, BLK)))
            skip = skip + dot(high, chosen_back(group)) + dot(low, chosen_back(group))
        flat(skip_out, heads(skip[:1]))
        flat(gain_out, mine([total[5:6, s * (INNER // 4) : (s + 1) * (INNER // 4)] for s in range(4)]))
        flat(input_gain_out, mine([total[7:8, s * SHARD : (s + 1) * SHARD] for s in range(4)]))
        squares = jnp.concatenate([total[7:8, D + 256 : D + 257], total[7:8, D + 384 : D + 385]], axis=1)
        flat(rms_out, jnp.sqrt(squares * (1.0 / entries)))


def settle(d_in, d_out, total, entries):
    steps = 3
    shapes = [
        (4, XBC // 4),
        (XBC // 4,),
        (HEADS // 4,),
        (HEADS // 4,),
        (HEADS // 4,),
        (INNER // 4,),
        (SHARD,),
        (2,),
    ]
    rows = -(-PROJ // steps // 16) * 16
    whole = lambda shape: pl.BlockSpec(shape, lambda i: (0,) * len(shape))
    blocks = [
        pl.BlockSpec((rows, SHARD), lambda i: (i, 0)),
        pl.BlockSpec((2 * SHARD // steps, D), lambda i: (i, 0)),
    ]
    d_in, d_out, taps, *rest = pl.pallas_call(
        functools.partial(settle_kernel, entries=entries),
        grid=(steps,),
        in_specs=[*blocks, whole((8, XBC))],
        out_specs=[*blocks, *[whole(shape) for shape in shapes]],
        out_shape=[
            jax.ShapeDtypeStruct((PROJ, SHARD), F32),
            jax.ShapeDtypeStruct((2 * SHARD, D), F32),
            *[jax.ShapeDtypeStruct(shape, F32) for shape in shapes],
        ],
        compiler_params=pltpu.CompilerParams(vmem_limit_bytes=VMEM_LIMIT),
        name="settle",
    )(d_in, d_out, total)
    return (d_in.T, d_out, taps.T, *[each.reshape(-1) for each in rest])


def passed_along(block, axis, distance):
    devices = range(lax.axis_size(axis))
    route = [(i - distance, i) for i in devices if i - distance in devices]
    return lax.ppermute(block, axis, route)


def pack_small(conv_taps, conv_bias, dt_bias, decay_log, skip_scale, mixer_gain, input_gain):
    width = conv_bias.shape[0]

    def line(*parts):
        flat = jnp.concatenate(parts)
        return jnp.pad(flat, (0, width - flat.shape[0]))[None]

    rows = jnp.concatenate(
        [
            conv_taps.T,
            conv_bias[None],
            line(mixer_gain),
            line(input_gain),
            line(dt_bias, decay_log, skip_scale),
        ],
        axis=0,
    )
    return jnp.pad(rows.astype(F32), ((0, 0), (0, SMALL_WIDTH - width)))


def unpack_small(whole, width):
    shards = whole.shape[0]
    joined = jnp.swapaxes(whole, 0, 1)
    taps = jnp.pad(joined[:5, :, :width].reshape(5, shards * width).astype(F32), ((0, 3), (0, 0)))
    gain = joined[5, :, : INNER // shards].reshape(1, INNER).astype(F32)
    input_gain = joined[6, :, : D // shards].reshape(1, D).astype(F32)
    own = HEADS // shards
    heads = joined[7, :, : 3 * own].reshape(shards, 3, own).swapaxes(0, 1).reshape(3, HEADS)
    heads = jnp.pad(heads.astype(F32), ((0, 5), (0, 128 - HEADS)))
    return taps, jnp.pad(gain, ((0, 7), (0, 0))), input_gain, heads


def on_device(
    inputs,
    segment_ids,
    out_grad,
    in_matrix,
    out_matrix,
    conv_taps,
    conv_bias,
    dt_bias,
    decay_log,
    skip_scale,
    mixer_gain,
    input_gain,
):
    shards, parts = lax.axis_size("fsdp"), lax.axis_size("ctx")
    place = lax.axis_index("ctx")
    units_low, cot = inputs[0], out_grad[0]
    seg_ids = segment_ids[0]
    length = units_low.shape[0]
    here = (shards, parts) == (4, PARTS)
    seg_row = segment_ids
    if here:
        (
            xs, y_local, incoming, b_rows, c_rows, dt, running, entering,
            kept, w_turned, out_whole, projected, normed_t, halo, taps, heads, gain, g_float, seg_lanes,
        ) = forward(
            in_matrix, out_matrix, units_low, seg_row,
            conv_taps.T, conv_bias, mixer_gain, input_gain, dt_bias, decay_log, skip_scale,
        )
        out_whole = out_whole.reshape(-1, D)
    else:
        units = units_low.astype(F32)
        inv_rms = lax.rsqrt(jnp.mean(units * units, axis=-1, keepdims=True) + epsilon)
        base_rows = units * inv_rms
        w_whole = jnp.pad(in_matrix, ((0, 0), (0, WIDTH - PROJ)))
        w_whole = lax.all_gather(w_whole, "fsdp", axis=0, tiled=True)
        out_whole = lax.all_gather(out_matrix, "fsdp", axis=0, tiled=True)
        rim_seg = passed_along(seg_ids[length - CONV + 1 :], "ctx", 1)
        small = pack_small(conv_taps, conv_bias, dt_bias, decay_log, skip_scale, mixer_gain, input_gain)
        taps, gain, g_float, heads = unpack_small(lax.all_gather(small, "fsdp"), conv_bias.shape[0])
        normed = (base_rows * g_float).astype(BF16)
        normed_t = normed.T
        projected = dot(normed, w_whole).astype(BF16)
        rim_rows = passed_along(projected[length - CONV + 1 :], "ctx", 1)
        halo = jnp.pad(rim_rows, ((PAD - CONV + 1, 0), (0, 0))).astype(F32)
        seg_ext = jnp.concatenate(
            [
                jnp.full((PAD - CONV + 1,), -1, jnp.int32),
                rim_seg,
                seg_ids,
                jnp.full((PAD,), -2, jnp.int32),
            ]
        )
        seg_lanes = jnp.broadcast_to(seg_ext[:, None], (length + 2 * PAD, 128))
        xs, y_local, state, b_rows, c_rows, dt, running, entering, keep = front(
            projected, halo, taps, heads, seg_lanes, seg_row
        )
        kept = lax.all_gather(keep, "ctx")
        incoming = joined_plainly(lax.all_gather(state, "ctx"), kept, place, True)
    mixer_t, dproj, dy, outgoing, column_sums, block_out, stats = tail(
        y_local, xs, projected, incoming, out_whole, c_rows, entering, heads, gain, cot, units_low
    )
    if not here:
        outgoing = joined_plainly(lax.all_gather(outgoing, "ctx"), kept, place, False)
    given = (
        projected, projected, halo, taps, heads, seg_lanes, seg_row, b_rows, c_rows, dt, running, dy, incoming, outgoing,
    )
    if here:
        d_in, d_out, input_grad, total = finish(
            given, normed_t, mixer_t.reshape(4, 2, SHARD, length), dproj, w_turned, cot, units_low, g_float, column_sums, stats, kept
        )
        sums = settle(d_in, d_out, total, length * shards * parts * D)
        return (block_out[None], input_grad[None], *sums)
    else:
        dproj, d_halo, d_taps, d_heads = back(given, dproj)
        returned = passed_along(d_halo.astype(BF16), "ctx", -1)
        last = lax.slice(dproj, (length - PAD, INNER), (length, INNER + XBC))
        last = (last.astype(F32) + returned.astype(F32)).astype(BF16)
        dproj = lax.dynamic_update_slice(dproj, last, (length - PAD, INNER))
        d_normed = dot_nt(dproj, w_whole)
        d_input_gain = jnp.sum(d_normed * base_rows, axis=0)
        d_base = d_normed * g_float
        d_units = inv_rms * (d_base - base_rows * jnp.mean(d_base * base_rows, axis=-1, keepdims=True))
        input_grad = (cot.astype(F32) + d_units).astype(BF16)

        def scattered(grad):
            return lax.psum_scatter(grad.astype(BF16), "fsdp", scatter_dimension=0, tiled=True)

        d_in = jnp.dot(normed_t, dproj, preferred_element_type=F32)[:, :PROJ]
        d_out = jnp.dot(mixer_t, cot, preferred_element_type=F32)
        d_in = lax.psum(scattered(d_in), "ctx").astype(F32)
        d_out = lax.psum(scattered(d_out), "ctx").astype(F32)
        total = lax.psum(small_sums(d_taps, column_sums, d_input_gain[None], d_heads, stats), ("fsdp", "ctx"))
    me = lax.axis_index("fsdp")

    def own(flat):
        size = flat.shape[-1] // shards
        return lax.dynamic_slice_in_dim(flat, me * size, size, flat.ndim - 1)

    skip_sums = jnp.sum(total[6, :INNER].reshape(HEADS, HDIM), axis=1)
    at = D + 256
    stat_sums = jnp.stack([total[7, at], total[7, at + 128]])
    rms_stats = jnp.sqrt(stat_sums / (length * shards * parts * D))
    return (
        block_out[None],
        input_grad[None],
        d_in,
        d_out,
        own(total[:4]).T,
        own(total[4]),
        own(total[7, D : D + HEADS]),
        own(total[7, D + 128 : D + 128 + HEADS]),
        own(skip_sums),
        own(total[5, :INNER]),
        own(total[7, :D]),
        rms_stats,
    )


def solution(mesh):
    return jax.shard_map(
        on_device,
        mesh=mesh,
        in_specs=(
            P("fsdp", "ctx", None),
            P("fsdp", "ctx"),
            P("fsdp", "ctx", None),
            P("fsdp", None),
            P("fsdp", None),
            P("fsdp", None),
            P("fsdp"),
            P("fsdp"),
            P("fsdp"),
            P("fsdp"),
            P("fsdp"),
            P("fsdp"),
        ),
        out_specs=(
            P("fsdp", "ctx", None),
            P("fsdp", "ctx", None),
            P("fsdp", None),
            P("fsdp", None),
            P("fsdp", None),
            P("fsdp"),
            P("fsdp"),
            P("fsdp"),
            P("fsdp"),
            P("fsdp"),
            P("fsdp"),
            P(),
        ),
        check_vma=False,
    )
```

```python
import functools

import jax
import jax.numpy as jnp
from jax import lax
from jax.experimental import pallas as pl
from jax.experimental.pallas import tpu as pltpu
from jax.sharding import PartitionSpec as P

D = 1536
HEADS = 48
HDIM = 64
STATE = 128
CONV = 4
INNER = 3072
XBC = 3328
PROJ = 6448
WIDTH = 6656

BLK = 256
GROUP = BLK // HDIM
STEPS = INNER // BLK
Q = 128
PAD = 8
WIDE = 512
SHARD = D // 4
PIECE = SHARD // 8
SMALL_WIDTH = 896
AHEAD = 2

epsilon = 1e-05
F32, BF16 = jnp.float32, jnp.bfloat16
HIGHEST = lax.Precision.HIGHEST
VMEM_LIMIT = 60 * 1024 * 1024


def communicating(number):
    return pltpu.CompilerParams(
        vmem_limit_bytes=VMEM_LIMIT, collective_id=number, has_side_effects=True
    )


def dot(a, b):
    return jnp.dot(a, b, preferred_element_type=F32)


def dot_nt(a, b):
    return lax.dot_general(a, b, (((1,), (1,)), ((), ())), preferred_element_type=F32)


def iota(shape, dim):
    return lax.broadcasted_iota(jnp.int32, shape, dim)


def sigmoid(v):
    return 0.5 + 0.5 * jnp.tanh(0.5 * v)


def in_two(a):
    high = a.astype(BF16)
    return high, (a - high.astype(F32)).astype(BF16)


def chosen(step):
    columns = step * GROUP + lax.shift_right_logical(iota((128, BLK), 1), 6)
    return (iota((128, BLK), 0) == columns).astype(BF16)


def chosen_back(step):
    heads = step * GROUP + lax.shift_right_logical(iota((BLK, 128), 0), 6)
    return (iota((BLK, 128), 1) == heads).astype(BF16)


def widen(per_head, select):
    high, low = in_two(per_head)
    return dot(high, select) + dot(low, select)


def halves(pair):
    first = iota(pair.shape, 1) < HDIM
    zero = jnp.zeros_like(pair)
    return jnp.concatenate([jnp.where(first, pair, zero), jnp.where(first, zero, pair)], axis=0)


def both(mask):
    return jnp.concatenate([mask, mask], axis=1)


def conv_rows(ext_ref, seg_ref, taps_ref, start, rows):
    own = seg_ref[start + PAD : start + PAD + rows, :]
    total = taps_ref[4:5, :] + taps_ref[3:4, :] * ext_ref[start + PAD : start + PAD + rows, :]
    for back in range(1, CONV):
        at = start + PAD - back
        same = both(seg_ref[at : at + rows, :] == own)
        total = total + jnp.where(
            same, taps_ref[3 - back : 4 - back, :] * ext_ref[at : at + rows, :], 0.0
        )
    return total


def chunk_flags(seg_ref, k):
    own = seg_ref[PAD + k * Q : PAD + (k + 1) * Q, :]
    before = seg_ref[PAD + k * Q - 1 : PAD + k * Q, :]
    last = seg_ref[PAD + (k + 1) * Q - 1 : PAD + (k + 1) * Q, :]
    return (own == before).astype(F32), (own == last).astype(F32)


def masked_scores(seg_ref, row_ref, b_rows, c_rows, k):
    own = seg_ref[PAD + k * Q : PAD + (k + 1) * Q, :]
    row = row_ref[0:1, k * Q : (k + 1) * Q]
    keep = (own == row) & (iota((Q, Q), 1) <= iota((Q, Q), 0))
    return jnp.where(keep, dot_nt(c_rows, b_rows), 0.0)


def remote(source, target, send, arrival, peer):
    return pltpu.make_async_remote_copy(
        src_ref=source,
        dst_ref=target,
        send_sem=send,
        recv_sem=arrival,
        device_id=peer,
        device_id_type=pl.DeviceIdType.MESH,
    )


def flipped(index, bit):
    return index + bit - 2 * bit * lax.rem(index // bit, 2)


class Gather:
    def __init__(self, locate, several, rows, loads, sends, arrivals):
        self.locate, self.several, self.rows = locate, several, rows
        self.loads, self.sends, self.arrivals = loads, sends, arrivals
        shard, part = lax.axis_index("fsdp"), lax.axis_index("ctx")
        self.own, self.other = shard, flipped(shard, 2)
        x, near = lax.rem(part, 2), lax.rem(part // 2, 2)
        self.mine, self.over_x, self.over_z = 2 * x + near, 2 * (1 - x) + near, 2 * x + 1 - near
        self.across = 2 * (1 - x) + 1 - near
        self.core, self.y = {"fsdp": flipped(shard, 1)}, {"fsdp": flipped(shard, 2)}
        self.to_x, self.to_z = {"ctx": flipped(part, 1)}, {"ctx": flipped(part, 2)}

    def whole(self, shard, k):
        return self.locate(k, shard, 0, self.rows)

    def quarter(self, shard, k, which):
        return self.locate(k, shard, which * (self.rows // 4), self.rows // 4)

    def half(self, shard, k, which, second):
        return self.locate(k, shard, (2 * which + second) * (self.rows // 8), self.rows // 8)

    def copy(self, place, kind, k, peer):
        return remote(place, place, self.sends.at[k], self.arrivals.at[kind, k], peer)

    def load(self, k, source):
        return pltpu.make_async_copy(source, self.whole(self.own, k), self.loads.at[k])

    def begin(self, k):
        self.load(k, self.whole(self.own, k)).wait()
        self.send_own(k)

    def send_own(self, k):
        self.copy(self.quarter(self.own, k, self.mine), 1, k, self.y).start()
        self.copy(self.whole(self.own, k), 0, k, self.core).start()

    def first(self, k):
        quarter = self.quarter(self.other, k, self.mine)
        self.copy(quarter, 1, k, self.y).wait_recv()
        self.copy(quarter, 2, k, self.to_x).start()
        self.copy(quarter, 3, k, self.to_z).start()

    def second(self, k):
        self.copy(self.quarter(self.other, k, self.over_x), 2, k, self.to_x).wait_recv()
        self.copy(self.half(self.other, k, self.over_x, 0), 4, k, self.to_z).start()
        self.copy(self.quarter(self.other, k, self.over_z), 3, k, self.to_z).wait_recv()
        self.copy(self.half(self.other, k, self.over_z, 1), 4, k, self.to_x).start()

    def third(self, k):
        self.copy(self.quarter(self.other, k, self.across), 4, k, self.to_x).wait_recv()
        self.copy(self.whole(self.other, k), 0, k, self.core).start()

    def complete(self, k):
        self.copy(self.several(k, 2), 0, k, self.core).wait_recv()

    def drain(self, k):
        self.copy(self.several(k, 3), 0, k, self.core).wait_send()


class PlainGather(Gather):
    def direct(self, shard, k):
        return self.locate(k, shard, 0, DIRECT * self.rows // 6)

    def part_of(self, shard, k, which):
        size = (6 - DIRECT) * self.rows // 12
        return self.locate(k, shard, DIRECT * self.rows // 6 + which * size, size)

    def send_own(self, k):
        self.copy(self.direct(self.own, k), 3, k, self.y).start()
        self.copy(self.part_of(self.own, k, self.mine // 2), 1, k, self.y).start()
        self.copy(self.whole(self.own, k), 0, k, self.core).start()

    def first(self, k):
        part = self.part_of(self.other, k, self.mine // 2)
        self.copy(part, 1, k, self.y).wait_recv()
        self.copy(part, 2, k, self.to_x).start()

    def second(self, k):
        self.copy(self.direct(self.other, k), 3, k, self.y).wait_recv()
        self.copy(self.part_of(self.other, k, self.over_x // 2), 2, k, self.to_x).wait_recv()
        self.copy(self.whole(self.other, k), 0, k, self.core).start()


def gather_sems(chunks):
    return [
        pltpu.SemaphoreType.DMA((chunks,)),
        pltpu.SemaphoreType.DMA((chunks,)),
        pltpu.SemaphoreType.DMA((5, chunks)),
    ]


PARTS = 8
SLAB = STATE // PARTS
UNIT = 2 * BLK
UNITS = INNER // UNIT


class Exchange:
    def __init__(self, held, gathered, joined, incoming, sems):
        self.held, self.gathered, self.joined, self.incoming, self.sems = held, gathered, joined, incoming, sems
        self.me = lax.axis_index("ctx")

    def others(self):
        return [lax.rem(self.me + hop, PARTS) for hop in range(1, PARTS)]

    def greet(self, *further):
        barrier = pltpu.get_barrier_semaphore()
        peers = [{"ctx": other} for other in self.others()] + list(further)
        for peer in peers:
            pl.semaphore_signal(barrier, inc=1, device_id=peer, device_id_type=pl.DeviceIdType.MESH)
        pl.semaphore_wait(barrier, len(peers))

    def copy(self, source, target, kind, group, other):
        return pltpu.make_async_remote_copy(
            src_ref=source,
            dst_ref=target,
            send_sem=self.sems.at[2 * kind, group],
            recv_sem=self.sems.at[2 * kind + 1, group],
            device_id={"ctx": other},
            device_id_type=pl.DeviceIdType.MESH,
        )

    def all_of(self, kind, group):
        source, target = ((self.held, self.gathered), (self.joined, self.incoming))[kind]
        some = pl.ds(0, PARTS - 1)
        return self.copy(source.at[group, some], target.at[group, some], kind, group, self.others()[0])

    def hold(self, group, half, state):
        self.held[group, :, :, half * BLK : (half + 1) * BLK] = state.astype(BF16).reshape(PARTS, SLAB, BLK)

    def spread(self, group):
        self.gathered[group, self.me] = self.held[group, self.me]
        for other in self.others():
            self.copy(self.held.at[group, other], self.gathered.at[group, self.me], 0, group, other).start()

    def join(self, group, kept, forward):
        self.all_of(0, group).wait_recv()
        total = jnp.zeros((SLAB, UNIT), F32)
        for part in range(PARTS) if forward else range(PARTS - 1, -1, -1):
            self.joined[group, part] = total.astype(BF16)
            total = kept[part : part + 1, :] * total + self.gathered[group, part].astype(F32)
        self.incoming[group, self.me] = self.joined[group, self.me]
        for other in self.others():
            self.copy(self.joined.at[group, other], self.incoming.at[group, self.me], 1, group, other).start()

    def finish(self, group):
        self.all_of(1, group).wait_recv()
        self.all_of(0, group).wait_send()
        self.all_of(1, group).wait_send()
        return self.incoming[group].reshape(STATE, UNIT)


def exchange_scratch():
    return [pltpu.VMEM((UNITS, PARTS, SLAB, UNIT), BF16) for _ in range(4)] + [pltpu.SemaphoreType.DMA((4, UNITS))]


def kept_of(kept_ref, unit):
    rows = jnp.concatenate([kept_ref[part, 0:1, :] for part in range(PARTS)], axis=0)
    return jnp.concatenate([widen(rows, chosen(2 * unit)), widen(rows, chosen(2 * unit + 1))], axis=1)


def joined_plainly(states, kept, place, forward):
    factors = jnp.repeat(kept[:, 0, :HEADS], HDIM, axis=1)[:, None, :]
    total = jnp.zeros(states.shape[1:], F32)
    result = total
    count = states.shape[0]
    for part in range(count) if forward else range(count - 1, -1, -1):
        result = jnp.where(place == part, total, result)
        total = factors[part] * total + states[part].astype(F32)
    return result.astype(BF16)


def prepare(
    bc_ref, dt_raw, halo_bc_ref, taps_bc_ref, heads_ref, seg_ref, row_ref, b_ref, c_ref, dt_ref, run_ref, in_ref,
    ext, scores, run_t, b_t, enter, leave,
):
    chunks = bc_ref.shape[0] // Q
    ext[0:PAD, :] = halo_bc_ref[...]
    ext[PAD:, :] = bc_ref[...].astype(F32)
    lane = iota((Q, 128), 1)
    lower = (iota((Q, Q), 1) <= iota((Q, Q), 0)).astype(F32)
    offset = jnp.zeros((1, 128), F32)
    for k in range(chunks):
        rows = slice(k * Q, (k + 1) * Q)
        total = conv_rows(ext, seg_ref, taps_bc_ref, k * Q, Q)
        active = total * sigmoid(total)
        b_rows, c_rows = active[:, :STATE], active[:, STATE:].astype(BF16)
        b_t[:, rows] = b_rows.T.astype(BF16)
        b_rows = b_rows.astype(BF16)
        b_ref[rows, :] = b_rows
        c_ref[rows, :] = c_rows
        scores[rows, :] = masked_scores(seg_ref, row_ref, b_rows, c_rows, k)
        raw = jnp.where(lane < HEADS, dt_raw(rows).astype(F32), 0.0) + heads_ref[0:1, :]
        dt = jnp.maximum(raw, 0.0) + jnp.log1p(jnp.exp(-jnp.abs(raw)))
        log_decay = -dt * jnp.exp(heads_ref[1:2, :])
        running = jnp.dot(lower, log_decay, precision=HIGHEST, preferred_element_type=F32)
        dt_ref[rows, :] = dt
        run_ref[rows, :] = running
        run_t[k] = running.T
        carry, tail = chunk_flags(seg_ref, k)
        enter[rows, :] = jnp.exp(running) * carry
        leave[rows, :] = jnp.exp(running[Q - 1 : Q, :] - running) * tail
        same = (seg_ref[PAD + k * Q : PAD + (k + 1) * Q, :] == seg_ref[PAD - 1 : PAD, :]).astype(F32)
        whole = jnp.exp(running + offset) * same
        in_ref[rows, :] = whole
        offset = offset + running[Q - 1 : Q, :]
    return jnp.broadcast_to(whole[Q - 1 : Q, :], (8, 128))


def front_kernel(
    x_ref, bc_ref, dtraw_ref, halo_ref, halo_bc_ref, taps_ref, taps_bc_ref, heads_ref, seg_ref, row_ref,
    xs_ref, y_ref, state_ref, b_ref, c_ref, dt_ref, run_ref, in_ref, keep_ref,
    ext, scores, run_t, b_t, enter, leave,
):
    step = pl.program_id(0)

    @pl.when(step == 0)
    def _():
        keep_ref[...] = prepare(
            bc_ref, lambda rows: dtraw_ref[rows, :128], halo_bc_ref, taps_bc_ref, heads_ref, seg_ref, row_ref,
            b_ref, c_ref, dt_ref, run_ref, in_ref, ext, scores, run_t, b_t, enter, leave,
        )

    state = local_scan(
        step, x_ref, halo_ref, taps_ref, seg_ref, xs_ref, y_ref, c_ref, dt_ref, run_ref,
        ext, scores, run_t, b_t, enter, leave,
    )
    state_ref[...] = state.astype(BF16)


def local_scan(
    step, x_ref, halo_ref, taps_ref, seg_ref, xs_ref, y_ref, c_ref, dt_ref, run_ref,
    ext, scores, run_t, b_t, enter, leave,
):
    chunks = x_ref.shape[0] // Q
    ext[0:PAD, :] = halo_ref[...]
    ext[PAD:, :] = x_ref[...].astype(F32)
    select = chosen(step)
    state = jnp.zeros((STATE, BLK), F32)
    for k in range(chunks):
        rows = slice(k * Q, (k + 1) * Q)
        total = conv_rows(ext, seg_ref, taps_ref, k * Q, Q)
        values = total * sigmoid(total)
        xs_ref[rows, :] = values.astype(BF16)
        scaled = (values * widen(dt_ref[rows, :], select)).astype(BF16)
        entering = widen(enter[rows, :], select)
        running = pltpu.roll(run_ref[rows, :], lax.rem(128 - step * GROUP, 128), 1)
        parts = []
        for pair in range(2):
            mixing = []
            for one in range(2):
                head = 2 * pair + one
                gap = running[:, head : head + 1] - run_t[k, pl.ds(step * GROUP + head, 1), :]
                mixing.append((jnp.exp(jnp.minimum(gap, 0.0)) * scores[rows, :]).astype(BF16))
            parts.append(
                dot(jnp.concatenate(mixing, axis=1), halves(scaled[:, pair * 128 : (pair + 1) * 128]))
            )
        inside = jnp.concatenate(parts, axis=1)
        y_ref[rows, :] = (inside + entering * dot(c_ref[rows, :], state.astype(BF16))).astype(BF16)
        weighted = (scaled.astype(F32) * widen(leave[rows, :], select)).astype(BF16)
        state = entering[Q - 1 : Q, :] * state + dot(b_t[:, rows], weighted)
    return state


def front_outputs(length, column, state_at, width=BLK):
    whole = lambda *shape: (pl.BlockSpec(shape, lambda j: (0, 0)), shape)
    columns = lambda rows, at: (pl.BlockSpec((rows, width), at), (rows, INNER))
    specs = [
        (columns(length, column), BF16),
        (columns(length, column), BF16),
        (columns(STATE, state_at), BF16),
        (whole(length, 128), BF16),
        (whole(length, 128), BF16),
        (whole(length, 128), F32),
        (whole(length, 128), F32),
        (whole(length, 128), F32),
    ]
    return [spec for (spec, _), _ in specs], [jax.ShapeDtypeStruct(shape, kind) for (_, shape), kind in specs]


def front_scratch(length):
    return [
        pltpu.VMEM((length + PAD, BLK), F32),
        pltpu.VMEM((length, Q), F32),
        pltpu.VMEM((length // Q, 128, Q), F32),
        pltpu.VMEM((128, length), BF16),
        pltpu.VMEM((length, 128), F32),
        pltpu.VMEM((length, 128), F32),
    ]


def front(projected, halo, taps, heads, seg_lanes, seg_row):
    length = projected.shape[0]
    whole = lambda *shape: pl.BlockSpec(shape, lambda j: (0,) * len(shape))
    columns = lambda rows, at: pl.BlockSpec((rows, BLK), at)
    out_specs, out_shape = front_outputs(length, lambda j: (0, j), lambda j: (0, j))
    return pl.pallas_call(
        front_kernel,
        grid=(STEPS,),
        in_specs=[
            columns(length, lambda j: (0, STEPS + j)),
            columns(length, lambda j: (0, 2 * STEPS)),
            columns(length, lambda j: (0, 2 * STEPS + 1)),
            columns(PAD, lambda j: (0, STEPS + j)),
            columns(PAD, lambda j: (0, 2 * STEPS)),
            columns(8, lambda j: (0, j)),
            columns(8, lambda j: (0, STEPS)),
            whole(8, 128),
            whole(length + 2 * PAD, 128),
            whole(1, length),
        ],
        out_specs=[*out_specs, whole(8, 128)],
        out_shape=[*out_shape, jax.ShapeDtypeStruct((8, 128), F32)],
        scratch_shapes=front_scratch(length),
        compiler_params=pltpu.CompilerParams(vmem_limit_bytes=VMEM_LIMIT),
        name="front",
    )(projected, projected, projected, halo, halo, taps, taps, heads, seg_lanes, seg_row)


ORDER = (2 * INNER // WIDE, *range(INNER // WIDE, 2 * INNER // WIDE), *range(INNER // WIDE))
MULTIPLY = 3
SCAN = MULTIPLY + 2
OUT_WIDE = 128
OUT_PIECES = D // OUT_WIDE
OUT_BEGIN, DIRECT = 4, 4
JOIN, DONE = 2, 4
SLOTS = MULTIPLY + len(ORDER)
EDGES = 1 + INNER // WIDE


def chunk_at(position):
    half = INNER // WIDE
    return jnp.where(position == 0, 2 * half, jnp.where(position <= half, position - 1 + half, position - 1 - half))


def forward_kernel(*refs):
    main_ref, shard_ref, units_ref, row_ref = refs[:4]
    conv_ref, bias_ref, mixer_ref, input_ref, *head_refs = refs[4:11]
    refs = refs[6:]
    xs_ref, y_ref, state_ref, b_ref, c_ref, dt_ref, run_ref, in_ref = refs[5:13]
    keep_ref, weight_ref, whole_ref, projected_ref, normed_t_ref = refs[13:18]
    halo_ref, taps_ref, heads_ref, gain_ref, input_gain_ref, seg_ref = refs[18:24]
    ext, scores, run_t, b_t, enter, leave = refs[24:30]
    exchange = Exchange(*refs[30:35])
    own_keep, keeps, keep_sends, keep_arrivals = refs[35:39]
    gathered, loads, sends, arrivals, stores = refs[39:44]
    out_gathered, out_loads, out_sends, out_arrivals, out_stores = refs[44:49]
    normed, blocks, taps, own_small, smalls, seg_tail, seg_head = refs[49:56]
    edges, halos, small_sends, small_arrivals, edge_sends, edge_arrivals = refs[56:]
    step = pl.program_id(0)
    length = units_ref.shape[0]
    shard, part = lax.axis_index("fsdp"), lax.axis_index("ctx")
    others = ({"fsdp": flipped(shard, 1)}, {"fsdp": flipped(shard, 2)}, {"fsdp": flipped(flipped(shard, 1), 2)})
    following = {"ctx": lax.rem(part + 1, PARTS)}

    def place_in(k, s, start, size):
        rows, columns = pl.multiple_of(start, size), pl.multiple_of(s * SHARD, SHARD)
        return gathered.at[k, pl.ds(rows, size), pl.ds(columns, SHARD)]

    def place_out(k, s, start, size):
        return out_gathered.at[k, s, pl.ds(pl.multiple_of(start, size), size)]

    several_in = lambda k, count: gathered.at[k, :, pl.ds(0, count * SHARD)]
    several_out = lambda k, count: out_gathered.at[k, pl.ds(0, count)]
    gather = Gather(place_in, several_in, WIDE, loads, sends, arrivals)
    gather_out = PlainGather(place_out, several_out, 2 * SHARD, out_loads, out_sends, out_arrivals)
    rest = PROJ % WIDE

    def load_rest():
        columns = pl.ds(pl.multiple_of(shard * SHARD, SHARD), SHARD)
        return pltpu.make_async_copy(
            main_ref.at[PROJ - rest : PROJ, :], gathered.at[0, pl.ds(0, rest), columns], loads.at[0]
        )

    def small_copy(hop):
        return remote(own_small, smalls.at[shard], small_sends.at[hop], small_arrivals.at[hop], others[hop])

    def seg_copy():
        return remote(seg_tail, seg_head, small_sends.at[3], small_arrivals.at[3], following)

    def edge_copy(k):
        return remote(edges.at[k], halos.at[k], edge_sends.at[k], edge_arrivals.at[k], following)

    def keep_copy(hop):
        peer = {"ctx": lax.rem(part + hop + 1, PARTS)}
        return remote(own_keep, keeps.at[part], keep_sends.at[hop], keep_arrivals.at[hop], peer)

    def store(k):
        rows = pl.ds(pl.multiple_of(chunk_at(k) * WIDE, WIDE), WIDE)
        return pltpu.make_async_copy(gathered.at[k], weight_ref.at[rows], stores.at[k])

    def store_out(k):
        columns = pl.ds(pl.multiple_of(k * OUT_WIDE, OUT_WIDE), OUT_WIDE)
        return pltpu.make_async_copy(out_gathered.at[k], whole_ref.at[:, :, columns], out_stores.at[k])

    @pl.when(step == 0)
    def _():
        barrier = pltpu.get_barrier_semaphore()
        greeted = [*[{"ctx": other} for other in exchange.others()], *others]
        for peer in greeted:
            pl.semaphore_signal(barrier, inc=1, device_id=peer, device_id_type=pl.DeviceIdType.MESH)
        load_rest().start()
        for k, chunk in enumerate(ORDER):
            if k:
                gather.load(k, main_ref.at[chunk * WIDE : (chunk + 1) * WIDE, :]).start()
        for k in range(OUT_PIECES):
            gather_out.load(k, shard_ref.at[:, k * OUT_WIDE : (k + 1) * OUT_WIDE]).start()
        own_small[...] = jnp.zeros((8, SMALL_WIDTH), F32)
        own_small[0:4, : XBC // 4] = conv_ref[...].astype(F32)
        for row, ref in ((4, bias_ref), (5, mixer_ref), (6, input_ref)):
            own_small[row : row + 1, : ref.shape[0]] = ref[...].astype(F32).reshape(1, ref.shape[0])
        for kind, ref in enumerate(head_refs):
            own_small[7:8, kind * 128 : kind * 128 + HEADS // 4] = ref[...].astype(F32).reshape(1, HEADS // 4)
        smalls[shard] = own_small[...]
        columns = pl.ds(pl.multiple_of(shard * SHARD, SHARD), SHARD)
        gathered[0, rest:, columns] = jnp.zeros((WIDE - rest, SHARD), BF16)
        for k in range(length // 128):
            ids = jnp.broadcast_to(row_ref[0:1, k * 128 : (k + 1) * 128].astype(F32), (128, 128))
            seg_ref[PAD + k * 128 : PAD + (k + 1) * 128, :] = ids.T.astype(jnp.int32)
        seg_tail[...] = seg_ref[length : length + PAD, :]
        pl.semaphore_wait(barrier, len(greeted))
        for hop in range(3):
            small_copy(hop).start()
        seg_copy().start()
        load_rest().wait()
        gather.send_own(0)
        for k in range(1, AHEAD):
            gather.begin(k)

    def take_small():
        for hop in range(3):
            small_copy(hop).wait()
        seg_copy().wait()
        seg_ref[0:PAD, :] = jnp.where(part == 0, -1, seg_head[...])
        seg_ref[PAD + length :, :] = jnp.full((PAD, 128), -2, jnp.int32)

    def normalise():
        gain = jnp.concatenate([smalls[s, 6:7, :SHARD] for s in range(4)], axis=1)
        input_gain_ref[...] = gain
        for k in range(length // Q):
            rows = slice(k * Q, (k + 1) * Q)
            units = units_ref[rows, :].astype(F32)
            norm = lax.rsqrt(jnp.sum(units * units, axis=1, keepdims=True) * (1.0 / D) + epsilon)
            normed[rows, :] = (units * norm * gain).astype(BF16)

    def take_taps():
        mixer_gain = jnp.concatenate([smalls[s, 5:6, : INNER // 4] for s in range(4)], axis=1)
        gain_ref[...] = jnp.broadcast_to(mixer_gain, (8, INNER))
        whole = jnp.zeros((8, XBC), F32)
        heads = jnp.zeros((8, 128), F32)
        row, lane = iota((8, 128), 0), iota((8, 128), 1)
        own = HEADS // 4
        for s in range(4):
            padded = jnp.concatenate([smalls[s], jnp.zeros((8, XBC - SMALL_WIDTH), F32)], axis=1)
            padded = jnp.where(iota((8, XBC), 1) < XBC // 4, padded, 0.0)
            whole = whole + (pltpu.roll(padded, s * (XBC // 4), 1) if s else padded)
            inside = (lane >= s * own) & (lane < (s + 1) * own)
            for kind in range(3):
                moved = jnp.broadcast_to(smalls[s, 7:8, kind * 128 : (kind + 1) * 128], (8, 128))
                moved = pltpu.roll(moved, s * own, 1) if s else moved
                heads = jnp.where(inside & (row == kind), moved, heads)
        taps_ref[...] = whole
        heads_ref[...] = heads
        for block in range(STEPS + 1):
            taps[block] = whole[:, block * BLK : (block + 1) * BLK]

    def complete_out(k):
        gather_out.complete(k)
        store_out(k).start()

    def stage(lag, count=len(ORDER)):
        def decorate(body):
            k = step - lag

            @pl.when((k >= 0) & (k < count))
            def _():
                body(k)

        return decorate

    def advance(tick):
        def at(lag, body, first=0, count=len(ORDER)):
            k = tick - lag

            @pl.when((k >= first) & (k < count))
            def _():
                body(k)

        def complete(k):
            gather.complete(k)
            store(k).start()

        at(-AHEAD, gather.begin, AHEAD)
        at(0, gather.first)
        at(1, gather.second)
        at(2, gather.third)
        at(3, complete)
        at(OUT_BEGIN, gather_out.begin, 0, OUT_PIECES)
        at(OUT_BEGIN + 2, gather_out.first, 0, OUT_PIECES)
        at(OUT_BEGIN + 4, gather_out.second, 0, OUT_PIECES)
        at(OUT_BEGIN + 6, complete_out, 0, OUT_PIECES)

    tick = jnp.where(step < SCAN, step, 2 * step - SCAN)
    advance(tick)
    pl.when(step == 0)(take_small)
    pl.when(step == 1)(normalise)
    pl.when(step == 2)(take_taps)

    for s in range(4):

        @pl.when(step == 2 + s // 2)
        def _():
            columns = slice(s * SHARD, (s + 1) * SHARD)
            normed_t_ref[s] = normed[:, columns].astype(F32).T.astype(BF16)

    @stage(MULTIPLY)
    def _(k):
        low = dot_nt(normed[...], gathered[k]).astype(BF16)
        projected_ref[...] = low

        @pl.when(k < EDGES)
        def _():
            edge = low[length - 16 :, :].astype(F32)[8:, :]
            for half in range(2):
                columns = slice(half * BLK, (half + 1) * BLK)
                blocks[2 * k + half] = low[:, columns]
                edges[k, half] = edge[:, columns]
            edge_copy(k).start()

    @stage(SCAN - 1, EDGES)
    def _(k):
        edge_copy(k).wait()
        for half in range(2):
            columns = slice(half * BLK, (half + 1) * BLK)
            halos[k, half] = jnp.where(part == 0, 0.0, halos[k, half])
            halo_ref[:, columns] = halos[k, half]

    @pl.when(step == SCAN - 1)
    def _():
        keep = prepare(
            blocks.at[0], lambda rows: blocks[1, rows, :128], halos.at[0, 0], taps.at[STEPS], heads_ref,
            seg_ref, row_ref, b_ref, c_ref, dt_ref, run_ref, in_ref, ext, scores, run_t, b_t, enter, leave,
        )
        own_keep[...] = keep
        keeps[part] = keep
        for hop in range(PARTS - 1):
            keep_copy(hop).start()

    for half in range(2):

        @stage(SCAN, UNITS)
        def _(unit):
            columns = pl.ds(half * BLK, BLK)
            group = 2 * unit + half
            state = local_scan(
                group, blocks.at[2 + group], halos.at[1 + unit, half], taps.at[group], seg_ref,
                xs_ref.at[:, columns], y_ref.at[:, columns], c_ref, dt_ref, run_ref, ext, scores, run_t, b_t, enter, leave,
            )
            exchange.hold(unit, half, state)

        if half == 0:

            @pl.when(step >= SCAN)
            def _():
                advance(tick + 1)

    stage(SCAN, UNITS)(exchange.spread)

    @pl.when(step == SCAN + JOIN)
    def _():
        for hop in range(PARTS - 1):
            keep_copy(hop).wait()
        keep_ref[...] = keeps[...]

    @stage(SCAN + JOIN, UNITS)
    def _(unit):
        exchange.join(unit, kept_of(keeps, unit), True)

    @stage(SCAN + DONE, UNITS)
    def _(unit):
        state_ref[...] = exchange.finish(unit)

    @pl.when(step == SLOTS - 1)
    def _():
        for k in range(len(ORDER)):
            gather.drain(k)
            store(k).wait()
        for k in range(OUT_PIECES):
            gather_out.drain(k)
            store_out(k).wait()


def forward(in_matrix, out_matrix, units, seg_row, *small):
    length = units.shape[0]
    chunks = len(ORDER)
    whole = lambda *shape: pl.BlockSpec(shape, lambda t: (0,) * len(shape))
    once = lambda *shape: pl.BlockSpec(shape, lambda t: (0,) * len(shape), pipeline_mode=pl.Buffered(1))
    anywhere = pl.BlockSpec(memory_space=pl.ANY)
    chunk = lambda rows, lag: pl.BlockSpec((rows, WIDE), lambda t: (0, chunk_at(jnp.clip(t - lag, 0, chunks - 1))))
    unit = lambda lag: lambda t: (0, jnp.clip(t - lag, 0, UNITS - 1))
    out_specs, out_shape = front_outputs(length, unit(SCAN), unit(SCAN + DONE), UNIT)
    shape = jax.ShapeDtypeStruct
    return pl.pallas_call(
        forward_kernel,
        grid=(SLOTS,),
        in_specs=[
            anywhere,
            anywhere,
            once(length, D),
            once(1, length),
            *[once(*each.shape) for each in small],
        ],
        out_specs=[
            *out_specs,
            whole(PARTS, 8, 128),
            anywhere,
            anywhere,
            chunk(length, MULTIPLY),
            once(4, SHARD, length),
            pl.BlockSpec((PAD, WIDE), lambda t: (0, chunk_at(jnp.clip(t - SCAN + 1, 0, EDGES - 1)))),
            whole(8, XBC),
            whole(8, 128),
            whole(8, INNER),
            whole(1, D),
            whole(length + 2 * PAD, 128),
        ],
        out_shape=[
            *out_shape,
            shape((PARTS, 8, 128), F32),
            shape((WIDTH, D), BF16),
            shape((4, 2 * SHARD, D), BF16),
            shape((length, WIDTH), BF16),
            shape((4, SHARD, length), BF16),
            shape((PAD, WIDTH), F32),
            shape((8, XBC), F32),
            shape((8, 128), F32),
            shape((8, INNER), F32),
            shape((1, D), F32),
            shape((length + 2 * PAD, 128), jnp.int32),
        ],
        scratch_shapes=[
            *front_scratch(length),
            *exchange_scratch(),
            pltpu.VMEM((8, 128), F32),
            pltpu.VMEM((PARTS, 8, 128), F32),
            pltpu.SemaphoreType.DMA((PARTS - 1,)),
            pltpu.SemaphoreType.DMA((PARTS - 1,)),
            pltpu.VMEM((chunks, WIDE, D), BF16),
            *gather_sems(chunks),
            pltpu.SemaphoreType.DMA((chunks,)),
            pltpu.VMEM((OUT_PIECES, 4, 2 * SHARD, OUT_WIDE), BF16),
            *gather_sems(OUT_PIECES),
            pltpu.SemaphoreType.DMA((OUT_PIECES,)),
            pltpu.VMEM((length, D), BF16),
            pltpu.VMEM((2 * EDGES, length, BLK), BF16),
            pltpu.VMEM((STEPS + 1, 8, BLK), F32),
            pltpu.VMEM((8, SMALL_WIDTH), F32),
            pltpu.VMEM((4, 8, SMALL_WIDTH), F32),
            pltpu.VMEM((PAD, 128), jnp.int32),
            pltpu.VMEM((PAD, 128), jnp.int32),
            pltpu.VMEM((EDGES, 2, PAD, BLK), F32),
            pltpu.VMEM((EDGES, 2, PAD, BLK), F32),
            pltpu.SemaphoreType.DMA((4,)),
            pltpu.SemaphoreType.DMA((4,)),
            pltpu.SemaphoreType.DMA((EDGES,)),
            pltpu.SemaphoreType.DMA((EDGES,)),
        ],
        compiler_params=communicating(1),
        name="forward",
    )(in_matrix.T, out_matrix, units, seg_row, *small)


TAIL_GROUPS = 6
TAIL_STEPS = STEPS // TAIL_GROUPS


def tail_kernel(
    y_ref, xs_ref, gate_ref, incoming_ref, out_ref, c_ref, in_ref, heads_ref, gain_ref, g_ref, units_ref,
    mixer_ref, dproj_ref, dy_ref, dsin_ref, sums_ref, block_ref, stats_ref,
    full, dmix, squares, products, mixed, c_t,
):
    step = pl.program_id(0)
    length = y_ref.shape[0]
    unit = lax.rem(step, TAIL_STEPS)
    half = length // 2

    @pl.when(step == 0)
    def _():
        squares[...] = jnp.zeros_like(squares)
        products[...] = jnp.zeros_like(products)
        mixed[...] = jnp.zeros_like(mixed)
        for k in range(length // Q):
            rows = slice(k * Q, (k + 1) * Q)
            c_t[:, rows] = c_ref[rows, :].astype(F32).T.astype(BF16)

    def earlier(one):
        columns = slice(one * BLK, (one + 1) * BLK)
        group = TAIL_GROUPS * unit + one
        select = chosen(group)
        incoming = incoming_ref[:, columns]
        skip = widen(heads_ref[...], select)[2:3, :]
        for k in range(2):
            rows = slice(k * half, (k + 1) * half)
            y = y_ref[rows, columns].astype(F32)
            y = y + widen(in_ref[rows, :], select) * dot(c_ref[rows, :], incoming)
            y = y + skip * xs_ref[rows, columns].astype(F32)
            full[group, rows, :] = y
            gate = gate_ref[rows, columns].astype(F32)
            gated = y * gate * sigmoid(gate)
            d_mixer = dot_nt(g_ref[rows, :], out_ref[columns, :])
            dmix[group, rows, :] = d_mixer
            square = gated * gated
            product = gated * d_mixer * gain_ref[0:1, columns]
            squares[rows, :] += square[:, :128] + square[:, 128:]
            products[rows, :] += product[:, :128] + product[:, 128:]

    def later(one):
        columns = slice(one * BLK, (one + 1) * BLK)
        group = TAIL_GROUPS * unit + one
        select = chosen(group)
        gain = gain_ref[0:1, columns]
        d_gain = jnp.zeros((1, BLK), F32)
        d_skip = jnp.zeros((1, BLK), F32)
        d_state = jnp.zeros((STATE, BLK), F32)
        for k in range(2):
            rows = slice(k * half, (k + 1) * half)
            norm, mean = both(squares[rows, :]), both(products[rows, :])
            y = full[group, rows, :]
            d_mixer = dmix[group, rows, :]
            gate = gate_ref[rows, columns].astype(F32)
            sig = sigmoid(gate)
            silu = gate * sig
            unscaled = y * silu * norm
            value = unscaled * gain
            mixer_ref[columns, rows] = value.T.astype(BF16)
            mixed[rows, :] += dot(value.astype(BF16), out_ref[columns, :])
            d_gain = d_gain + jnp.sum(d_mixer * unscaled, axis=0, keepdims=True)
            d_gated = norm * (d_mixer * gain - unscaled * mean)
            dproj_ref[rows, columns] = (d_gated * y * (sig * (1.0 + gate * (1.0 - sig)))).astype(BF16)
            dy = (d_gated * silu).astype(BF16)
            dy_ref[rows, columns] = dy
            dy = dy.astype(F32)
            d_skip = d_skip + jnp.sum(dy * xs_ref[rows, columns].astype(F32), axis=0, keepdims=True)
            d_state = d_state + dot(c_t[:, rows], (dy * widen(in_ref[rows, :], select)).astype(BF16))
        dsin_ref[:, columns] = d_state.astype(BF16)
        sums_ref[:, columns] = jnp.concatenate([d_gain, d_skip, jnp.zeros((6, BLK), F32)], axis=0)

    @pl.when(step < TAIL_STEPS)
    def _():
        for one in range(TAIL_GROUPS):
            earlier(one)

    @pl.when(step == TAIL_STEPS)
    def _():
        norm = lax.rsqrt(jnp.sum(squares[...], axis=1, keepdims=True) * (1.0 / INNER) + epsilon)
        mean = norm * jnp.sum(products[...], axis=1, keepdims=True) * (1.0 / INNER)
        squares[...] = jnp.broadcast_to(norm, squares.shape)
        products[...] = jnp.broadcast_to(mean, products.shape)

    @pl.when(step >= TAIL_STEPS)
    def _():
        for one in range(TAIL_GROUPS):
            later(one)

    @pl.when(step == 2 * TAIL_STEPS - 1)
    def _():
        total = units_ref[...].astype(F32) + mixed[...]
        block_ref[...] = total.astype(BF16)
        first = jnp.sum(total * total, axis=0, keepdims=True)
        second = jnp.sum(mixed[...] * mixed[...], axis=0, keepdims=True)
        stats_ref[...] = jnp.concatenate([first, second, jnp.zeros((6, D), F32)], axis=0)


def tail(y, xs, projected, incoming, out_whole, c_rows, entering, heads, gain, cot, units):
    length = y.shape[0]
    unit = lambda i: lax.rem(i, TAIL_STEPS)
    second = lambda i: jnp.maximum(i - TAIL_STEPS, 0)
    early = lambda rows: pl.BlockSpec((rows, TAIL_GROUPS * BLK), lambda i: (0, jnp.minimum(i, TAIL_STEPS - 1)))
    late = lambda rows: pl.BlockSpec((rows, TAIL_GROUPS * BLK), lambda i: (0, second(i)))
    each = lambda rows: pl.BlockSpec((rows, TAIL_GROUPS * BLK), lambda i: (0, unit(i)))
    whole = lambda *shape: pl.BlockSpec(shape, lambda i: (0,) * len(shape))
    return pl.pallas_call(
        tail_kernel,
        grid=(2 * TAIL_STEPS,),
        in_specs=[
            early(length),
            each(length),
            each(length),
            early(STATE),
            pl.BlockSpec((TAIL_GROUPS * BLK, D), lambda i: (unit(i), 0)),
            whole(length, 128),
            whole(length, 128),
            whole(8, 128),
            each(8),
            whole(length, D),
            whole(length, D),
        ],
        out_specs=[
            pl.BlockSpec((TAIL_GROUPS * BLK, length), lambda i: (second(i), 0)),
            late(length),
            late(length),
            pl.BlockSpec((STATE, TAIL_GROUPS * BLK), lambda i: (0, second(i))),
            late(8),
            whole(length, D),
            whole(8, D),
        ],
        out_shape=[
            jax.ShapeDtypeStruct((INNER, length), BF16),
            jax.ShapeDtypeStruct((length, WIDTH), BF16),
            jax.ShapeDtypeStruct((length, INNER), BF16),
            jax.ShapeDtypeStruct((STATE, INNER), BF16),
            jax.ShapeDtypeStruct((8, INNER), F32),
            jax.ShapeDtypeStruct((length, D), BF16),
            jax.ShapeDtypeStruct((8, D), F32),
        ],
        scratch_shapes=[
            pltpu.VMEM((STEPS, length, BLK), F32),
            pltpu.VMEM((STEPS, length, BLK), F32),
            pltpu.VMEM((length, 128), F32),
            pltpu.VMEM((length, 128), F32),
            pltpu.VMEM((length, D), F32),
            pltpu.VMEM((128, length), BF16),
        ],
        compiler_params=pltpu.CompilerParams(vmem_limit_bytes=VMEM_LIMIT),
        cost_estimate=pl.CostEstimate(
            flops=12 * 10**9, bytes_accessed=50 * 10**6, transcendentals=4 * 10**6
        ),
        name="tail",
    )(y, xs, projected, incoming, out_whole, c_rows, entering, heads, gain, cot, units)


def back_steps(step, given, scratch, write, write_halo, write_taps, write_heads):
    (
        x_ref, dtraw_ref, halo_ref, taps_ref, heads_ref, seg_ref, row_ref, b_ref, c_ref, dt_ref, run_ref, dy_ref, sin_ref, dout_ref,
    ) = given
    (
        ext, pre, dact, dbuf, scores, dscores, run_t, b_t, c_t, enter, leave, d_b, d_c, suffix, prefix, d_dt, fixed, states,
    ) = scratch
    length = x_ref.shape[0]
    chunks = length // Q

    @pl.when(step == 0)
    def _():
        for k in range(chunks):
            rows = slice(k * Q, (k + 1) * Q)
            b_rows, c_rows = b_ref[rows, :], c_ref[rows, :]
            b_t[:, rows] = b_rows.astype(F32).T.astype(BF16)
            c_t[:, rows] = c_rows.astype(F32).T.astype(BF16)
            scores[rows, :] = masked_scores(seg_ref, row_ref, b_rows, c_rows, k)
            running = run_ref[rows, :]
            run_t[k] = running.T
            carry, tail = chunk_flags(seg_ref, k)
            enter[rows, :] = jnp.exp(running) * carry
            leave[rows, :] = jnp.exp(running[Q - 1 : Q, :] - running) * tail
        for each in (dscores, d_b, d_c, suffix, prefix, d_dt, fixed):
            each[...] = jnp.zeros_like(each)
        dbuf[0:PAD, :] = jnp.zeros((PAD, BLK), F32)
        dbuf[PAD + length :, :] = jnp.zeros((PAD, BLK), F32)

    @pl.when(step <= STEPS)
    def _():
        ext[0:PAD, :] = halo_ref[...]
        ext[PAD:, :] = x_ref[...].astype(F32)
        for k in range(chunks):
            pre[k * Q : (k + 1) * Q, :] = conv_rows(ext, seg_ref, taps_ref, k * Q, Q)

    @pl.when(step < STEPS)
    def _():
        select = chosen(step)
        gather = chosen_back(step)
        skip = widen(heads_ref[...], select)[2:3, :]
        state = sin_ref[...].astype(F32)
        for k in range(chunks):
            rows = slice(k * Q, (k + 1) * Q)
            states[k] = state
            if k + 1 < chunks:
                total = pre[rows, :]
                scaled = total * sigmoid(total) * widen(dt_ref[rows, :], select)
                weighted = (scaled.astype(BF16).astype(F32) * widen(leave[rows, :], select)).astype(BF16)
                last = widen(enter[rows.stop - 8 : rows.stop, :], select)[7:8, :]
                state = last * state + dot(b_t[:, rows], weighted)
        d_state = dout_ref[...].astype(F32)
        for k in range(chunks - 1, -1, -1):
            rows = slice(k * Q, (k + 1) * Q)
            total = pre[rows, :]
            values = total * sigmoid(total)
            step_size = widen(dt_ref[rows, :], select)
            entering = widen(enter[rows, :], select)
            leaving = widen(leave[rows, :], select)
            scaled = (values * step_size).astype(BF16)
            scaled_wide = scaled.astype(F32)
            dy = dy_ref[rows, :]
            dy_wide = dy.astype(F32)
            before = states[k]
            before_low = before.astype(BF16)
            d_low = d_state.astype(BF16)
            running = pltpu.roll(run_ref[rows, :], lax.rem(128 - step * GROUP, 128), 1)
            insides, backs = [], []
            d_score = dscores[rows, :]
            for pair in range(2):
                lanes = slice(pair * 128, (pair + 1) * 128)
                mixing, turned, decays = [], [], []
                for one in range(2):
                    head = 2 * pair + one
                    gap = running[:, head : head + 1] - run_t[k, pl.ds(step * GROUP + head, 1), :]
                    decay = jnp.exp(jnp.minimum(gap, 0.0))
                    mixed = decay * scores[rows, :]
                    decays.append(decay)
                    mixing.append(mixed.astype(BF16))
                    turned.append(mixed.T.astype(BF16))
                spread = halves(scaled[:, lanes])
                insides.append(dot(jnp.concatenate(mixing, axis=1), spread))
                backs.append(dot(jnp.concatenate(turned, axis=1), halves(dy[:, lanes])))
                products = dot_nt(dy[:, lanes], spread)
                d_score = d_score + decays[0] * products[:, :Q] + decays[1] * products[:, Q:]
            dscores[rows, :] = d_score
            inside = jnp.concatenate(insides, axis=1) + entering * dot(c_ref[rows, :], before_low)
            back_inside = jnp.concatenate(backs, axis=1)
            back_state = leaving * dot(b_ref[rows, :], d_low)
            high, low = in_two(dy_wide * inside - scaled_wide * back_inside)
            suffix[rows, :] += dot(high, gather) + dot(low, gather)
            prefix[rows, :] += dot((scaled_wide * back_state).astype(BF16), gather)
            back = back_inside + back_state
            d_dt[rows, :] += dot((values * back).astype(BF16), gather)
            entered = (dy_wide * entering).astype(BF16)
            d_c[rows, :] += dot_nt(entered, before_low)
            d_b[rows, :] += dot_nt((scaled_wide * leaving).astype(BF16), d_low)
            kept = entering[Q - 1 : Q, :]
            through = jnp.sum(before * d_state, axis=0, keepdims=True) * kept
            high, low = in_two(jnp.broadcast_to(through, (8, BLK)))
            fixed[k * 8 : (k + 1) * 8, :] += dot(high, gather) + dot(low, gather)
            d_state = kept * d_state + dot(c_t[:, rows], entered)
            dact[rows, :] = back * step_size + skip * dy_wide

    @pl.when(step == STEPS)
    def _():
        for k in range(chunks):
            rows = slice(k * Q, (k + 1) * Q)
            own = seg_ref[PAD + k * Q : PAD + (k + 1) * Q, :]
            keep = (own == row_ref[0:1, rows]) & (iota((Q, Q), 1) <= iota((Q, Q), 0))
            d_score = jnp.where(keep, dscores[rows, :], 0.0)
            dact[rows, STATE:] = d_c[rows, :] + dot(d_score.astype(BF16), b_ref[rows, :])
            dact[rows, :STATE] = d_b[rows, :] + dot(d_score.T.astype(BF16), c_ref[rows, :])

    @pl.when(step <= STEPS)
    def _():
        sums = [jnp.zeros((1, BLK), F32) for _ in range(CONV + 1)]
        for k in range(chunks):
            rows = slice(k * Q, (k + 1) * Q)
            total = pre[rows, :]
            sig = sigmoid(total)
            d_conv = dact[rows, :] * (sig * (1.0 + total * (1.0 - sig)))
            dbuf[PAD + k * Q : PAD + (k + 1) * Q, :] = d_conv
            sums[4] = sums[4] + jnp.sum(d_conv, axis=0, keepdims=True)
            own = seg_ref[PAD + k * Q : PAD + (k + 1) * Q, :]
            for shift in range(CONV):
                at = PAD + k * Q - shift
                term = d_conv * ext[at : at + Q, :]
                if shift:
                    term = jnp.where(both(seg_ref[at : at + Q, :] == own), term, 0.0)
                sums[3 - shift] = sums[3 - shift] + jnp.sum(term, axis=0, keepdims=True)
        write_taps(jnp.concatenate(sums + [jnp.zeros((3, BLK), F32)], axis=0))

        def returned(at, rows):
            own = seg_ref[at : at + rows, :]
            result = taps_ref[3:4, :] * dbuf[at : at + rows, :]
            for shift in range(1, CONV):
                same = both(seg_ref[at + shift : at + shift + rows, :] == own)
                result = result + jnp.where(
                    same, taps_ref[3 - shift : 4 - shift, :] * dbuf[at + shift : at + shift + rows, :], 0.0
                )
            return result

        write_halo(returned(0, PAD))
        for k in range(chunks):
            write(slice(k * Q, (k + 1) * Q), returned(PAD + k * Q, Q).astype(BF16))

    @pl.when(step == STEPS + 1)
    def _():
        lower = (iota((Q, Q), 1) < iota((Q, Q), 0)).astype(F32)
        upper = (iota((Q, Q), 1) >= iota((Q, Q), 0)).astype(F32)
        lane = iota((Q, 128), 1)
        rate = jnp.exp(heads_ref[1:2, :])
        bias_sum = jnp.zeros((1, 128), F32)
        decay_sum = jnp.zeros((1, 128), F32)
        for k in range(chunks):
            rows = slice(k * Q, (k + 1) * Q)
            d_log = jnp.dot(upper, suffix[rows, :], precision=HIGHEST, preferred_element_type=F32)
            d_log = d_log + jnp.dot(lower, prefix[rows, :], precision=HIGHEST, preferred_element_type=F32)
            d_log = d_log + fixed[k * 8 : k * 8 + 1, :]
            raw = jnp.where(lane < HEADS, dtraw_ref[rows, :128].astype(F32), 0.0) + heads_ref[0:1, :]
            d_raw = jnp.where(lane < HEADS, (d_dt[rows, :] - rate * d_log) * sigmoid(raw), 0.0)
            bias_sum = bias_sum + jnp.sum(d_raw, axis=0, keepdims=True)
            decay_sum = decay_sum - jnp.sum(d_log * dt_ref[rows, :] * rate, axis=0, keepdims=True)
            write(rows, jnp.concatenate([d_raw, jnp.zeros_like(d_raw)], axis=1).astype(BF16))
        write_heads(jnp.concatenate([bias_sum, decay_sum, jnp.zeros((6, 128), F32)], axis=0))


def back_kernel(*refs):
    given, (_, dproj_ref, dhalo_ref, dtaps_ref, dheads_ref), scratch = refs[:14], refs[14:19], refs[19:]

    def write(rows, value):
        dproj_ref[rows, :] = value

    def write_halo(value):
        dhalo_ref[...] = value

    def write_taps(value):
        dtaps_ref[...] = value

    def write_heads(value):
        dheads_ref[...] = value

    back_steps(pl.program_id(0), given, scratch, write, write_halo, write_taps, write_heads)


def back_scratch(length):
    return [
        pltpu.VMEM((length + PAD, BLK), F32),
        pltpu.VMEM((length, BLK), F32),
        pltpu.VMEM((length, BLK), F32),
        pltpu.VMEM((length + 2 * PAD, BLK), F32),
        pltpu.VMEM((length, Q), F32),
        pltpu.VMEM((length, Q), F32),
        pltpu.VMEM((length // Q, 128, Q), F32),
        pltpu.VMEM((128, length), BF16),
        pltpu.VMEM((128, length), BF16),
        *[pltpu.VMEM((length, 128), F32) for _ in range(7)],
        pltpu.VMEM((8 * (length // Q), 128), F32),
        pltpu.VMEM((length // Q, STATE, BLK), F32),
    ]


def back_inputs(length, late=0):
    whole = lambda *shape: pl.BlockSpec(shape, lambda j: (0,) * len(shape))
    upto = lambda last, first=0: lambda j: (0, first + jnp.clip(j - late, 0, last))
    return [
        pl.BlockSpec((length, BLK), upto(STEPS, STEPS)),
        pl.BlockSpec((length, BLK), lambda j: (0, 2 * STEPS + 1)),
        pl.BlockSpec((PAD, BLK), upto(STEPS, STEPS)),
        pl.BlockSpec((8, BLK), upto(STEPS)),
        whole(8, 128),
        whole(length + 2 * PAD, 128),
        whole(1, length),
        whole(length, 128),
        whole(length, 128),
        whole(length, 128),
        whole(length, 128),
        pl.BlockSpec((length, BLK), upto(STEPS - 1)),
        pl.BlockSpec((STATE, BLK), upto(STEPS - 1)),
        whole(STATE, INNER) if late else pl.BlockSpec((STATE, BLK), upto(STEPS - 1)),
    ]


def back(given, dproj):
    length = dproj.shape[0]
    upto = lambda last, first=0: lambda j: (0, first + jnp.minimum(j, last))
    return pl.pallas_call(
        back_kernel,
        grid=(STEPS + 2,),
        in_specs=[*back_inputs(length), pl.BlockSpec(memory_space=pl.ANY)],
        out_specs=[
            pl.BlockSpec((length, BLK), lambda j: (0, STEPS + j)),
            pl.BlockSpec((PAD, BLK), upto(STEPS)),
            pl.BlockSpec((8, BLK), upto(STEPS)),
            pl.BlockSpec((8, 128), lambda j: (0, 0)),
        ],
        out_shape=[
            jax.ShapeDtypeStruct((length, WIDTH), BF16),
            jax.ShapeDtypeStruct((PAD, XBC), F32),
            jax.ShapeDtypeStruct((8, XBC), F32),
            jax.ShapeDtypeStruct((8, 128), F32),
        ],
        scratch_shapes=back_scratch(length),
        input_output_aliases={14: 0},
        compiler_params=pltpu.CompilerParams(vmem_limit_bytes=VMEM_LIMIT),
        name="back",
    )(*given, dproj)


OUT_CHUNKS = 2 * D // WIDE
GATE_CHUNKS = INNER // WIDE
IN_CHUNKS = WIDTH // WIDE
CHUNKS = OUT_CHUNKS + IN_CHUNKS
LAGS = 8
RING = 8
LATE = 3
LAST_WIDE = 384


def small_sums(taps, columns, input_gain, heads, stats):
    fill = lambda width: jnp.zeros((1, width), F32)
    squares = [jnp.broadcast_to(jnp.sum(stats[i : i + 1], axis=1, keepdims=True), (1, 128)) for i in range(2)]
    return jnp.concatenate(
        [
            taps[:5],
            jnp.concatenate([columns[0:1], fill(XBC - INNER)], axis=1),
            jnp.concatenate([columns[1:2], fill(XBC - INNER)], axis=1),
            jnp.concatenate([input_gain, heads[0:1], heads[1:2], *squares, fill(XBC - D - 512)], axis=1),
        ],
        axis=0,
    )


def finish_kernel(*refs):
    given, refs = refs[:14], refs[14:]
    lhs_in, lhs_out, gate_ref, weight_ref, cot_ref, units_ref, gain_ref, columns_ref, stats_ref, kept_ref = refs[:10]
    din_ref, dout_ref, input_grad_ref, total_ref = refs[10:14]
    scratch, refs = refs[14:32], refs[32:]
    exchange, outgoing, refs = Exchange(*refs[:5]), refs[5], refs[6:]
    grads, edges, halos, taps, heads, d_normed = refs[:6]
    own, core_send, core_recv, y_recv, x_recv, z_recv, w_recv, final, small_send, small_recv = refs[6:16]
    send_sems, recv_sems, small_send_sems, small_recv_sems, edge_sends, edge_arrivals = refs[16:]
    step = pl.program_id(0)
    length = cot_ref.shape[0]
    shard, part = lax.axis_index("fsdp"), lax.axis_index("ctx")
    core, y = lax.rem(shard, 2), shard // 2
    x, z = lax.rem(part, 2), part // 2
    near, far = lax.rem(z, 2), z // 2
    peers = (
        {"fsdp": flipped(shard, 1)},
        {"fsdp": flipped(shard, 2)},
        {"ctx": flipped(part, 1)},
        {"ctx": flipped(part, 2)},
        {"ctx": flipped(part, 4)},
    )
    preceding = lax.rem(part + PARTS - 1, PARTS)

    def ring(k):
        return lax.rem(k, RING)

    class Sent:
        def __init__(self, stage, k, source, target, peer):
            self.given = stage, k, source, target, peer

        def act(self, name):
            stage, k, source, target, peer = self.given
            for last in range(2):

                @pl.when((k == CHUNKS - 1) == bool(last))
                def _():
                    ends = source, target
                    if last:
                        columns = (*[slice(None)] * (len(source.shape) - 1), pl.ds(0, LAST_WIDE))
                        ends = source.at[columns], target.at[columns]
                    copy = remote(*ends, send_sems.at[stage, k], recv_sems.at[stage, k], peers[peer])
                    getattr(copy, name)()

        def start(self):
            self.act("start")

        def wait_send(self):
            self.act("wait_send")

        def wait_recv(self):
            self.act("wait_recv")

    sent = Sent

    copies = (
        lambda k: sent(0, k, core_send.at[lax.rem(k, 2)], core_recv.at[ring(k)], 0),
        lambda k: sent(1, k, core_recv.at[ring(k), 1 - y], y_recv.at[ring(k)], 1),
        lambda k: sent(2, k, y_recv.at[ring(k), 1 - x], x_recv.at[ring(k)], 2),
        lambda k: sent(3, k, x_recv.at[ring(k), 1 - near], z_recv.at[ring(k)], 3),
        lambda k: sent(4, k, z_recv.at[ring(k), 1 - far], w_recv.at[ring(k)], 4),
        lambda k: sent(5, k, final.at[ring(k), x, near, far], final.at[ring(k), x, near, far], 4),
        lambda k: sent(6, k, final.at[ring(k), x, near], final.at[ring(k), x, near], 3),
        lambda k: sent(7, k, final.at[ring(k), x], final.at[ring(k), x], 2),
    )
    arrivals = copies[:5] + (
        lambda k: sent(5, k, final.at[ring(k), x, near, 1 - far], final.at[ring(k), x, near, 1 - far], 4),
        lambda k: sent(6, k, final.at[ring(k), x, 1 - near], final.at[ring(k), x, 1 - near], 3),
        lambda k: sent(7, k, final.at[ring(k), 1 - x], final.at[ring(k), 1 - x], 2),
    )

    def small_copy(stage):
        return remote(
            small_send.at[stage], small_recv.at[stage], small_send_sems.at[stage], small_recv_sems.at[stage], peers[stage]
        )

    def edge_copy(block):
        return remote(
            edges.at[block], halos.at[block], edge_sends.at[block], edge_arrivals.at[block], {"ctx": preceding}
        )

    @pl.when(step == 0)
    def _():
        exchange.greet(peers[0], peers[1])
        for group in range(STEPS):
            exchange.hold(group // 2, group % 2, given[13][:, group * BLK : (group + 1) * BLK])
            if group % 2:
                exchange.spread(group // 2)
        d_normed[...] = jnp.zeros_like(d_normed)

    def partial(lhs_of, rhs):
        for row in range(2):
            value = dot(lhs_of(2 * row + 1 - core), rhs).astype(BF16)
            core_send[lax.rem(step, 2), row] = value.reshape(2, 2, 2, PIECE, WIDE)
        copies[0](step).start()
        for row in range(2):
            own[row] = dot(lhs_of(2 * row + core), rhs).reshape(2, 2, 2, PIECE, WIDE)

    def in_chunk(rhs):
        partial(lambda s: lhs_in[s], rhs)
        d_normed[...] += dot(rhs, weight_ref[...])

    @pl.when(step < OUT_CHUNKS)
    def _():
        columns = lax.rem(step, D // WIDE) * WIDE
        rhs = cot_ref[:, pl.ds(pl.multiple_of(columns, WIDE), WIDE)]
        partial(lambda s: lhs_out[s, step // (D // WIDE)], rhs)

    @pl.when((step >= OUT_CHUNKS) & (step < OUT_CHUNKS + GATE_CHUNKS))
    def _():
        in_chunk(gate_ref[...])

    @pl.when((step >= OUT_CHUNKS + GATE_CHUNKS) & (step < CHUNKS))
    def _():
        first = 2 * (step - OUT_CHUNKS - GATE_CHUNKS)
        for done in (first, first + 1):

            @pl.when(done <= STEPS)
            def _():
                edge_copy(done).wait()
                tail = slice(length - 16, length)
                more = jnp.where(part == PARTS - 1, 0.0, halos[done])
                more = jnp.concatenate([jnp.zeros_like(more), more], axis=0)
                grads[done, tail, :] = (grads[done, tail, :].astype(F32) + more).astype(BF16)

        in_chunk(jnp.concatenate([grads[first], grads[first + 1]], axis=1))

    for half in range(2):

        @pl.when(step == 1 + half)
        def _():
            for unit in range(half * UNITS // 2, (half + 1) * UNITS // 2):
                exchange.join(unit, kept_of(kept_ref, unit), False)

    block = step - LATE

    def write(rows, value):
        grads[block, rows, :] = value

    def write_halo(value):
        edges[block] = value
        edge_copy(block).start()

    def write_taps(value):
        taps[block] = value

    def write_heads(value):
        heads[...] = value

    @pl.when((block >= 0) & (block < STEPS) & (lax.rem(block, 2) == 0))
    def _():
        both_groups = exchange.finish(block // 2)
        outgoing[0] = both_groups[:, :BLK]
        outgoing[1] = both_groups[:, BLK:]

    @pl.when(block >= 0)
    def _():
        back_steps(block, (*given[:13], outgoing.at[lax.rem(block, 2)]), scratch, write, write_halo, write_taps, write_heads)

    @pl.when(step < CHUNKS)
    def _():
        arrivals[0](step).wait_recv()
        for row in (1 - y, y):
            core_recv[ring(step), row] = (own[row] + core_recv[ring(step), row].astype(F32)).astype(BF16)
        copies[1](step).start()

    def stage(lag):
        def decorate(body):
            k = step - lag

            @pl.when((k >= 0) & (k < CHUNKS))
            def _():
                body(k, ring(k))

        return decorate

    def summed(a, b):
        return (a.astype(F32) + b.astype(F32)).astype(BF16)

    @stage(1)
    def _(k, at):
        arrivals[1](k).wait_recv()
        y_recv[at] = summed(y_recv[at], core_recv[at, y])
        copies[2](k).start()
        copies[0](k).wait_send()

    @stage(2)
    def _(k, at):
        arrivals[2](k).wait_recv()
        x_recv[at] = summed(x_recv[at], y_recv[at, x])
        copies[3](k).start()

    @stage(3)
    def _(k, at):
        arrivals[3](k).wait_recv()
        z_recv[at] = summed(z_recv[at], x_recv[at, near])
        copies[4](k).start()
        copies[1](k).wait_send()

    @stage(4)
    def _(k, at):
        arrivals[4](k).wait_recv()
        final[at, x, near, far] = summed(w_recv[at], z_recv[at, far])
        copies[5](k).start()
        copies[2](k).wait_send()

    @stage(5)
    def _(k, at):
        arrivals[5](k).wait_recv()
        copies[6](k).start()
        copies[3](k).wait_send()

    @stage(6)
    def _(k, at):
        arrivals[6](k).wait_recv()
        copies[7](k).start()
        copies[4](k).wait_send()

    @stage(7)
    def _(k, at):
        arrivals[7](k).wait_recv()
        for one in (5, 6, 7):
            copies[one](k).wait_send()
        whole = final[at].reshape(SHARD, WIDE)

        @pl.when(k < OUT_CHUNKS)
        def _():
            dout_ref[...] = whole

        @pl.when(k >= OUT_CHUNKS)
        def _():
            din_ref[...] = whole.astype(F32).T.astype(BF16)

    @pl.when(step == CHUNKS)
    def _():
        input_gain = jnp.zeros((1, D), F32)
        for k in range(length // Q):
            rows = slice(k * Q, (k + 1) * Q)
            units = units_ref[rows, :].astype(F32)
            norm = lax.rsqrt(jnp.sum(units * units, axis=1, keepdims=True) * (1.0 / D) + epsilon)
            base = units * norm
            grad = d_normed[rows, :]
            input_gain = input_gain + jnp.sum(grad * base, axis=0, keepdims=True)
            scaled = grad * gain_ref[0:1, :]
            mean = jnp.sum(scaled * base, axis=1, keepdims=True) * (1.0 / D)
            input_grad_ref[rows, :] = (cot_ref[rows, :].astype(F32) + norm * (scaled - base * mean)).astype(BF16)
        whole = jnp.concatenate([taps[one] for one in range(STEPS + 1)], axis=1)
        small_send[0] = small_sums(whole, columns_ref[...], input_gain, heads[...], stats_ref[...])
        small_copy(0).start()

    for stage_of_small in range(5):

        @pl.when(step == CHUNKS + 1 + stage_of_small)
        def _():
            small_copy(stage_of_small).wait()
            total = small_send[stage_of_small] + small_recv[stage_of_small]
            if stage_of_small < 4:
                small_send[stage_of_small + 1] = total
                small_copy(stage_of_small + 1).start()
            else:
                total_ref[...] = total


def finish(given, normed_t, mixer_t, dproj, w_turned, cot, units, input_gain, column_sums, stats, kept):
    length = cot.shape[0]
    per_half = D // WIDE
    once = pl.Buffered(1)
    whole = lambda *shape: pl.BlockSpec(shape, lambda t: (0,) * len(shape), pipeline_mode=once)
    in_chunk = lambda t: jnp.clip(t - OUT_CHUNKS, 0, IN_CHUNKS - 1)

    def out_block(t):
        k = jnp.clip(t - LAGS + 1, 0, OUT_CHUNKS - 1)
        return (k // per_half, lax.rem(k, per_half))

    slots = lambda *shape: pltpu.VMEM((RING, *shape, PIECE, WIDE), BF16)
    return pl.pallas_call(
        finish_kernel,
        grid=(CHUNKS + LAGS - 1,),
        in_specs=[
            *back_inputs(length, LATE),
            whole(4, SHARD, length),
            whole(4, 2, SHARD, length),
            pl.BlockSpec((length, WIDE), lambda t: (0, jnp.minimum(in_chunk(t), GATE_CHUNKS - 1))),
            pl.BlockSpec((WIDE, D), lambda t: (in_chunk(t), 0)),
            whole(length, D),
            whole(length, D),
            whole(1, D),
            whole(8, INNER),
            whole(8, D),
            whole(PARTS, 8, 128),
        ],
        out_specs=[
            pl.BlockSpec((WIDE, SHARD), lambda t: (in_chunk(t - LAGS + 1), 0)),
            pl.BlockSpec((SHARD, WIDE), out_block),
            pl.BlockSpec((length, D), lambda t: (0, 0)),
            pl.BlockSpec((8, XBC), lambda t: (0, 0)),
        ],
        out_shape=[
            jax.ShapeDtypeStruct((PROJ, SHARD), BF16),
            jax.ShapeDtypeStruct((2 * SHARD, D), BF16),
            jax.ShapeDtypeStruct((length, D), BF16),
            jax.ShapeDtypeStruct((8, XBC), F32),
        ],
        scratch_shapes=[
            *back_scratch(length),
            *exchange_scratch(),
            pltpu.VMEM((2, STATE, BLK), BF16),
            pltpu.VMEM((STEPS + 2, length, BLK), BF16),
            pltpu.VMEM((STEPS + 1, PAD, BLK), F32),
            pltpu.VMEM((STEPS + 1, PAD, BLK), F32),
            pltpu.VMEM((STEPS + 1, 8, BLK), F32),
            pltpu.VMEM((8, 128), F32),
            pltpu.VMEM((length, D), F32),
            pltpu.VMEM((2, 2, 2, 2, PIECE, WIDE), F32),
            pltpu.VMEM((2, 2, 2, 2, 2, PIECE, WIDE), BF16),
            slots(2, 2, 2, 2),
            slots(2, 2, 2),
            slots(2, 2),
            slots(2),
            slots(),
            slots(2, 2, 2),
            pltpu.VMEM((5, 8, XBC), F32),
            pltpu.VMEM((5, 8, XBC), F32),
            pltpu.SemaphoreType.DMA((8, CHUNKS)),
            pltpu.SemaphoreType.DMA((8, CHUNKS)),
            pltpu.SemaphoreType.DMA((5,)),
            pltpu.SemaphoreType.DMA((5,)),
            pltpu.SemaphoreType.DMA((STEPS + 1,)),
            pltpu.SemaphoreType.DMA((STEPS + 1,)),
        ],
        compiler_params=communicating(0),
        name="finish",
    )(*given, normed_t, mixer_t, dproj, w_turned, cot, units, input_gain, column_sums, stats, kept)


def settle_kernel(din_ref, dout_ref, total_ref, *outs, entries):
    (
        din_out, dout_out, taps_out, bias_out, step_bias_out, decay_out, skip_out, gain_out, input_gain_out, rms_out,
    ) = outs
    din_out[...] = din_ref[...].astype(F32)
    dout_out[...] = dout_ref[...].astype(F32)

    @pl.when(pl.program_id(0) == 0)
    def _():
        shard = lax.axis_index("fsdp")
        own = HEADS // 4
        width = XBC // 4

        def mine(pieces):
            result = pieces[0]
            for s in range(1, 4):
                result = jnp.where(shard == s, pieces[s], result)
            return result

        def flat(ref, row):
            ref[...] = row.reshape(ref.shape)

        total = total_ref[...]
        columns = mine([pltpu.roll(total, (XBC - s * width) % XBC, 1) if s else total for s in range(4)])
        taps_out[...] = columns[:4, :width]
        flat(bias_out, columns[4:5, :width])

        def heads(row):
            rows = jnp.broadcast_to(row, (8, 128))
            rows = mine([pltpu.roll(rows, (128 - s * own) % 128, 1) if s else rows for s in range(4)])
            return rows[:1, :own]

        flat(step_bias_out, heads(total[7:8, D : D + 128]))
        flat(decay_out, heads(total[7:8, D + 128 : D + 256]))
        skip = jnp.zeros((8, 128), F32)
        for group in range(STEPS):
            high, low = in_two(jnp.broadcast_to(total[6:7, group * BLK : (group + 1) * BLK], (8, BLK)))
            skip = skip + dot(high, chosen_back(group)) + dot(low, chosen_back(group))
        flat(skip_out, heads(skip[:1]))
        flat(gain_out, mine([total[5:6, s * (INNER // 4) : (s + 1) * (INNER // 4)] for s in range(4)]))
        flat(input_gain_out, mine([total[7:8, s * SHARD : (s + 1) * SHARD] for s in range(4)]))
        squares = jnp.concatenate([total[7:8, D + 256 : D + 257], total[7:8, D + 384 : D + 385]], axis=1)
        flat(rms_out, jnp.sqrt(squares * (1.0 / entries)))


def settle(d_in, d_out, total, entries):
    steps = 3
    shapes = [
        (4, XBC // 4),
        (XBC // 4,),
        (HEADS // 4,),
        (HEADS // 4,),
        (HEADS // 4,),
        (INNER // 4,),
        (SHARD,),
        (2,),
    ]
    rows = -(-PROJ // steps // 16) * 16
    whole = lambda shape: pl.BlockSpec(shape, lambda i: (0,) * len(shape))
    blocks = [
        pl.BlockSpec((rows, SHARD), lambda i: (i, 0)),
        pl.BlockSpec((2 * SHARD // steps, D), lambda i: (i, 0)),
    ]
    d_in, d_out, taps, *rest = pl.pallas_call(
        functools.partial(settle_kernel, entries=entries),
        grid=(steps,),
        in_specs=[*blocks, whole((8, XBC))],
        out_specs=[*blocks, *[whole(shape) for shape in shapes]],
        out_shape=[
            jax.ShapeDtypeStruct((PROJ, SHARD), F32),
            jax.ShapeDtypeStruct((2 * SHARD, D), F32),
            *[jax.ShapeDtypeStruct(shape, F32) for shape in shapes],
        ],
        compiler_params=pltpu.CompilerParams(vmem_limit_bytes=VMEM_LIMIT),
        name="settle",
    )(d_in, d_out, total)
    return (d_in.T, d_out, taps.T, *[each.reshape(-1) for each in rest])


def passed_along(block, axis, distance):
    devices = range(lax.axis_size(axis))
    route = [(i - distance, i) for i in devices if i - distance in devices]
    return lax.ppermute(block, axis, route)


def pack_small(conv_taps, conv_bias, dt_bias, decay_log, skip_scale, mixer_gain, input_gain):
    width = conv_bias.shape[0]

    def line(*parts):
        flat = jnp.concatenate(parts)
        return jnp.pad(flat, (0, width - flat.shape[0]))[None]

    rows = jnp.concatenate(
        [
            conv_taps.T,
            conv_bias[None],
            line(mixer_gain),
            line(input_gain),
            line(dt_bias, decay_log, skip_scale),
        ],
        axis=0,
    )
    return jnp.pad(rows.astype(F32), ((0, 0), (0, SMALL_WIDTH - width)))


def unpack_small(whole, width):
    shards = whole.shape[0]
    joined = jnp.swapaxes(whole, 0, 1)
    taps = jnp.pad(joined[:5, :, :width].reshape(5, shards * width).astype(F32), ((0, 3), (0, 0)))
    gain = joined[5, :, : INNER // shards].reshape(1, INNER).astype(F32)
    input_gain = joined[6, :, : D // shards].reshape(1, D).astype(F32)
    own = HEADS // shards
    heads = joined[7, :, : 3 * own].reshape(shards, 3, own).swapaxes(0, 1).reshape(3, HEADS)
    heads = jnp.pad(heads.astype(F32), ((0, 5), (0, 128 - HEADS)))
    return taps, jnp.pad(gain, ((0, 7), (0, 0))), input_gain, heads


def on_device(
    inputs,
    segment_ids,
    out_grad,
    in_matrix,
    out_matrix,
    conv_taps,
    conv_bias,
    dt_bias,
    decay_log,
    skip_scale,
    mixer_gain,
    input_gain,
):
    shards, parts = lax.axis_size("fsdp"), lax.axis_size("ctx")
    place = lax.axis_index("ctx")
    units_low, cot = inputs[0], out_grad[0]
    seg_ids = segment_ids[0]
    length = units_low.shape[0]
    here = (shards, parts) == (4, PARTS)
    seg_row = segment_ids
    if here:
        (
            xs, y_local, incoming, b_rows, c_rows, dt, running, entering,
            kept, w_turned, out_whole, projected, normed_t, halo, taps, heads, gain, g_float, seg_lanes,
        ) = forward(
            in_matrix, out_matrix, units_low, seg_row,
            conv_taps.T, conv_bias, mixer_gain, input_gain, dt_bias, decay_log, skip_scale,
        )
        out_whole = out_whole.reshape(-1, D)
    else:
        units = units_low.astype(F32)
        inv_rms = lax.rsqrt(jnp.mean(units * units, axis=-1, keepdims=True) + epsilon)
        base_rows = units * inv_rms
        w_whole = jnp.pad(in_matrix, ((0, 0), (0, WIDTH - PROJ)))
        w_whole = lax.all_gather(w_whole, "fsdp", axis=0, tiled=True)
        out_whole = lax.all_gather(out_matrix, "fsdp", axis=0, tiled=True)
        rim_seg = passed_along(seg_ids[length - CONV + 1 :], "ctx", 1)
        small = pack_small(conv_taps, conv_bias, dt_bias, decay_log, skip_scale, mixer_gain, input_gain)
        taps, gain, g_float, heads = unpack_small(lax.all_gather(small, "fsdp"), conv_bias.shape[0])
        normed = (base_rows * g_float).astype(BF16)
        normed_t = normed.T
        projected = dot(normed, w_whole).astype(BF16)
        rim_rows = passed_along(projected[length - CONV + 1 :], "ctx", 1)
        halo = jnp.pad(rim_rows, ((PAD - CONV + 1, 0), (0, 0))).astype(F32)
        seg_ext = jnp.concatenate(
            [
                jnp.full((PAD - CONV + 1,), -1, jnp.int32),
                rim_seg,
                seg_ids,
                jnp.full((PAD,), -2, jnp.int32),
            ]
        )
        seg_lanes = jnp.broadcast_to(seg_ext[:, None], (length + 2 * PAD, 128))
        xs, y_local, state, b_rows, c_rows, dt, running, entering, keep = front(
            projected, halo, taps, heads, seg_lanes, seg_row
        )
        kept = lax.all_gather(keep, "ctx")
        incoming = joined_plainly(lax.all_gather(state, "ctx"), kept, place, True)
    mixer_t, dproj, dy, outgoing, column_sums, block_out, stats = tail(
        y_local, xs, projected, incoming, out_whole, c_rows, entering, heads, gain, cot, units_low
    )
    if not here:
        outgoing = joined_plainly(lax.all_gather(outgoing, "ctx"), kept, place, False)
    given = (
        projected, projected, halo, taps, heads, seg_lanes, seg_row, b_rows, c_rows, dt, running, dy, incoming, outgoing,
    )
    if here:
        d_in, d_out, input_grad, total = finish(
            given, normed_t, mixer_t.reshape(4, 2, SHARD, length), dproj, w_turned, cot, units_low, g_float, column_sums, stats, kept
        )
        sums = settle(d_in, d_out, total, length * shards * parts * D)
        return (block_out[None], input_grad[None], *sums)
    else:
        dproj, d_halo, d_taps, d_heads = back(given, dproj)
        returned = passed_along(d_halo.astype(BF16), "ctx", -1)
        last = lax.slice(dproj, (length - PAD, INNER), (length, INNER + XBC))
        last = (last.astype(F32) + returned.astype(F32)).astype(BF16)
        dproj = lax.dynamic_update_slice(dproj, last, (length - PAD, INNER))
        d_normed = dot_nt(dproj, w_whole)
        d_input_gain = jnp.sum(d_normed * base_rows, axis=0)
        d_base = d_normed * g_float
        d_units = inv_rms * (d_base - base_rows * jnp.mean(d_base * base_rows, axis=-1, keepdims=True))
        input_grad = (cot.astype(F32) + d_units).astype(BF16)

        def scattered(grad):
            return lax.psum_scatter(grad.astype(BF16), "fsdp", scatter_dimension=0, tiled=True)

        d_in = jnp.dot(normed_t, dproj, preferred_element_type=F32)[:, :PROJ]
        d_out = jnp.dot(mixer_t, cot, preferred_element_type=F32)
        d_in = lax.psum(scattered(d_in), "ctx").astype(F32)
        d_out = lax.psum(scattered(d_out), "ctx").astype(F32)
        total = lax.psum(small_sums(d_taps, column_sums, d_input_gain[None], d_heads, stats), ("fsdp", "ctx"))
    me = lax.axis_index("fsdp")

    def own(flat):
        size = flat.shape[-1] // shards
        return lax.dynamic_slice_in_dim(flat, me * size, size, flat.ndim - 1)

    skip_sums = jnp.sum(total[6, :INNER].reshape(HEADS, HDIM), axis=1)
    at = D + 256
    stat_sums = jnp.stack([total[7, at], total[7, at + 128]])
    rms_stats = jnp.sqrt(stat_sums / (length * shards * parts * D))
    return (
        block_out[None],
        input_grad[None],
        d_in,
        d_out,
        own(total[:4]).T,
        own(total[4]),
        own(total[7, D : D + HEADS]),
        own(total[7, D + 128 : D + 128 + HEADS]),
        own(skip_sums),
        own(total[5, :INNER]),
        own(total[7, :D]),
        rms_stats,
    )


def solution(mesh):
    return jax.shard_map(
        on_device,
        mesh=mesh,
        in_specs=(
            P("fsdp", "ctx", None),
            P("fsdp", "ctx"),
            P("fsdp", "ctx", None),
            P("fsdp", None),
            P("fsdp", None),
            P("fsdp", None),
            P("fsdp"),
            P("fsdp"),
            P("fsdp"),
            P("fsdp"),
            P("fsdp"),
            P("fsdp"),
        ),
        out_specs=(
            P("fsdp", "ctx", None),
            P("fsdp", "ctx", None),
            P("fsdp", None),
            P("fsdp", None),
            P("fsdp", None),
            P("fsdp"),
            P("fsdp"),
            P("fsdp"),
            P("fsdp"),
            P("fsdp"),
            P("fsdp"),
            P(),
        ),
        check_vma=False,
    )
```
